32 devices in a mesh: seq: 4 (over z), dp: 8 (over y, x, core).
Axes of the slice: x: 2, y: 2, z: 4, core: 2. Of those that a mesh axis runs over, the one named last changes fastest.
Arguments:
- x_heads: bfloat16 [16, 512, 1024], P('dp', None, 'seq'), may hold values from -6 to 6
- cotangent: bfloat16 [16, 512, 1024], P('dp', 'seq'), may hold values from -6 to 6
- doc_starts: int32 [16, 8], P('dp'), may hold values from 0 to 512, as said below
- norm_gain: bfloat16 [1024], P(('seq', 'dp')), may hold values from 0.5 to 1.5
- gelu_weight: bfloat16 [1024, 1536], P(('seq', 'dp')), may hold values from -0.1875 to 0.1875
- input_weight: bfloat16 [1024, 1536], P(('seq', 'dp')), may hold values from -0.1875 to 0.1875
- conv_weight: bfloat16 [1536, 4], P(('seq', 'dp')), may hold values from -3 to 3
- decay_weight: bfloat16 [1536, 1536], P(('seq', 'dp')), may hold values from -0.15625 to 0.15625
- decay_bias: bfloat16 [1536], P(('seq', 'dp')), may hold values from -3 to 3
- admit_weight: bfloat16 [1536, 1536], P(('seq', 'dp')), may hold values from -0.15625 to 0.15625
- admit_bias: bfloat16 [1536], P(('seq', 'dp')), may hold values from -3 to 3
- decay_rate: bfloat16 [1536], P(('seq', 'dp')), may hold values from 4 to 12
- mixer_output: bfloat16 [1536, 1024], P(('seq', 'dp')), may hold values from -0.4375 to 0.4375
- feed_gain: bfloat16 [1024], P(('seq', 'dp')), may hold values from 0.5 to 1.5
- feed_gate: bfloat16 [1024, 3072], P(('seq', 'dp')), may hold values from -0.1875 to 0.1875
- feed_up: bfloat16 [1024, 3072], P(('seq', 'dp')), may hold values from -0.1875 to 0.1875
- feed_down: bfloat16 [3072, 1024], P(('seq', 'dp')), may hold values from -0.21875 to 0.21875
Outputs:
- block_output: bfloat16 [16, 512, 1024], P('dp', 'seq')
- input_grad: bfloat16 [16, 512, 1024], P('dp', None, 'seq')
- norm_gain_grad: float32 [1024], P(('seq', 'dp'))
- gelu_weight_grad: float32 [1024, 1536], P(('seq', 'dp'))
- input_weight_grad: float32 [1024, 1536], P(('seq', 'dp'))
- conv_weight_grad: float32 [1536, 4], P(('seq', 'dp'))
- decay_weight_grad: float32 [1536, 1536], P(('seq', 'dp'))
- decay_bias_grad: float32 [1536], P(('seq', 'dp'))
- admit_weight_grad: float32 [1536, 1536], P(('seq', 'dp'))
- admit_bias_grad: float32 [1536], P(('seq', 'dp'))
- decay_rate_grad: float32 [1536], P(('seq', 'dp'))
- mixer_output_grad: float32 [1536, 1024], P(('seq', 'dp'))
- feed_gain_grad: float32 [1024], P(('seq', 'dp'))
- feed_gate_grad: float32 [1024, 3072], P(('seq', 'dp'))
- feed_up_grad: float32 [1024, 3072], P(('seq', 'dp'))
- feed_down_grad: float32 [3072, 1024], P(('seq', 'dp'))
- gate_mean: float32 [1536], P(('seq', 'dp'))
The draws below stay inside these ranges and needn't reach their ends.
Inputs may be any that keep to these rules, and one draw needn't show every extreme that they name: `doc_starts`: each row lists its document starts in increasing order, first 0, all distinct; unused entries at the end equal 512.
All inputs are finite; a program needn't handle non-finite values.
Results may differ from the reference program's by a relative error of at most 0.03.
Values may be sent and summed in bfloat16 or wider, within the bound.
A program may use at most 256 MiB of HBM per device.

```python
import jax
import jax.numpy as jnp
from jax import lax

D = 1024
LRU = 1536
FF = 3072
CONV = 4
NDOC = 8
ROWS_DEV = 2
SEQ = 512
ROWS = 16


def draw_doc_starts(key, part):
    key_pos, key_count, key_pick = jax.random.split(key, 3)
    row_keys = jax.random.split(key_pos, ROWS)

    def one_row(row_key):
        return jax.random.permutation(row_key, SEQ - 1)[:NDOC - 1] + 1
    picked = jax.vmap(one_row)(row_keys).astype(jnp.int32)
    counts = jax.random.randint(key_count, (ROWS, 1), 0, NDOC)
    slot_index = jnp.arange(NDOC - 1, dtype=jnp.int32)[None, :]
    chosen = jnp.where(slot_index < counts, picked, SEQ)
    single = jax.random.randint(key_pick, (ROWS // ROWS_DEV, 1), 0, ROWS_DEV)
    row_in_block = (jnp.arange(ROWS, dtype=jnp.int32) % ROWS_DEV).reshape(ROWS // ROWS_DEV, ROWS_DEV)
    lone_row = (row_in_block == single).reshape(ROWS, 1)
    chosen = jnp.sort(jnp.where(lone_row, SEQ, chosen), axis=1)
    return jnp.concatenate([jnp.zeros((ROWS, 1), jnp.int32), chosen], axis=1).astype(jnp.int32)


def levels(rng, extent, shards, low, top_value):
    gain, own = 1.0, jax.random.fold_in(rng, 6)
    for axis_at, blocks in shards:
        steps = jnp.exp(jax.random.uniform(jax.random.fold_in(own, axis_at), (blocks,), jnp.float32, low / len(shards), top_value / len(shards)))
        gain = gain * jnp.repeat(steps, extent[axis_at] // blocks).reshape([-1 if axis == axis_at else 1 for axis in range(len(extent))])
    return gain


def bell_draw(own_key, dims, spread, bound, pieces=(), held_as=jnp.bfloat16):
    drawn = jax.random.normal(own_key, dims, jnp.float32) * spread
    if len(pieces) > 0:
        drawn = levels(own_key, dims, pieces, -0.22, 0.18) * drawn
    return jnp.clip(drawn, min=-bound, max=bound).astype(held_as)


def setup_inputs(seed: int = 0) -> dict:
    seeds = jax.random.split(jax.random.key(seed), 18)
    return {
        "x_heads": bell_draw(seeds[0], (ROWS, SEQ, D), 1.0, 6.0, ((0, 8), (2, 4))),
        "cotangent": bell_draw(seeds[1], (ROWS, SEQ, D), 1.0, 6.0, ((0, 8), (1, 4))),
        "doc_starts": draw_doc_starts(jax.random.fold_in(seeds[17], 71), 0),
        "norm_gain": jnp.clip(1.0 + 0.1 * jax.random.normal(seeds[3], (D,), jnp.float32), 0.5, 1.5).astype(jnp.bfloat16),
        "gelu_weight": bell_draw(seeds[4], (D, LRU), D ** -0.5, 0.1875, ((0, 32),)),
        "input_weight": bell_draw(seeds[5], (D, LRU), D ** -0.5, 0.1875, ((0, 32),)),
        "conv_weight": bell_draw(seeds[6], (LRU, CONV), CONV ** -0.5, 3.0, ((0, 32),)),
        "decay_weight": bell_draw(seeds[7], (LRU, LRU), LRU ** -0.5, 0.15625, ((0, 32),)),
        "decay_bias": bell_draw(seeds[8], (LRU,), 0.5, 3.0, ((0, 32),)),
        "admit_weight": bell_draw(seeds[9], (LRU, LRU), LRU ** -0.5, 0.15625, ((0, 32),)),
        "admit_bias": bell_draw(seeds[10], (LRU,), 0.5, 3.0, ((0, 32),)),
        "decay_rate": jnp.clip(4.0 + 8.0 * jax.random.uniform(seeds[11], (LRU,), jnp.float32) ** levels(seeds[11], (LRU,), ((0, 32),), -0.2, 0.2), 4.0, 12.0).astype(jnp.bfloat16),
        "mixer_output": bell_draw(seeds[12], (LRU, D), (LRU // 8) ** -0.5, 0.4375, ((0, 32),)),
        "feed_gain": jnp.clip(1.0 + 0.1 * jax.random.normal(seeds[13], (D,), jnp.float32), 0.5, 1.5).astype(jnp.bfloat16),
        "feed_gate": bell_draw(seeds[14], (D, FF), D ** -0.5, 0.1875, ((0, 32),)),
        "feed_up": bell_draw(seeds[15], (D, FF), D ** -0.5, 0.1875, ((0, 32),)),
        "feed_down": bell_draw(seeds[16], (FF, D), (FF // 4) ** -0.5, 0.21875, ((0, 32),)),
    }


EPSILON = 1e-06
DECAY_SCALE = 8.0

@jax.custom_vjp
def low(v):
    return lax.optimization_barrier(v.astype(jnp.bfloat16)).astype(jnp.float32)

@jax.custom_vjp
def low_back(v):
    return v

def low_keep(v):
    return (low(v), None)

def low_pass(kept, grad):
    return (grad,)

def back_keep(v):
    return (v, None)

def back_low(kept, grad):
    return (low(grad),)
low.defvjp(low_keep, low_pass)
low_back.defvjp(back_keep, back_low)

def rms_norm(values, gain_vec):
    return values * lax.rsqrt(lax.optimization_barrier(jnp.mean(values * values, axis=-1, keepdims=True)) + EPSILON) * gain_vec

def smooth_gate(values):
    return jax.nn.gelu(values, approximate=True)

def compose(earlier, latter):
    return (earlier[0] * latter[0], latter[0] * earlier[1] + latter[1])

def since_start(doc_starts, positions):
    begins = lax.optimization_barrier(jnp.max(jnp.where(doc_starts[:, None, :] <= positions[None, :, None], doc_starts[:, None, :], 0), axis=-1))
    return positions[None, :] - begins

def coefficients(decay_pre, admit_pre, conv_vals, rate_vec, reset_mask):
    recall = jax.nn.sigmoid(decay_pre)
    admit_vals = jax.nn.sigmoid(admit_pre)
    log_decay = -DECAY_SCALE * recall * jax.nn.softplus(-rate_vec)
    decay_vals = jnp.exp(log_decay)
    keep_mask = 1.0 - reset_mask
    scale_in = reset_mask + keep_mask * jnp.sqrt(-jnp.expm1(2.0 * log_decay))
    return (decay_vals * keep_mask, scale_in * admit_vals * conv_vals, decay_vals)

def product(left, right):
    return jnp.einsum('rtd,df->rtf', left, right, precision=lax.Precision.HIGHEST)

def forward(stream_in, doc_starts, params):
    gain_one, gelu_full, input_full, conv_full, decay_full, decay_shift, admit_full, admit_shift, rate_full, mixer_full, gain_two, gate_full, up_full, down_full = params
    normed = low(rms_norm(stream_in, gain_one))
    gelu_vals = smooth_gate(low_back(product(normed, gelu_full)))
    branch = low_back(low(product(normed, input_full)))
    seq_len = stream_in.shape[1]
    since_here = since_start(doc_starts, jnp.arange(seq_len, dtype=jnp.int32))
    padded = jnp.pad(branch, ((0, 0), (CONV - 1, 0), (0, 0)))
    conv_vals = jnp.zeros_like(branch)
    for offset in range(CONV):
        window = padded[:, CONV - 1 - offset:CONV - 1 - offset + seq_len, :]
        conv_vals = conv_vals + conv_full[:, offset] * window * (since_here >= offset)[..., None].astype(jnp.float32)
    conv_low = low_back(low(conv_vals))
    decay_pre = low_back(product(conv_low, decay_full) + decay_shift)
    admit_pre = low_back(product(conv_low, admit_full) + admit_shift)
    reset_mask = (since_here == 0).astype(jnp.float32)[..., None]
    decay_eff, update, decay_vals = coefficients(decay_pre, admit_pre, conv_low, rate_full, reset_mask)
    unused, state_vals = lax.associative_scan(compose, (decay_eff, update), axis=1)
    mixed = low(state_vals * gelu_vals)
    middle = stream_in + low_back(product(mixed, mixer_full))
    normed_two = low(rms_norm(middle, gain_two))
    gate_pre = low_back(product(normed_two, gate_full))
    up_vals = low_back(product(normed_two, up_full))
    hidden = low(smooth_gate(gate_pre) * up_vals)
    return (middle + low_back(product(hidden, down_full)), lax.optimization_barrier(jnp.sum(decay_vals, axis=(0, 1))))

def reference(x_heads, cotangent, doc_starts, norm_gain, gelu_weight, input_weight, conv_weight, decay_weight, decay_bias, admit_weight, admit_bias, decay_rate, mixer_output, feed_gain, feed_gate, feed_up, feed_down):
    params = (norm_gain.astype(jnp.float32), gelu_weight.astype(jnp.float32), input_weight.astype(jnp.float32), conv_weight.astype(jnp.float32), decay_weight.astype(jnp.float32), decay_bias.astype(jnp.float32), admit_weight.astype(jnp.float32), admit_bias.astype(jnp.float32), decay_rate.astype(jnp.float32), mixer_output.astype(jnp.float32), feed_gain.astype(jnp.float32), feed_gate.astype(jnp.float32), feed_up.astype(jnp.float32), feed_down.astype(jnp.float32))
    group_size = 2
    stream = x_heads.astype(jnp.float32).reshape(ROWS // group_size, group_size, SEQ, D)
    grads_in = cotangent.astype(jnp.float32).reshape(ROWS // group_size, group_size, SEQ, D)
    starts_in = doc_starts.reshape(ROWS // group_size, group_size, NDOC)

    def one_group(running, group_item):
        grad_sums, decay_total = running
        stream_part, grad_part, starts_part = group_item

        def run_group(values, weights):
            return forward(values, starts_part, weights)
        out_part, pull, decay_part = jax.vjp(run_group, stream_part, params, has_aux=True)
        grad_stream, grad_params = pull(grad_part)
        grad_sums = jax.tree.map(lambda left, right: left + right, grad_sums, grad_params)
        return ((grad_sums, decay_total + decay_part), (out_part.astype(jnp.bfloat16), grad_stream.astype(jnp.bfloat16)))
    start_sums = jax.tree.map(jnp.zeros_like, params)
    (grad_sums, decay_total), (outputs, input_grads) = lax.scan(one_group, (start_sums, jnp.zeros((LRU,), jnp.float32)), (stream, grads_in, starts_in))
    gate_mean = decay_total / (ROWS * SEQ)
    return (outputs.reshape(ROWS, SEQ, D), input_grads.reshape(ROWS, SEQ, D), grad_sums[0], grad_sums[1], grad_sums[2], grad_sums[3], grad_sums[4], grad_sums[5], grad_sums[6], grad_sums[7], grad_sums[8], grad_sums[9], grad_sums[10], grad_sums[11], grad_sums[12], grad_sums[13], gate_mean)
```

```python
from functools import partial

import jax
import jax.numpy as jnp
from jax import lax
from jax.experimental import pallas as pl
from jax.experimental.pallas import tpu as pltpu
from jax.sharding import PartitionSpec as P

EPSILON = 1e-06
DECAY_SCALE = 8.0
ALL = ("seq", "dp")
F32 = jnp.float32
BF16 = jnp.bfloat16


def rms_norm(values, gain_vec):
    return (
        values * lax.rsqrt(jnp.mean(values * values, axis=-1, keepdims=True) + EPSILON) * gain_vec
    )


def smooth_gate(values):
    return jax.nn.gelu(values, approximate=True)


def compose(earlier, latter):
    return (earlier[0] * latter[0], latter[0] * earlier[1] + latter[1])


def since_start(doc_starts, positions):
    begins = jnp.max(
        jnp.where(doc_starts[:, None, :] <= positions[None, :, None], doc_starts[:, None, :], 0),
        axis=-1,
    )
    return positions[None, :] - begins


def coefficients(decay_pre, admit_pre, conv_vals, rate_vec, reset_mask):
    recall = jax.nn.sigmoid(decay_pre)
    admit_vals = jax.nn.sigmoid(admit_pre)
    log_decay = -DECAY_SCALE * recall * jax.nn.softplus(-rate_vec)
    decay_vals = jnp.exp(log_decay)
    keep_mask = 1.0 - reset_mask
    scale_in = reset_mask + keep_mask * jnp.sqrt(-jnp.expm1(2.0 * log_decay))
    return (decay_vals * keep_mask, scale_in * admit_vals * conv_vals, decay_vals)


def dot(left, right):
    return jnp.dot(left, right, preferred_element_type=F32)


def outer_sum(left, right):
    return lax.dot_general(left, right, (((0,), (0,)), ((), ())), preferred_element_type=F32)


def back_prod(grad_rows, weight):
    return lax.dot_general(
        grad_rows, weight, (((1,), (1,)), ((), ())), preferred_element_type=F32
    )


def gather_rows(shard):
    return lax.all_gather(shard, ALL, axis=0, tiled=True)


def scatter_rows(partial):
    return lax.psum_scatter(partial.astype(BF16), ALL, scatter_dimension=0, tiled=True).astype(F32)


def shift_seq(values, step, seq_count):
    pairs = [(i, i + step) for i in range(seq_count) if 0 <= i + step < seq_count]
    return lax.ppermute(values, "seq", pairs)


def pack_small(pieces):
    return jnp.concatenate([p.reshape(1, -1) for p in pieces], axis=1)


def split_small(packed, widths):
    out, at = [], 0
    for width in widths:
        out.append(packed[:, at : at + width])
        at += width
    return out


MESH = pl.DeviceIdType.MESH
PLANE = 2


def fast_shapes(shards, seq_count, dp_count):
    return dp_count == 2 * PLANE * PLANE and seq_count > 1 and all(
        s.shape[0] % 16 == 0 and s.shape[1] % 1024 == 0 for s in shards
    )


class Place:
    def __init__(self, seq_count):
        self.nz = seq_count
        self.z = lax.axis_index("seq")
        self.d = lax.axis_index("dp")
        self.c = lax.rem(self.d, 2)
        self.b = lax.rem(self.d // 2, 2)
        self.a = self.d // 4
        self.core = (self.z, self.d + 1 - 2 * self.c)
        self.peer = {
            "b": (self.z, self.d + 2 - 4 * self.b),
            "a": (self.z, self.d + 4 - 8 * self.a),
        }

    def at(self, z):
        return (z, self.d)

    def greet(self):
        barrier = pltpu.get_barrier_semaphore()
        others = [self.core, self.peer["a"], self.peer["b"]]
        others += [self.at(lax.rem(self.z + o, self.nz)) for o in range(1, self.nz)]
        for other in others:
            pl.semaphore_signal(barrier, inc=1, device_id=other, device_id_type=MESH)
        pl.semaphore_wait(barrier, len(others))


def step_cols(width):
    unit = width // 8
    return {"A": (0, 3 * unit), "B": (3 * unit, 6 * unit), "C": (6 * unit, width)}


def chunk_list(shapes):
    chunks = []
    for i, (rows, cols) in enumerate(shapes):
        wide = min(cols, 3072)
        tall = rows if wide < 3072 and rows <= 48 else (48 if wide < 3072 else 16)
        for c0 in range(0, cols, wide):
            for r0 in range(0, rows, tall):
                chunks.append((i, r0, tall, c0, wide))
    return chunks


class Gather:
    def __init__(self, place, outs, chunks, send, recv, done):
        self.p, self.outs, self.chunks = place, outs, chunks
        self.send, self.recv, self.done = send, recv, done
        self.started = []
        nz = place.nz
        self.depth = nz + 4

    def view(self, k, z, a, b, c, route):
        i, r0, nr, c0, nc = self.chunks[k]
        lo, hi = (0, nc) if route is None else step_cols(nc)[route]
        full = slice(None)
        one = lambda v: full if v is None else pl.ds(v, 1)
        return self.outs[i].at[
            one(z), one(a), one(b), one(c), pl.ds(r0, nr), pl.ds(c0 + lo, hi - lo)
        ]

    def copy(self, k, view, s_at, r_at, dev):
        return pltpu.make_async_remote_copy(
            view, view, self.send.at[k, s_at], self.recv.at[k, r_at], device_id=dev, device_id_type=MESH
        )

    def put(self, k, view, s_at, r_at, dev, cond=None):
        cp = self.copy(k, view, s_at, r_at, dev)
        if cond is None:
            cp.start()
        else:
            pl.when(cond)(cp.start)
        self.started.append((cp, cond))

    def take(self, k, view, r_at, cond=None):
        cp = self.copy(k, view, 0, r_at, self.p.core)
        if cond is None:
            cp.wait_recv()
        else:
            pl.when(cond)(cp.wait_recv)

    def base(self, route):
        return {"A": 0, "B": 16, "C": 32}[route] * self.p.nz // 4 + 0

    def sem(self, route, phase, z=0):
        nz = self.p.nz
        slot = {"first": 0, "up": 1, "down": 1 + nz, "mid": 1 + 2 * nz, "last": 1 + 3 * nz}[phase]
        return {"A": 0, "B": 1, "C": 2}[route] * (1 + 4 * nz) + slot + z

    @staticmethod
    def sem_count(nz):
        return 3 * (1 + 4 * nz) + 1

    def order(self, k, route):
        if route == "C":
            return ("a", "b") if k % 2 else ("b", "a")
        return ("b", "a") if route == "A" else ("a", "b")

    def z_unit(self, k, route, z):
        p = self.p
        first = self.order(k, route)[0]
        a = None if route != "C" and first == "a" else p.a
        b = None if route != "C" and first == "b" else p.b
        return self.view(k, z, a, b, p.c, route)

    def z_own(self, k, route):
        p = self.p
        unit = self.z_unit(k, route, p.z)
        self.put(k, unit, self.sem(route, "up", p.z), self.sem(route, "up", p.z), p.at(p.z + 1), p.z < p.nz - 1)
        self.put(k, unit, self.sem(route, "down", p.z), self.sem(route, "down", p.z), p.at(p.z - 1), p.z > 0)
        self.after(k, route, p.z, None)

    def after(self, k, route, z, cond):
        p = self.p
        first, second = self.order(k, route)
        dim = first if route == "C" else second
        name = "mid" if route == "C" else "last"
        self.put(k, self.z_unit(k, route, z), self.sem(route, name, z), self.sem(route, name, z), p.peer[dim], cond)

    def z_hop(self, k, route, h):
        p = self.p
        low, high = p.z - h, p.z + h
        has_low, has_high = low >= 0, high < p.nz
        low_at, high_at = jnp.maximum(low, 0), jnp.minimum(high, p.nz - 1)
        unit = self.z_unit(k, route, low_at)
        self.take(k, unit, self.sem(route, "up", low_at), has_low)
        if h < p.nz - 1:
            self.put(k, unit, self.sem(route, "up", low_at), self.sem(route, "up", low_at), p.at(p.z + 1), has_low & (p.z < p.nz - 1))
        self.after(k, route, low_at, has_low)
        unit = self.z_unit(k, route, high_at)
        self.take(k, unit, self.sem(route, "down", high_at), has_high)
        if h < p.nz - 1:
            self.put(k, unit, self.sem(route, "down", high_at), self.sem(route, "down", high_at), p.at(p.z - 1), has_high & (p.z > 0))
        self.after(k, route, high_at, has_high)

    def c_last(self, k, z, cond):
        p = self.p
        first, second = self.order(k, "C")
        a = None if first == "a" else p.a
        b = None if first == "b" else p.b
        peer_a = 1 - p.a if first == "a" else p.a
        peer_b = 1 - p.b if first == "b" else p.b
        self.take(k, self.view(k, z, peer_a, peer_b, p.c, "C"), self.sem("C", "mid", z), cond)
        self.put(k, self.view(k, z, a, b, p.c, "C"), self.sem("C", "last", z), self.sem("C", "last", z), p.peer[second], cond)

    def c_last_hop(self, k, h):
        p = self.p
        if h == 0:
            self.c_last(k, p.z, None)
            return
        low, high = p.z - h, p.z + h
        self.c_last(k, jnp.maximum(low, 0), low >= 0)
        self.c_last(k, jnp.minimum(high, p.nz - 1), high < p.nz)

    def stage(self, k, s):
        p, nz = self.p, self.p.nz
        if s == 0:
            for route in "AB":
                first = self.order(k, route)[0]
                at = self.sem(route, "first")
                self.put(k, self.view(k, p.z, p.a, p.b, p.c, route), at, at, p.peer[first])
            self.z_own(k, "C")
        if s == 1:
            for route in "AB":
                first = self.order(k, route)[0]
                a = 1 - p.a if first == "a" else p.a
                b = 1 - p.b if first == "b" else p.b
                self.take(k, self.view(k, p.z, a, b, p.c, route), self.sem(route, "first"))
                self.z_own(k, route)
        if 1 <= s < nz:
            self.z_hop(k, "C", s)
        if 2 <= s <= nz:
            self.z_hop(k, "A", s - 1)
            self.z_hop(k, "B", s - 1)
        if 2 <= s < nz + 2:
            self.c_last_hop(k, s - 2)
        if s == nz + 2:
            for z in range(nz):
                for route in "ABC":
                    second = self.order(k, route)[1]
                    a = 1 - p.a if second == "a" else None
                    b = 1 - p.b if second == "b" else None
                    self.take(k, self.view(k, z, a, b, p.c, route), self.sem(route, "last", z))
            at = self.sem_count(nz) - 1
            self.put(k, self.view(k, None, None, None, p.c, None), at, at, p.core)
        if s == nz + 3:
            at = self.sem_count(nz) - 1
            self.take(k, self.view(k, None, None, None, 1 - p.c, None), at)

    def tick(self, t):
        for s in range(self.depth - 1, -1, -1):
            if 0 <= t - s < len(self.chunks):
                self.stage(t - s, s)

    def ticks(self):
        return len(self.chunks) + self.depth - 1

    def finish(self):
        for cp, cond in self.started:
            if cond is None:
                cp.wait_send()
            else:
                pl.when(cond)(cp.wait_send)


def gather_kernel(seq_count, joins, chunks, *refs):
    n_src = sum(len(j) for j in joins)
    x_ref, small_ref, srcs = refs[0], refs[1], refs[2 : 2 + n_src]
    at = 2 + n_src
    xs_ref, small_out, outs = refs[at], refs[at + 1], refs[at + 2 : at + 2 + len(joins)]
    send, recv, own_sem, x_send, x_recv, s_send, s_recv = refs[at + 2 + len(joins) :]
    p = Place(seq_count)
    one = pl.ds
    copies = []
    k = 0
    for out, group in zip(outs, joins):
        col = 0
        for _ in group:
            src = srcs[k]
            rows, cols = src.shape[-2:]
            dst = out.at[one(p.z, 1), one(p.a, 1), one(p.b, 1), one(p.c, 1), :, one(col, cols)]
            copies.append(pltpu.make_async_copy(src, dst, own_sem.at[k]))
            col += cols
            k += 1
    tok, feat = xs_ref.shape[1], x_ref.shape[2]
    copies.append(
        pltpu.make_async_copy(
            x_ref.at[:, one(p.z * tok, tok), :], xs_ref.at[:, :, one(p.z * feat, feat)], own_sem.at[k]
        )
    )
    copies.append(pltpu.make_async_copy(small_ref, small_out.at[one(p.z, 1), one(p.d, 1)], own_sem.at[k + 1]))
    for cp in copies:
        cp.start()
    p.greet()
    x_moves = []
    for o in range(1, p.nz):
        to, frm = lax.rem(p.z + o, p.nz), lax.rem(p.z + p.nz - o, p.nz)
        cp = pltpu.make_async_remote_copy(
            x_ref.at[:, one(to * tok, tok), :],
            xs_ref.at[:, :, one(pl.multiple_of(p.z * feat, 128), feat)],
            x_send.at[o - 1],
            x_recv.at[o - 1],
            device_id=p.at(to),
            device_id_type=MESH,
        )
        cp.start()
        x_moves.append(cp)
    for cp in copies:
        cp.wait()

    def small_view(z, d, n):
        return small_out.at[one(z, 1), one(d, n)]

    s_moves = []

    def small_put(view, at, dev):
        cp = pltpu.make_async_remote_copy(view, view, s_send.at[at], s_recv.at[at], device_id=dev, device_id_type=MESH)
        cp.start()
        s_moves.append(cp)

    own, pair = p.d, p.d - p.c
    small_put(small_view(p.z, own, 1), 0, p.core)
    g = Gather(p, outs, chunks, send, recv, None)
    for t in range(g.ticks()):
        g.tick(t)
        if t == 0:
            s_moves[0].wait_recv()
            small_put(small_view(p.z, pair, 2), 1, p.peer["b"])
        if t == 1:
            s_moves[1].wait_recv()
            small_put(small_view(p.z, 4 * p.a, 4), 2, p.peer["a"])
        if t == 2:
            s_moves[2].wait_recv()
            for o in range(1, p.nz):
                small_put(small_view(p.z, 0, 8), 2 + o, p.at(lax.rem(p.z + o, p.nz)))
    for cp in s_moves[3:]:
        cp.wait_recv()
    for cp in s_moves:
        cp.wait_send()
    for cp in x_moves:
        cp.wait()
    g.finish()


def gather_all(x_heads, small, shard_groups, seq_count):
    rows_cols = [(g[0].shape[0], sum(s.shape[1] for s in g)) for g in shard_groups]
    chunks = chunk_list(rows_cols)
    row_count, row_len, feat = x_heads.shape
    tok = row_len // seq_count
    srcs = [s.reshape(1, 1, 1, 1, *s.shape) for g in shard_groups for s in g]
    hbm = pl.BlockSpec(memory_space=pltpu.HBM)
    out_shape = [
        jax.ShapeDtypeStruct((row_count, tok, feat * seq_count), BF16),
        jax.ShapeDtypeStruct((seq_count, 8, 8, 128), F32),
    ]
    out_shape += [jax.ShapeDtypeStruct((seq_count, PLANE, PLANE, 2, r, c), BF16) for r, c in rows_cols]
    sems = Gather.sem_count(seq_count)
    dma = pltpu.SemaphoreType.DMA
    outs = pl.pallas_call(
        partial(gather_kernel, seq_count, [[0] * len(g) for g in shard_groups], chunks),
        out_shape=out_shape,
        in_specs=[hbm] * (2 + len(srcs)),
        out_specs=[hbm] * len(out_shape),
        scratch_shapes=[
            dma((len(chunks), sems)),
            dma((len(chunks), sems)),
            dma((len(srcs) + 2,)),
            dma((seq_count,)),
            dma((seq_count,)),
            dma((seq_count + 3,)),
            dma((seq_count + 3,)),
        ],
        compiler_params=pltpu.CompilerParams(collective_id=0, has_side_effects=True),
        name="gather_weights",
    )(x_heads, small.reshape(1, 1, 8, 128), *srcs)
    full = [o.reshape(-1, c) for o, (r, c) in zip(outs[2:], rows_cols)]
    return outs[0], outs[1].reshape(seq_count * 8, 8 * 128), full


def local(
    x_heads,
    cotangent,
    doc_starts,
    norm_gain,
    gelu_weight,
    input_weight,
    conv_weight,
    decay_weight,
    decay_bias,
    admit_weight,
    admit_bias,
    decay_rate,
    mixer_output,
    feed_gain,
    feed_gate,
    feed_up,
    feed_down,
):
    seq_count = lax.axis_size("seq")
    dev_count = seq_count * lax.axis_size("dp")
    seq_at = lax.axis_index("seq")
    row_count, tok_count, model = cotangent.shape
    flat = row_count * tok_count
    lru = gelu_weight.shape[1]
    feed = feed_gate.shape[1]
    taps = conv_weight.shape[1]
    rim = taps - 1

    smalls = (norm_gain, conv_weight, decay_bias, admit_bias, decay_rate, feed_gain)
    groups = (
        (gelu_weight, input_weight),
        (decay_weight, admit_weight),
        (mixer_output,),
        (feed_gate, feed_up),
        (feed_down,),
    )
    shards = [jnp.concatenate(g, axis=1) for g in groups]
    small_row = pack_small(smalls)
    if fast_shapes(shards, seq_count, lax.axis_size("dp")):
        wide = jnp.pad(small_row.astype(F32), ((0, 0), (0, 1024 - small_row.shape[1])))
        stream, packed, full = gather_all(x_heads, wide, groups, seq_count)
    else:
        stream = lax.all_to_all(x_heads, "seq", split_axis=1, concat_axis=2, tiled=True)
        packed = lax.all_gather(small_row, ALL, axis=0, tiled=True).astype(F32)
        full = [gather_rows(s) for s in shards]
    gelu_input, decay_admit, mixer_full, gate_up, down_full = full
    parts = split_small(packed, [v.size for v in smalls])
    gain_one = parts[0].reshape(-1)
    conv_taps = parts[1].reshape(lru, taps)
    decay_shift, admit_shift, rate_vec, gain_two = [p.reshape(-1) for p in parts[2:]]

    stream_in = stream.reshape(flat, model).astype(F32)
    normed_one, norm_one_pull = jax.vjp(rms_norm, stream_in, gain_one)
    normed_low = normed_one.astype(BF16)
    both = dot(normed_low, gelu_input)
    gelu_vals, gelu_pull = jax.vjp(smooth_gate, both[:, :lru])
    branch = both[:, lru:].astype(BF16).reshape(row_count, tok_count, lru)
    halo = shift_seq(branch[:, tok_count - rim :, :], 1, seq_count)
    extended = jnp.concatenate([halo, branch], axis=1).astype(F32)
    positions = seq_at * tok_count + jnp.arange(tok_count + rim, dtype=jnp.int32)
    since_ext = since_start(doc_starts, positions)
    since_here = since_ext[:, :tok_count]
    conv_vals = jnp.zeros((row_count, tok_count, lru), F32)
    for k in range(taps):
        window = extended[:, rim - k : rim - k + tok_count, :]
        conv_vals = conv_vals + conv_taps[:, k] * window * (since_here >= k)[..., None].astype(F32)
    conv_low = conv_vals.astype(BF16)
    conv_flat = conv_low.reshape(flat, lru)
    gates = dot(conv_flat, decay_admit)
    decay_pre = (gates[:, :lru] + decay_shift).reshape(row_count, tok_count, lru)
    admit_pre = (gates[:, lru:] + admit_shift).reshape(row_count, tok_count, lru)
    reset_mask = (since_here == 0).astype(F32)[..., None]

    def coefs(dp, ap, cv, rv):
        return coefficients(dp, ap, cv, rv, reset_mask)

    (decay_eff, update, decay_vals), coef_pull = jax.vjp(
        coefs, decay_pre, admit_pre, conv_low.astype(F32), rate_vec
    )
    decay_prod, local_state = lax.associative_scan(compose, (decay_eff, update), axis=1)
    ends = jnp.stack([decay_prod[:, -1], local_state[:, -1]])
    all_ends = lax.all_gather(ends, "seq", axis=0)
    carry = jnp.zeros((row_count, lru), F32)
    carry_in = carry
    for i in range(seq_count - 1):
        carry = all_ends[i, 0] * carry + all_ends[i, 1]
        carry_in = jnp.where(seq_at == i + 1, carry, carry_in)
    state = local_state + decay_prod * carry_in[:, None, :]
    state_flat = state.reshape(flat, lru)
    mixed_low = (state_flat * gelu_vals).astype(BF16)
    middle = stream_in + dot(mixed_low, mixer_full)
    normed_two, norm_two_pull = jax.vjp(rms_norm, middle, gain_two)
    normed_two_low = normed_two.astype(BF16)
    gate_up_pre = dot(normed_two_low, gate_up)
    gate_act, gate_pull = jax.vjp(smooth_gate, gate_up_pre[:, :feed])
    up_vals = gate_up_pre[:, feed:]
    hidden_low = (gate_act * up_vals).astype(BF16)
    block_output = (middle + dot(hidden_low, down_full)).astype(BF16)
    block_output = block_output.reshape(row_count, tok_count, model)

    cot = cotangent.reshape(flat, model)
    down_grad = scatter_rows(outer_sum(hidden_low, cot))
    grad_hidden = back_prod(cot, down_full)
    grad_gate = gate_pull(grad_hidden * up_vals)[0].astype(BF16)
    grad_up = (grad_hidden * gate_act).astype(BF16)
    grad_gu = jnp.concatenate([grad_gate, grad_up], axis=1)
    gate_up_grad = scatter_rows(outer_sum(normed_two_low, grad_gu))
    grad_mid_norm, gain_two_grad = norm_two_pull(back_prod(grad_gu, gate_up))
    grad_middle = cot.astype(F32) + grad_mid_norm
    grad_out = grad_middle.astype(BF16)
    mixer_grad = scatter_rows(outer_sum(mixed_low, grad_out))
    grad_mixed = back_prod(grad_out, mixer_full)
    grad_gelu = gelu_pull(grad_mixed * state_flat)[0].astype(BF16)
    direct = (grad_mixed * gelu_vals).reshape(row_count, tok_count, lru)
    decay_next = jnp.concatenate([decay_eff[:, 1:, :], jnp.ones_like(decay_eff[:, :1, :])], axis=1)
    tail_prod, tail_state = lax.associative_scan(
        compose, (decay_next, direct), axis=1, reverse=True
    )
    back_ends = lax.all_gather(decay_eff[:, 0] * tail_state[:, 0], "seq", axis=0)
    back = jnp.zeros((row_count, lru), F32)
    back_in = back
    for i in range(seq_count - 1, 0, -1):
        back = all_ends[i, 0] * back + back_ends[i]
        back_in = jnp.where(seq_at == i - 1, back, back_in)
    adjoint = tail_state + tail_prod * back_in[:, None, :]
    state_prev = jnp.concatenate([carry_in[:, None, :], state[:, :-1, :]], axis=1)
    decay_pre_grad, admit_pre_grad, conv_direct, rate_grad = coef_pull(
        (adjoint * state_prev, adjoint, jnp.zeros_like(decay_vals))
    )
    grad_decay = decay_pre_grad.reshape(flat, lru).astype(BF16)
    grad_admit = admit_pre_grad.reshape(flat, lru).astype(BF16)
    grad_da = jnp.concatenate([grad_decay, grad_admit], axis=1)
    decay_admit_grad = scatter_rows(outer_sum(conv_flat, grad_da))
    decay_b_grad = jnp.sum(grad_decay, axis=0, dtype=F32)
    admit_b_grad = jnp.sum(grad_admit, axis=0, dtype=F32)
    grad_conv = (conv_direct.reshape(flat, lru) + back_prod(grad_da, decay_admit)).astype(BF16)
    grad_conv = grad_conv.reshape(row_count, tok_count, lru)
    grad_conv_wide = grad_conv.astype(F32)
    tap_grads = []
    for k in range(taps):
        window = extended[:, rim - k : rim - k + tok_count, :]
        mask = (since_here >= k)[..., None].astype(F32)
        tap_grads.append(jnp.sum(grad_conv_wide * window * mask, axis=(0, 1)))
    conv_grad = jnp.stack(tap_grads, axis=1)
    rim_after = shift_seq(grad_conv[:, :rim, :], -1, seq_count)
    grad_ext = jnp.concatenate([grad_conv, rim_after], axis=1).astype(F32)
    branch_grad = jnp.zeros((row_count, tok_count, lru), F32)
    for k in range(taps):
        ahead = (since_ext[:, k : k + tok_count] >= k)[..., None].astype(F32)
        branch_grad = branch_grad + conv_taps[:, k] * grad_ext[:, k : k + tok_count, :] * ahead
    branch_grad_low = branch_grad.reshape(flat, lru).astype(BF16)
    grad_gi = jnp.concatenate([grad_gelu, branch_grad_low], axis=1)
    gelu_input_grad = scatter_rows(outer_sum(normed_low, grad_gi))
    grad_in_norm, gain_one_grad = norm_one_pull(back_prod(grad_gi, gelu_input))
    input_grad_tok = (grad_middle + grad_in_norm).astype(BF16)
    input_grad_tok = input_grad_tok.reshape(row_count, tok_count, model)
    input_grad = lax.all_to_all(input_grad_tok, "seq", split_axis=2, concat_axis=1, tiled=True)
    gate_term = jnp.sum(decay_vals, axis=(0, 1)) / float(flat * dev_count)
    small_grads = (
        gain_one_grad,
        conv_grad,
        decay_b_grad,
        admit_b_grad,
        rate_grad,
        gain_two_grad,
        gate_term,
    )
    packed_grads = jnp.concatenate([g.reshape(dev_count, -1) for g in small_grads], axis=1)
    reduced = lax.psum_scatter(packed_grads, ALL, scatter_dimension=0, tiled=True)
    own = split_small(reduced, [g.size // dev_count for g in small_grads])
    return (
        block_output,
        input_grad,
        own[0].reshape(-1),
        gelu_input_grad[:, :lru],
        gelu_input_grad[:, lru:],
        own[1].reshape(-1, taps),
        decay_admit_grad[:, :lru],
        own[2].reshape(-1),
        decay_admit_grad[:, lru:],
        own[3].reshape(-1),
        own[4].reshape(-1),
        mixer_grad,
        own[5].reshape(-1),
        gate_up_grad[:, :feed],
        gate_up_grad[:, feed:],
        down_grad,
        own[6].reshape(-1),
    )


def solution(mesh):
    rows = P(ALL, None)
    vec = P(ALL)
    placed = (
        P("dp", None, "seq"),
        P("dp", "seq", None),
        P("dp", None),
        vec,
        rows,
        rows,
        rows,
        rows,
        vec,
        rows,
        vec,
        vec,
        rows,
        vec,
        rows,
        rows,
        rows,
    )
    outs = (
        P("dp", "seq", None),
        P("dp", None, "seq"),
        vec,
        rows,
        rows,
        rows,
        rows,
        vec,
        rows,
        vec,
        vec,
        rows,
        vec,
        rows,
        rows,
        rows,
        vec,
    )
    return jax.shard_map(local, mesh=mesh, in_specs=placed, out_specs=outs, check_vma=False)
```

```python
from functools import partial

import jax
import jax.numpy as jnp
from jax import lax
from jax.experimental import pallas as pl
from jax.experimental.pallas import tpu as pltpu
from jax.sharding import PartitionSpec as P

EPSILON = 1e-06
DECAY_SCALE = 8.0
ALL = ("seq", "dp")
F32 = jnp.float32
BF16 = jnp.bfloat16


def rms_norm(values, gain_vec):
    return (
        values * lax.rsqrt(jnp.mean(values * values, axis=-1, keepdims=True) + EPSILON) * gain_vec
    )


def smooth_gate(values):
    return jax.nn.gelu(values, approximate=True)


def compose(earlier, latter):
    return (earlier[0] * latter[0], latter[0] * earlier[1] + latter[1])


def since_start(doc_starts, positions):
    begins = jnp.max(
        jnp.where(doc_starts[:, None, :] <= positions[None, :, None], doc_starts[:, None, :], 0),
        axis=-1,
    )
    return positions[None, :] - begins


def coefficients(decay_pre, admit_pre, conv_vals, rate_vec, reset_mask):
    recall = jax.nn.sigmoid(decay_pre)
    admit_vals = jax.nn.sigmoid(admit_pre)
    log_decay = -DECAY_SCALE * recall * jax.nn.softplus(-rate_vec)
    decay_vals = jnp.exp(log_decay)
    keep_mask = 1.0 - reset_mask
    scale_in = reset_mask + keep_mask * jnp.sqrt(-jnp.expm1(2.0 * log_decay))
    return (decay_vals * keep_mask, scale_in * admit_vals * conv_vals, decay_vals)


def dot(left, right):
    return jnp.dot(left, right, preferred_element_type=F32)


def outer_sum(left, right):
    return lax.dot_general(left, right, (((0,), (0,)), ((), ())), preferred_element_type=F32)


def back_prod(grad_rows, weight):
    return lax.dot_general(
        grad_rows, weight, (((1,), (1,)), ((), ())), preferred_element_type=F32
    )


def gather_rows(shard):
    return lax.all_gather(shard, ALL, axis=0, tiled=True)


def scatter_rows(partial):
    return lax.psum_scatter(partial.astype(BF16), ALL, scatter_dimension=0, tiled=True).astype(F32)


def shift_seq(values, step, seq_count):
    pairs = [(i, i + step) for i in range(seq_count) if 0 <= i + step < seq_count]
    return lax.ppermute(values, "seq", pairs)


def pack_small(pieces):
    return jnp.concatenate([p.reshape(1, -1) for p in pieces], axis=1)


def split_small(packed, widths):
    out, at = [], 0
    for width in widths:
        out.append(packed[:, at : at + width])
        at += width
    return out


MESH = pl.DeviceIdType.MESH
PLANE = 2


def fast_shapes(shards, seq_count, dp_count):
    return dp_count == 2 * PLANE * PLANE and seq_count > 1 and all(
        s.shape[0] % 16 == 0 and s.shape[1] % 1024 == 0 for s in shards
    )


class Place:
    def __init__(self, seq_count):
        self.nz = seq_count
        self.z = lax.axis_index("seq")
        self.d = lax.axis_index("dp")
        self.c = lax.rem(self.d, 2)
        self.b = lax.rem(self.d // 2, 2)
        self.a = self.d // 4
        self.core = (self.z, self.d + 1 - 2 * self.c)
        self.peer = {
            "b": (self.z, self.d + 2 - 4 * self.b),
            "a": (self.z, self.d + 4 - 8 * self.a),
        }

    def at(self, z):
        return (z, self.d)

    def greet(self):
        barrier = pltpu.get_barrier_semaphore()
        others = [self.core, self.peer["a"], self.peer["b"]]
        others += [self.at(lax.rem(self.z + o, self.nz)) for o in range(1, self.nz)]
        for other in others:
            pl.semaphore_signal(barrier, inc=1, device_id=other, device_id_type=MESH)
        pl.semaphore_wait(barrier, len(others))


def step_cols(width):
    unit = width // 8
    return {"A": (0, 3 * unit), "B": (3 * unit, 6 * unit), "C": (6 * unit, width)}


def chunk_list(shapes):
    chunks = []
    for i, (rows, cols) in enumerate(shapes):
        wide = min(cols, 3072)
        tall = rows if wide < 3072 and rows <= 48 else (48 if wide < 3072 else 16)
        for c0 in range(0, cols, wide):
            for r0 in range(0, rows, tall):
                chunks.append((i, r0, tall, c0, wide))
    return chunks


class Gather:
    def __init__(self, place, outs, chunks, send, recv, done):
        self.p, self.outs, self.chunks = place, outs, chunks
        self.send, self.recv, self.done = send, recv, done
        self.started = []
        nz = place.nz
        self.depth = nz + 4

    def view(self, k, z, a, b, c, route):
        i, r0, nr, c0, nc = self.chunks[k]
        lo, hi = (0, nc) if route is None else step_cols(nc)[route]
        full = slice(None)
        one = lambda v: full if v is None else pl.ds(v, 1)
        return self.outs[i].at[
            one(z), one(a), one(b), one(c), pl.ds(r0, nr), pl.ds(c0 + lo, hi - lo)
        ]

    def copy(self, k, view, s_at, r_at, dev):
        return pltpu.make_async_remote_copy(
            view, view, self.send.at[k, s_at], self.recv.at[k, r_at], device_id=dev, device_id_type=MESH
        )

    def put(self, k, view, s_at, r_at, dev, cond=None):
        cp = self.copy(k, view, s_at, r_at, dev)
        if cond is None:
            cp.start()
        else:
            pl.when(cond)(cp.start)
        self.started.append((cp, cond))

    def take(self, k, view, r_at, cond=None):
        cp = self.copy(k, view, 0, r_at, self.p.core)
        if cond is None:
            cp.wait_recv()
        else:
            pl.when(cond)(cp.wait_recv)

    def base(self, route):
        return {"A": 0, "B": 16, "C": 32}[route] * self.p.nz // 4 + 0

    def sem(self, route, phase, z=0):
        nz = self.p.nz
        slot = {"first": 0, "up": 1, "down": 1 + nz, "mid": 1 + 2 * nz, "last": 1 + 3 * nz}[phase]
        return {"A": 0, "B": 1, "C": 2}[route] * (1 + 4 * nz) + slot + z

    @staticmethod
    def sem_count(nz):
        return 3 * (1 + 4 * nz) + 1

    def order(self, k, route):
        if route == "C":
            return ("a", "b") if k % 2 else ("b", "a")
        return ("b", "a") if route == "A" else ("a", "b")

    def z_unit(self, k, route, z):
        p = self.p
        first = self.order(k, route)[0]
        a = None if route != "C" and first == "a" else p.a
        b = None if route != "C" and first == "b" else p.b
        return self.view(k, z, a, b, p.c, route)

    def z_own(self, k, route):
        p = self.p
        unit = self.z_unit(k, route, p.z)
        self.put(k, unit, self.sem(route, "up", p.z), self.sem(route, "up", p.z), p.at(p.z + 1), p.z < p.nz - 1)
        self.put(k, unit, self.sem(route, "down", p.z), self.sem(route, "down", p.z), p.at(p.z - 1), p.z > 0)
        self.after(k, route, p.z, None)

    def after(self, k, route, z, cond):
        p = self.p
        first, second = self.order(k, route)
        dim = first if route == "C" else second
        name = "mid" if route == "C" else "last"
        self.put(k, self.z_unit(k, route, z), self.sem(route, name, z), self.sem(route, name, z), p.peer[dim], cond)

    def z_hop(self, k, route, h):
        p = self.p
        low, high = p.z - h, p.z + h
        has_low, has_high = low >= 0, high < p.nz
        low_at, high_at = jnp.maximum(low, 0), jnp.minimum(high, p.nz - 1)
        unit = self.z_unit(k, route, low_at)
        self.take(k, unit, self.sem(route, "up", low_at), has_low)
        if h < p.nz - 1:
            self.put(k, unit, self.sem(route, "up", low_at), self.sem(route, "up", low_at), p.at(p.z + 1), has_low & (p.z < p.nz - 1))
        self.after(k, route, low_at, has_low)
        unit = self.z_unit(k, route, high_at)
        self.take(k, unit, self.sem(route, "down", high_at), has_high)
        if h < p.nz - 1:
            self.put(k, unit, self.sem(route, "down", high_at), self.sem(route, "down", high_at), p.at(p.z - 1), has_high & (p.z > 0))
        self.after(k, route, high_at, has_high)

    def c_last(self, k, z, cond):
        p = self.p
        first, second = self.order(k, "C")
        a = None if first == "a" else p.a
        b = None if first == "b" else p.b
        peer_a = 1 - p.a if first == "a" else p.a
        peer_b = 1 - p.b if first == "b" else p.b
        self.take(k, self.view(k, z, peer_a, peer_b, p.c, "C"), self.sem("C", "mid", z), cond)
        self.put(k, self.view(k, z, a, b, p.c, "C"), self.sem("C", "last", z), self.sem("C", "last", z), p.peer[second], cond)

    def c_last_hop(self, k, h):
        p = self.p
        if h == 0:
            self.c_last(k, p.z, None)
            return
        low, high = p.z - h, p.z + h
        self.c_last(k, jnp.maximum(low, 0), low >= 0)
        self.c_last(k, jnp.minimum(high, p.nz - 1), high < p.nz)

    def stage(self, k, s):
        p, nz = self.p, self.p.nz
        if s == 0:
            for route in "AB":
                first = self.order(k, route)[0]
                at = self.sem(route, "first")
                self.put(k, self.view(k, p.z, p.a, p.b, p.c, route), at, at, p.peer[first])
            self.z_own(k, "C")
        if s == 1:
            for route in "AB":
                first = self.order(k, route)[0]
                a = 1 - p.a if first == "a" else p.a
                b = 1 - p.b if first == "b" else p.b
                self.take(k, self.view(k, p.z, a, b, p.c, route), self.sem(route, "first"))
                self.z_own(k, route)
        if 1 <= s < nz:
            self.z_hop(k, "C", s)
        if 2 <= s <= nz:
            self.z_hop(k, "A", s - 1)
            self.z_hop(k, "B", s - 1)
        if 2 <= s < nz + 2:
            self.c_last_hop(k, s - 2)
        if s == nz + 2:
            for z in range(nz):
                for route in "ABC":
                    second = self.order(k, route)[1]
                    a = 1 - p.a if second == "a" else None
                    b = 1 - p.b if second == "b" else None
                    self.take(k, self.view(k, z, a, b, p.c, route), self.sem(route, "last", z))
            at = self.sem_count(nz) - 1
            self.put(k, self.view(k, None, None, None, p.c, None), at, at, p.core)
        if s == nz + 3:
            at = self.sem_count(nz) - 1
            self.take(k, self.view(k, None, None, None, 1 - p.c, None), at)

    def tick(self, t):
        for s in range(self.depth - 1, -1, -1):
            if 0 <= t - s < len(self.chunks):
                self.stage(t - s, s)

    def ticks(self):
        return len(self.chunks) + self.depth - 1

    def finish(self):
        for cp, cond in self.started:
            if cond is None:
                cp.wait_send()
            else:
                pl.when(cond)(cp.wait_send)


def gather_kernel(seq_count, joins, chunks, *refs):
    n_src = sum(len(j) for j in joins)
    x_ref, small_ref, srcs = refs[0], refs[1], refs[2 : 2 + n_src]
    at = 2 + n_src
    xs_ref, small_out, outs = refs[at], refs[at + 1], refs[at + 2 : at + 2 + len(joins)]
    send, recv, own_sem, x_send, x_recv, s_send, s_recv = refs[at + 2 + len(joins) :]
    p = Place(seq_count)
    one = pl.ds
    copies = []
    k = 0
    for out, group in zip(outs, joins):
        col = 0
        for _ in group:
            src = srcs[k]
            rows, cols = src.shape[-2:]
            dst = out.at[one(p.z, 1), one(p.a, 1), one(p.b, 1), one(p.c, 1), :, one(col, cols)]
            copies.append(pltpu.make_async_copy(src, dst, own_sem.at[k]))
            col += cols
            k += 1
    tok, feat = xs_ref.shape[1], x_ref.shape[2]
    copies.append(
        pltpu.make_async_copy(
            x_ref.at[:, one(p.z * tok, tok), :], xs_ref.at[:, :, one(p.z * feat, feat)], own_sem.at[k]
        )
    )
    copies.append(pltpu.make_async_copy(small_ref, small_out.at[one(p.z, 1), one(p.d, 1)], own_sem.at[k + 1]))
    for cp in copies:
        cp.start()
    p.greet()
    x_moves = []
    for o in range(1, p.nz):
        to, frm = lax.rem(p.z + o, p.nz), lax.rem(p.z + p.nz - o, p.nz)
        cp = pltpu.make_async_remote_copy(
            x_ref.at[:, one(to * tok, tok), :],
            xs_ref.at[:, :, one(pl.multiple_of(p.z * feat, 128), feat)],
            x_send.at[o - 1],
            x_recv.at[o - 1],
            device_id=p.at(to),
            device_id_type=MESH,
        )
        cp.start()
        x_moves.append(cp)
    for cp in copies:
        cp.wait()

    def small_view(z, d, n):
        return small_out.at[one(z, 1), one(d, n)]

    s_moves = []

    def small_put(view, at, dev):
        cp = pltpu.make_async_remote_copy(view, view, s_send.at[at], s_recv.at[at], device_id=dev, device_id_type=MESH)
        cp.start()
        s_moves.append(cp)

    own, pair = p.d, p.d - p.c
    small_put(small_view(p.z, own, 1), 0, p.core)
    g = Gather(p, outs, chunks, send, recv, None)
    for t in range(g.ticks()):
        g.tick(t)
        if t == 0:
            s_moves[0].wait_recv()
            small_put(small_view(p.z, pair, 2), 1, p.peer["b"])
        if t == 1:
            s_moves[1].wait_recv()
            small_put(small_view(p.z, 4 * p.a, 4), 2, p.peer["a"])
        if t == 2:
            s_moves[2].wait_recv()
            for o in range(1, p.nz):
                small_put(small_view(p.z, 0, 8), 2 + o, p.at(lax.rem(p.z + o, p.nz)))
    for cp in s_moves[3:]:
        cp.wait_recv()
    for cp in s_moves:
        cp.wait_send()
    for cp in x_moves:
        cp.wait()
    g.finish()


def gather_all(x_heads, small, shard_groups, seq_count):
    rows_cols = [(g[0].shape[0], sum(s.shape[1] for s in g)) for g in shard_groups]
    chunks = chunk_list(rows_cols)
    row_count, row_len, feat = x_heads.shape
    tok = row_len // seq_count
    srcs = [s.reshape(1, 1, 1, 1, *s.shape) for g in shard_groups for s in g]
    hbm = pl.BlockSpec(memory_space=pltpu.HBM)
    out_shape = [
        jax.ShapeDtypeStruct((row_count, tok, feat * seq_count), BF16),
        jax.ShapeDtypeStruct((seq_count, 8, 8, 128), F32),
    ]
    out_shape += [jax.ShapeDtypeStruct((seq_count, PLANE, PLANE, 2, r, c), BF16) for r, c in rows_cols]
    sems = Gather.sem_count(seq_count)
    dma = pltpu.SemaphoreType.DMA
    outs = pl.pallas_call(
        partial(gather_kernel, seq_count, [[0] * len(g) for g in shard_groups], chunks),
        out_shape=out_shape,
        in_specs=[hbm] * (2 + len(srcs)),
        out_specs=[hbm] * len(out_shape),
        scratch_shapes=[
            dma((len(chunks), sems)),
            dma((len(chunks), sems)),
            dma((len(srcs) + 2,)),
            dma((seq_count,)),
            dma((seq_count,)),
            dma((seq_count + 3,)),
            dma((seq_count + 3,)),
        ],
        compiler_params=pltpu.CompilerParams(collective_id=0, has_side_effects=True),
        name="gather_weights",
    )(x_heads, small.reshape(1, 1, 8, 128), *srcs)
    full = [o.reshape(-1, c) for o, (r, c) in zip(outs[2:], rows_cols)]
    return outs[0], outs[1].reshape(seq_count * 8, 8 * 128), full


class Reduce:
    def __init__(self, place, chunks, bufs, send, recv):
        self.p, self.chunks, self.bufs = place, chunks, bufs
        self.send, self.recv = send, recv
        self.started = []
        self.depth = place.nz + 3

    @staticmethod
    def shapes(nz, r, w):
        wa, wc = 3 * w // 8, w // 4
        plane = PLANE
        return {
            "C": (nz, plane, plane, r, w),
            "YA": (nz, 1, plane, r, wa),
            "YB": (nz, plane, 1, r, wa),
            "YC": (nz, plane, 1, r, wc),
            "PC": (nz, 1, 1, r, wc),
            "UA": (nz, 1, plane, r, wa),
            "DA": (nz, 1, plane, r, wa),
            "UB": (nz, plane, 1, r, wa),
            "DB": (nz, plane, 1, r, wa),
            "UC": (nz, 1, 1, r, wc),
            "DC": (nz, 1, 1, r, wc),
            "XA": (1, 1, 1, r, wa),
            "XB": (1, 1, 1, r, wa),
        }

    NAMES = ("C", "YA", "YB", "YC", "PC", "UA", "DA", "UB", "DB", "UC", "DC", "XA", "XB")

    def buf(self, k, name):
        return self.bufs[k][name]

    def order(self, k, route):
        if route == "C":
            return ("a", "b") if k % 2 else ("b", "a")
        return ("b", "a") if route == "A" else ("a", "b")

    def cols(self, k, route):
        lo, hi = step_cols(self.chunks[k][4])[route]
        return pl.ds(lo, hi - lo)

    def part(self, k, route, z, a, b):
        full = slice(None)
        one = lambda v: full if v is None else v if isinstance(v, slice) else pl.ds(v, 1)
        return self.buf(k, "C").at[one(z), one(a), one(b), :, self.cols(k, route)]

    def put(self, k, name, src, dst, dev):
        self.copy(k, name, src, dst, dev).start()
        self.started.append((lambda: self.copy(k, name, src, dst, dev), None))

    def copy(self, k, name, src, dst, dev):
        at = self.NAMES.index(name)
        return pltpu.make_async_remote_copy(
            src, dst, self.send.at[k, at], self.recv.at[k, at], device_id=dev, device_id_type=MESH
        )

    def z_put(self, k, route, way, z):
        p = self.p
        name = ("U" if way > 0 else "D") + route
        span = slice(z + 1, p.nz) if way > 0 else slice(0, z)

        def make():
            a = p.a if route != "B" else None
            b = p.b if route != "A" else None
            src = self.part(k, route, span, a, b)
            return self.copy(k, name, src, self.buf(k, name).at[span], p.at(z + way))

        make().start()
        self.started.append((make, z))

    def take(self, k, name, dst):
        at = self.NAMES.index(name)
        pltpu.make_async_remote_copy(
            dst, dst, self.send.at[k, at], self.recv.at[k, at], device_id=self.p.core, device_id_type=MESH
        ).wait_recv()

    def add(self, into, other):
        n = into.shape[0]

        def one(t, carry):
            into[t] = into[t] + other[t]
            return carry

        lax.fori_loop(0, n, one, 0)

    def wave(self, k, route, s):
        p, nz = self.p, self.p.nz
        a = p.a if route != "B" else None
        b = p.b if route != "A" else None
        low, high = s - 1, nz - s

        @pl.when(p.z == low)
        def _():
            if low > 0:
                got = self.buf(k, "U" + route).at[low:nz]
                self.take(k, "U" + route, got)
                self.add(self.part(k, route, slice(low, nz), a, b), got)
            if low < nz - 1:
                self.z_put(k, route, 1, low)

        @pl.when(p.z == high)
        def _():
            if high < nz - 1:
                got = self.buf(k, "D" + route).at[0 : high + 1]
                self.take(k, "D" + route, got)
                self.add(self.part(k, route, slice(0, high + 1), a, b), got)
            if high > 0:
                self.z_put(k, route, -1, high)

    def plane_peer(self, k, dim):
        p = self.p
        return (1 - p.a if dim == "a" else None), (1 - p.b if dim == "b" else None)

    def stage(self, k, s):
        p, nz = self.p, self.p.nz
        if s == 0:
            self.begin(k)
        if s == 1:
            self.arrive(k)
            a, b = self.plane_peer(k, "a")
            self.put(k, "YA", self.part(k, "A", None, a, b), self.buf(k, "YA"), p.peer["a"])
            a, b = self.plane_peer(k, "b")
            self.put(k, "YB", self.part(k, "B", None, a, b), self.buf(k, "YB"), p.peer["b"])
            q = self.order(k, "C")[1]
            a, b = self.plane_peer(k, q)
            src = self.part(k, "C", None, a, b)
            self.put(k, "YC", src, self.yc(k), p.peer[q])
        if s == 2:
            self.take(k, "YA", self.buf(k, "YA"))
            self.add(self.part(k, "A", None, p.a, None), self.buf(k, "YA"))
            self.take(k, "YB", self.buf(k, "YB"))
            self.add(self.part(k, "B", None, None, p.b), self.buf(k, "YB"))
            first, q = self.order(k, "C")
            self.take(k, "YC", self.yc(k))
            self.add(self.part(k, "C", None, p.a if q == "a" else None, p.b if q == "b" else None), self.yc(k))
            a = 1 - p.a if first == "a" else p.a
            b = 1 - p.b if first == "b" else p.b
            self.put(k, "PC", self.part(k, "C", None, a, b), self.buf(k, "PC"), p.peer[first])
        if s == 3:
            self.take(k, "PC", self.buf(k, "PC"))
            self.add(self.part(k, "C", None, p.a, p.b), self.buf(k, "PC"))
        if 2 <= s <= nz + 1:
            self.wave(k, "A", s - 1)
            self.wave(k, "B", s - 1)
        if 3 <= s <= nz + 2:
            self.wave(k, "C", s - 2)
        if s == nz + 1:
            self.put(k, "XA", self.part(k, "A", p.z, p.a, 1 - p.b), self.buf(k, "XA"), p.peer["b"])
            self.put(k, "XB", self.part(k, "B", p.z, 1 - p.a, p.b), self.buf(k, "XB"), p.peer["a"])
        if s == nz + 2:
            self.take(k, "XA", self.buf(k, "XA"))
            self.take(k, "XB", self.buf(k, "XB"))
            self.deliver(k)

    def yc(self, k):
        buf = self.buf(k, "YC")
        nz, plane, _, r, w = buf.shape
        return buf if self.order(k, "C")[1] == "b" else buf.reshape(nz, 1, plane, r, w)

    def result(self, k, route):
        p = self.p
        block = self.part(k, route, p.z, p.a, p.b)[0, 0, 0].astype(F32)
        if route != "C":
            block = block + self.buf(k, "X" + route)[0, 0, 0].astype(F32)
        return block

    def tick(self, t):
        for s in range(self.depth - 1, -1, -1):
            if 0 <= t - s < len(self.chunks):
                self.stage(t - s, s)

    def ticks(self):
        return len(self.chunks) + self.depth - 1

    def finish(self):
        for make, z in self.started:
            if z is None:
                make().wait_send()
            else:

                @pl.when(self.p.z == z)
                def _():
                    make().wait_send()


class ReduceFromHbm(Reduce):
    def attach(self, partials, outs, load, load_sem, stage_out, out_sem):
        self.partials, self.outs = partials, outs
        self.load, self.load_sem = load, load_sem
        self.stage_out, self.out_sem = stage_out, out_sem
        self.loads, self.stores = {}, {}

    def shape_kind(self, k):
        return 0 if self.chunks[k][4] > 1024 else 1

    def begin(self, k):
        p = self.p
        i, r0, nr, c0, nc = self.chunks[k]
        src = lambda c: self.partials[i].at[:, :, :, c, pl.ds(r0, nr), pl.ds(c0, nc)]
        self.put(k, "C", src(1 - p.c), self.buf(k, "C"), p.core)
        kind = self.shape_kind(k)
        cp = pltpu.make_async_copy(src(p.c), self.load[kind].at[k % 2], self.load_sem.at[k % 2])
        cp.start()
        self.loads[k] = cp

    def arrive(self, k):
        self.loads[k].wait()
        self.take(k, "C", self.buf(k, "C"))
        self.add(self.buf(k, "C"), self.load[self.shape_kind(k)].at[k % 2])

    def deliver(self, k):
        i, r0, nr, c0, nc = self.chunks[k]
        kind = self.shape_kind(k)
        at = k % 2
        if k - 2 in self.stores:
            self.stores.pop(k - 2).wait()
        for route in "ABC":
            self.stage_out[kind][at, :, self.cols(k, route)] = self.result(k, route)
        cp = pltpu.make_async_copy(
            self.stage_out[kind].at[at], self.outs[i].at[pl.ds(r0, nr), pl.ds(c0, nc)], self.out_sem.at[at]
        )
        cp.start()
        self.stores[k] = cp

    def finish(self):
        for cp in self.stores.values():
            cp.wait()
        super().finish()


def reduce_kernel(seq_count, n_arr, chunks, kinds, *refs):
    xg_ref, small_ref, partials = refs[0], refs[1], refs[2 : 2 + n_arr]
    at = 2 + n_arr
    xo_ref, small_out, outs = refs[at], refs[at + 1], refs[at + 2 : at + 2 + n_arr]
    rest = list(refs[at + 2 + n_arr :])
    names = Reduce.NAMES
    pools = [dict(zip(names, rest[i * len(names) : (i + 1) * len(names)])) for i in range(2)]
    rest = rest[2 * len(names) :]
    load, stage_out = rest[0:2], rest[2:4]
    s_own, s_core, s_b, s_a, s_z, s_res = rest[4:10]
    send, recv, load_sem, out_sem, x_send, x_recv, s_send, s_recv, one_sem = rest[10:]
    p = Place(seq_count)
    one = pl.ds
    bufs, seen = [], [0, 0]
    for kind in kinds:
        j = seen[kind]
        seen[kind] += 1
        bufs.append({n: pools[kind][n].at[j] for n in names})
    r = ReduceFromHbm(p, chunks, bufs, send, recv)
    r.attach(partials, outs, load, load_sem, stage_out, out_sem)
    tok, feat = xg_ref.shape[1], xo_ref.shape[2]
    own_x = pltpu.make_async_copy(
        xg_ref.at[:, :, one(pl.multiple_of(p.z * feat, 128), feat)], xo_ref.at[:, one(p.z * tok, tok), :], one_sem.at[0]
    )
    own_s = pltpu.make_async_copy(small_ref, s_own, one_sem.at[1])
    own_x.start()
    own_s.start()
    p.greet()
    moves = []

    def small_put(at, src, dst, dev):
        cp = pltpu.make_async_remote_copy(src, dst, s_send.at[at], s_recv.at[at], device_id=dev, device_id_type=MESH)
        cp.start()
        moves.append(cp)
        return cp

    own_s.wait()
    c1 = small_put(0, s_own.at[:, :, :, 1 - p.c], s_core, p.core)
    z_moves = []
    for t in range(r.ticks()):
        r.tick(t)
        if t == 0:
            for o in range(1, p.nz):
                to = lax.rem(p.z + o, p.nz)
                cp = pltpu.make_async_remote_copy(
                    xg_ref.at[:, :, one(pl.multiple_of(to * feat, 128), feat)],
                    xo_ref.at[:, one(p.z * tok, tok), :],
                    x_send.at[o - 1],
                    x_recv.at[o - 1],
                    device_id=p.at(to),
                    device_id_type=MESH,
                )
                cp.start()
                z_moves.append(cp)
        if t == 1:
            c1.wait_recv()
            s_core[...] = s_core[...] + s_own[:, :, :, p.c]
            c2 = small_put(1, s_core.at[:, :, 1 - p.b], s_b, p.peer["b"])
        if t == 2:
            c2.wait_recv()
            s_b[...] = s_b[...] + s_core[:, :, p.b]
            c3 = small_put(2, s_b.at[:, 1 - p.a], s_a, p.peer["a"])
        if t == 3:
            c3.wait_recv()
            s_a[...] = s_a[...] + s_b[:, p.a]
            for o in range(1, p.nz):
                to = lax.rem(p.z + o, p.nz)
                small_put(2 + o, s_a.at[to], s_z.at[o - 1], p.at(to))
        if t == 4:
            total = s_a[p.z]
            for o in range(1, p.nz):
                moves[2 + o].wait_recv()
                total = total + s_z[o - 1]
            s_res[...] = total
    own_r = pltpu.make_async_copy(s_res, small_out, one_sem.at[1])
    own_r.start()
    own_x.wait()
    for cp in z_moves:
        cp.wait()
    for cp in moves:
        cp.wait_send()
    own_r.wait()
    r.finish()


def reduce_all(x_grad, small, partials, own_rows, seq_count):
    rows_cols = [(r, g.shape[1]) for g, r in zip(partials, own_rows)]
    chunks = []
    for i in (4, 3, 2, 1, 0):
        chunks += [c for c in chunk_list(rows_cols) if c[0] == i]
    kinds = [0 if c[4] > 1024 else 1 for c in chunks]
    sizes = [(16, 3072), (48, 1024)]
    row_count, tok, model = x_grad.shape
    hbm = pl.BlockSpec(memory_space=pltpu.HBM)
    srcs = [g.reshape(seq_count, PLANE, PLANE, 2, r, c) for g, (r, c) in zip(partials, rows_cols)]
    out_shape = [
        jax.ShapeDtypeStruct((row_count, tok * seq_count, model // seq_count), BF16),
        jax.ShapeDtypeStruct((8, 128), F32),
    ] + [jax.ShapeDtypeStruct(rc, F32) for rc in rows_cols]
    scratch = []
    for kind, (r, w) in enumerate(sizes):
        shapes = Reduce.shapes(seq_count, r, w)
        scratch += [pltpu.VMEM((kinds.count(kind), *shapes[n]), BF16) for n in Reduce.NAMES]
    scratch += [pltpu.VMEM((2, *Reduce.shapes(seq_count, r, w)["C"]), BF16) for r, w in sizes]
    scratch += [pltpu.VMEM((2, r, w), F32) for r, w in sizes]
    scratch += [
        pltpu.VMEM((seq_count, 2, 2, 2, 8, 128), F32),
        pltpu.VMEM((seq_count, 2, 2, 8, 128), F32),
        pltpu.VMEM((seq_count, 2, 8, 128), F32),
        pltpu.VMEM((seq_count, 8, 128), F32),
        pltpu.VMEM((seq_count, 8, 128), F32),
        pltpu.VMEM((8, 128), F32),
    ]
    dma = pltpu.SemaphoreType.DMA
    n_names = len(Reduce.NAMES)
    scratch += [
        dma((len(chunks), n_names)),
        dma((len(chunks), n_names)),
        dma((2,)),
        dma((2,)),
        dma((seq_count,)),
        dma((seq_count,)),
        dma((seq_count + 3,)),
        dma((seq_count + 3,)),
        dma((2,)),
    ]
    outs = pl.pallas_call(
        partial(reduce_kernel, seq_count, len(partials), chunks, kinds),
        out_shape=out_shape,
        in_specs=[hbm] * (2 + len(srcs)),
        out_specs=[hbm] * len(out_shape),
        scratch_shapes=scratch,
        compiler_params=pltpu.CompilerParams(
            collective_id=1, has_side_effects=True, vmem_limit_bytes=60 << 20
        ),
        name="reduce_gradients",
    )(x_grad, small.reshape(seq_count, 2, 2, 2, 8, 128), *srcs)
    return outs[0], outs[1], outs[2:]


def local(
    x_heads,
    cotangent,
    doc_starts,
    norm_gain,
    gelu_weight,
    input_weight,
    conv_weight,
    decay_weight,
    decay_bias,
    admit_weight,
    admit_bias,
    decay_rate,
    mixer_output,
    feed_gain,
    feed_gate,
    feed_up,
    feed_down,
):
    seq_count = lax.axis_size("seq")
    dev_count = seq_count * lax.axis_size("dp")
    seq_at = lax.axis_index("seq")
    row_count, tok_count, model = cotangent.shape
    flat = row_count * tok_count
    lru = gelu_weight.shape[1]
    feed = feed_gate.shape[1]
    taps = conv_weight.shape[1]
    rim = taps - 1

    smalls = (norm_gain, conv_weight, decay_bias, admit_bias, decay_rate, feed_gain)
    groups = (
        (gelu_weight, input_weight),
        (decay_weight, admit_weight),
        (mixer_output,),
        (feed_gate, feed_up),
        (feed_down,),
    )
    shards = [jnp.concatenate(g, axis=1) for g in groups]
    small_row = pack_small(smalls)
    fast = fast_shapes(shards, seq_count, lax.axis_size("dp"))
    if fast:
        wide = jnp.pad(small_row.astype(F32), ((0, 0), (0, 1024 - small_row.shape[1])))
        stream, packed, full = gather_all(x_heads, wide, groups, seq_count)
    else:
        stream = lax.all_to_all(x_heads, "seq", split_axis=1, concat_axis=2, tiled=True)
        packed = lax.all_gather(small_row, ALL, axis=0, tiled=True).astype(F32)
        full = [gather_rows(s) for s in shards]
    gelu_input, decay_admit, mixer_full, gate_up, down_full = full
    parts = split_small(packed, [v.size for v in smalls])
    gain_one = parts[0].reshape(-1)
    conv_taps = parts[1].reshape(lru, taps)
    decay_shift, admit_shift, rate_vec, gain_two = [p.reshape(-1) for p in parts[2:]]

    stream_in = stream.reshape(flat, model).astype(F32)
    normed_one, norm_one_pull = jax.vjp(rms_norm, stream_in, gain_one)
    normed_low = normed_one.astype(BF16)
    both = dot(normed_low, gelu_input)
    gelu_vals, gelu_pull = jax.vjp(smooth_gate, both[:, :lru])
    branch = both[:, lru:].astype(BF16).reshape(row_count, tok_count, lru)
    halo = shift_seq(branch[:, tok_count - rim :, :], 1, seq_count)
    extended = jnp.concatenate([halo, branch], axis=1).astype(F32)
    positions = seq_at * tok_count + jnp.arange(tok_count + rim, dtype=jnp.int32)
    since_ext = since_start(doc_starts, positions)
    since_here = since_ext[:, :tok_count]
    conv_vals = jnp.zeros((row_count, tok_count, lru), F32)
    for k in range(taps):
        window = extended[:, rim - k : rim - k + tok_count, :]
        conv_vals = conv_vals + conv_taps[:, k] * window * (since_here >= k)[..., None].astype(F32)
    conv_low = conv_vals.astype(BF16)
    conv_flat = conv_low.reshape(flat, lru)
    gates = dot(conv_flat, decay_admit)
    decay_pre = (gates[:, :lru] + decay_shift).reshape(row_count, tok_count, lru)
    admit_pre = (gates[:, lru:] + admit_shift).reshape(row_count, tok_count, lru)
    reset_mask = (since_here == 0).astype(F32)[..., None]

    def coefs(dp, ap, cv, rv):
        return coefficients(dp, ap, cv, rv, reset_mask)

    (decay_eff, update, decay_vals), coef_pull = jax.vjp(
        coefs, decay_pre, admit_pre, conv_low.astype(F32), rate_vec
    )
    decay_prod, local_state = lax.associative_scan(compose, (decay_eff, update), axis=1)
    ends = jnp.stack([decay_prod[:, -1], local_state[:, -1]])
    all_ends = lax.all_gather(ends, "seq", axis=0)
    carry = jnp.zeros((row_count, lru), F32)
    carry_in = carry
    for i in range(seq_count - 1):
        carry = all_ends[i, 0] * carry + all_ends[i, 1]
        carry_in = jnp.where(seq_at == i + 1, carry, carry_in)
    state = local_state + decay_prod * carry_in[:, None, :]
    state_flat = state.reshape(flat, lru)
    mixed_low = (state_flat * gelu_vals).astype(BF16)
    middle = stream_in + dot(mixed_low, mixer_full)
    normed_two, norm_two_pull = jax.vjp(rms_norm, middle, gain_two)
    normed_two_low = normed_two.astype(BF16)
    gate_up_pre = dot(normed_two_low, gate_up)
    gate_act, gate_pull = jax.vjp(smooth_gate, gate_up_pre[:, :feed])
    up_vals = gate_up_pre[:, feed:]
    hidden_low = (gate_act * up_vals).astype(BF16)
    block_output = (middle + dot(hidden_low, down_full)).astype(BF16)
    block_output = block_output.reshape(row_count, tok_count, model)

    cot = cotangent.reshape(flat, model)
    down_part = outer_sum(hidden_low, cot).astype(BF16)
    grad_hidden = back_prod(cot, down_full)
    grad_gate = gate_pull(grad_hidden * up_vals)[0].astype(BF16)
    grad_up = (grad_hidden * gate_act).astype(BF16)
    grad_gu = jnp.concatenate([grad_gate, grad_up], axis=1)
    gate_up_part = outer_sum(normed_two_low, grad_gu).astype(BF16)
    grad_mid_norm, gain_two_grad = norm_two_pull(back_prod(grad_gu, gate_up))
    grad_middle = cot.astype(F32) + grad_mid_norm
    grad_out = grad_middle.astype(BF16)
    mixer_part = outer_sum(mixed_low, grad_out).astype(BF16)
    grad_mixed = back_prod(grad_out, mixer_full)
    grad_gelu = gelu_pull(grad_mixed * state_flat)[0].astype(BF16)
    direct = (grad_mixed * gelu_vals).reshape(row_count, tok_count, lru)
    decay_next = jnp.concatenate([decay_eff[:, 1:, :], jnp.ones_like(decay_eff[:, :1, :])], axis=1)
    tail_prod, tail_state = lax.associative_scan(
        compose, (decay_next, direct), axis=1, reverse=True
    )
    back_ends = lax.all_gather(decay_eff[:, 0] * tail_state[:, 0], "seq", axis=0)
    back = jnp.zeros((row_count, lru), F32)
    back_in = back
    for i in range(seq_count - 1, 0, -1):
        back = all_ends[i, 0] * back + back_ends[i]
        back_in = jnp.where(seq_at == i - 1, back, back_in)
    adjoint = tail_state + tail_prod * back_in[:, None, :]
    state_prev = jnp.concatenate([carry_in[:, None, :], state[:, :-1, :]], axis=1)
    decay_pre_grad, admit_pre_grad, conv_direct, rate_grad = coef_pull(
        (adjoint * state_prev, adjoint, jnp.zeros_like(decay_vals))
    )
    grad_decay = decay_pre_grad.reshape(flat, lru).astype(BF16)
    grad_admit = admit_pre_grad.reshape(flat, lru).astype(BF16)
    grad_da = jnp.concatenate([grad_decay, grad_admit], axis=1)
    decay_admit_part = outer_sum(conv_flat, grad_da).astype(BF16)
    decay_b_grad = jnp.sum(grad_decay, axis=0, dtype=F32)
    admit_b_grad = jnp.sum(grad_admit, axis=0, dtype=F32)
    grad_conv = (conv_direct.reshape(flat, lru) + back_prod(grad_da, decay_admit)).astype(BF16)
    grad_conv = grad_conv.reshape(row_count, tok_count, lru)
    grad_conv_wide = grad_conv.astype(F32)
    tap_grads = []
    for k in range(taps):
        window = extended[:, rim - k : rim - k + tok_count, :]
        mask = (since_here >= k)[..., None].astype(F32)
        tap_grads.append(jnp.sum(grad_conv_wide * window * mask, axis=(0, 1)))
    conv_grad = jnp.stack(tap_grads, axis=1)
    rim_after = shift_seq(grad_conv[:, :rim, :], -1, seq_count)
    grad_ext = jnp.concatenate([grad_conv, rim_after], axis=1).astype(F32)
    branch_grad = jnp.zeros((row_count, tok_count, lru), F32)
    for k in range(taps):
        ahead = (since_ext[:, k : k + tok_count] >= k)[..., None].astype(F32)
        branch_grad = branch_grad + conv_taps[:, k] * grad_ext[:, k : k + tok_count, :] * ahead
    branch_grad_low = branch_grad.reshape(flat, lru).astype(BF16)
    grad_gi = jnp.concatenate([grad_gelu, branch_grad_low], axis=1)
    gelu_input_part = outer_sum(normed_low, grad_gi).astype(BF16)
    grad_in_norm, gain_one_grad = norm_one_pull(back_prod(grad_gi, gelu_input))
    input_grad_tok = (grad_middle + grad_in_norm).astype(BF16)
    input_grad_tok = input_grad_tok.reshape(row_count, tok_count, model)
    gate_term = jnp.sum(decay_vals, axis=(0, 1)) / float(flat * dev_count)
    small_grads = (
        gain_one_grad,
        conv_grad,
        decay_b_grad,
        admit_b_grad,
        rate_grad,
        gain_two_grad,
        gate_term,
    )
    packed_grads = jnp.concatenate([g.reshape(dev_count, -1) for g in small_grads], axis=1)
    partials = (gelu_input_part, decay_admit_part, mixer_part, gate_up_part, down_part)
    if fast:
        wide = jnp.pad(packed_grads, ((0, 0), (0, 1024 - packed_grads.shape[1])))
        input_grad, reduced, summed = reduce_all(
            input_grad_tok, wide, partials, [s.shape[0] for s in shards], seq_count
        )
        reduced = reduced.reshape(1, 1024)
    else:
        input_grad = lax.all_to_all(input_grad_tok, "seq", split_axis=2, concat_axis=1, tiled=True)
        reduced = lax.psum_scatter(packed_grads, ALL, scatter_dimension=0, tiled=True)
        summed = [scatter_rows(g) for g in partials]
    gelu_input_grad, decay_admit_grad, mixer_grad, gate_up_grad, down_grad = summed
    own = split_small(reduced, [g.size // dev_count for g in small_grads])
    return (
        block_output,
        input_grad,
        own[0].reshape(-1),
        gelu_input_grad[:, :lru],
        gelu_input_grad[:, lru:],
        own[1].reshape(-1, taps),
        decay_admit_grad[:, :lru],
        own[2].reshape(-1),
        decay_admit_grad[:, lru:],
        own[3].reshape(-1),
        own[4].reshape(-1),
        mixer_grad,
        own[5].reshape(-1),
        gate_up_grad[:, :feed],
        gate_up_grad[:, feed:],
        down_grad,
        own[6].reshape(-1),
    )


def solution(mesh):
    rows = P(ALL, None)
    vec = P(ALL)
    placed = (
        P("dp", None, "seq"),
        P("dp", "seq", None),
        P("dp", None),
        vec,
        rows,
        rows,
        rows,
        rows,
        vec,
        rows,
        vec,
        vec,
        rows,
        vec,
        rows,
        rows,
        rows,
    )
    outs = (
        P("dp", "seq", None),
        P("dp", None, "seq"),
        vec,
        rows,
        rows,
        rows,
        rows,
        vec,
        rows,
        vec,
        vec,
        rows,
        vec,
        rows,
        rows,
        rows,
        vec,
    )
    return jax.shard_map(local, mesh=mesh, in_specs=placed, out_specs=outs, check_vma=False)
```

```python
from functools import partial

import jax
import jax.numpy as jnp
from jax import lax
from jax.experimental import pallas as pl
from jax.experimental.pallas import tpu as pltpu
from jax.sharding import PartitionSpec as P

EPSILON = 1e-06
DECAY_SCALE = 8.0
ALL = ("seq", "dp")
F32 = jnp.float32
BF16 = jnp.bfloat16


def rms_norm(values, gain_vec):
    return (
        values * lax.rsqrt(jnp.mean(values * values, axis=-1, keepdims=True) + EPSILON) * gain_vec
    )


def smooth_gate(values):
    return jax.nn.gelu(values, approximate=True)


def since_start(doc_starts, positions):
    begins = jnp.max(
        jnp.where(doc_starts[:, None, :] <= positions[None, :, None], doc_starts[:, None, :], 0),
        axis=-1,
    )
    return positions[None, :] - begins


def coefficients(decay_pre, admit_pre, conv_vals, rate_vec, reset_mask):
    recall = jax.nn.sigmoid(decay_pre)
    admit_vals = jax.nn.sigmoid(admit_pre)
    log_decay = -DECAY_SCALE * recall * jax.nn.softplus(-rate_vec)
    decay_vals = jnp.exp(log_decay)
    keep_mask = 1.0 - reset_mask
    scale_in = reset_mask + keep_mask * jnp.sqrt(-jnp.expm1(2.0 * log_decay))
    return (decay_vals * keep_mask, scale_in * admit_vals * conv_vals, decay_vals)


def dot(left, right):
    return jnp.dot(left, right, preferred_element_type=F32)


def outer_sum(left, right):
    return lax.dot_general(left, right, (((0,), (0,)), ((), ())), preferred_element_type=F32)


def back_prod(grad_rows, weight):
    return lax.dot_general(
        grad_rows, weight, (((1,), (1,)), ((), ())), preferred_element_type=F32
    )


def gather_rows(shard):
    return lax.all_gather(shard, ALL, axis=0, tiled=True)


def scatter_rows(partial):
    return lax.psum_scatter(partial.astype(BF16), ALL, scatter_dimension=0, tiled=True).astype(F32)


def shift_seq(values, step, seq_count):
    pairs = [(i, i + step) for i in range(seq_count) if 0 <= i + step < seq_count]
    return lax.ppermute(values, "seq", pairs)


def pack_small(pieces):
    return jnp.concatenate([p.reshape(1, -1) for p in pieces], axis=1)


def split_small(packed, widths):
    out, at = [], 0
    for width in widths:
        out.append(packed[:, at : at + width])
        at += width
    return out


def scan_kernel(reverse, decay_ref, value_ref, prod_ref, state_ref):
    prod, state = decay_ref[0], value_ref[0]
    length = prod.shape[0]
    at = lax.broadcasted_iota(jnp.int32, prod.shape, 0)
    step = 1
    while step < length:
        inside = at < length - step if reverse else at >= step
        turn = length - step if reverse else step
        prod_far = jnp.where(inside, pltpu.roll(prod, turn, 0), 1.0)
        state_far = jnp.where(inside, pltpu.roll(state, turn, 0), 0.0)
        state = prod * state_far + state
        prod = prod * prod_far
        step *= 2
    prod_ref[0] = prod
    state_ref[0] = state


def scan_rows(decay, value, reverse=False):
    row_count, length, width = decay.shape
    block = pl.BlockSpec((1, length, 128), lambda r, c: (r, 0, c))
    return pl.pallas_call(
        partial(scan_kernel, reverse),
        grid=(row_count, width // 128),
        in_specs=[block, block],
        out_specs=[block, block],
        out_shape=[jax.ShapeDtypeStruct(decay.shape, F32)] * 2,
        name="scan_rows",
    )(decay, value)


MESH = pl.DeviceIdType.MESH
PLANE = 2


def fast_shapes(shards, seq_count, dp_count):
    return dp_count == 2 * PLANE * PLANE and seq_count > 1 and all(
        s.shape[0] % 16 == 0 and s.shape[1] % 1024 == 0 for s in shards
    )


class Place:
    def __init__(self, seq_count):
        self.nz = seq_count
        self.z = lax.axis_index("seq")
        self.d = lax.axis_index("dp")
        self.c = lax.rem(self.d, 2)
        self.b = lax.rem(self.d // 2, 2)
        self.a = self.d // 4
        self.core = (self.z, self.d + 1 - 2 * self.c)
        self.peer = {
            "b": (self.z, self.d + 2 - 4 * self.b),
            "a": (self.z, self.d + 4 - 8 * self.a),
        }

    def at(self, z):
        return (z, self.d)

    def greet(self):
        barrier = pltpu.get_barrier_semaphore()
        others = [self.core, self.peer["a"], self.peer["b"]]
        others += [self.at(lax.rem(self.z + o, self.nz)) for o in range(1, self.nz)]
        for other in others:
            pl.semaphore_signal(barrier, inc=1, device_id=other, device_id_type=MESH)
        pl.semaphore_wait(barrier, len(others))


def step_cols(width):
    unit = width // 8
    return {"A": (0, 3 * unit), "B": (3 * unit, 6 * unit), "C": (6 * unit, width)}


def chunk_list(shapes):
    chunks = []
    for i, (rows, cols) in enumerate(shapes):
        wide = min(cols, 3072)
        tall = rows if wide < 3072 and rows <= 48 else (48 if wide < 3072 else 16)
        for c0 in range(0, cols, wide):
            for r0 in range(0, rows, tall):
                chunks.append((i, r0, tall, c0, wide))
    return chunks


class Gather:
    def __init__(self, place, outs, chunks, send, recv, done):
        self.p, self.outs, self.chunks = place, outs, chunks
        self.send, self.recv, self.done = send, recv, done
        self.started = []
        nz = place.nz
        self.depth = nz + 4

    def view(self, k, z, a, b, c, route):
        i, r0, nr, c0, nc = self.chunks[k]
        lo, hi = (0, nc) if route is None else step_cols(nc)[route]
        full = slice(None)
        one = lambda v: full if v is None else pl.ds(v, 1)
        return self.outs[i].at[
            one(z), one(a), one(b), one(c), pl.ds(r0, nr), pl.ds(c0 + lo, hi - lo)
        ]

    def copy(self, k, view, s_at, r_at, dev):
        return pltpu.make_async_remote_copy(
            view, view, self.send.at[k, s_at], self.recv.at[k, r_at], device_id=dev, device_id_type=MESH
        )

    def put(self, k, view, s_at, r_at, dev, cond=None):
        cp = self.copy(k, view, s_at, r_at, dev)
        if cond is None:
            cp.start()
        else:
            pl.when(cond)(cp.start)
        self.started.append((cp, cond))

    def take(self, k, view, r_at, cond=None):
        cp = self.copy(k, view, 0, r_at, self.p.core)
        if cond is None:
            cp.wait_recv()
        else:
            pl.when(cond)(cp.wait_recv)

    def base(self, route):
        return {"A": 0, "B": 16, "C": 32}[route] * self.p.nz // 4 + 0

    def sem(self, route, phase, z=0):
        nz = self.p.nz
        slot = {"first": 0, "up": 1, "down": 1 + nz, "mid": 1 + 2 * nz, "last": 1 + 3 * nz}[phase]
        return {"A": 0, "B": 1, "C": 2}[route] * (1 + 4 * nz) + slot + z

    @staticmethod
    def sem_count(nz):
        return 3 * (1 + 4 * nz) + 1

    def order(self, k, route):
        if route == "C":
            return ("a", "b") if k % 2 else ("b", "a")
        return ("b", "a") if route == "A" else ("a", "b")

    def z_unit(self, k, route, z):
        p = self.p
        first = self.order(k, route)[0]
        a = None if route != "C" and first == "a" else p.a
        b = None if route != "C" and first == "b" else p.b
        return self.view(k, z, a, b, p.c, route)

    def z_own(self, k, route):
        p = self.p
        unit = self.z_unit(k, route, p.z)
        self.put(k, unit, self.sem(route, "up", p.z), self.sem(route, "up", p.z), p.at(p.z + 1), p.z < p.nz - 1)
        self.put(k, unit, self.sem(route, "down", p.z), self.sem(route, "down", p.z), p.at(p.z - 1), p.z > 0)
        self.after(k, route, p.z, None)

    def after(self, k, route, z, cond):
        p = self.p
        first, second = self.order(k, route)
        dim = first if route == "C" else second
        name = "mid" if route == "C" else "last"
        self.put(k, self.z_unit(k, route, z), self.sem(route, name, z), self.sem(route, name, z), p.peer[dim], cond)

    def z_hop(self, k, route, h):
        p = self.p
        low, high = p.z - h, p.z + h
        has_low, has_high = low >= 0, high < p.nz
        low_at, high_at = jnp.maximum(low, 0), jnp.minimum(high, p.nz - 1)
        unit = self.z_unit(k, route, low_at)
        self.take(k, unit, self.sem(route, "up", low_at), has_low)
        if h < p.nz - 1:
            self.put(k, unit, self.sem(route, "up", low_at), self.sem(route, "up", low_at), p.at(p.z + 1), has_low & (p.z < p.nz - 1))
        self.after(k, route, low_at, has_low)
        unit = self.z_unit(k, route, high_at)
        self.take(k, unit, self.sem(route, "down", high_at), has_high)
        if h < p.nz - 1:
            self.put(k, unit, self.sem(route, "down", high_at), self.sem(route, "down", high_at), p.at(p.z - 1), has_high & (p.z > 0))
        self.after(k, route, high_at, has_high)

    def c_last(self, k, z, cond):
        p = self.p
        first, second = self.order(k, "C")
        a = None if first == "a" else p.a
        b = None if first == "b" else p.b
        peer_a = 1 - p.a if first == "a" else p.a
        peer_b = 1 - p.b if first == "b" else p.b
        self.take(k, self.view(k, z, peer_a, peer_b, p.c, "C"), self.sem("C", "mid", z), cond)
        self.put(k, self.view(k, z, a, b, p.c, "C"), self.sem("C", "last", z), self.sem("C", "last", z), p.peer[second], cond)

    def c_last_hop(self, k, h):
        p = self.p
        if h == 0:
            self.c_last(k, p.z, None)
            return
        low, high = p.z - h, p.z + h
        self.c_last(k, jnp.maximum(low, 0), low >= 0)
        self.c_last(k, jnp.minimum(high, p.nz - 1), high < p.nz)

    def stage(self, k, s):
        p, nz = self.p, self.p.nz
        if s == 0:
            for route in "AB":
                first = self.order(k, route)[0]
                at = self.sem(route, "first")
                self.put(k, self.view(k, p.z, p.a, p.b, p.c, route), at, at, p.peer[first])
            self.z_own(k, "C")
        if s == 1:
            for route in "AB":
                first = self.order(k, route)[0]
                a = 1 - p.a if first == "a" else p.a
                b = 1 - p.b if first == "b" else p.b
                self.take(k, self.view(k, p.z, a, b, p.c, route), self.sem(route, "first"))
                self.z_own(k, route)
        if 1 <= s < nz:
            self.z_hop(k, "C", s)
        if 2 <= s <= nz:
            self.z_hop(k, "A", s - 1)
            self.z_hop(k, "B", s - 1)
        if 2 <= s < nz + 2:
            self.c_last_hop(k, s - 2)
        if s == nz + 2:
            for z in range(nz):
                for route in "ABC":
                    second = self.order(k, route)[1]
                    a = 1 - p.a if second == "a" else None
                    b = 1 - p.b if second == "b" else None
                    self.take(k, self.view(k, z, a, b, p.c, route), self.sem(route, "last", z))
            at = self.sem_count(nz) - 1
            self.put(k, self.view(k, None, None, None, p.c, None), at, at, p.core)
        if s == nz + 3:
            at = self.sem_count(nz) - 1
            self.take(k, self.view(k, None, None, None, 1 - p.c, None), at)

    def tick(self, t):
        for s in range(self.depth - 1, -1, -1):
            if 0 <= t - s < len(self.chunks):
                self.stage(t - s, s)

    def ticks(self):
        return len(self.chunks) + self.depth - 1

    def finish(self):
        for cp, cond in self.started:
            if cond is None:
                cp.wait_send()
            else:
                pl.when(cond)(cp.wait_send)


def gather_kernel(seq_count, joins, chunks, *refs):
    n_src = sum(len(j) for j in joins)
    x_ref, small_ref, srcs = refs[0], refs[1], refs[2 : 2 + n_src]
    at = 2 + n_src
    xs_ref, small_out, outs = refs[at], refs[at + 1], refs[at + 2 : at + 2 + len(joins)]
    send, recv, own_sem, x_send, x_recv, s_send, s_recv = refs[at + 2 + len(joins) :]
    p = Place(seq_count)
    one = pl.ds
    copies = []
    k = 0
    for out, group in zip(outs, joins):
        col = 0
        for _ in group:
            src = srcs[k]
            rows, cols = src.shape[-2:]
            dst = out.at[one(p.z, 1), one(p.a, 1), one(p.b, 1), one(p.c, 1), :, one(col, cols)]
            copies.append(pltpu.make_async_copy(src, dst, own_sem.at[k]))
            col += cols
            k += 1
    tok, feat = xs_ref.shape[1], x_ref.shape[2]
    copies.append(
        pltpu.make_async_copy(
            x_ref.at[:, one(p.z * tok, tok), :], xs_ref.at[:, :, one(p.z * feat, feat)], own_sem.at[k]
        )
    )
    copies.append(pltpu.make_async_copy(small_ref, small_out.at[one(p.z, 1), one(p.d, 1)], own_sem.at[k + 1]))
    for cp in copies:
        cp.start()
    p.greet()
    x_moves = []
    for o in range(1, p.nz):
        to, frm = lax.rem(p.z + o, p.nz), lax.rem(p.z + p.nz - o, p.nz)
        cp = pltpu.make_async_remote_copy(
            x_ref.at[:, one(to * tok, tok), :],
            xs_ref.at[:, :, one(pl.multiple_of(p.z * feat, 128), feat)],
            x_send.at[o - 1],
            x_recv.at[o - 1],
            device_id=p.at(to),
            device_id_type=MESH,
        )
        cp.start()
        x_moves.append(cp)
    for cp in copies:
        cp.wait()

    def small_view(z, d, n):
        return small_out.at[one(z, 1), one(d, n)]

    s_moves = []

    def small_put(view, at, dev):
        cp = pltpu.make_async_remote_copy(view, view, s_send.at[at], s_recv.at[at], device_id=dev, device_id_type=MESH)
        cp.start()
        s_moves.append(cp)

    own, pair = p.d, p.d - p.c
    small_put(small_view(p.z, own, 1), 0, p.core)
    g = Gather(p, outs, chunks, send, recv, None)
    for t in range(g.ticks()):
        g.tick(t)
        if t == 0:
            s_moves[0].wait_recv()
            small_put(small_view(p.z, pair, 2), 1, p.peer["b"])
        if t == 1:
            s_moves[1].wait_recv()
            small_put(small_view(p.z, 4 * p.a, 4), 2, p.peer["a"])
        if t == 2:
            s_moves[2].wait_recv()
            for o in range(1, p.nz):
                small_put(small_view(p.z, 0, 8), 2 + o, p.at(lax.rem(p.z + o, p.nz)))
    for cp in s_moves[3:]:
        cp.wait_recv()
    for cp in s_moves:
        cp.wait_send()
    for cp in x_moves:
        cp.wait()
    g.finish()


def gather_all(x_heads, small, shard_groups, seq_count):
    rows_cols = [(g[0].shape[0], sum(s.shape[1] for s in g)) for g in shard_groups]
    chunks = chunk_list(rows_cols)
    row_count, row_len, feat = x_heads.shape
    tok = row_len // seq_count
    srcs = [s.reshape(1, 1, 1, 1, *s.shape) for g in shard_groups for s in g]
    hbm = pl.BlockSpec(memory_space=pltpu.HBM)
    out_shape = [
        jax.ShapeDtypeStruct((row_count, tok, feat * seq_count), BF16),
        jax.ShapeDtypeStruct((seq_count, 8, 8, 128), F32),
    ]
    out_shape += [jax.ShapeDtypeStruct((seq_count, PLANE, PLANE, 2, r, c), BF16) for r, c in rows_cols]
    sems = Gather.sem_count(seq_count)
    dma = pltpu.SemaphoreType.DMA
    outs = pl.pallas_call(
        partial(gather_kernel, seq_count, [[0] * len(g) for g in shard_groups], chunks),
        out_shape=out_shape,
        in_specs=[hbm] * (2 + len(srcs)),
        out_specs=[hbm] * len(out_shape),
        scratch_shapes=[
            dma((len(chunks), sems)),
            dma((len(chunks), sems)),
            dma((len(srcs) + 2,)),
            dma((seq_count,)),
            dma((seq_count,)),
            dma((seq_count + 3,)),
            dma((seq_count + 3,)),
        ],
        compiler_params=pltpu.CompilerParams(collective_id=0, has_side_effects=True),
        name="gather_weights",
    )(x_heads, small.reshape(1, 1, 8, 128), *srcs)
    full = [o.reshape(-1, c) for o, (r, c) in zip(outs[2:], rows_cols)]
    return outs[0], outs[1].reshape(seq_count * 8, 8 * 128), full


class Reduce:
    def __init__(self, place, chunks, bufs, send, recv):
        self.p, self.chunks, self.bufs = place, chunks, bufs
        self.send, self.recv = send, recv
        self.started = []
        self.depth = place.nz + 3

    @staticmethod
    def shapes(nz, r, w):
        wa, wc = 3 * w // 8, w // 4
        plane = PLANE
        return {
            "C": (nz, plane, plane, r, w),
            "YA": (nz, 1, plane, r, wa),
            "YB": (nz, plane, 1, r, wa),
            "YC": (nz, plane, 1, r, wc),
            "PC": (nz, 1, 1, r, wc),
            "UA": (nz, 1, plane, r, wa),
            "DA": (nz, 1, plane, r, wa),
            "UB": (nz, plane, 1, r, wa),
            "DB": (nz, plane, 1, r, wa),
            "UC": (nz, 1, 1, r, wc),
            "DC": (nz, 1, 1, r, wc),
            "XA": (1, 1, 1, r, wa),
            "XB": (1, 1, 1, r, wa),
        }

    NAMES = ("C", "YA", "YB", "YC", "PC", "UA", "DA", "UB", "DB", "UC", "DC", "XA", "XB")

    def buf(self, k, name):
        return self.bufs[k][name]

    def order(self, k, route):
        if route == "C":
            return ("a", "b") if k % 2 else ("b", "a")
        return ("b", "a") if route == "A" else ("a", "b")

    def cols(self, k, route):
        lo, hi = step_cols(self.chunks[k][4])[route]
        return pl.ds(lo, hi - lo)

    def part(self, k, route, z, a, b):
        full = slice(None)
        one = lambda v: full if v is None else v if isinstance(v, slice) else pl.ds(v, 1)
        return self.buf(k, "C").at[one(z), one(a), one(b), :, self.cols(k, route)]

    def put(self, k, name, src, dst, dev):
        self.copy(k, name, src, dst, dev).start()
        self.started.append((lambda: self.copy(k, name, src, dst, dev), None))

    def copy(self, k, name, src, dst, dev):
        at = self.NAMES.index(name)
        return pltpu.make_async_remote_copy(
            src, dst, self.send.at[k, at], self.recv.at[k, at], device_id=dev, device_id_type=MESH
        )

    def z_put(self, k, route, way, z):
        p = self.p
        name = ("U" if way > 0 else "D") + route
        span = slice(z + 1, p.nz) if way > 0 else slice(0, z)

        def make():
            a = p.a if route != "B" else None
            b = p.b if route != "A" else None
            src = self.part(k, route, span, a, b)
            return self.copy(k, name, src, self.buf(k, name).at[span], p.at(z + way))

        make().start()
        self.started.append((make, z))

    def take(self, k, name, dst):
        at = self.NAMES.index(name)
        pltpu.make_async_remote_copy(
            dst, dst, self.send.at[k, at], self.recv.at[k, at], device_id=self.p.core, device_id_type=MESH
        ).wait_recv()

    def add(self, into, other):
        n = into.shape[0]

        def one(t, carry):
            into[t] = into[t] + other[t]
            return carry

        lax.fori_loop(0, n, one, 0)

    def wave(self, k, route, s):
        p, nz = self.p, self.p.nz
        a = p.a if route != "B" else None
        b = p.b if route != "A" else None
        low, high = s - 1, nz - s

        @pl.when(p.z == low)
        def _():
            if low > 0:
                got = self.buf(k, "U" + route).at[low:nz]
                self.take(k, "U" + route, got)
                self.add(self.part(k, route, slice(low, nz), a, b), got)
            if low < nz - 1:
                self.z_put(k, route, 1, low)

        @pl.when(p.z == high)
        def _():
            if high < nz - 1:
                got = self.buf(k, "D" + route).at[0 : high + 1]
                self.take(k, "D" + route, got)
                self.add(self.part(k, route, slice(0, high + 1), a, b), got)
            if high > 0:
                self.z_put(k, route, -1, high)

    def plane_peer(self, k, dim):
        p = self.p
        return (1 - p.a if dim == "a" else None), (1 - p.b if dim == "b" else None)

    def stage(self, k, s):
        p, nz = self.p, self.p.nz
        if s == 0:
            self.begin(k)
        if s == 1:
            self.arrive(k)
            a, b = self.plane_peer(k, "a")
            self.put(k, "YA", self.part(k, "A", None, a, b), self.buf(k, "YA"), p.peer["a"])
            a, b = self.plane_peer(k, "b")
            self.put(k, "YB", self.part(k, "B", None, a, b), self.buf(k, "YB"), p.peer["b"])
            q = self.order(k, "C")[1]
            a, b = self.plane_peer(k, q)
            src = self.part(k, "C", None, a, b)
            self.put(k, "YC", src, self.yc(k), p.peer[q])
        if s == 2:
            self.take(k, "YA", self.buf(k, "YA"))
            self.add(self.part(k, "A", None, p.a, None), self.buf(k, "YA"))
            self.take(k, "YB", self.buf(k, "YB"))
            self.add(self.part(k, "B", None, None, p.b), self.buf(k, "YB"))
            first, q = self.order(k, "C")
            self.take(k, "YC", self.yc(k))
            self.add(self.part(k, "C", None, p.a if q == "a" else None, p.b if q == "b" else None), self.yc(k))
            a = 1 - p.a if first == "a" else p.a
            b = 1 - p.b if first == "b" else p.b
            self.put(k, "PC", self.part(k, "C", None, a, b), self.buf(k, "PC"), p.peer[first])
        if s == 3:
            self.take(k, "PC", self.buf(k, "PC"))
            self.add(self.part(k, "C", None, p.a, p.b), self.buf(k, "PC"))
        if 2 <= s <= nz + 1:
            self.wave(k, "A", s - 1)
            self.wave(k, "B", s - 1)
        if 3 <= s <= nz + 2:
            self.wave(k, "C", s - 2)
        if s == nz + 1:
            self.put(k, "XA", self.part(k, "A", p.z, p.a, 1 - p.b), self.buf(k, "XA"), p.peer["b"])
            self.put(k, "XB", self.part(k, "B", p.z, 1 - p.a, p.b), self.buf(k, "XB"), p.peer["a"])
        if s == nz + 2:
            self.take(k, "XA", self.buf(k, "XA"))
            self.take(k, "XB", self.buf(k, "XB"))
            self.deliver(k)

    def yc(self, k):
        buf = self.buf(k, "YC")
        nz, plane, _, r, w = buf.shape
        return buf if self.order(k, "C")[1] == "b" else buf.reshape(nz, 1, plane, r, w)

    def result(self, k, route):
        p = self.p
        block = self.part(k, route, p.z, p.a, p.b)[0, 0, 0].astype(F32)
        if route != "C":
            block = block + self.buf(k, "X" + route)[0, 0, 0].astype(F32)
        return block

    def tick(self, t):
        for s in range(self.depth - 1, -1, -1):
            if 0 <= t - s < len(self.chunks):
                self.stage(t - s, s)

    def ticks(self):
        return len(self.chunks) + self.depth - 1

    def finish(self):
        for make, z in self.started:
            if z is None:
                make().wait_send()
            else:

                @pl.when(self.p.z == z)
                def _():
                    make().wait_send()


class ReduceFromHbm(Reduce):
    def attach(self, partials, outs, load, load_sem, stage_out, out_sem):
        self.partials, self.outs = partials, outs
        self.load, self.load_sem = load, load_sem
        self.stage_out, self.out_sem = stage_out, out_sem
        self.loads, self.stores = {}, {}

    def shape_kind(self, k):
        return 0 if self.chunks[k][4] > 1024 else 1

    def begin(self, k):
        p = self.p
        i, r0, nr, c0, nc = self.chunks[k]
        src = lambda c: self.partials[i].at[:, :, :, c, pl.ds(r0, nr), pl.ds(c0, nc)]
        self.put(k, "C", src(1 - p.c), self.buf(k, "C"), p.core)
        kind = self.shape_kind(k)
        cp = pltpu.make_async_copy(src(p.c), self.load[kind].at[k % 2], self.load_sem.at[k % 2])
        cp.start()
        self.loads[k] = cp

    def arrive(self, k):
        self.loads[k].wait()
        self.take(k, "C", self.buf(k, "C"))
        self.add(self.buf(k, "C"), self.load[self.shape_kind(k)].at[k % 2])

    def deliver(self, k):
        i, r0, nr, c0, nc = self.chunks[k]
        kind = self.shape_kind(k)
        at = k % 2
        if k - 2 in self.stores:
            self.stores.pop(k - 2).wait()
        for route in "ABC":
            self.stage_out[kind][at, :, self.cols(k, route)] = self.result(k, route)
        cp = pltpu.make_async_copy(
            self.stage_out[kind].at[at], self.outs[i].at[pl.ds(r0, nr), pl.ds(c0, nc)], self.out_sem.at[at]
        )
        cp.start()
        self.stores[k] = cp

    def finish(self):
        for cp in self.stores.values():
            cp.wait()
        super().finish()


def reduce_kernel(seq_count, n_arr, chunks, kinds, *refs):
    xg_ref, small_ref, partials = refs[0], refs[1], refs[2 : 2 + n_arr]
    at = 2 + n_arr
    xo_ref, small_out, outs = refs[at], refs[at + 1], refs[at + 2 : at + 2 + n_arr]
    rest = list(refs[at + 2 + n_arr :])
    names = Reduce.NAMES
    pools = [dict(zip(names, rest[i * len(names) : (i + 1) * len(names)])) for i in range(2)]
    rest = rest[2 * len(names) :]
    load, stage_out = rest[0:2], rest[2:4]
    s_own, s_core, s_b, s_a, s_z, s_res = rest[4:10]
    send, recv, load_sem, out_sem, x_send, x_recv, s_send, s_recv, one_sem = rest[10:]
    p = Place(seq_count)
    one = pl.ds
    bufs, seen = [], [0, 0]
    for kind in kinds:
        j = seen[kind]
        seen[kind] += 1
        bufs.append({n: pools[kind][n].at[j] for n in names})
    r = ReduceFromHbm(p, chunks, bufs, send, recv)
    r.attach(partials, outs, load, load_sem, stage_out, out_sem)
    tok, feat = xg_ref.shape[1], xo_ref.shape[2]
    own_x = pltpu.make_async_copy(
        xg_ref.at[:, :, one(pl.multiple_of(p.z * feat, 128), feat)], xo_ref.at[:, one(p.z * tok, tok), :], one_sem.at[0]
    )
    own_s = pltpu.make_async_copy(small_ref, s_own, one_sem.at[1])
    own_x.start()
    own_s.start()
    p.greet()
    moves = []

    def small_put(at, src, dst, dev):
        cp = pltpu.make_async_remote_copy(src, dst, s_send.at[at], s_recv.at[at], device_id=dev, device_id_type=MESH)
        cp.start()
        moves.append(cp)
        return cp

    own_s.wait()
    c1 = small_put(0, s_own.at[:, :, :, 1 - p.c], s_core, p.core)
    z_moves = []
    for t in range(r.ticks()):
        r.tick(t)
        if t == 0:
            for o in range(1, p.nz):
                to = lax.rem(p.z + o, p.nz)
                cp = pltpu.make_async_remote_copy(
                    xg_ref.at[:, :, one(pl.multiple_of(to * feat, 128), feat)],
                    xo_ref.at[:, one(p.z * tok, tok), :],
                    x_send.at[o - 1],
                    x_recv.at[o - 1],
                    device_id=p.at(to),
                    device_id_type=MESH,
                )
                cp.start()
                z_moves.append(cp)
        if t == 1:
            c1.wait_recv()
            s_core[...] = s_core[...] + s_own[:, :, :, p.c]
            c2 = small_put(1, s_core.at[:, :, 1 - p.b], s_b, p.peer["b"])
        if t == 2:
            c2.wait_recv()
            s_b[...] = s_b[...] + s_core[:, :, p.b]
            c3 = small_put(2, s_b.at[:, 1 - p.a], s_a, p.peer["a"])
        if t == 3:
            c3.wait_recv()
            s_a[...] = s_a[...] + s_b[:, p.a]
            for o in range(1, p.nz):
                to = lax.rem(p.z + o, p.nz)
                small_put(2 + o, s_a.at[to], s_z.at[o - 1], p.at(to))
        if t == 4:
            total = s_a[p.z]
            for o in range(1, p.nz):
                moves[2 + o].wait_recv()
                total = total + s_z[o - 1]
            s_res[...] = total
    own_r = pltpu.make_async_copy(s_res, small_out, one_sem.at[1])
    own_r.start()
    own_x.wait()
    for cp in z_moves:
        cp.wait()
    for cp in moves:
        cp.wait_send()
    own_r.wait()
    r.finish()


def reduce_all(x_grad, small, partials, own_rows, seq_count):
    rows_cols = [(r, g.shape[1]) for g, r in zip(partials, own_rows)]
    chunks = []
    for i in (4, 3, 2, 1, 0):
        chunks += [c for c in chunk_list(rows_cols) if c[0] == i]
    kinds = [0 if c[4] > 1024 else 1 for c in chunks]
    sizes = [(16, 3072), (48, 1024)]
    row_count, tok, model = x_grad.shape
    hbm = pl.BlockSpec(memory_space=pltpu.HBM)
    srcs = [g.reshape(seq_count, PLANE, PLANE, 2, r, c) for g, (r, c) in zip(partials, rows_cols)]
    out_shape = [
        jax.ShapeDtypeStruct((row_count, tok * seq_count, model // seq_count), BF16),
        jax.ShapeDtypeStruct((8, 128), F32),
    ] + [jax.ShapeDtypeStruct(rc, F32) for rc in rows_cols]
    scratch = []
    for kind, (r, w) in enumerate(sizes):
        shapes = Reduce.shapes(seq_count, r, w)
        scratch += [pltpu.VMEM((kinds.count(kind), *shapes[n]), BF16) for n in Reduce.NAMES]
    scratch += [pltpu.VMEM((2, *Reduce.shapes(seq_count, r, w)["C"]), BF16) for r, w in sizes]
    scratch += [pltpu.VMEM((2, r, w), F32) for r, w in sizes]
    scratch += [
        pltpu.VMEM((seq_count, 2, 2, 2, 8, 128), F32),
        pltpu.VMEM((seq_count, 2, 2, 8, 128), F32),
        pltpu.VMEM((seq_count, 2, 8, 128), F32),
        pltpu.VMEM((seq_count, 8, 128), F32),
        pltpu.VMEM((seq_count, 8, 128), F32),
        pltpu.VMEM((8, 128), F32),
    ]
    dma = pltpu.SemaphoreType.DMA
    n_names = len(Reduce.NAMES)
    scratch += [
        dma((len(chunks), n_names)),
        dma((len(chunks), n_names)),
        dma((2,)),
        dma((2,)),
        dma((seq_count,)),
        dma((seq_count,)),
        dma((seq_count + 3,)),
        dma((seq_count + 3,)),
        dma((2,)),
    ]
    outs = pl.pallas_call(
        partial(reduce_kernel, seq_count, len(partials), chunks, kinds),
        out_shape=out_shape,
        in_specs=[hbm] * (2 + len(srcs)),
        out_specs=[hbm] * len(out_shape),
        scratch_shapes=scratch,
        compiler_params=pltpu.CompilerParams(
            collective_id=1, has_side_effects=True, vmem_limit_bytes=60 << 20
        ),
        name="reduce_gradients",
    )(x_grad, small.reshape(seq_count, 2, 2, 2, 8, 128), *srcs)
    return outs[0], outs[1], outs[2:]


def local(
    x_heads,
    cotangent,
    doc_starts,
    norm_gain,
    gelu_weight,
    input_weight,
    conv_weight,
    decay_weight,
    decay_bias,
    admit_weight,
    admit_bias,
    decay_rate,
    mixer_output,
    feed_gain,
    feed_gate,
    feed_up,
    feed_down,
):
    seq_count = lax.axis_size("seq")
    dev_count = seq_count * lax.axis_size("dp")
    seq_at = lax.axis_index("seq")
    row_count, tok_count, model = cotangent.shape
    flat = row_count * tok_count
    lru = gelu_weight.shape[1]
    feed = feed_gate.shape[1]
    taps = conv_weight.shape[1]
    rim = taps - 1

    smalls = (norm_gain, conv_weight, decay_bias, admit_bias, decay_rate, feed_gain)
    groups = (
        (gelu_weight, input_weight),
        (decay_weight, admit_weight),
        (mixer_output,),
        (feed_gate, feed_up),
        (feed_down,),
    )
    shards = [jnp.concatenate(g, axis=1) for g in groups]
    small_row = pack_small(smalls)
    fast = fast_shapes(shards, seq_count, lax.axis_size("dp"))
    if fast:
        wide = jnp.pad(small_row.astype(F32), ((0, 0), (0, 1024 - small_row.shape[1])))
        stream, packed, full = gather_all(x_heads, wide, groups, seq_count)
    else:
        stream = lax.all_to_all(x_heads, "seq", split_axis=1, concat_axis=2, tiled=True)
        packed = lax.all_gather(small_row, ALL, axis=0, tiled=True).astype(F32)
        full = [gather_rows(s) for s in shards]
    gelu_input, decay_admit, mixer_full, gate_up, down_full = full
    parts = split_small(packed, [v.size for v in smalls])
    gain_one = parts[0].reshape(-1)
    conv_taps = parts[1].reshape(lru, taps)
    decay_shift, admit_shift, rate_vec, gain_two = [p.reshape(-1) for p in parts[2:]]

    stream_in = stream.reshape(flat, model).astype(F32)
    normed_one, norm_one_pull = jax.vjp(rms_norm, stream_in, gain_one)
    normed_low = normed_one.astype(BF16)
    both = dot(normed_low, gelu_input)
    gelu_vals, gelu_pull = jax.vjp(smooth_gate, both[:, :lru])
    branch = both[:, lru:].astype(BF16).reshape(row_count, tok_count, lru)
    halo = shift_seq(branch[:, tok_count - rim :, :], 1, seq_count)
    extended = jnp.concatenate([halo, branch], axis=1).astype(F32)
    positions = seq_at * tok_count + jnp.arange(tok_count + rim, dtype=jnp.int32)
    since_ext = since_start(doc_starts, positions)
    since_here = since_ext[:, :tok_count]
    conv_vals = jnp.zeros((row_count, tok_count, lru), F32)
    for k in range(taps):
        window = extended[:, rim - k : rim - k + tok_count, :]
        conv_vals = conv_vals + conv_taps[:, k] * window * (since_here >= k)[..., None].astype(F32)
    conv_low = conv_vals.astype(BF16)
    conv_flat = conv_low.reshape(flat, lru)
    gates = dot(conv_flat, decay_admit)
    decay_pre = (gates[:, :lru] + decay_shift).reshape(row_count, tok_count, lru)
    admit_pre = (gates[:, lru:] + admit_shift).reshape(row_count, tok_count, lru)
    reset_mask = (since_here == 0).astype(F32)[..., None]

    def coefs(dp, ap, cv, rv):
        return coefficients(dp, ap, cv, rv, reset_mask)

    (decay_eff, update, decay_vals), coef_pull = jax.vjp(
        coefs, decay_pre, admit_pre, conv_low.astype(F32), rate_vec
    )
    decay_prod, local_state = scan_rows(decay_eff, update)
    ends = jnp.stack([decay_prod[:, -1], local_state[:, -1]])
    all_ends = lax.all_gather(ends, "seq", axis=0)
    carry = jnp.zeros((row_count, lru), F32)
    carry_in = carry
    for i in range(seq_count - 1):
        carry = all_ends[i, 0] * carry + all_ends[i, 1]
        carry_in = jnp.where(seq_at == i + 1, carry, carry_in)
    state = local_state + decay_prod * carry_in[:, None, :]
    state_flat = state.reshape(flat, lru)
    mixed_low = (state_flat * gelu_vals).astype(BF16)
    middle = stream_in + dot(mixed_low, mixer_full)
    normed_two, norm_two_pull = jax.vjp(rms_norm, middle, gain_two)
    normed_two_low = normed_two.astype(BF16)
    gate_up_pre = dot(normed_two_low, gate_up)
    gate_act, gate_pull = jax.vjp(smooth_gate, gate_up_pre[:, :feed])
    up_vals = gate_up_pre[:, feed:]
    hidden_low = (gate_act * up_vals).astype(BF16)
    block_output = (middle + dot(hidden_low, down_full)).astype(BF16)
    block_output = block_output.reshape(row_count, tok_count, model)

    cot = cotangent.reshape(flat, model)
    down_part = outer_sum(hidden_low, cot).astype(BF16)
    grad_hidden = back_prod(cot, down_full)
    grad_gate = gate_pull(grad_hidden * up_vals)[0].astype(BF16)
    grad_up = (grad_hidden * gate_act).astype(BF16)
    grad_gu = jnp.concatenate([grad_gate, grad_up], axis=1)
    gate_up_part = outer_sum(normed_two_low, grad_gu).astype(BF16)
    grad_mid_norm, gain_two_grad = norm_two_pull(back_prod(grad_gu, gate_up))
    grad_middle = cot.astype(F32) + grad_mid_norm
    grad_out = grad_middle.astype(BF16)
    mixer_part = outer_sum(mixed_low, grad_out).astype(BF16)
    grad_mixed = back_prod(grad_out, mixer_full)
    grad_gelu = gelu_pull(grad_mixed * state_flat)[0].astype(BF16)
    direct = (grad_mixed * gelu_vals).reshape(row_count, tok_count, lru)
    decay_next = jnp.concatenate([decay_eff[:, 1:, :], jnp.ones_like(decay_eff[:, :1, :])], axis=1)
    tail_prod, tail_state = scan_rows(decay_next, direct, reverse=True)
    back_ends = lax.all_gather(decay_eff[:, 0] * tail_state[:, 0], "seq", axis=0)
    back = jnp.zeros((row_count, lru), F32)
    back_in = back
    for i in range(seq_count - 1, 0, -1):
        back = all_ends[i, 0] * back + back_ends[i]
        back_in = jnp.where(seq_at == i - 1, back, back_in)
    adjoint = tail_state + tail_prod * back_in[:, None, :]
    state_prev = jnp.concatenate([carry_in[:, None, :], state[:, :-1, :]], axis=1)
    decay_pre_grad, admit_pre_grad, conv_direct, rate_grad = coef_pull(
        (adjoint * state_prev, adjoint, jnp.zeros_like(decay_vals))
    )
    grad_decay = decay_pre_grad.reshape(flat, lru).astype(BF16)
    grad_admit = admit_pre_grad.reshape(flat, lru).astype(BF16)
    grad_da = jnp.concatenate([grad_decay, grad_admit], axis=1)
    decay_admit_part = outer_sum(conv_flat, grad_da).astype(BF16)
    decay_b_grad = jnp.sum(grad_decay, axis=0, dtype=F32)
    admit_b_grad = jnp.sum(grad_admit, axis=0, dtype=F32)
    grad_conv = (conv_direct.reshape(flat, lru) + back_prod(grad_da, decay_admit)).astype(BF16)
    grad_conv = grad_conv.reshape(row_count, tok_count, lru)
    grad_conv_wide = grad_conv.astype(F32)
    tap_grads = []
    for k in range(taps):
        window = extended[:, rim - k : rim - k + tok_count, :]
        mask = (since_here >= k)[..., None].astype(F32)
        tap_grads.append(jnp.sum(grad_conv_wide * window * mask, axis=(0, 1)))
    conv_grad = jnp.stack(tap_grads, axis=1)
    rim_after = shift_seq(grad_conv[:, :rim, :], -1, seq_count)
    grad_ext = jnp.concatenate([grad_conv, rim_after], axis=1).astype(F32)
    branch_grad = jnp.zeros((row_count, tok_count, lru), F32)
    for k in range(taps):
        ahead = (since_ext[:, k : k + tok_count] >= k)[..., None].astype(F32)
        branch_grad = branch_grad + conv_taps[:, k] * grad_ext[:, k : k + tok_count, :] * ahead
    branch_grad_low = branch_grad.reshape(flat, lru).astype(BF16)
    grad_gi = jnp.concatenate([grad_gelu, branch_grad_low], axis=1)
    gelu_input_part = outer_sum(normed_low, grad_gi).astype(BF16)
    grad_in_norm, gain_one_grad = norm_one_pull(back_prod(grad_gi, gelu_input))
    input_grad_tok = (grad_middle + grad_in_norm).astype(BF16)
    input_grad_tok = input_grad_tok.reshape(row_count, tok_count, model)
    gate_term = jnp.sum(decay_vals, axis=(0, 1)) / float(flat * dev_count)
    small_grads = (
        gain_one_grad,
        conv_grad,
        decay_b_grad,
        admit_b_grad,
        rate_grad,
        gain_two_grad,
        gate_term,
    )
    packed_grads = jnp.concatenate([g.reshape(dev_count, -1) for g in small_grads], axis=1)
    partials = (gelu_input_part, decay_admit_part, mixer_part, gate_up_part, down_part)
    if fast:
        wide = jnp.pad(packed_grads, ((0, 0), (0, 1024 - packed_grads.shape[1])))
        input_grad, reduced, summed = reduce_all(
            input_grad_tok, wide, partials, [s.shape[0] for s in shards], seq_count
        )
        reduced = reduced.reshape(1, 1024)
    else:
        input_grad = lax.all_to_all(input_grad_tok, "seq", split_axis=2, concat_axis=1, tiled=True)
        reduced = lax.psum_scatter(packed_grads, ALL, scatter_dimension=0, tiled=True)
        summed = [scatter_rows(g) for g in partials]
    gelu_input_grad, decay_admit_grad, mixer_grad, gate_up_grad, down_grad = summed
    own = split_small(reduced, [g.size // dev_count for g in small_grads])
    return (
        block_output,
        input_grad,
        own[0].reshape(-1),
        gelu_input_grad[:, :lru],
        gelu_input_grad[:, lru:],
        own[1].reshape(-1, taps),
        decay_admit_grad[:, :lru],
        own[2].reshape(-1),
        decay_admit_grad[:, lru:],
        own[3].reshape(-1),
        own[4].reshape(-1),
        mixer_grad,
        own[5].reshape(-1),
        gate_up_grad[:, :feed],
        gate_up_grad[:, feed:],
        down_grad,
        own[6].reshape(-1),
    )


def solution(mesh):
    rows = P(ALL, None)
    vec = P(ALL)
    placed = (
        P("dp", None, "seq"),
        P("dp", "seq", None),
        P("dp", None),
        vec,
        rows,
        rows,
        rows,
        rows,
        vec,
        rows,
        vec,
        vec,
        rows,
        vec,
        rows,
        rows,
        rows,
    )
    outs = (
        P("dp", "seq", None),
        P("dp", None, "seq"),
        vec,
        rows,
        rows,
        rows,
        rows,
        vec,
        rows,
        vec,
        vec,
        rows,
        vec,
        rows,
        rows,
        rows,
        vec,
    )
    return jax.shard_map(local, mesh=mesh, in_specs=placed, out_specs=outs, check_vma=False)
```

```python
from functools import partial

import jax
import jax.numpy as jnp
from jax import lax
from jax.experimental import pallas as pl
from jax.experimental.pallas import tpu as pltpu
from jax.sharding import PartitionSpec as P

EPSILON = 1e-06
DECAY_SCALE = 8.0
ALL = ("seq", "dp")
F32 = jnp.float32
BF16 = jnp.bfloat16
GELU_C = 0.7978845608028654
STARTS = (0, 0, 1, 1, 2, 2, 3, 4, 5, 6, 7, 8)


def rms_norm(values, gain_vec):
    return (
        values * lax.rsqrt(jnp.mean(values * values, axis=-1, keepdims=True) + EPSILON) * gain_vec
    )


def smooth_gate(values):
    return jax.nn.gelu(values, approximate=True)


def compose(earlier, latter):
    return (earlier[0] * latter[0], latter[0] * earlier[1] + latter[1])


def since_start(doc_starts, positions):
    begins = jnp.max(
        jnp.where(doc_starts[:, None, :] <= positions[None, :, None], doc_starts[:, None, :], 0),
        axis=-1,
    )
    return positions[None, :] - begins


def coefficients(decay_pre, admit_pre, conv_vals, rate_vec, reset_mask):
    recall = jax.nn.sigmoid(decay_pre)
    admit_vals = jax.nn.sigmoid(admit_pre)
    log_decay = -DECAY_SCALE * recall * jax.nn.softplus(-rate_vec)
    decay_vals = jnp.exp(log_decay)
    keep_mask = 1.0 - reset_mask
    scale_in = reset_mask + keep_mask * jnp.sqrt(-jnp.expm1(2.0 * log_decay))
    return (decay_vals * keep_mask, scale_in * admit_vals * conv_vals, decay_vals)


def dot(left, right):
    return jnp.dot(left, right, preferred_element_type=F32)


def outer_sum(left, right):
    return lax.dot_general(left, right, (((0,), (0,)), ((), ())), preferred_element_type=F32)


def back_prod(grad_rows, weight):
    return lax.dot_general(
        grad_rows, weight, (((1,), (1,)), ((), ())), preferred_element_type=F32
    )


def gather_rows(shard):
    return lax.all_gather(shard, ALL, axis=0, tiled=True)


def scatter_rows(partial):
    return lax.psum_scatter(partial.astype(BF16), ALL, scatter_dimension=0, tiled=True).astype(F32)


def shift_seq(values, step, seq_count):
    pairs = [(i, i + step) for i in range(seq_count) if 0 <= i + step < seq_count]
    return lax.ppermute(values, "seq", pairs)


def pack_small(pieces):
    return jnp.concatenate([p.reshape(1, -1) for p in pieces], axis=1)


def split_small(packed, widths):
    out, at = [], 0
    for width in widths:
        out.append(packed[:, at : at + width])
        at += width
    return out


def scan_kernel(reverse, decay_ref, value_ref, prod_ref, state_ref):
    prod, state = decay_ref[0], value_ref[0]
    length = prod.shape[0]
    at = lax.broadcasted_iota(jnp.int32, prod.shape, 0)
    step = 1
    while step < length:
        inside = at < length - step if reverse else at >= step
        turn = length - step if reverse else step
        prod_far = jnp.where(inside, pltpu.roll(prod, turn, 0), 1.0)
        state_far = jnp.where(inside, pltpu.roll(state, turn, 0), 0.0)
        state = prod * state_far + state
        prod = prod * prod_far
        step *= 2
    prod_ref[0] = prod
    state_ref[0] = state


def scan_rows(decay, value, reverse=False):
    row_count, length, width = decay.shape
    block = pl.BlockSpec((1, length, 128), lambda r, c: (r, 0, c))
    return pl.pallas_call(
        partial(scan_kernel, reverse),
        grid=(row_count, width // 128),
        in_specs=[block, block],
        out_specs=[block, block],
        out_shape=[jax.ShapeDtypeStruct(decay.shape, F32)] * 2,
        name="scan_rows",
    )(decay, value)


MESH = pl.DeviceIdType.MESH
PLANE = 2


def fast_shapes(shards, seq_count, dp_count, row_count, tok_count):
    if dp_count != 2 * PLANE * PLANE or seq_count < 2 or row_count != 2 or tok_count != 128:
        return False
    return all(s.shape[0] in (32, 48, 96) and s.shape[1] % 512 == 0 for s in shards)


class Place:
    def __init__(self, seq_count):
        self.nz = seq_count
        self.z = lax.axis_index("seq")
        self.d = lax.axis_index("dp")
        self.c = lax.rem(self.d, 2)
        self.b = lax.rem(self.d // 2, 2)
        self.a = self.d // 4
        self.core = (self.z, self.d + 1 - 2 * self.c)
        self.peer = {
            "b": (self.z, self.d + 2 - 4 * self.b),
            "a": (self.z, self.d + 4 - 8 * self.a),
        }

    def at(self, z):
        return (z, self.d)

    def greet(self):
        barrier = pltpu.get_barrier_semaphore()
        others = [self.core, self.peer["a"], self.peer["b"]]
        others += [self.at(lax.rem(self.z + o, self.nz)) for o in range(1, self.nz)]
        for other in others:
            pl.semaphore_signal(barrier, inc=1, device_id=other, device_id_type=MESH)
        pl.semaphore_wait(barrier, len(others))


def step_cols(width):
    unit = width // 8
    return {"A": (0, 3 * unit), "B": (3 * unit, 6 * unit), "C": (6 * unit, width)}


def chunk_list(shapes):
    chunks = []
    for i, (rows, cols) in enumerate(shapes):
        wide = min(cols, 3072)
        tall = rows if wide < 3072 and rows <= 48 else (48 if wide < 3072 else 16)
        for c0 in range(0, cols, wide):
            for r0 in range(0, rows, tall):
                chunks.append((i, r0, tall, c0, wide))
    return chunks


class Gather:
    def __init__(self, place, outs, chunks, send, recv, starts):
        self.p, self.outs, self.chunks = place, outs, chunks
        self.send, self.recv, self.starts = send, recv, starts
        self.started = []
        nz = place.nz
        self.depth = nz + 4

    def view(self, k, z, a, b, c, route):
        i, r0, nr, c0, nc = self.chunks[k]
        lo, hi = (0, nc) if route is None else step_cols(nc)[route]
        full = slice(None)
        one = lambda v: full if v is None else pl.ds(v, 1)
        return self.outs[i].at[
            one(z), one(a), one(b), one(c), pl.ds(r0, nr), pl.ds(c0 + lo, hi - lo)
        ]

    def copy(self, k, view, s_at, r_at, dev):
        return pltpu.make_async_remote_copy(
            view, view, self.send.at[k, s_at], self.recv.at[k, r_at], device_id=dev, device_id_type=MESH
        )

    def put(self, k, view, s_at, r_at, dev, cond=None):
        cp = self.copy(k, view, s_at, r_at, dev)
        if cond is None:
            cp.start()
        else:
            pl.when(cond)(cp.start)
        self.started.append((cp, cond))

    def take(self, k, view, r_at, cond=None):
        cp = self.copy(k, view, 0, r_at, self.p.core)
        if cond is None:
            cp.wait_recv()
        else:
            pl.when(cond)(cp.wait_recv)

    def sem(self, route, phase, z=0):
        nz = self.p.nz
        slot = {"first": 0, "up": 1, "down": 1 + nz, "mid": 1 + 2 * nz, "last": 1 + 3 * nz}[phase]
        return {"A": 0, "B": 1, "C": 2}[route] * (1 + 4 * nz) + slot + z

    @staticmethod
    def sem_count(nz):
        return 3 * (1 + 4 * nz) + 1

    def order(self, k, route):
        if route == "C":
            return ("a", "b") if k % 2 else ("b", "a")
        return ("b", "a") if route == "A" else ("a", "b")

    def z_unit(self, k, route, z):
        p = self.p
        first = self.order(k, route)[0]
        a = None if route != "C" and first == "a" else p.a
        b = None if route != "C" and first == "b" else p.b
        return self.view(k, z, a, b, p.c, route)

    def z_own(self, k, route):
        p = self.p
        unit = self.z_unit(k, route, p.z)
        self.put(k, unit, self.sem(route, "up", p.z), self.sem(route, "up", p.z), p.at(p.z + 1), p.z < p.nz - 1)
        self.put(k, unit, self.sem(route, "down", p.z), self.sem(route, "down", p.z), p.at(p.z - 1), p.z > 0)
        self.after(k, route, p.z, None)

    def after(self, k, route, z, cond):
        p = self.p
        first, second = self.order(k, route)
        dim = first if route == "C" else second
        name = "mid" if route == "C" else "last"
        self.put(k, self.z_unit(k, route, z), self.sem(route, name, z), self.sem(route, name, z), p.peer[dim], cond)

    def z_hop(self, k, route, h):
        p = self.p
        low, high = p.z - h, p.z + h
        has_low, has_high = low >= 0, high < p.nz
        low_at, high_at = jnp.maximum(low, 0), jnp.minimum(high, p.nz - 1)
        unit = self.z_unit(k, route, low_at)
        self.take(k, unit, self.sem(route, "up", low_at), has_low)
        if h < p.nz - 1:
            self.put(k, unit, self.sem(route, "up", low_at), self.sem(route, "up", low_at), p.at(p.z + 1), has_low & (p.z < p.nz - 1))
        self.after(k, route, low_at, has_low)
        unit = self.z_unit(k, route, high_at)
        self.take(k, unit, self.sem(route, "down", high_at), has_high)
        if h < p.nz - 1:
            self.put(k, unit, self.sem(route, "down", high_at), self.sem(route, "down", high_at), p.at(p.z - 1), has_high & (p.z > 0))
        self.after(k, route, high_at, has_high)

    def c_last(self, k, z, cond):
        p = self.p
        first, second = self.order(k, "C")
        a = None if first == "a" else p.a
        b = None if first == "b" else p.b
        peer_a = 1 - p.a if first == "a" else p.a
        peer_b = 1 - p.b if first == "b" else p.b
        self.take(k, self.view(k, z, peer_a, peer_b, p.c, "C"), self.sem("C", "mid", z), cond)
        self.put(k, self.view(k, z, a, b, p.c, "C"), self.sem("C", "last", z), self.sem("C", "last", z), p.peer[second], cond)

    def c_last_hop(self, k, h):
        p = self.p
        if h == 0:
            self.c_last(k, p.z, None)
            return
        low, high = p.z - h, p.z + h
        self.c_last(k, jnp.maximum(low, 0), low >= 0)
        self.c_last(k, jnp.minimum(high, p.nz - 1), high < p.nz)

    def stage(self, k, s):
        p, nz = self.p, self.p.nz
        if s == 0:
            for route in "AB":
                first = self.order(k, route)[0]
                at = self.sem(route, "first")
                self.put(k, self.view(k, p.z, p.a, p.b, p.c, route), at, at, p.peer[first])
            self.z_own(k, "C")
        if s == 1:
            for route in "AB":
                first = self.order(k, route)[0]
                a = 1 - p.a if first == "a" else p.a
                b = 1 - p.b if first == "b" else p.b
                self.take(k, self.view(k, p.z, a, b, p.c, route), self.sem(route, "first"))
                self.z_own(k, route)
        if 1 <= s < nz:
            self.z_hop(k, "C", s)
        if 2 <= s <= nz:
            self.z_hop(k, "A", s - 1)
            self.z_hop(k, "B", s - 1)
        if 2 <= s < nz + 2:
            self.c_last_hop(k, s - 2)
        if s == nz + 2:
            for z in range(nz):
                for route in "ABC":
                    second = self.order(k, route)[1]
                    a = 1 - p.a if second == "a" else None
                    b = 1 - p.b if second == "b" else None
                    self.take(k, self.view(k, z, a, b, p.c, route), self.sem(route, "last", z))
            at = self.sem_count(nz) - 1
            self.put(k, self.view(k, None, None, None, p.c, None), at, at, p.core)
        if s == nz + 3:
            at = self.sem_count(nz) - 1
            self.take(k, self.view(k, None, None, None, 1 - p.c, None), at)

    def tick(self, t):
        for k in range(len(self.chunks)):
            s = t - self.starts[k]
            if 0 <= s < self.depth:
                self.stage(k, s)

    def ticks(self):
        return max(self.starts) + self.depth

    def finish(self):
        for cp, cond in self.started:
            if cond is None:
                cp.wait_send()
            else:
                pl.when(cond)(cp.wait_send)


class Reduce:
    def __init__(self, place, chunks, bufs, send, recv):
        self.p, self.chunks, self.bufs = place, chunks, bufs
        self.send, self.recv = send, recv
        self.started = []
        self.depth = place.nz + 3

    @staticmethod
    def shapes(nz, r, w):
        wa, wc = 3 * w // 8, w // 4
        plane = PLANE
        return {
            "C": (nz, plane, plane, r, w),
            "YA": (nz, 1, plane, r, wa),
            "YB": (nz, plane, 1, r, wa),
            "YC": (nz, plane, 1, r, wc),
            "PC": (nz, 1, 1, r, wc),
            "UA": (nz, 1, plane, r, wa),
            "DA": (nz, 1, plane, r, wa),
            "UB": (nz, plane, 1, r, wa),
            "DB": (nz, plane, 1, r, wa),
            "UC": (nz, 1, 1, r, wc),
            "DC": (nz, 1, 1, r, wc),
            "XA": (1, 1, 1, r, wa),
            "XB": (1, 1, 1, r, wa),
        }

    NAMES = ("C", "YA", "YB", "YC", "PC", "UA", "DA", "UB", "DB", "UC", "DC", "XA", "XB")

    def buf(self, k, name):
        return self.bufs[k][name]

    def order(self, k, route):
        if route == "C":
            return ("a", "b") if k % 2 else ("b", "a")
        return ("b", "a") if route == "A" else ("a", "b")

    def cols(self, k, route):
        lo, hi = step_cols(self.chunks[k][4])[route]
        return pl.ds(lo, hi - lo)

    def part(self, k, route, z, a, b):
        full = slice(None)
        one = lambda v: full if v is None else v if isinstance(v, slice) else pl.ds(v, 1)
        return self.buf(k, "C").at[one(z), one(a), one(b), :, self.cols(k, route)]

    def put(self, k, name, src, dst, dev):
        self.copy(k, name, src, dst, dev).start()
        self.started.append((lambda: self.copy(k, name, src, dst, dev), None))

    def copy(self, k, name, src, dst, dev):
        at = self.NAMES.index(name)
        return pltpu.make_async_remote_copy(
            src, dst, self.send.at[k, at], self.recv.at[k, at], device_id=dev, device_id_type=MESH
        )

    def z_put(self, k, route, way, z):
        p = self.p
        name = ("U" if way > 0 else "D") + route
        span = slice(z + 1, p.nz) if way > 0 else slice(0, z)

        def make():
            a = p.a if route != "B" else None
            b = p.b if route != "A" else None
            src = self.part(k, route, span, a, b)
            return self.copy(k, name, src, self.buf(k, name).at[span], p.at(z + way))

        make().start()
        self.started.append((make, z))

    def take(self, k, name, dst):
        at = self.NAMES.index(name)
        pltpu.make_async_remote_copy(
            dst, dst, self.send.at[k, at], self.recv.at[k, at], device_id=self.p.core, device_id_type=MESH
        ).wait_recv()

    def add(self, into, other):
        n = into.shape[0]

        def one(t, carry):
            into[t] = into[t] + other[t]
            return carry

        lax.fori_loop(0, n, one, 0)

    def wave(self, k, route, s):
        p, nz = self.p, self.p.nz
        a = p.a if route != "B" else None
        b = p.b if route != "A" else None
        low, high = s - 1, nz - s

        @pl.when(p.z == low)
        def _():
            if low > 0:
                got = self.buf(k, "U" + route).at[low:nz]
                self.take(k, "U" + route, got)
                self.add(self.part(k, route, slice(low, nz), a, b), got)
            if low < nz - 1:
                self.z_put(k, route, 1, low)

        @pl.when(p.z == high)
        def _():
            if high < nz - 1:
                got = self.buf(k, "D" + route).at[0 : high + 1]
                self.take(k, "D" + route, got)
                self.add(self.part(k, route, slice(0, high + 1), a, b), got)
            if high > 0:
                self.z_put(k, route, -1, high)

    def plane_peer(self, k, dim):
        p = self.p
        return (1 - p.a if dim == "a" else None), (1 - p.b if dim == "b" else None)

    def stage(self, k, s):
        p, nz = self.p, self.p.nz
        if s == 0:
            self.begin(k)
        if s == 1:
            self.arrive(k)
            a, b = self.plane_peer(k, "a")
            self.put(k, "YA", self.part(k, "A", None, a, b), self.buf(k, "YA"), p.peer["a"])
            a, b = self.plane_peer(k, "b")
            self.put(k, "YB", self.part(k, "B", None, a, b), self.buf(k, "YB"), p.peer["b"])
            q = self.order(k, "C")[1]
            a, b = self.plane_peer(k, q)
            src = self.part(k, "C", None, a, b)
            self.put(k, "YC", src, self.yc(k), p.peer[q])
        if s == 2:
            self.take(k, "YA", self.buf(k, "YA"))
            self.add(self.part(k, "A", None, p.a, None), self.buf(k, "YA"))
            self.take(k, "YB", self.buf(k, "YB"))
            self.add(self.part(k, "B", None, None, p.b), self.buf(k, "YB"))
            first, q = self.order(k, "C")
            self.take(k, "YC", self.yc(k))
            self.add(self.part(k, "C", None, p.a if q == "a" else None, p.b if q == "b" else None), self.yc(k))
            a = 1 - p.a if first == "a" else p.a
            b = 1 - p.b if first == "b" else p.b
            self.put(k, "PC", self.part(k, "C", None, a, b), self.buf(k, "PC"), p.peer[first])
        if s == 3:
            self.take(k, "PC", self.buf(k, "PC"))
            self.add(self.part(k, "C", None, p.a, p.b), self.buf(k, "PC"))
        if 2 <= s <= nz + 1:
            self.wave(k, "A", s - 1)
            self.wave(k, "B", s - 1)
        if 3 <= s <= nz + 2:
            self.wave(k, "C", s - 2)
        if s == nz + 1:
            self.put(k, "XA", self.part(k, "A", p.z, p.a, 1 - p.b), self.buf(k, "XA"), p.peer["b"])
            self.put(k, "XB", self.part(k, "B", p.z, 1 - p.a, p.b), self.buf(k, "XB"), p.peer["a"])
        if s == nz + 2:
            self.take(k, "XA", self.buf(k, "XA"))
            self.take(k, "XB", self.buf(k, "XB"))
            self.deliver(k)

    def yc(self, k):
        buf = self.buf(k, "YC")
        nz, plane, _, r, w = buf.shape
        return buf if self.order(k, "C")[1] == "b" else buf.reshape(nz, 1, plane, r, w)

    def result(self, k, route):
        p = self.p
        block = self.part(k, route, p.z, p.a, p.b)[0, 0, 0].astype(F32)
        if route != "C":
            block = block + self.buf(k, "X" + route)[0, 0, 0].astype(F32)
        return block

    def tick(self, t):
        for s in range(self.depth - 1, -1, -1):
            if 0 <= t - s < len(self.chunks):
                self.stage(t - s, s)

    def ticks(self):
        return len(self.chunks) + self.depth - 1

    def finish(self):
        for make, z in self.started:
            if z is None:
                make().wait_send()
            else:

                @pl.when(self.p.z == z)
                def _():
                    make().wait_send()


class ReduceFromHbm(Reduce):
    def attach(self, partials, outs, load, load_sem, stage_out, out_sem):
        self.partials, self.outs = partials, outs
        self.load, self.load_sem = load, load_sem
        self.stage_out, self.out_sem = stage_out, out_sem
        self.loads, self.stores = {}, {}

    def shape_kind(self, k):
        return 0 if self.chunks[k][4] > 1024 else 1

    def begin(self, k):
        p = self.p
        i, r0, nr, c0, nc = self.chunks[k]
        src = lambda c: self.partials[i].at[:, :, :, c, pl.ds(r0, nr), pl.ds(c0, nc)]
        self.put(k, "C", src(1 - p.c), self.buf(k, "C"), p.core)
        kind = self.shape_kind(k)
        cp = pltpu.make_async_copy(src(p.c), self.load[kind].at[k % 2], self.load_sem.at[k % 2])
        cp.start()
        self.loads[k] = cp

    def arrive(self, k):
        self.loads[k].wait()
        self.take(k, "C", self.buf(k, "C"))
        self.add(self.buf(k, "C"), self.load[self.shape_kind(k)].at[k % 2])

    def deliver(self, k):
        i, r0, nr, c0, nc = self.chunks[k]
        kind = self.shape_kind(k)
        at = k % 2
        if k - 2 in self.stores:
            self.stores.pop(k - 2).wait()
        for route in "ABC":
            self.stage_out[kind][at, :, self.cols(k, route)] = self.result(k, route)
        cp = pltpu.make_async_copy(
            self.stage_out[kind].at[at], self.outs[i].at[pl.ds(r0, nr), pl.ds(c0, nc)], self.out_sem.at[at]
        )
        cp.start()
        self.stores[k] = cp

    def finish(self):
        for cp in self.stores.values():
            cp.wait()
        super().finish()


def reduce_kernel(seq_count, n_arr, chunks, kinds, *refs):
    xg_ref, small_ref, partials = refs[0], refs[1], refs[2 : 2 + n_arr]
    at = 2 + n_arr
    xo_ref, small_out, outs = refs[at], refs[at + 1], refs[at + 2 : at + 2 + n_arr]
    rest = list(refs[at + 2 + n_arr :])
    names = Reduce.NAMES
    pools = [dict(zip(names, rest[i * len(names) : (i + 1) * len(names)])) for i in range(2)]
    rest = rest[2 * len(names) :]
    load, stage_out = rest[0:2], rest[2:4]
    s_own, s_core, s_b, s_a, s_z, s_res = rest[4:10]
    send, recv, load_sem, out_sem, x_send, x_recv, s_send, s_recv, one_sem = rest[10:]
    p = Place(seq_count)
    one = pl.ds
    bufs, seen = [], [0, 0]
    for kind in kinds:
        j = seen[kind]
        seen[kind] += 1
        bufs.append({n: pools[kind][n].at[j] for n in names})
    r = ReduceFromHbm(p, chunks, bufs, send, recv)
    r.attach(partials, outs, load, load_sem, stage_out, out_sem)
    tok, feat = xg_ref.shape[1], xo_ref.shape[2]
    own_x = pltpu.make_async_copy(
        xg_ref.at[:, :, one(pl.multiple_of(p.z * feat, 128), feat)], xo_ref.at[:, one(p.z * tok, tok), :], one_sem.at[0]
    )
    own_s = pltpu.make_async_copy(small_ref, s_own, one_sem.at[1])
    own_x.start()
    own_s.start()
    p.greet()
    moves = []

    def small_put(at, src, dst, dev):
        cp = pltpu.make_async_remote_copy(src, dst, s_send.at[at], s_recv.at[at], device_id=dev, device_id_type=MESH)
        cp.start()
        moves.append(cp)
        return cp

    own_s.wait()
    c1 = small_put(0, s_own.at[:, :, :, 1 - p.c], s_core, p.core)
    z_moves = []
    for t in range(r.ticks()):
        r.tick(t)
        if t == 0:
            for o in range(1, p.nz):
                to = lax.rem(p.z + o, p.nz)
                cp = pltpu.make_async_remote_copy(
                    xg_ref.at[:, :, one(pl.multiple_of(to * feat, 128), feat)],
                    xo_ref.at[:, one(p.z * tok, tok), :],
                    x_send.at[o - 1],
                    x_recv.at[o - 1],
                    device_id=p.at(to),
                    device_id_type=MESH,
                )
                cp.start()
                z_moves.append(cp)
        if t == 1:
            c1.wait_recv()
            s_core[...] = s_core[...] + s_own[:, :, :, p.c]
            c2 = small_put(1, s_core.at[:, :, 1 - p.b], s_b, p.peer["b"])
        if t == 2:
            c2.wait_recv()
            s_b[...] = s_b[...] + s_core[:, :, p.b]
            c3 = small_put(2, s_b.at[:, 1 - p.a], s_a, p.peer["a"])
        if t == 3:
            c3.wait_recv()
            s_a[...] = s_a[...] + s_b[:, p.a]
            for o in range(1, p.nz):
                to = lax.rem(p.z + o, p.nz)
                small_put(2 + o, s_a.at[to], s_z.at[o - 1], p.at(to))
        if t == 4:
            total = s_a[p.z]
            for o in range(1, p.nz):
                moves[2 + o].wait_recv()
                total = total + s_z[o - 1]
            s_res[...] = total
    own_r = pltpu.make_async_copy(s_res, small_out, one_sem.at[1])
    own_r.start()
    own_x.wait()
    for cp in z_moves:
        cp.wait()
    for cp in moves:
        cp.wait_send()
    own_r.wait()
    r.finish()


def reduce_all(x_grad, small, partials, own_rows, seq_count):
    rows_cols = [(r, g.shape[1]) for g, r in zip(partials, own_rows)]
    chunks = []
    for i in (4, 3, 2, 1, 0):
        chunks += [c for c in chunk_list(rows_cols) if c[0] == i]
    kinds = [0 if c[4] > 1024 else 1 for c in chunks]
    sizes = [(16, 3072), (48, 1024)]
    row_count, tok, model = x_grad.shape
    hbm = pl.BlockSpec(memory_space=pltpu.HBM)
    srcs = [g.reshape(seq_count, PLANE, PLANE, 2, r, c) for g, (r, c) in zip(partials, rows_cols)]
    out_shape = [
        jax.ShapeDtypeStruct((row_count, tok * seq_count, model // seq_count), BF16),
        jax.ShapeDtypeStruct((8, 128), F32),
    ] + [jax.ShapeDtypeStruct(rc, F32) for rc in rows_cols]
    scratch = []
    for kind, (r, w) in enumerate(sizes):
        shapes = Reduce.shapes(seq_count, r, w)
        scratch += [pltpu.VMEM((kinds.count(kind), *shapes[n]), BF16) for n in Reduce.NAMES]
    scratch += [pltpu.VMEM((2, *Reduce.shapes(seq_count, r, w)["C"]), BF16) for r, w in sizes]
    scratch += [pltpu.VMEM((2, r, w), F32) for r, w in sizes]
    scratch += [
        pltpu.VMEM((seq_count, 2, 2, 2, 8, 128), F32),
        pltpu.VMEM((seq_count, 2, 2, 8, 128), F32),
        pltpu.VMEM((seq_count, 2, 8, 128), F32),
        pltpu.VMEM((seq_count, 8, 128), F32),
        pltpu.VMEM((seq_count, 8, 128), F32),
        pltpu.VMEM((8, 128), F32),
    ]
    dma = pltpu.SemaphoreType.DMA
    n_names = len(Reduce.NAMES)
    scratch += [
        dma((len(chunks), n_names)),
        dma((len(chunks), n_names)),
        dma((2,)),
        dma((2,)),
        dma((seq_count,)),
        dma((seq_count,)),
        dma((seq_count + 3,)),
        dma((seq_count + 3,)),
        dma((2,)),
    ]
    outs = pl.pallas_call(
        partial(reduce_kernel, seq_count, len(partials), chunks, kinds),
        out_shape=out_shape,
        in_specs=[hbm] * (2 + len(srcs)),
        out_specs=[hbm] * len(out_shape),
        scratch_shapes=scratch,
        compiler_params=pltpu.CompilerParams(
            collective_id=1, has_side_effects=True, vmem_limit_bytes=60 << 20
        ),
        name="reduce_gradients",
    )(x_grad, small.reshape(seq_count, 2, 2, 2, 8, 128), *srcs)
    return outs[0], outs[1], outs[2:]


LANE = 128


def spread_constants(model, lru, dev_count):
    out = []
    for width in (model, lru):
        per = width // dev_count
        lane = jnp.arange(width, dtype=jnp.int32)[None, :]
        out.append((lane % per == jnp.arange(LANE, dtype=jnp.int32)[:, None]).astype(BF16))
        out.append((lane // per == jnp.arange(dev_count, dtype=jnp.int32)[:, None]).astype(F32))
    return out


def small_rows(norm_gain, conv_weight, decay_bias, admit_bias, decay_rate, feed_gain):
    rate = decay_rate.astype(F32)
    scale = -DECAY_SCALE * jax.nn.softplus(-rate)
    high = lax.reduce_precision(scale, 8, 7)
    mid = lax.reduce_precision(scale - high, 8, 7)
    low = lax.reduce_precision(scale - high - mid, 8, 7)
    taps = [conv_weight[:, k] for k in range(conv_weight.shape[1])]
    rows = [norm_gain, feed_gain, decay_bias, admit_bias, high, mid, low, rate, *taps]
    rows = [jnp.pad(v.astype(F32), (0, LANE - v.shape[0])) for v in rows]
    return jnp.stack(rows + [jnp.zeros((LANE,), F32)] * (16 - len(rows)))


def decay_terms(pre, scale):
    recall = jax.nn.sigmoid(pre)
    log_decay = recall * scale
    decay = jnp.exp(log_decay)
    y = 2.0 * log_decay
    series = 1.0 + y * (1 / 7)
    for n in (6, 5, 4, 3, 2):
        series = 1.0 + y * (1 / n) * series
    lost = jnp.where(y > -0.35, -y * series, 1.0 - decay * decay)
    return recall, decay, lost


def scan_block(prod, state, reverse=False):
    length = prod.shape[0]
    at = lax.broadcasted_iota(jnp.int32, prod.shape, 0)
    step = 1
    while step < length:
        inside = at < length - step if reverse else at >= step
        turn = length - step if reverse else step
        prod_far = jnp.where(inside, pltpu.roll(prod, turn, 0), 1.0)
        state_far = jnp.where(inside, pltpu.roll(state, turn, 0), 0.0)
        state = prod * state_far + state
        prod = prod * prod_far
        step *= 2
    return prod, state


def lanes(c, width=LANE):
    return pl.ds(pl.multiple_of(c * width, width), width)


def loop(count, body):
    def step(i, carry):
        body(i)
        return carry

    lax.fori_loop(0, count, step, 0)


def stream_tiles(count, fetch, use):
    for cp in fetch(0, 0):
        cp.start()

    def step(j, carry):
        slot = lax.rem(j, 2)

        @pl.when(j + 1 < count)
        def _():
            for cp in fetch(j + 1, 1 - slot):
                cp.start()

        for cp in fetch(j, slot):
            cp.wait()
        use(j, slot)
        return carry

    lax.fori_loop(0, count, step, 0)


def mat(value):
    return value.reshape(-1, value.shape[-1])


class Forward:
    def __init__(self, refs, place, weights):
        self.__dict__.update(refs)
        self.p, self.weights = place, weights
        self.tok = self.xs.shape[1]
        self.rows = self.xs.shape[0]
        self.flat = self.rows * self.tok
        self.lru = self.gelu_pre.shape[1]
        self.model = self.xs.shape[2]
        self.feed = self.hidden.shape[1]
        self.stores = []

    def save(self, name):
        cp = pltpu.make_async_copy(getattr(self, name), self.keep[name], self.keep_sem.at[len(self.stores)])
        cp.start()
        self.stores.append(cp)

    def fetch(self, i, buf, sem, starts, width):
        def copies(j, slot):
            out = []
            for n, start in enumerate(starts):
                src = self.weights[i].at[:, :, :, :, :, pl.ds(pl.multiple_of(start + j * width, LANE), width)]
                dst = buf.at[slot, :, :, :, :, :, pl.ds(n * width, width)]
                out.append(pltpu.make_async_copy(src, dst, sem.at[slot, n]))
            return out

        return copies

    def vectors(self):
        cp = pltpu.make_async_copy(self.small_all, self.small_vm, self.misc_sem.at[0])
        cp.start()
        cp.wait()
        nz = self.p.nz

        def spread(row, hot, mask):
            vals = self.small_vm[:, :, row, :].reshape(nz * 8, LANE).astype(BF16)
            wide = jnp.dot(vals, hot[...], preferred_element_type=F32)
            return jnp.sum(wide * mask[...], axis=0, keepdims=True)

        for row in range(2):
            self.vec[row : row + 1, 0 : self.model] = spread(row, self.hot_m, self.mask_m)
        for row in range(2, 12):
            self.vec[row : row + 1, :] = spread(row, self.hot_l, self.mask_l)
        self.vec[4:5, :] = self.vec[4:5, :] + self.vec[5:6, :] + self.vec[6:7, :]

    def norm(self, load, count, gain_row, out):
        gain = self.vec[gain_row : gain_row + 1, 0 : self.model]

        def body(i):
            v = load(i)
            q = lax.rsqrt(jnp.mean(v * v, axis=-1, keepdims=True) + EPSILON)
            out[pl.ds(pl.multiple_of(i * 32, 32), 32), :] = (v * q * gain).astype(BF16)

        loop(count, body)

    def norm_one(self):
        per = self.tok // 32

        def main(i):
            return self.xs[i // per, pl.ds(pl.multiple_of(lax.rem(i, per) * 32, 32), 32), :].astype(F32)

        self.norm(main, self.flat // 32, 0, self.normed.at[0 : self.flat])
        self.norm(
            lambda i: self.halo_x[...].reshape(2 * 16, self.model).astype(F32),
            1,
            0,
            self.normed.at[self.flat : self.flat + 32],
        )
        self.save("normed_main")
        self.save("xs")

    def gelu_input(self):
        half = self.lru // 512

        def use(j, slot):
            res = jnp.dot(self.normed[0 : self.flat, :], mat(self.w_gi[slot]), preferred_element_type=F32)
            self.gelu_pre[:, lanes(j, 512)] = res

        stream_tiles(half, self.fetch(0, self.w_gi, self.w_sem, (0,), 512), use)

        def use_two(j, slot):
            res = jnp.dot(self.normed[...], mat(self.w_gi[slot]), preferred_element_type=F32).astype(BF16)
            self.branch[:, lanes(j, 512)] = res

        stream_tiles(half, self.fetch(0, self.w_gi, self.w_sem, (self.lru,), 512), use_two)

        def conv(c):
            for r in range(self.rows):
                at = slice(r * self.tok, (r + 1) * self.tok)
                head = self.branch[self.flat + 16 * r : self.flat + 16 * (r + 1), lanes(c)].astype(F32)
                wide = jnp.concatenate([head, self.branch[at, lanes(c)].astype(F32)], axis=0)
                since = self.since[at, :]
                total = jnp.zeros((self.tok, LANE), F32)
                for k in range(4):
                    moved = wide if k == 0 else pltpu.roll(wide, k, 0)
                    tap = self.vec[8 + k : 9 + k, lanes(c)]
                    total = total + tap * moved[16:] * (since >= k).astype(F32)
                self.conv[at, lanes(c)] = total.astype(BF16)

        loop(self.lru // LANE, conv)
        self.save("gelu_pre")
        self.save("branch")
        self.save("conv")

    def gates(self, first, count):
        self.sums[...] = jnp.zeros_like(self.sums) if first == 0 else self.sums[...]

        def use(j, slot):
            self.tile[...] = jnp.dot(self.conv[...], mat(self.w_da[slot]), preferred_element_type=F32)
            base = (first + j) * 4

            def block(i):
                c = base + i
                gate_sum = jnp.zeros((1, LANE), F32)
                for r in range(self.rows):
                    at = slice(r * self.tok, (r + 1) * self.tok)
                    pre = self.tile[at, lanes(i)] + self.vec[2:3, lanes(c)]
                    admit_pre = self.tile[at, lanes(i + 4)] + self.vec[3:4, lanes(c)]
                    self.decay_pre[at, lanes(c)] = pre
                    self.admit_pre[at, lanes(c)] = admit_pre
                    recall, decay, lost = decay_terms(pre, self.vec[4:5, lanes(c)])
                    reset = (self.since[at, :] == 0).astype(F32)
                    keep = 1.0 - reset
                    scale_in = reset + keep * jnp.sqrt(lost)
                    update = scale_in * jax.nn.sigmoid(admit_pre) * self.conv[at, lanes(c)].astype(F32)
                    prod, state = scan_block(decay * keep, update)
                    self.prod[at, lanes(c)] = prod
                    self.state[at, lanes(c)] = state
                    self.ends[self.p.z, r : r + 1, lanes(c)] = prod[self.tok - 1 :, :]
                    self.ends[self.p.z, 8 + r : 9 + r, lanes(c)] = state[self.tok - 1 :, :]
                    gate_sum = gate_sum + jnp.sum(decay, axis=0, keepdims=True)
                self.sums[0:1, lanes(c)] = gate_sum

            loop(4, block)

        starts = (first * 512, self.lru + first * 512)
        stream_tiles(count, self.fetch(1, self.w_da, self.w_sem, starts, 512), use)

    def gates_saved(self):
        self.save("decay_pre")
        self.save("admit_pre")
        self.save("sums")

    def send_ends(self):
        p = self.p
        self.end_moves = []
        for o in range(1, p.nz):
            view = self.ends.at[p.z]
            cp = pltpu.make_async_remote_copy(
                view, view, self.e_send.at[o - 1], self.e_recv.at[o - 1],
                device_id=p.at(lax.rem(p.z + o, p.nz)), device_id_type=MESH,
            )
            cp.start()
            self.end_moves.append(cp)

    def mix(self):
        p = self.p
        for o in range(1, p.nz):
            view = self.ends.at[lax.rem(p.z + p.nz - o, p.nz)]
            pltpu.make_async_remote_copy(
                view, view, self.e_send.at[o - 1], self.e_recv.at[o - 1],
                device_id=p.core, device_id_type=MESH,
            ).wait_recv()

        def block(c):
            carry = jnp.zeros((8, LANE), F32)
            into = carry
            for i in range(p.nz - 1):
                carry = self.ends[i, 0:8, lanes(c)] * carry + self.ends[i, 8:16, lanes(c)]
                into = jnp.where(p.z == i + 1, carry, into)
            self.carry[:, lanes(c)] = into
            for r in range(self.rows):
                at = slice(r * self.tok, (r + 1) * self.tok)
                state = self.state[at, lanes(c)] + self.prod[at, lanes(c)] * into[r : r + 1, :]
                self.state[at, lanes(c)] = state
                gelu = smooth_gate(self.gelu_pre[at, lanes(c)])
                self.mixed[at, lanes(c)] = (state * gelu).astype(BF16)

        loop(self.lru // LANE, block)
        self.save("state")
        self.save("carry")
        self.save("ends")
        self.save("mixed")

        def use(j, slot):
            res = jnp.dot(self.mixed[...], mat(self.w_mx[slot]), preferred_element_type=F32)
            x = self.xs[:, :, lanes(j, 512)].astype(F32).reshape(self.flat, 512)
            self.middle[:, lanes(j, 512)] = x + res

        stream_tiles(self.model // 512, self.fetch(2, self.w_mx, self.w_sem, (0,), 512), use)
        self.norm(
            lambda i: self.middle[pl.ds(pl.multiple_of(i * 32, 32), 32), :], self.flat // 32, 1, self.normed_two
        )
        self.save("middle")
        self.save("normed_two")

    def gate_up(self, first, count):
        def use(j, slot):
            res = jnp.dot(self.normed_two[...], mat(self.w_gu[slot]), preferred_element_type=F32)
            gate, up = res[:, 0:512], res[:, 512:1024]
            at = lanes(first + j, 512)
            self.gate_pre[:, at] = gate
            self.up[:, at] = up
            self.hidden[:, at] = (smooth_gate(gate) * up).astype(BF16)

        starts = (first * 512, self.feed + first * 512)
        stream_tiles(count, self.fetch(3, self.w_gu, self.w_sem, starts, 512), use)

    def gate_saved(self):
        self.save("gate_pre")
        self.save("up")
        self.save("hidden")

    def down(self):
        def use(j, slot):
            res = jnp.dot(self.hidden[...], mat(self.w_dn[slot]), preferred_element_type=F32)
            self.block[:, lanes(j, 256)] = (self.middle[:, lanes(j, 256)] + res).astype(BF16)

        stream_tiles(self.model // 256, self.fetch(4, self.w_dn, self.w_sem, (0,), 256), use)
        self.save("block")

    def finish(self):
        for cp in self.stores:
            cp.wait()
        for cp in self.end_moves:
            cp.wait_send()


KEEP = (
    "xs", "normed_main", "gelu_pre", "branch", "conv", "decay_pre", "admit_pre", "sums", "state", "carry",
    "ends", "mixed", "middle", "normed_two", "gate_pre", "up", "hidden", "block",
)


def forward_kernel(seq_count, starts, chunks, names, n_keep, *refs):
    refs = list(refs)
    x_ref, small_ref, since, hot_m, mask_m, hot_l, mask_l = refs[:7]
    srcs = refs[7:15]
    at = 15
    small_all, vec = refs[at : at + 2]
    outs = refs[at + 2 : at + 7]
    keep = dict(zip(KEEP, refs[at + 7 : at + 7 + n_keep]))
    at += 7 + n_keep
    table = dict(zip(names, refs[at : at + len(names)]))
    p = Place(seq_count)
    table.update(
        small_all=small_all, vec=vec, since=since, hot_m=hot_m, mask_m=mask_m, hot_l=hot_l, mask_l=mask_l, keep=keep,
    )
    table["normed_main"] = table["normed"].at[0 : since.shape[0]]
    f = Forward(table, p, outs)
    one = pl.ds
    copies = []
    own_sem = table["own_sem"]
    k = 0
    for out, count in zip(outs, (2, 2, 1, 2, 1)):
        col = 0
        for _ in range(count):
            cols = srcs[k].shape[-1]
            dst = out.at[one(p.z, 1), one(p.a, 1), one(p.b, 1), one(p.c, 1), :, one(col, cols)]
            copies.append(pltpu.make_async_copy(srcs[k], dst, own_sem.at[k]))
            col += cols
            k += 1
    tok, feat = f.tok, x_ref.shape[2]
    here = one(pl.multiple_of(p.z * feat, LANE), feat)
    copies.append(pltpu.make_async_copy(x_ref.at[:, one(p.z * tok, tok), :], f.xs.at[:, :, here], own_sem.at[k]))
    copies.append(pltpu.make_async_copy(small_ref, small_all.at[one(p.z, 1), one(p.d, 1)], own_sem.at[k + 1]))
    for cp in copies:
        cp.start()

    def halo(z):
        return x_ref.at[:, one(pl.multiple_of(jnp.maximum(z * tok - 16, 0), 16), 16), :]

    own_halo = lambda: pltpu.make_async_copy(halo(p.z), f.halo_x.at[:, :, here], own_sem.at[k + 2])

    @pl.when(p.z > 0)
    def _():
        own_halo().start()

    @pl.when(p.z == 0)
    def _():
        f.halo_x[...] = jnp.zeros_like(f.halo_x)

    f.ends[...] = jnp.zeros_like(f.ends)
    f.sums[...] = jnp.zeros_like(f.sums)
    p.greet()
    x_moves = []

    def x_copy(o):
        to = lax.rem(p.z + o, p.nz)
        return pltpu.make_async_remote_copy(
            x_ref.at[:, one(pl.multiple_of(to * tok, 16), tok), :], f.xs.at[:, :, here], table["x_send"].at[o - 1],
            table["x_recv"].at[o - 1], device_id=p.at(to), device_id_type=MESH,
        )

    def h_copy(o):
        to = lax.rem(p.z + o, p.nz)
        return to > 0, pltpu.make_async_remote_copy(
            halo(to), f.halo_x.at[:, :, here], table["h_send"].at[o - 1],
            table["h_recv"].at[o - 1], device_id=p.at(to), device_id_type=MESH,
        )

    for o in range(1, p.nz):
        x_copy(o).start()
        cond, cp = h_copy(o)
        pl.when(cond)(cp.start)
    for cp in copies:
        cp.wait()
    s_send, s_recv = table["s_send"], table["s_recv"]
    s_moves = []

    def small_put(view, at, dev):
        cp = pltpu.make_async_remote_copy(view, view, s_send.at[at], s_recv.at[at], device_id=dev, device_id_type=MESH)
        cp.start()
        s_moves.append(cp)

    def small_view(d, n):
        return small_all.at[one(p.z, 1), one(d, n)]

    small_put(small_view(p.d, 1), 0, p.core)
    g = Gather(p, outs, chunks, table["send"], table["recv"], starts)
    last = [max(starts[i] for i in range(len(chunks)) if chunks[i][0] == w) + g.depth - 1 for w in range(5)]
    plan = {
        3: [f.vectors, f.norm_one],
        last[0]: [f.gelu_input],
        max(last[1], last[0] + 1): [lambda: f.gates(0, 2)],
        max(last[1], last[0] + 1) + 1: [lambda: f.gates(2, 1), f.send_ends, f.gates_saved],
        max(last[2], max(last[1], last[0] + 1) + 2): [f.mix],
    }
    plan.setdefault(last[3], []).append(lambda: f.gate_up(0, 2))
    plan.setdefault(last[3] + 1, []).append(lambda: f.gate_up(2, 2))
    plan.setdefault(max(last[3] + 2, last[4]), []).extend([lambda: f.gate_up(4, 2), f.gate_saved, f.down])
    ticks = max(g.ticks(), max(plan) + 1)
    for t in range(ticks):
        g.tick(t)
        if t == 0:
            s_moves[0].wait_recv()
            small_put(small_view(p.d - p.c, 2), 1, p.peer["b"])
        if t == 1:
            s_moves[1].wait_recv()
            small_put(small_view(4 * p.a, 4), 2, p.peer["a"])
        if t == 2:
            s_moves[2].wait_recv()
            for o in range(1, p.nz):
                small_put(small_view(0, 8), 2 + o, p.at(lax.rem(p.z + o, p.nz)))
        if t == 3:
            for cp in s_moves[3:]:
                cp.wait_recv()
            for o in range(1, p.nz):
                x_copy(o).wait_recv()
                pl.when(p.z > 0)(h_copy(o)[1].wait_recv)

            @pl.when(p.z > 0)
            def _():
                own_halo().wait()

        for action in plan.get(t, ()):
            action()
    for cp in s_moves:
        cp.wait_send()
    for o in range(1, p.nz):
        x_copy(o).wait_send()
        cond, cp = h_copy(o)
        pl.when(cond)(cp.wait_send)
    f.finish()
    g.finish()


def forward_pass(x_heads, small, since, shards, seq_count, starts):
    groups = ((0, 1), (2, 3), (4,), (5, 6), (7,))
    rows_cols = [(shards[g[0]].shape[0], sum(shards[i].shape[1] for i in g)) for g in groups]
    chunks = chunk_list(rows_cols)
    row_count, row_len, feat = x_heads.shape
    tok, model = row_len // seq_count, feat * seq_count
    flat = row_count * tok
    lru, feed = rows_cols[0][1] // 2, rows_cols[3][1] // 2
    nz = seq_count
    srcs = [s.reshape(1, 1, 1, 1, *s.shape) for s in shards]
    hbm = pl.BlockSpec(memory_space=pltpu.HBM)
    vmem = pl.BlockSpec(memory_space=pltpu.VMEM)
    keep_shapes = {
        "xs": ((row_count, tok, model), BF16),
        "normed_main": ((flat, model), BF16),
        "gelu_pre": ((flat, lru), F32),
        "branch": ((flat + 32, lru), BF16),
        "conv": ((flat, lru), BF16),
        "decay_pre": ((flat, lru), F32),
        "admit_pre": ((flat, lru), F32),
        "sums": ((8, lru), F32),
        "state": ((flat, lru), F32),
        "carry": ((8, lru), F32),
        "ends": ((nz, 16, lru), F32),
        "mixed": ((flat, lru), BF16),
        "middle": ((flat, model), F32),
        "normed_two": ((flat, model), BF16),
        "gate_pre": ((flat, feed), F32),
        "up": ((flat, feed), F32),
        "hidden": ((flat, feed), BF16),
        "block": ((flat, model), BF16),
    }
    scratch = {n: pltpu.VMEM(*s) for n, s in keep_shapes.items() if n != "normed_main"}
    dma = pltpu.SemaphoreType.DMA
    sems = Gather.sem_count(nz)
    scratch.update(
        normed=pltpu.VMEM((flat + 32, model), BF16),
        halo_x=pltpu.VMEM((row_count, 16, model), BF16),
        small_vm=pltpu.VMEM((nz, 8, 16, LANE), F32),
        prod=pltpu.VMEM((flat, lru), F32),
        tile=pltpu.VMEM((flat, 1024), F32),
        w_gi=pltpu.VMEM((2, nz, 2, 2, 2, rows_cols[0][0], 512), BF16),
        w_da=pltpu.VMEM((2, nz, 2, 2, 2, rows_cols[1][0], 1024), BF16),
        w_mx=pltpu.VMEM((2, nz, 2, 2, 2, rows_cols[2][0], 512), BF16),
        w_gu=pltpu.VMEM((2, nz, 2, 2, 2, rows_cols[3][0], 1024), BF16),
        w_dn=pltpu.VMEM((2, nz, 2, 2, 2, rows_cols[4][0], 256), BF16),
        w_sem=dma((2, 2)),
        keep_sem=dma((len(KEEP),)),
        misc_sem=dma((1,)),
        own_sem=dma((len(srcs) + 3,)),
        x_send=dma((nz,)),
        x_recv=dma((nz,)),
        h_send=dma((nz,)),
        h_recv=dma((nz,)),
        s_send=dma((nz + 3,)),
        s_recv=dma((nz + 3,)),
        e_send=dma((nz,)),
        e_recv=dma((nz,)),
        send=dma((len(chunks), sems)),
        recv=dma((len(chunks), sems)),
    )
    names = list(scratch)
    out_shape = [jax.ShapeDtypeStruct((nz, 8, 16, LANE), F32), jax.ShapeDtypeStruct((16, lru), F32)]
    out_shape += [jax.ShapeDtypeStruct((nz, PLANE, PLANE, 2, r, c), BF16) for r, c in rows_cols]
    out_shape += [jax.ShapeDtypeStruct(*keep_shapes[n]) for n in KEEP]
    outs = pl.pallas_call(
        partial(forward_kernel, nz, starts, chunks, names, len(KEEP)),
        out_shape=out_shape,
        in_specs=[hbm, hbm] + [vmem] * 5 + [hbm] * 8,
        out_specs=[hbm, vmem] + [hbm] * (5 + len(KEEP)),
        scratch_shapes=[scratch[n] for n in names],
        compiler_params=pltpu.CompilerParams(
            collective_id=0, has_side_effects=True, vmem_limit_bytes=61 << 20
        ),
        name="forward_pass",
    )(
        x_heads,
        small.reshape(1, 1, 16, LANE),
        jnp.broadcast_to(since.reshape(flat, 1), (flat, LANE)),
        *spread_constants(model, lru, nz * 8),
        *srcs,
    )
    return outs[1], outs[2:7], dict(zip(KEEP, outs[7:]))


def gelu_slope(x):
    inner = GELU_C * (x + 0.044715 * x * x * x)
    t = jnp.tanh(inner)
    return 0.5 * (1.0 + t) + 0.5 * x * (1.0 - t * t) * GELU_C * (1.0 + 3 * 0.044715 * x * x)


def rms_back(values, gain, grad):
    q = lax.rsqrt(jnp.mean(values * values, axis=-1, keepdims=True) + EPSILON)
    inner = jnp.mean(values * gain * grad, axis=-1, keepdims=True)
    back = q * gain * grad - values * (q * q * q) * inner
    return back, grad * values * q


def local_fast(x_heads, cotangent, doc_starts, smalls, shards):
    norm_gain, conv_weight, decay_bias, admit_bias, decay_rate, feed_gain = smalls
    seq_count = lax.axis_size("seq")
    dev_count = seq_count * lax.axis_size("dp")
    seq_at = lax.axis_index("seq")
    row_count, tok_count, model = cotangent.shape
    flat = row_count * tok_count
    lru, feed, taps = shards[0].shape[1], shards[5].shape[1], conv_weight.shape[1]
    rim = taps - 1
    positions = seq_at * tok_count + jnp.arange(tok_count + rim, dtype=jnp.int32)
    since_ext = since_start(doc_starts, positions)
    since_here = since_ext[:, :tok_count]
    small = small_rows(norm_gain, conv_weight, decay_bias, admit_bias, decay_rate, feed_gain)
    vec, full, kept = forward_pass(x_heads, small, since_here, shards, seq_count, STARTS)
    gelu_input, decay_admit, mixer_full, gate_up, down_full = [w.reshape(-1, w.shape[-1]) for w in full]
    gain_one, gain_two = vec[0, :model], vec[1, :model]
    scale_vec, rate_vec, conv_taps = vec[4], vec[7], vec[8 : 8 + taps].T

    cot = cotangent.reshape(flat, model)
    down_part = outer_sum(kept["hidden"], cot).astype(BF16)
    grad_hidden = back_prod(cot, down_full)
    gate_pre, up_vals = kept["gate_pre"], kept["up"]
    grad_gate = (gelu_slope(gate_pre) * up_vals * grad_hidden).astype(BF16)
    grad_up = (grad_hidden * smooth_gate(gate_pre)).astype(BF16)
    grad_gu = jnp.concatenate([grad_gate, grad_up], axis=1)
    gate_up_part = outer_sum(kept["normed_two"], grad_gu).astype(BF16)
    back, gain_terms = rms_back(kept["middle"], gain_two, back_prod(grad_gu, gate_up))
    gain_two_grad = jnp.sum(gain_terms, axis=0)
    grad_middle = cot.astype(F32) + back
    grad_out = grad_middle.astype(BF16)
    mixer_part = outer_sum(kept["mixed"], grad_out).astype(BF16)
    grad_mixed = back_prod(grad_out, mixer_full)
    state = kept["state"]
    grad_gelu = (gelu_slope(kept["gelu_pre"]) * grad_mixed * state).astype(BF16)
    direct = (grad_mixed * smooth_gate(kept["gelu_pre"])).reshape(row_count, tok_count, lru)
    recall, decay, lost = decay_terms(kept["decay_pre"], scale_vec)
    reset = (since_here.reshape(flat, 1) == 0).astype(F32)
    keep = 1.0 - reset
    root = jnp.sqrt(lost)
    decay_eff = (decay * keep).reshape(row_count, tok_count, lru)
    decay_next = jnp.concatenate([decay_eff[:, 1:, :], jnp.ones_like(decay_eff[:, :1, :])], axis=1)
    tail_prod, tail_state = scan_rows(decay_next, direct, reverse=True)
    back_ends = lax.all_gather(decay_eff[:, 0] * tail_state[:, 0], "seq", axis=0)
    tail = jnp.zeros((row_count, lru), F32)
    back_in = tail
    for i in range(seq_count - 1, 0, -1):
        tail = kept["ends"][i, :row_count] * tail + back_ends[i]
        back_in = jnp.where(seq_at == i - 1, tail, back_in)
    adjoint = (tail_state + tail_prod * back_in[:, None, :]).reshape(flat, lru)
    state_rows = state.reshape(row_count, tok_count, lru)
    state_prev = jnp.concatenate([kept["carry"][:row_count, None, :], state_rows[:, :-1, :]], axis=1)
    conv = kept["conv"].astype(F32)
    admit = jax.nn.sigmoid(kept["admit_pre"])
    scale_in = reset + keep * root
    grad_log = adjoint * keep * (state_prev.reshape(flat, lru) * decay - admit * conv * decay * decay / root)
    grad_decay = (grad_log * scale_vec * recall * (1.0 - recall)).astype(BF16)
    grad_admit = (adjoint * scale_in * conv * admit * (1.0 - admit)).astype(BF16)
    rate_grad = jnp.sum(grad_log * recall, axis=0) * DECAY_SCALE * jax.nn.sigmoid(-rate_vec)
    grad_da = jnp.concatenate([grad_decay, grad_admit], axis=1)
    decay_admit_part = outer_sum(kept["conv"], grad_da).astype(BF16)
    bias_grads = jnp.sum(grad_da, axis=0, dtype=F32)
    grad_conv = (adjoint * scale_in * admit + back_prod(grad_da, decay_admit)).astype(BF16)
    grad_conv = grad_conv.reshape(row_count, tok_count, lru)
    grad_conv_wide = grad_conv.astype(F32)
    branch_main = kept["branch"][:flat].reshape(row_count, tok_count, lru)
    branch_head = kept["branch"][flat:].reshape(row_count, 16, lru)[:, 16 - rim :]
    extended = jnp.concatenate([branch_head, branch_main], axis=1).astype(F32)
    tap_grads = []
    for k in range(taps):
        window = extended[:, rim - k : rim - k + tok_count, :]
        mask = (since_here >= k)[..., None].astype(F32)
        tap_grads.append(jnp.sum(grad_conv_wide * window * mask, axis=(0, 1)))
    conv_grad = jnp.stack(tap_grads, axis=1)
    rim_after = shift_seq(grad_conv[:, :rim, :], -1, seq_count)
    grad_ext = jnp.concatenate([grad_conv, rim_after], axis=1).astype(F32)
    branch_grad = jnp.zeros((row_count, tok_count, lru), F32)
    for k in range(taps):
        ahead = (since_ext[:, k : k + tok_count] >= k)[..., None].astype(F32)
        branch_grad = branch_grad + conv_taps[:, k] * grad_ext[:, k : k + tok_count, :] * ahead
    grad_gi = jnp.concatenate([grad_gelu, branch_grad.reshape(flat, lru).astype(BF16)], axis=1)
    gelu_input_part = outer_sum(kept["normed_main"], grad_gi).astype(BF16)
    stream_in = kept["xs"].reshape(flat, model).astype(F32)
    back_one, gain_terms = rms_back(stream_in, gain_one, back_prod(grad_gi, gelu_input))
    gain_one_grad = jnp.sum(gain_terms, axis=0)
    input_grad_tok = (grad_middle + back_one).astype(BF16).reshape(row_count, tok_count, model)
    gate_term = kept["sums"][0] / float(flat * dev_count)
    small_grads = (
        gain_one_grad, conv_grad, bias_grads[:lru], bias_grads[lru:], rate_grad, gain_two_grad, gate_term,
    )
    packed_grads = jnp.concatenate([g.reshape(dev_count, -1) for g in small_grads], axis=1)
    partials = (gelu_input_part, decay_admit_part, mixer_part, gate_up_part, down_part)
    wide = jnp.pad(packed_grads, ((0, 0), (0, 1024 - packed_grads.shape[1])))
    own_rows = [shards[i].shape[0] for i in (0, 2, 4, 5, 7)]
    input_grad, reduced, summed = reduce_all(input_grad_tok, wide, partials, own_rows, seq_count)
    own = split_small(reduced.reshape(1, 1024), [g.size // dev_count for g in small_grads])
    gi, da, mx, gu, dn = summed
    return (
        kept["block"].reshape(row_count, tok_count, model),
        input_grad,
        own[0].reshape(-1),
        gi[:, :lru],
        gi[:, lru:],
        own[1].reshape(-1, taps),
        da[:, :lru],
        own[2].reshape(-1),
        da[:, lru:],
        own[3].reshape(-1),
        own[4].reshape(-1),
        mx,
        own[5].reshape(-1),
        gu[:, :feed],
        gu[:, feed:],
        dn,
        own[6].reshape(-1),
    )


def local(
    x_heads,
    cotangent,
    doc_starts,
    norm_gain,
    gelu_weight,
    input_weight,
    conv_weight,
    decay_weight,
    decay_bias,
    admit_weight,
    admit_bias,
    decay_rate,
    mixer_output,
    feed_gain,
    feed_gate,
    feed_up,
    feed_down,
):
    seq_count = lax.axis_size("seq")
    dev_count = seq_count * lax.axis_size("dp")
    seq_at = lax.axis_index("seq")
    row_count, tok_count, model = cotangent.shape
    flat = row_count * tok_count
    lru = gelu_weight.shape[1]
    feed = feed_gate.shape[1]
    taps = conv_weight.shape[1]
    rim = taps - 1

    smalls = (norm_gain, conv_weight, decay_bias, admit_bias, decay_rate, feed_gain)
    shards = (
        gelu_weight, input_weight, decay_weight, admit_weight, mixer_output, feed_gate, feed_up, feed_down,
    )
    if fast_shapes(shards, seq_count, lax.axis_size("dp"), row_count, tok_count):
        return local_fast(x_heads, cotangent, doc_starts, smalls, shards)
    packed = lax.all_gather(pack_small(smalls), ALL, axis=0, tiled=True).astype(F32)
    parts = split_small(packed, [v.size for v in smalls])
    gain_one = parts[0].reshape(-1)
    conv_taps = parts[1].reshape(lru, taps)
    decay_shift, admit_shift, rate_vec, gain_two = [p.reshape(-1) for p in parts[2:]]

    gelu_input = gather_rows(jnp.concatenate([gelu_weight, input_weight], axis=1))
    decay_admit = gather_rows(jnp.concatenate([decay_weight, admit_weight], axis=1))
    mixer_full = gather_rows(mixer_output)
    gate_up = gather_rows(jnp.concatenate([feed_gate, feed_up], axis=1))
    down_full = gather_rows(feed_down)

    stream = lax.all_to_all(x_heads, "seq", split_axis=1, concat_axis=2, tiled=True)
    stream_in = stream.reshape(flat, model).astype(F32)
    normed_one, norm_one_pull = jax.vjp(rms_norm, stream_in, gain_one)
    normed_low = normed_one.astype(BF16)
    both = dot(normed_low, gelu_input)
    gelu_vals, gelu_pull = jax.vjp(smooth_gate, both[:, :lru])
    branch = both[:, lru:].astype(BF16).reshape(row_count, tok_count, lru)
    halo = shift_seq(branch[:, tok_count - rim :, :], 1, seq_count)
    extended = jnp.concatenate([halo, branch], axis=1).astype(F32)
    positions = seq_at * tok_count + jnp.arange(tok_count + rim, dtype=jnp.int32)
    since_ext = since_start(doc_starts, positions)
    since_here = since_ext[:, :tok_count]
    conv_vals = jnp.zeros((row_count, tok_count, lru), F32)
    for k in range(taps):
        window = extended[:, rim - k : rim - k + tok_count, :]
        conv_vals = conv_vals + conv_taps[:, k] * window * (since_here >= k)[..., None].astype(F32)
    conv_low = conv_vals.astype(BF16)
    conv_flat = conv_low.reshape(flat, lru)
    gates = dot(conv_flat, decay_admit)
    decay_pre = (gates[:, :lru] + decay_shift).reshape(row_count, tok_count, lru)
    admit_pre = (gates[:, lru:] + admit_shift).reshape(row_count, tok_count, lru)
    reset_mask = (since_here == 0).astype(F32)[..., None]

    def coefs(dp, ap, cv, rv):
        return coefficients(dp, ap, cv, rv, reset_mask)

    (decay_eff, update, decay_vals), coef_pull = jax.vjp(
        coefs, decay_pre, admit_pre, conv_low.astype(F32), rate_vec
    )
    decay_prod, local_state = lax.associative_scan(compose, (decay_eff, update), axis=1)
    ends = jnp.stack([decay_prod[:, -1], local_state[:, -1]])
    all_ends = lax.all_gather(ends, "seq", axis=0)
    carry = jnp.zeros((row_count, lru), F32)
    carry_in = carry
    for i in range(seq_count - 1):
        carry = all_ends[i, 0] * carry + all_ends[i, 1]
        carry_in = jnp.where(seq_at == i + 1, carry, carry_in)
    state = local_state + decay_prod * carry_in[:, None, :]
    state_flat = state.reshape(flat, lru)
    mixed_low = (state_flat * gelu_vals).astype(BF16)
    middle = stream_in + dot(mixed_low, mixer_full)
    normed_two, norm_two_pull = jax.vjp(rms_norm, middle, gain_two)
    normed_two_low = normed_two.astype(BF16)
    gate_up_pre = dot(normed_two_low, gate_up)
    gate_act, gate_pull = jax.vjp(smooth_gate, gate_up_pre[:, :feed])
    up_vals = gate_up_pre[:, feed:]
    hidden_low = (gate_act * up_vals).astype(BF16)
    block_output = (middle + dot(hidden_low, down_full)).astype(BF16)
    block_output = block_output.reshape(row_count, tok_count, model)

    cot = cotangent.reshape(flat, model)
    down_grad = scatter_rows(outer_sum(hidden_low, cot))
    grad_hidden = back_prod(cot, down_full)
    grad_gate = gate_pull(grad_hidden * up_vals)[0].astype(BF16)
    grad_up = (grad_hidden * gate_act).astype(BF16)
    grad_gu = jnp.concatenate([grad_gate, grad_up], axis=1)
    gate_up_grad = scatter_rows(outer_sum(normed_two_low, grad_gu))
    grad_mid_norm, gain_two_grad = norm_two_pull(back_prod(grad_gu, gate_up))
    grad_middle = cot.astype(F32) + grad_mid_norm
    grad_out = grad_middle.astype(BF16)
    mixer_grad = scatter_rows(outer_sum(mixed_low, grad_out))
    grad_mixed = back_prod(grad_out, mixer_full)
    grad_gelu = gelu_pull(grad_mixed * state_flat)[0].astype(BF16)
    direct = (grad_mixed * gelu_vals).reshape(row_count, tok_count, lru)
    decay_next = jnp.concatenate([decay_eff[:, 1:, :], jnp.ones_like(decay_eff[:, :1, :])], axis=1)
    tail_prod, tail_state = lax.associative_scan(
        compose, (decay_next, direct), axis=1, reverse=True
    )
    back_ends = lax.all_gather(decay_eff[:, 0] * tail_state[:, 0], "seq", axis=0)
    back = jnp.zeros((row_count, lru), F32)
    back_in = back
    for i in range(seq_count - 1, 0, -1):
        back = all_ends[i, 0] * back + back_ends[i]
        back_in = jnp.where(seq_at == i - 1, back, back_in)
    adjoint = tail_state + tail_prod * back_in[:, None, :]
    state_prev = jnp.concatenate([carry_in[:, None, :], state[:, :-1, :]], axis=1)
    decay_pre_grad, admit_pre_grad, conv_direct, rate_grad = coef_pull(
        (adjoint * state_prev, adjoint, jnp.zeros_like(decay_vals))
    )
    grad_decay = decay_pre_grad.reshape(flat, lru).astype(BF16)
    grad_admit = admit_pre_grad.reshape(flat, lru).astype(BF16)
    grad_da = jnp.concatenate([grad_decay, grad_admit], axis=1)
    decay_admit_grad = scatter_rows(outer_sum(conv_flat, grad_da))
    decay_b_grad = jnp.sum(grad_decay, axis=0, dtype=F32)
    admit_b_grad = jnp.sum(grad_admit, axis=0, dtype=F32)
    grad_conv = (conv_direct.reshape(flat, lru) + back_prod(grad_da, decay_admit)).astype(BF16)
    grad_conv = grad_conv.reshape(row_count, tok_count, lru)
    grad_conv_wide = grad_conv.astype(F32)
    tap_grads = []
    for k in range(taps):
        window = extended[:, rim - k : rim - k + tok_count, :]
        mask = (since_here >= k)[..., None].astype(F32)
        tap_grads.append(jnp.sum(grad_conv_wide * window * mask, axis=(0, 1)))
    conv_grad = jnp.stack(tap_grads, axis=1)
    rim_after = shift_seq(grad_conv[:, :rim, :], -1, seq_count)
    grad_ext = jnp.concatenate([grad_conv, rim_after], axis=1).astype(F32)
    branch_grad = jnp.zeros((row_count, tok_count, lru), F32)
    for k in range(taps):
        ahead = (since_ext[:, k : k + tok_count] >= k)[..., None].astype(F32)
        branch_grad = branch_grad + conv_taps[:, k] * grad_ext[:, k : k + tok_count, :] * ahead
    branch_grad_low = branch_grad.reshape(flat, lru).astype(BF16)
    grad_gi = jnp.concatenate([grad_gelu, branch_grad_low], axis=1)
    gelu_input_grad = scatter_rows(outer_sum(normed_low, grad_gi))
    grad_in_norm, gain_one_grad = norm_one_pull(back_prod(grad_gi, gelu_input))
    input_grad_tok = (grad_middle + grad_in_norm).astype(BF16)
    input_grad_tok = input_grad_tok.reshape(row_count, tok_count, model)
    input_grad = lax.all_to_all(input_grad_tok, "seq", split_axis=2, concat_axis=1, tiled=True)
    gate_term = jnp.sum(decay_vals, axis=(0, 1)) / float(flat * dev_count)
    small_grads = (
        gain_one_grad,
        conv_grad,
        decay_b_grad,
        admit_b_grad,
        rate_grad,
        gain_two_grad,
        gate_term,
    )
    packed_grads = jnp.concatenate([g.reshape(dev_count, -1) for g in small_grads], axis=1)
    reduced = lax.psum_scatter(packed_grads, ALL, scatter_dimension=0, tiled=True)
    own = split_small(reduced, [g.size // dev_count for g in small_grads])
    return (
        block_output,
        input_grad,
        own[0].reshape(-1),
        gelu_input_grad[:, :lru],
        gelu_input_grad[:, lru:],
        own[1].reshape(-1, taps),
        decay_admit_grad[:, :lru],
        own[2].reshape(-1),
        decay_admit_grad[:, lru:],
        own[3].reshape(-1),
        own[4].reshape(-1),
        mixer_grad,
        own[5].reshape(-1),
        gate_up_grad[:, :feed],
        gate_up_grad[:, feed:],
        down_grad,
        own[6].reshape(-1),
    )


def solution(mesh):
    rows = P(ALL, None)
    vec = P(ALL)
    placed = (
        P("dp", None, "seq"),
        P("dp", "seq", None),
        P("dp", None),
        vec,
        rows,
        rows,
        rows,
        rows,
        vec,
        rows,
        vec,
        vec,
        rows,
        vec,
        rows,
        rows,
        rows,
    )
    outs = (
        P("dp", "seq", None),
        P("dp", None, "seq"),
        vec,
        rows,
        rows,
        rows,
        rows,
        vec,
        rows,
        vec,
        vec,
        rows,
        vec,
        rows,
        rows,
        rows,
        vec,
    )
    return jax.shard_map(local, mesh=mesh, in_specs=placed, out_specs=outs, check_vma=False)
```

```python
from functools import partial

import jax
import jax.numpy as jnp
from jax import lax
from jax.experimental import pallas as pl
from jax.experimental.pallas import tpu as pltpu
from jax.sharding import PartitionSpec as P

EPSILON = 1e-06
DECAY_SCALE = 8.0
ALL = ("seq", "dp")
F32 = jnp.float32
BF16 = jnp.bfloat16
GELU_C = 0.7978845608028654
STARTS = (0, 0, 1, 1, 2, 2, 3, 4, 5, 6, 7, 8)


def rms_norm(values, gain_vec):
    return (
        values * lax.rsqrt(jnp.mean(values * values, axis=-1, keepdims=True) + EPSILON) * gain_vec
    )


def smooth_gate(values):
    return jax.nn.gelu(values, approximate=True)


def compose(earlier, latter):
    return (earlier[0] * latter[0], latter[0] * earlier[1] + latter[1])


def since_start(doc_starts, positions):
    begins = jnp.max(
        jnp.where(doc_starts[:, None, :] <= positions[None, :, None], doc_starts[:, None, :], 0),
        axis=-1,
    )
    return positions[None, :] - begins


def coefficients(decay_pre, admit_pre, conv_vals, rate_vec, reset_mask):
    recall = jax.nn.sigmoid(decay_pre)
    admit_vals = jax.nn.sigmoid(admit_pre)
    log_decay = -DECAY_SCALE * recall * jax.nn.softplus(-rate_vec)
    decay_vals = jnp.exp(log_decay)
    keep_mask = 1.0 - reset_mask
    scale_in = reset_mask + keep_mask * jnp.sqrt(-jnp.expm1(2.0 * log_decay))
    return (decay_vals * keep_mask, scale_in * admit_vals * conv_vals, decay_vals)


def dot(left, right):
    return jnp.dot(left, right, preferred_element_type=F32)


def outer_sum(left, right):
    return lax.dot_general(left, right, (((0,), (0,)), ((), ())), preferred_element_type=F32)


def back_prod(grad_rows, weight):
    return lax.dot_general(
        grad_rows, weight, (((1,), (1,)), ((), ())), preferred_element_type=F32
    )


def gather_rows(shard):
    return lax.all_gather(shard, ALL, axis=0, tiled=True)


def scatter_rows(partial):
    return lax.psum_scatter(partial.astype(BF16), ALL, scatter_dimension=0, tiled=True).astype(F32)


def shift_seq(values, step, seq_count):
    pairs = [(i, i + step) for i in range(seq_count) if 0 <= i + step < seq_count]
    return lax.ppermute(values, "seq", pairs)


def pack_small(pieces):
    return jnp.concatenate([p.reshape(1, -1) for p in pieces], axis=1)


def split_small(packed, widths):
    out, at = [], 0
    for width in widths:
        out.append(packed[:, at : at + width])
        at += width
    return out


MESH = pl.DeviceIdType.MESH
PLANE = 2


def fast_shapes(shards, seq_count, dp_count, row_count, tok_count):
    if dp_count != 2 * PLANE * PLANE or seq_count < 2 or row_count != 2 or tok_count != 128:
        return False
    return all(s.shape[0] in (32, 48, 96) and s.shape[1] % 512 == 0 for s in shards)


class Place:
    def __init__(self, seq_count):
        self.nz = seq_count
        self.z = lax.axis_index("seq")
        self.d = lax.axis_index("dp")
        self.c = lax.rem(self.d, 2)
        self.b = lax.rem(self.d // 2, 2)
        self.a = self.d // 4
        self.core = (self.z, self.d + 1 - 2 * self.c)
        self.peer = {
            "b": (self.z, self.d + 2 - 4 * self.b),
            "a": (self.z, self.d + 4 - 8 * self.a),
        }

    def at(self, z):
        return (z, self.d)

    def greet(self):
        barrier = pltpu.get_barrier_semaphore()
        others = [self.core, self.peer["a"], self.peer["b"]]
        others += [self.at(lax.rem(self.z + o, self.nz)) for o in range(1, self.nz)]
        for other in others:
            pl.semaphore_signal(barrier, inc=1, device_id=other, device_id_type=MESH)
        pl.semaphore_wait(barrier, len(others))


def step_cols(width):
    unit = width // 8
    return {"A": (0, 3 * unit), "B": (3 * unit, 6 * unit), "C": (6 * unit, width)}


def chunk_list(shapes):
    chunks = []
    for i, (rows, cols) in enumerate(shapes):
        wide = min(cols, 3072)
        tall = rows if wide < 3072 and rows <= 48 else (48 if wide < 3072 else 16)
        for c0 in range(0, cols, wide):
            for r0 in range(0, rows, tall):
                chunks.append((i, r0, tall, c0, wide))
    return chunks


class Gather:
    def __init__(self, place, outs, chunks, send, recv, starts):
        self.p, self.outs, self.chunks = place, outs, chunks
        self.send, self.recv, self.starts = send, recv, starts
        self.started = []
        nz = place.nz
        self.depth = nz + 4

    def view(self, k, z, a, b, c, route):
        i, r0, nr, c0, nc = self.chunks[k]
        lo, hi = (0, nc) if route is None else step_cols(nc)[route]
        full = slice(None)
        one = lambda v: full if v is None else pl.ds(v, 1)
        return self.outs[i].at[
            one(z), one(a), one(b), one(c), pl.ds(r0, nr), pl.ds(c0 + lo, hi - lo)
        ]

    def copy(self, k, view, s_at, r_at, dev):
        return pltpu.make_async_remote_copy(
            view, view, self.send.at[k, s_at], self.recv.at[k, r_at], device_id=dev, device_id_type=MESH
        )

    def put(self, k, view, s_at, r_at, dev, cond=None):
        cp = self.copy(k, view, s_at, r_at, dev)
        if cond is None:
            cp.start()
        else:
            pl.when(cond)(cp.start)
        self.started.append((cp, cond))

    def take(self, k, view, r_at, cond=None):
        cp = self.copy(k, view, 0, r_at, self.p.core)
        if cond is None:
            cp.wait_recv()
        else:
            pl.when(cond)(cp.wait_recv)

    def sem(self, route, phase, z=0):
        nz = self.p.nz
        slot = {"first": 0, "up": 1, "down": 1 + nz, "mid": 1 + 2 * nz, "last": 1 + 3 * nz}[phase]
        return {"A": 0, "B": 1, "C": 2}[route] * (1 + 4 * nz) + slot + z

    @staticmethod
    def sem_count(nz):
        return 3 * (1 + 4 * nz) + 1

    def order(self, k, route):
        if route == "C":
            return ("a", "b") if k % 2 else ("b", "a")
        return ("b", "a") if route == "A" else ("a", "b")

    def z_unit(self, k, route, z):
        p = self.p
        first = self.order(k, route)[0]
        a = None if route != "C" and first == "a" else p.a
        b = None if route != "C" and first == "b" else p.b
        return self.view(k, z, a, b, p.c, route)

    def z_own(self, k, route):
        p = self.p
        unit = self.z_unit(k, route, p.z)
        self.put(k, unit, self.sem(route, "up", p.z), self.sem(route, "up", p.z), p.at(p.z + 1), p.z < p.nz - 1)
        self.put(k, unit, self.sem(route, "down", p.z), self.sem(route, "down", p.z), p.at(p.z - 1), p.z > 0)
        self.after(k, route, p.z, None)

    def after(self, k, route, z, cond):
        p = self.p
        first, second = self.order(k, route)
        dim = first if route == "C" else second
        name = "mid" if route == "C" else "last"
        self.put(k, self.z_unit(k, route, z), self.sem(route, name, z), self.sem(route, name, z), p.peer[dim], cond)

    def z_hop(self, k, route, h):
        p = self.p
        low, high = p.z - h, p.z + h
        has_low, has_high = low >= 0, high < p.nz
        low_at, high_at = jnp.maximum(low, 0), jnp.minimum(high, p.nz - 1)
        unit = self.z_unit(k, route, low_at)
        self.take(k, unit, self.sem(route, "up", low_at), has_low)
        if h < p.nz - 1:
            self.put(k, unit, self.sem(route, "up", low_at), self.sem(route, "up", low_at), p.at(p.z + 1), has_low & (p.z < p.nz - 1))
        self.after(k, route, low_at, has_low)
        unit = self.z_unit(k, route, high_at)
        self.take(k, unit, self.sem(route, "down", high_at), has_high)
        if h < p.nz - 1:
            self.put(k, unit, self.sem(route, "down", high_at), self.sem(route, "down", high_at), p.at(p.z - 1), has_high & (p.z > 0))
        self.after(k, route, high_at, has_high)

    def c_last(self, k, z, cond):
        p = self.p
        first, second = self.order(k, "C")
        a = None if first == "a" else p.a
        b = None if first == "b" else p.b
        peer_a = 1 - p.a if first == "a" else p.a
        peer_b = 1 - p.b if first == "b" else p.b
        self.take(k, self.view(k, z, peer_a, peer_b, p.c, "C"), self.sem("C", "mid", z), cond)
        self.put(k, self.view(k, z, a, b, p.c, "C"), self.sem("C", "last", z), self.sem("C", "last", z), p.peer[second], cond)

    def c_last_hop(self, k, h):
        p = self.p
        if h == 0:
            self.c_last(k, p.z, None)
            return
        low, high = p.z - h, p.z + h
        self.c_last(k, jnp.maximum(low, 0), low >= 0)
        self.c_last(k, jnp.minimum(high, p.nz - 1), high < p.nz)

    def stage(self, k, s):
        p, nz = self.p, self.p.nz
        if s == 0:
            for route in "AB":
                first = self.order(k, route)[0]
                at = self.sem(route, "first")
                self.put(k, self.view(k, p.z, p.a, p.b, p.c, route), at, at, p.peer[first])
            self.z_own(k, "C")
        if s == 1:
            for route in "AB":
                first = self.order(k, route)[0]
                a = 1 - p.a if first == "a" else p.a
                b = 1 - p.b if first == "b" else p.b
                self.take(k, self.view(k, p.z, a, b, p.c, route), self.sem(route, "first"))
                self.z_own(k, route)
        if 1 <= s < nz:
            self.z_hop(k, "C", s)
        if 2 <= s <= nz:
            self.z_hop(k, "A", s - 1)
            self.z_hop(k, "B", s - 1)
        if 2 <= s < nz + 2:
            self.c_last_hop(k, s - 2)
        if s == nz + 2:
            for z in range(nz):
                for route in "ABC":
                    second = self.order(k, route)[1]
                    a = 1 - p.a if second == "a" else None
                    b = 1 - p.b if second == "b" else None
                    self.take(k, self.view(k, z, a, b, p.c, route), self.sem(route, "last", z))
            at = self.sem_count(nz) - 1
            self.put(k, self.view(k, None, None, None, p.c, None), at, at, p.core)
        if s == nz + 3:
            at = self.sem_count(nz) - 1
            self.take(k, self.view(k, None, None, None, 1 - p.c, None), at)

    def tick(self, t):
        for k in range(len(self.chunks)):
            s = t - self.starts[k]
            if 0 <= s < self.depth:
                self.stage(k, s)

    def ticks(self):
        return max(self.starts) + self.depth

    def finish(self):
        for cp, cond in self.started:
            if cond is None:
                cp.wait_send()
            else:
                pl.when(cond)(cp.wait_send)


LANE = 128


def spread_constants(model, lru, dev_count):
    out = []
    for width in (model, lru):
        per = width // dev_count
        lane = jnp.arange(width, dtype=jnp.int32)[None, :]
        out.append((lane % per == jnp.arange(LANE, dtype=jnp.int32)[:, None]).astype(BF16))
        out.append((lane // per == jnp.arange(dev_count, dtype=jnp.int32)[:, None]).astype(F32))
    return out


def small_rows(norm_gain, conv_weight, decay_bias, admit_bias, decay_rate, feed_gain):
    rate = decay_rate.astype(F32)
    scale = -DECAY_SCALE * jax.nn.softplus(-rate)
    high = lax.reduce_precision(scale, 8, 7)
    mid = lax.reduce_precision(scale - high, 8, 7)
    low = lax.reduce_precision(scale - high - mid, 8, 7)
    taps = [conv_weight[:, k] for k in range(conv_weight.shape[1])]
    rows = [norm_gain, feed_gain, decay_bias, admit_bias, high, mid, low, rate, *taps]
    rows = [jnp.pad(v.astype(F32), (0, LANE - v.shape[0])) for v in rows]
    return jnp.stack(rows + [jnp.zeros((LANE,), F32)] * (16 - len(rows)))


def decay_terms(pre, scale):
    recall = jax.nn.sigmoid(pre)
    log_decay = recall * scale
    decay = jnp.exp(log_decay)
    y = 2.0 * log_decay
    series = 1.0 + y * (1 / 7)
    for n in (6, 5, 4, 3, 2):
        series = 1.0 + y * (1 / n) * series
    lost = jnp.where(y > -0.35, -y * series, 1.0 - decay * decay)
    return recall, decay, lost


def scan_block(prod, state, reverse=False):
    length = prod.shape[0]
    at = lax.broadcasted_iota(jnp.int32, prod.shape, 0)
    step = 1
    while step < length:
        inside = at < length - step if reverse else at >= step
        turn = length - step if reverse else step
        prod_far = jnp.where(inside, pltpu.roll(prod, turn, 0), 1.0)
        state_far = jnp.where(inside, pltpu.roll(state, turn, 0), 0.0)
        state = prod * state_far + state
        prod = prod * prod_far
        step *= 2
    return prod, state


def lanes(c, width=LANE):
    return pl.ds(pl.multiple_of(c * width, width), width)


def loop(count, body):
    def step(i, carry):
        body(i)
        return carry

    lax.fori_loop(0, count, step, 0)


def stream_tiles(count, fetch, use):
    for cp in fetch(0, 0):
        cp.start()

    def step(j, carry):
        slot = lax.rem(j, 2)

        @pl.when(j + 1 < count)
        def _():
            for cp in fetch(j + 1, 1 - slot):
                cp.start()

        for cp in fetch(j, slot):
            cp.wait()
        use(j, slot)
        return carry

    lax.fori_loop(0, count, step, 0)


def mat(value):
    return value.reshape(-1, value.shape[-1])


class Forward:
    def __init__(self, refs, place, weights):
        self.__dict__.update(refs)
        self.p, self.weights = place, weights
        self.tok = self.xs.shape[1]
        self.rows = self.xs.shape[0]
        self.flat = self.rows * self.tok
        self.lru = self.gelu_pre.shape[1]
        self.model = self.xs.shape[2]
        self.feed = self.hidden.shape[1]
        self.stores = []

    def save(self, name):
        cp = pltpu.make_async_copy(getattr(self, name), self.keep[name], self.keep_sem.at[len(self.stores)])
        cp.start()
        self.stores.append(cp)

    def fetch(self, i, buf, sem, starts, width):
        def copies(j, slot):
            out = []
            for n, start in enumerate(starts):
                src = self.weights[i].at[:, :, :, :, :, pl.ds(pl.multiple_of(start + j * width, LANE), width)]
                dst = buf.at[slot, :, :, :, :, :, pl.ds(n * width, width)]
                out.append(pltpu.make_async_copy(src, dst, sem.at[slot, n]))
            return out

        return copies

    def vectors(self):
        cp = pltpu.make_async_copy(self.small_all, self.small_vm, self.misc_sem.at[0])
        cp.start()
        cp.wait()
        nz = self.p.nz

        def spread(row, hot, mask):
            vals = self.small_vm[:, :, row, :].reshape(nz * 8, LANE).astype(BF16)
            wide = jnp.dot(vals, hot[...], preferred_element_type=F32)
            return jnp.sum(wide * mask[...], axis=0, keepdims=True)

        for row in range(2):
            self.vec[row : row + 1, 0 : self.model] = spread(row, self.hot_m, self.mask_m)
        for row in range(2, 12):
            self.vec[row : row + 1, :] = spread(row, self.hot_l, self.mask_l)
        self.vec[4:5, :] = self.vec[4:5, :] + self.vec[5:6, :] + self.vec[6:7, :]

    def norm(self, load, count, gain_row, out):
        gain = self.vec[gain_row : gain_row + 1, 0 : self.model]

        def body(i):
            v = load(i)
            q = lax.rsqrt(jnp.mean(v * v, axis=-1, keepdims=True) + EPSILON)
            out[pl.ds(pl.multiple_of(i * 32, 32), 32), :] = (v * q * gain).astype(BF16)

        loop(count, body)

    def norm_one(self):
        per = self.tok // 32

        def main(i):
            return self.xs[i // per, pl.ds(pl.multiple_of(lax.rem(i, per) * 32, 32), 32), :].astype(F32)

        self.norm(main, self.flat // 32, 0, self.normed.at[0 : self.flat])
        self.norm(
            lambda i: self.halo_x[...].reshape(2 * 16, self.model).astype(F32),
            1,
            0,
            self.normed.at[self.flat : self.flat + 32],
        )
        self.save("normed_main")
        self.save("xs")

    def gelu_input(self):
        half = self.lru // 512

        def use(j, slot):
            res = jnp.dot(self.normed[0 : self.flat, :], mat(self.w_gi[slot]), preferred_element_type=F32)
            self.gelu_pre[:, lanes(j, 512)] = res

        stream_tiles(half, self.fetch(0, self.w_gi, self.w_sem, (0,), 512), use)

        def use_two(j, slot):
            res = jnp.dot(self.normed[...], mat(self.w_gi[slot]), preferred_element_type=F32).astype(BF16)
            self.branch[:, lanes(j, 512)] = res

        stream_tiles(half, self.fetch(0, self.w_gi, self.w_sem, (self.lru,), 512), use_two)

        def conv(c):
            for r in range(self.rows):
                at = slice(r * self.tok, (r + 1) * self.tok)
                head = self.branch[self.flat + 16 * r : self.flat + 16 * (r + 1), lanes(c)].astype(F32)
                wide = jnp.concatenate([head, self.branch[at, lanes(c)].astype(F32)], axis=0)
                since = self.since[at, :]
                total = jnp.zeros((self.tok, LANE), F32)
                for k in range(4):
                    moved = wide if k == 0 else pltpu.roll(wide, k, 0)
                    tap = self.vec[8 + k : 9 + k, lanes(c)]
                    total = total + tap * moved[16:] * (since >= k).astype(F32)
                self.conv[at, lanes(c)] = total.astype(BF16)

        loop(self.lru // LANE, conv)
        self.save("gelu_pre")
        self.save("branch")
        self.save("conv")

    def gates(self, first, count):
        self.sums[...] = jnp.zeros_like(self.sums) if first == 0 else self.sums[...]

        def use(j, slot):
            self.tile[...] = jnp.dot(self.conv[...], mat(self.w_da[slot]), preferred_element_type=F32)
            base = (first + j) * 4

            def block(i):
                c = base + i
                gate_sum = jnp.zeros((1, LANE), F32)
                for r in range(self.rows):
                    at = slice(r * self.tok, (r + 1) * self.tok)
                    pre = self.tile[at, lanes(i)] + self.vec[2:3, lanes(c)]
                    admit_pre = self.tile[at, lanes(i + 4)] + self.vec[3:4, lanes(c)]
                    self.decay_pre[at, lanes(c)] = pre
                    self.admit_pre[at, lanes(c)] = admit_pre
                    recall, decay, lost = decay_terms(pre, self.vec[4:5, lanes(c)])
                    reset = (self.since[at, :] == 0).astype(F32)
                    keep = 1.0 - reset
                    scale_in = reset + keep * jnp.sqrt(lost)
                    update = scale_in * jax.nn.sigmoid(admit_pre) * self.conv[at, lanes(c)].astype(F32)
                    prod, state = scan_block(decay * keep, update)
                    self.prod[at, lanes(c)] = prod
                    self.state[at, lanes(c)] = state
                    self.ends[self.p.z, r : r + 1, lanes(c)] = prod[self.tok - 1 :, :]
                    self.ends[self.p.z, 8 + r : 9 + r, lanes(c)] = state[self.tok - 1 :, :]
                    gate_sum = gate_sum + jnp.sum(decay, axis=0, keepdims=True)
                self.sums[0:1, lanes(c)] = gate_sum

            loop(4, block)

        starts = (first * 512, self.lru + first * 512)
        stream_tiles(count, self.fetch(1, self.w_da, self.w_sem, starts, 512), use)

    def gates_saved(self):
        self.save("decay_pre")
        self.save("admit_pre")
        self.save("sums")

    def send_ends(self):
        p = self.p
        self.end_moves = []
        for o in range(1, p.nz):
            view = self.ends.at[p.z]
            cp = pltpu.make_async_remote_copy(
                view, view, self.e_send.at[o - 1], self.e_recv.at[o - 1],
                device_id=p.at(lax.rem(p.z + o, p.nz)), device_id_type=MESH,
            )
            cp.start()
            self.end_moves.append(cp)

    def mix(self):
        p = self.p
        for o in range(1, p.nz):
            view = self.ends.at[lax.rem(p.z + p.nz - o, p.nz)]
            pltpu.make_async_remote_copy(
                view, view, self.e_send.at[o - 1], self.e_recv.at[o - 1],
                device_id=p.core, device_id_type=MESH,
            ).wait_recv()

        def block(c):
            carry = jnp.zeros((8, LANE), F32)
            into = carry
            for i in range(p.nz - 1):
                carry = self.ends[i, 0:8, lanes(c)] * carry + self.ends[i, 8:16, lanes(c)]
                into = jnp.where(p.z == i + 1, carry, into)
            self.carry[:, lanes(c)] = into
            for r in range(self.rows):
                at = slice(r * self.tok, (r + 1) * self.tok)
                state = self.state[at, lanes(c)] + self.prod[at, lanes(c)] * into[r : r + 1, :]
                self.state[at, lanes(c)] = state
                gelu = smooth_gate(self.gelu_pre[at, lanes(c)])
                self.mixed[at, lanes(c)] = (state * gelu).astype(BF16)

        loop(self.lru // LANE, block)
        self.save("state")
        self.save("carry")
        self.save("ends")
        self.save("mixed")

        def use(j, slot):
            res = jnp.dot(self.mixed[...], mat(self.w_mx[slot]), preferred_element_type=F32)
            x = self.xs[:, :, lanes(j, 512)].astype(F32).reshape(self.flat, 512)
            self.middle[:, lanes(j, 512)] = x + res

        stream_tiles(self.model // 512, self.fetch(2, self.w_mx, self.w_sem, (0,), 512), use)
        self.norm(
            lambda i: self.middle[pl.ds(pl.multiple_of(i * 32, 32), 32), :], self.flat // 32, 1, self.normed_two
        )
        self.save("middle")
        self.save("normed_two")

    def gate_up(self, first, count):
        def use(j, slot):
            res = jnp.dot(self.normed_two[...], mat(self.w_gu[slot]), preferred_element_type=F32)
            gate, up = res[:, 0:512], res[:, 512:1024]
            at = lanes(first + j, 512)
            self.gate_pre[:, at] = gate
            self.up[:, at] = up
            self.hidden[:, at] = (smooth_gate(gate) * up).astype(BF16)

        starts = (first * 512, self.feed + first * 512)
        stream_tiles(count, self.fetch(3, self.w_gu, self.w_sem, starts, 512), use)

    def gate_saved(self):
        self.save("gate_pre")
        self.save("up")
        self.save("hidden")

    def down(self):
        def use(j, slot):
            res = jnp.dot(self.hidden[...], mat(self.w_dn[slot]), preferred_element_type=F32)
            self.block[:, lanes(j, 256)] = (self.middle[:, lanes(j, 256)] + res).astype(BF16)

        stream_tiles(self.model // 256, self.fetch(4, self.w_dn, self.w_sem, (0,), 256), use)
        self.save("block")

    def finish(self):
        for cp in self.stores:
            cp.wait()
        for cp in self.end_moves:
            cp.wait_send()


KEEP = (
    "xs", "normed_main", "gelu_pre", "branch", "conv", "decay_pre", "admit_pre", "sums", "state", "carry",
    "ends", "mixed", "middle", "normed_two", "gate_pre", "up", "hidden", "block",
)


def forward_kernel(seq_count, starts, chunks, names, n_keep, *refs):
    refs = list(refs)
    x_ref, small_ref, since, hot_m, mask_m, hot_l, mask_l = refs[:7]
    srcs = refs[7:15]
    at = 15
    small_all, vec = refs[at : at + 2]
    outs = refs[at + 2 : at + 7]
    keep = dict(zip(KEEP, refs[at + 7 : at + 7 + n_keep]))
    at += 7 + n_keep
    table = dict(zip(names, refs[at : at + len(names)]))
    p = Place(seq_count)
    table.update(
        small_all=small_all, vec=vec, since=since, hot_m=hot_m, mask_m=mask_m, hot_l=hot_l, mask_l=mask_l, keep=keep,
    )
    table["normed_main"] = table["normed"].at[0 : since.shape[0]]
    f = Forward(table, p, outs)
    one = pl.ds
    copies = []
    own_sem = table["own_sem"]
    k = 0
    for out, count in zip(outs, (2, 2, 1, 2, 1)):
        col = 0
        for _ in range(count):
            cols = srcs[k].shape[-1]
            dst = out.at[one(p.z, 1), one(p.a, 1), one(p.b, 1), one(p.c, 1), :, one(col, cols)]
            copies.append(pltpu.make_async_copy(srcs[k], dst, own_sem.at[k]))
            col += cols
            k += 1
    tok, feat = f.tok, x_ref.shape[2]
    here = one(pl.multiple_of(p.z * feat, LANE), feat)
    copies.append(pltpu.make_async_copy(x_ref.at[:, one(p.z * tok, tok), :], f.xs.at[:, :, here], own_sem.at[k]))
    copies.append(pltpu.make_async_copy(small_ref, small_all.at[one(p.z, 1), one(p.d, 1)], own_sem.at[k + 1]))
    for cp in copies:
        cp.start()

    def halo(z):
        return x_ref.at[:, one(pl.multiple_of(jnp.maximum(z * tok - 16, 0), 16), 16), :]

    own_halo = lambda: pltpu.make_async_copy(halo(p.z), f.halo_x.at[:, :, here], own_sem.at[k + 2])

    @pl.when(p.z > 0)
    def _():
        own_halo().start()

    @pl.when(p.z == 0)
    def _():
        f.halo_x[...] = jnp.zeros_like(f.halo_x)

    f.ends[...] = jnp.zeros_like(f.ends)
    f.sums[...] = jnp.zeros_like(f.sums)
    p.greet()
    x_moves = []

    def x_copy(o):
        to = lax.rem(p.z + o, p.nz)
        return pltpu.make_async_remote_copy(
            x_ref.at[:, one(pl.multiple_of(to * tok, 16), tok), :], f.xs.at[:, :, here], table["x_send"].at[o - 1],
            table["x_recv"].at[o - 1], device_id=p.at(to), device_id_type=MESH,
        )

    def h_copy(o):
        to = lax.rem(p.z + o, p.nz)
        return to > 0, pltpu.make_async_remote_copy(
            halo(to), f.halo_x.at[:, :, here], table["h_send"].at[o - 1],
            table["h_recv"].at[o - 1], device_id=p.at(to), device_id_type=MESH,
        )

    for o in range(1, p.nz):
        x_copy(o).start()
        cond, cp = h_copy(o)
        pl.when(cond)(cp.start)
    for cp in copies:
        cp.wait()
    s_send, s_recv = table["s_send"], table["s_recv"]
    s_moves = []

    def small_put(view, at, dev):
        cp = pltpu.make_async_remote_copy(view, view, s_send.at[at], s_recv.at[at], device_id=dev, device_id_type=MESH)
        cp.start()
        s_moves.append(cp)

    def small_view(d, n):
        return small_all.at[one(p.z, 1), one(d, n)]

    small_put(small_view(p.d, 1), 0, p.core)
    g = Gather(p, outs, chunks, table["send"], table["recv"], starts)
    last = [max(starts[i] for i in range(len(chunks)) if chunks[i][0] == w) + g.depth - 1 for w in range(5)]
    plan = {
        3: [f.vectors, f.norm_one],
        last[0]: [f.gelu_input],
        max(last[1], last[0] + 1): [lambda: f.gates(0, 2)],
        max(last[1], last[0] + 1) + 1: [lambda: f.gates(2, 1), f.send_ends, f.gates_saved],
        max(last[2], max(last[1], last[0] + 1) + 2): [f.mix],
    }
    plan.setdefault(last[3], []).append(lambda: f.gate_up(0, 2))
    plan.setdefault(last[3] + 1, []).append(lambda: f.gate_up(2, 2))
    plan.setdefault(max(last[3] + 2, last[4]), []).extend([lambda: f.gate_up(4, 2), f.gate_saved, f.down])
    ticks = max(g.ticks(), max(plan) + 1)
    for t in range(ticks):
        g.tick(t)
        if t == 0:
            s_moves[0].wait_recv()
            small_put(small_view(p.d - p.c, 2), 1, p.peer["b"])
        if t == 1:
            s_moves[1].wait_recv()
            small_put(small_view(4 * p.a, 4), 2, p.peer["a"])
        if t == 2:
            s_moves[2].wait_recv()
            for o in range(1, p.nz):
                small_put(small_view(0, 8), 2 + o, p.at(lax.rem(p.z + o, p.nz)))
        if t == 3:
            for cp in s_moves[3:]:
                cp.wait_recv()
            for o in range(1, p.nz):
                x_copy(o).wait_recv()
                pl.when(p.z > 0)(h_copy(o)[1].wait_recv)

            @pl.when(p.z > 0)
            def _():
                own_halo().wait()

        for action in plan.get(t, ()):
            action()
    for cp in s_moves:
        cp.wait_send()
    for o in range(1, p.nz):
        x_copy(o).wait_send()
        cond, cp = h_copy(o)
        pl.when(cond)(cp.wait_send)
    f.finish()
    g.finish()


def forward_pass(x_heads, small, since, shards, seq_count, starts):
    groups = ((0, 1), (2, 3), (4,), (5, 6), (7,))
    rows_cols = [(shards[g[0]].shape[0], sum(shards[i].shape[1] for i in g)) for g in groups]
    chunks = chunk_list(rows_cols)
    row_count, row_len, feat = x_heads.shape
    tok, model = row_len // seq_count, feat * seq_count
    flat = row_count * tok
    lru, feed = rows_cols[0][1] // 2, rows_cols[3][1] // 2
    nz = seq_count
    srcs = [s.reshape(1, 1, 1, 1, *s.shape) for s in shards]
    hbm = pl.BlockSpec(memory_space=pltpu.HBM)
    vmem = pl.BlockSpec(memory_space=pltpu.VMEM)
    keep_shapes = {
        "xs": ((row_count, tok, model), BF16),
        "normed_main": ((flat, model), BF16),
        "gelu_pre": ((flat, lru), F32),
        "branch": ((flat + 32, lru), BF16),
        "conv": ((flat, lru), BF16),
        "decay_pre": ((flat, lru), F32),
        "admit_pre": ((flat, lru), F32),
        "sums": ((8, lru), F32),
        "state": ((flat, lru), F32),
        "carry": ((8, lru), F32),
        "ends": ((nz, 16, lru), F32),
        "mixed": ((flat, lru), BF16),
        "middle": ((flat, model), F32),
        "normed_two": ((flat, model), BF16),
        "gate_pre": ((flat, feed), F32),
        "up": ((flat, feed), F32),
        "hidden": ((flat, feed), BF16),
        "block": ((flat, model), BF16),
    }
    scratch = {n: pltpu.VMEM(*s) for n, s in keep_shapes.items() if n != "normed_main"}
    dma = pltpu.SemaphoreType.DMA
    sems = Gather.sem_count(nz)
    scratch.update(
        normed=pltpu.VMEM((flat + 32, model), BF16),
        halo_x=pltpu.VMEM((row_count, 16, model), BF16),
        small_vm=pltpu.VMEM((nz, 8, 16, LANE), F32),
        prod=pltpu.VMEM((flat, lru), F32),
        tile=pltpu.VMEM((flat, 1024), F32),
        w_gi=pltpu.VMEM((2, nz, 2, 2, 2, rows_cols[0][0], 512), BF16),
        w_da=pltpu.VMEM((2, nz, 2, 2, 2, rows_cols[1][0], 1024), BF16),
        w_mx=pltpu.VMEM((2, nz, 2, 2, 2, rows_cols[2][0], 512), BF16),
        w_gu=pltpu.VMEM((2, nz, 2, 2, 2, rows_cols[3][0], 1024), BF16),
        w_dn=pltpu.VMEM((2, nz, 2, 2, 2, rows_cols[4][0], 256), BF16),
        w_sem=dma((2, 2)),
        keep_sem=dma((len(KEEP),)),
        misc_sem=dma((1,)),
        own_sem=dma((len(srcs) + 3,)),
        x_send=dma((nz,)),
        x_recv=dma((nz,)),
        h_send=dma((nz,)),
        h_recv=dma((nz,)),
        s_send=dma((nz + 3,)),
        s_recv=dma((nz + 3,)),
        e_send=dma((nz,)),
        e_recv=dma((nz,)),
        send=dma((len(chunks), sems)),
        recv=dma((len(chunks), sems)),
    )
    names = list(scratch)
    out_shape = [jax.ShapeDtypeStruct((nz, 8, 16, LANE), F32), jax.ShapeDtypeStruct((16, lru), F32)]
    out_shape += [jax.ShapeDtypeStruct((nz, PLANE, PLANE, 2, r, c), BF16) for r, c in rows_cols]
    out_shape += [jax.ShapeDtypeStruct(*keep_shapes[n]) for n in KEEP]
    outs = pl.pallas_call(
        partial(forward_kernel, nz, starts, chunks, names, len(KEEP)),
        out_shape=out_shape,
        in_specs=[hbm, hbm] + [vmem] * 5 + [hbm] * 8,
        out_specs=[hbm, vmem] + [hbm] * (5 + len(KEEP)),
        scratch_shapes=[scratch[n] for n in names],
        compiler_params=pltpu.CompilerParams(
            collective_id=0, has_side_effects=True, vmem_limit_bytes=61 << 20
        ),
        name="forward_pass",
    )(
        x_heads,
        small.reshape(1, 1, 16, LANE),
        jnp.broadcast_to(since.reshape(flat, 1), (flat, LANE)),
        *spread_constants(model, lru, nz * 8),
        *srcs,
    )
    return outs[1], outs[2:7], dict(zip(KEEP, outs[7:]))


C_RING, RING = 8, 5


class Chunk:
    def __init__(self, name, lhs, rhs, rows, width, first):
        self.name, self.lhs, self.rhs = name, lhs, rhs
        self.rows, self.width, self.first = rows, width, first
        self.across = width // 512


class Reduce:
    NAMES = ("C", "YA", "YB", "YC", "PC", "UA", "DA", "UB", "DB", "UC", "DC", "XA", "XB")
    PIECES = {"A": pl.ds(0, 2), "B": pl.ds(2, 2), "C": pl.ds(4, 2)}

    @staticmethod
    def shapes(nz):
        tail = (2, 16, 512)
        plane = PLANE
        a, b, c = (nz, 1, plane), (nz, plane, 1), (nz, 1, 1)
        lead = {
            "YA": a, "YB": b, "YC": b, "PC": c, "UA": a, "DA": a, "UB": b, "DB": b, "UC": c, "DC": c,
            "XA": (1, 1, 1), "XB": (1, 1, 1),
        }
        out = {n: (RING, *v, *tail) for n, v in lead.items()}
        out["C"] = (C_RING, nz, plane, plane, 6, 16, 512)
        return out

    def __init__(self, place, bufs, full, send, recv, produce, deliver):
        self.p, self.bufs, self.full = place, bufs, full
        self.send, self.recv = send, recv
        self.produce, self.deliver = produce, deliver
        self.started = {}
        self.depth = place.nz + 4

    def buf(self, k, name):
        return self.bufs[name].at[k % (C_RING if name == "C" else RING)]

    def order(self, k):
        return ("a", "b") if k % 2 else ("b", "a")

    def part(self, k, route, z, a, b):
        full = slice(None)
        one = lambda v: full if v is None else v if isinstance(v, slice) else pl.ds(v, 1)
        return self.buf(k, "C").at[one(z), one(a), one(b), self.PIECES[route]]

    def copy(self, k, name, src, dst, dev):
        at = self.NAMES.index(name)
        return pltpu.make_async_remote_copy(
            src, dst, self.send.at[k, at], self.recv.at[k, at], device_id=dev, device_id_type=MESH
        )

    def put(self, k, name, src, dst, dev):
        make = lambda: self.copy(k, name, src(), dst(), dev)
        make().start()
        self.started.setdefault(k, []).append((make, None))

    def z_put(self, k, route, way, z):
        p = self.p
        name = ("U" if way > 0 else "D") + route
        span = slice(z + 1, p.nz) if way > 0 else slice(0, z)

        def make():
            a = p.a if route != "B" else None
            b = p.b if route != "A" else None
            return self.copy(k, name, self.part(k, route, span, a, b), self.buf(k, name).at[span], p.at(z + way))

        make().start()
        self.started.setdefault(k, []).append((make, z))

    def take(self, k, name, dst):
        self.copy(k, name, dst, dst, self.p.core).wait_recv()

    def add(self, into, other):
        def one(t):
            into[t] = into[t] + other[t]

        loop(into.shape[0], one)

    def wave(self, k, route, s):
        p, nz = self.p, self.p.nz
        low, high = s - 1, nz - s

        def gather(name, span):
            got = self.buf(k, name).at[span]
            self.take(k, name, got)
            a = p.a if route != "B" else None
            b = p.b if route != "A" else None
            self.add(self.part(k, route, span, a, b), got)

        @pl.when(p.z == low)
        def _():
            if low > 0:
                gather("U" + route, slice(low, nz))
            if low < nz - 1:
                self.z_put(k, route, 1, low)

        @pl.when(p.z == high)
        def _():
            if high < nz - 1:
                gather("D" + route, slice(0, high + 1))
            if high > 0:
                self.z_put(k, route, -1, high)

    def yc(self, k):
        buf = self.buf(k, "YC")
        if self.order(k)[1] == "b":
            return buf
        nz, plane, _, n, r, w = buf.shape
        return buf.reshape(nz, 1, plane, n, r, w)

    def stage(self, k, s):
        p, nz = self.p, self.p.nz
        if s == 0:
            self.produce(k)
            slot = self.full.at[k % 2]
            self.put(k, "C", lambda: slot.at[:, :, :, 1 - p.c], lambda: self.buf(k, "C"), p.core)
        if s == 1:
            self.take(k, "C", self.buf(k, "C"))
            into, own = self.buf(k, "C"), self.full.at[k % 2]

            def one(t):
                for a in range(PLANE):
                    for b in range(PLANE):
                        into[t, a, b] = into[t, a, b] + own[t, a, b, p.c]

            loop(nz, one)
            self.put(k, "YA", lambda: self.part(k, "A", None, 1 - p.a, None), lambda: self.buf(k, "YA"), p.peer["a"])
            self.put(k, "YB", lambda: self.part(k, "B", None, None, 1 - p.b), lambda: self.buf(k, "YB"), p.peer["b"])
            q = self.order(k)[1]
            src = lambda: self.part(k, "C", None, 1 - p.a if q == "a" else None, 1 - p.b if q == "b" else None)
            self.put(k, "YC", src, lambda: self.yc(k), p.peer[q])
        if s == 2:
            make, _ = self.started[k].pop(0)
            make().wait_send()
            self.take(k, "YA", self.buf(k, "YA"))
            self.add(self.part(k, "A", None, p.a, None), self.buf(k, "YA"))
            self.take(k, "YB", self.buf(k, "YB"))
            self.add(self.part(k, "B", None, None, p.b), self.buf(k, "YB"))
            first, q = self.order(k)
            self.take(k, "YC", self.yc(k))
            self.add(self.part(k, "C", None, p.a if q == "a" else None, p.b if q == "b" else None), self.yc(k))
            src = lambda: self.part(
                k, "C", None, 1 - p.a if first == "a" else p.a, 1 - p.b if first == "b" else p.b
            )
            self.put(k, "PC", src, lambda: self.buf(k, "PC"), p.peer[first])
        if s == 3:
            self.take(k, "PC", self.buf(k, "PC"))
            self.add(self.part(k, "C", None, p.a, p.b), self.buf(k, "PC"))
        if 2 <= s <= nz + 1:
            self.wave(k, "A", s - 1)
            self.wave(k, "B", s - 1)
        if 3 <= s <= nz + 2:
            self.wave(k, "C", s - 2)
        if s == nz + 1:
            self.put(k, "XA", lambda: self.part(k, "A", p.z, p.a, 1 - p.b), lambda: self.buf(k, "XA"), p.peer["b"])
            self.put(k, "XB", lambda: self.part(k, "B", p.z, 1 - p.a, p.b), lambda: self.buf(k, "XB"), p.peer["a"])
        if s == nz + 2:
            self.take(k, "XA", self.buf(k, "XA"))
            self.take(k, "XB", self.buf(k, "XB"))
            self.deliver(k)
        if s == nz + 3:
            for make, z in self.started.pop(k):
                if z is None:
                    make().wait_send()
                else:

                    @pl.when(p.z == z)
                    def _():
                        make().wait_send()

    def result(self, k, route):
        p = self.p
        block = self.part(k, route, p.z, p.a, p.b)[0, 0, 0].astype(F32)
        if route != "C":
            block = block + self.buf(k, "X" + route)[0, 0, 0].astype(F32)
        return block

    def tick(self, t, count):
        for k in range(count):
            if 0 <= t - k < self.depth:
                self.stage(k, t - k)


class Backward:
    def __init__(self, refs, place):
        self.__dict__.update(refs)
        self.p = place
        self.flat, self.model = self.cot.shape
        self.lru, self.feed = self.q.shape[1], self.hidden.shape[1]
        self.rows = 2
        self.tok = self.flat // self.rows
        self.outs_going = {}
        c = Chunk
        self.chunks = [c("dn", "hidden", "cot", 96, 512, j * 512) for j in range(2)]
        self.chunks += [c("gu", "normed_two", "ggu", 32, 1536, j * 1536) for j in range(4)]
        self.chunks += [c("mx", "mixed", "grad_out", 48, 1024, 0), c("gi", "normed", "ggi", 32, 1536, 0)]
        self.chunks += [c("da", "conv", "hidden", 48, 1024, j * 1024) for j in range(3)]
        self.chunks += [c("gi", "normed", "ggi", 32, 1536, 1536)]

    def load(self, names):
        for name in names:
            self.loader(name).start()

    def loader(self, name):
        src, dst, at = self.loads[name]
        return pltpu.make_async_copy(src, dst, self.load_sem.at[at])

    def ready(self, names):
        for name in names:
            self.loader(name).wait()

    def produce(self, k):
        ch = self.chunks[k]
        lhs, rhs = getattr(self, ch.lhs), getattr(self, ch.rhs)
        span = 8 * ch.rows
        slot = self.full.at[k % 2]

        def one(z):
            left = lhs[:, pl.ds(pl.multiple_of(z * span, LANE), span)]
            for n in range(ch.across):
                right = rhs[:, ch.first + n * 512 : ch.first + (n + 1) * 512]
                val = outer_sum(left, right).astype(BF16).reshape(8, ch.rows // 16, 16, 512)
                for i in range(ch.rows // 16):
                    slot[z, :, :, :, i * ch.across + n] = val[:, i].reshape(2, 2, 2, 16, 512)

        loop(self.p.nz, one)

    def out_copies(self, k):
        ch = self.chunks[k]
        copies = []
        for i in range(ch.rows // 16):
            for n in range(ch.across):
                at = i * ch.across + n
                col = ch.first + n * 512
                names = self.out_names[ch.name]
                width = self.weight_outs[names[0]].shape[1]
                out = self.weight_outs[names[col // width]]
                dst = out.at[pl.ds(i * 16, 16), pl.ds(col % width, 512)]
                copies.append(pltpu.make_async_copy(self.staged.at[k % 2, at], dst, self.out_sem.at[k % 2, at]))
        return copies

    def deliver(self, k):
        if k >= 2:
            for cp in self.out_copies(k - 2):
                cp.wait()
        for route, at in (("A", 0), ("B", 2), ("C", 4)):
            self.staged[k % 2, at : at + 2] = self.reduce.result(k, route)
        for cp in self.out_copies(k):
            cp.start()

    def by_z(self, weight, buf, sem, extra=None, parts=1):
        width = weight.shape[-1] // parts

        def copies(j, slot):
            z = j // parts
            rows = weight.shape[4]
            src = weight.at[z, :, :, :, :, pl.ds(pl.multiple_of(lax.rem(j, parts) * width, LANE), width)]
            dst = buf.at[slot, :, :, :, 0:rows, 0:width]
            out = [pltpu.make_async_copy(src, dst, sem.at[slot, 0])]
            return out + (extra(j, slot) if extra else [])

        return copies

    def feed_back(self):
        span = self.feed // self.p.nz
        half = lambda slot: pl.ds(pl.multiple_of(slot * span, LANE), span)

        def extra(j, slot):
            at = pl.ds(pl.multiple_of(j * span, LANE), span)
            return [
                pltpu.make_async_copy(self.gate_pre.at[:, at], self.gelu_pre.at[:, half(slot)], self.w_sem.at[slot, 1]),
                pltpu.make_async_copy(self.up.at[:, at], self.state.at[:, half(slot)], self.w_sem.at[slot, 2]),
            ]

        def use(j, slot):
            self.wide_tile[...] = back_prod(self.cot[...], mat(self.w_dn[slot]))
            at = pl.ds(pl.multiple_of(j * span, LANE), span)
            at_up = pl.ds(pl.multiple_of(self.feed + j * span, LANE), span)

            def block(i):
                rows = pl.ds(pl.multiple_of(i * 16, 16), 16)
                grad = self.wide_tile[rows, :]
                gate = self.gelu_pre[rows, half(slot)]
                act, slope = gelu_both(gate)
                self.ggu[rows, at] = (slope * self.state[rows, half(slot)] * grad).astype(BF16)
                self.ggu[rows, at_up] = (act * grad).astype(BF16)

            loop(self.flat // 16, block)

        stream_tiles(self.p.nz, self.by_z(self.dn, self.w_dn, self.w_sem, extra), use)

    def norm_back(self, values, grads, gain_row, extra, out):
        gain = self.vec[gain_row : gain_row + 1, 0 : self.model]

        def block(i, total):
            rows = pl.ds(pl.multiple_of(i * 16, 16), 16)
            v, e = values(rows), grads(rows)
            back, terms = rms_back(v, gain, e)
            out(rows, extra(rows) + back)
            return total + jnp.sum(terms, axis=0, keepdims=True)

        total = lax.fori_loop(0, self.flat // 16, block, jnp.zeros((1, self.model), F32))
        self.sums[gain_row : gain_row + 1, 0 : self.model] = total

    def norm_two_back(self):
        half = self.feed

        def use(j, slot):
            left = self.ggu[:, pl.ds(pl.multiple_of(lax.rem(j, 2) * half, LANE), half)]
            rows = self.gu.shape[4]
            res = back_prod(left, mat(self.w_big[slot, :, :, :, 0:rows, 0:half]))
            at = lanes(j // 2, 8 * rows)

            @pl.when(lax.rem(j, 2) == 0)
            def _():
                self.q[:, at] = res

            @pl.when(lax.rem(j, 2) == 1)
            def _():
                self.q[:, at] = self.q[:, at] + res

        stream_tiles(2 * self.p.nz, self.by_z(self.gu, self.w_big, self.w_sem, None, 2), use)
        self.ready(["middle"])

        def out(rows, val):
            self.middle[rows, :] = val
            self.grad_out[rows, :] = val.astype(BF16)

        self.norm_back(
            lambda rows: self.middle[rows, :],
            lambda rows: self.q[rows, 0 : self.model],
            1,
            lambda rows: self.cot[rows, :].astype(F32),
            out,
        )

    def scan_back(self):
        self.ready(["gelu_pre", "state", "decay_pre"])
        rows = self.mx.shape[4]
        span = 8 * rows

        def use(j, slot):
            self.wide_tile[:, 0:span] = back_prod(self.grad_out[...], mat(self.w_big[slot, :, :, :, 0:rows, 0 : self.model]))

            def block(i):
                c = j * (span // LANE) + i
                for r in range(self.rows):
                    at = slice(r * self.tok, (r + 1) * self.tok)
                    grad = self.wide_tile[at, lanes(i)]
                    act, slope = gelu_both(self.gelu_pre[at, lanes(c)])
                    self.ggi[at, lanes(c)] = (slope * grad * self.state[at, lanes(c)]).astype(BF16)
                    _, decay, _ = decay_terms(self.decay_pre[at, lanes(c)], self.vec[4:5, lanes(c)])
                    since = self.since[r * (self.tok + 16) : r * (self.tok + 16) + self.tok, :]
                    eff = decay * (since != 0).astype(F32)
                    place = lax.broadcasted_iota(jnp.int32, eff.shape, 0)
                    after = jnp.where(place < self.tok - 1, pltpu.roll(eff, self.tok - 1, 0), 1.0)
                    prod, tail = scan_block(after, act * grad, reverse=True)
                    self.q[at, lanes(c)] = prod
                    self.gelu_pre[at, lanes(c)] = tail
                    self.tails[self.p.z, r : r + 1, lanes(c)] = eff[0:1, :] * tail[0:1, :]

            loop(span // LANE, block)

        stream_tiles(self.p.nz, self.by_z(self.mx, self.w_big, self.w_sem), use)

    def tail_copy(self, o, recv):
        p = self.p
        view = self.tails.at[lax.rem(p.z + p.nz - o, p.nz) if recv else p.z]
        return pltpu.make_async_remote_copy(
            view, view, self.t_send.at[o - 1], self.t_recv.at[o - 1],
            device_id=p.at(lax.rem(p.z + o, p.nz)), device_id_type=MESH,
        )

    def send_tails(self):
        for o in range(1, self.p.nz):
            self.tail_copy(o, False).start()

    def gates_back(self):
        p = self.p
        for o in range(1, p.nz):
            self.tail_copy(o, True).wait_recv()
        self.ready(["admit_pre", "conv"])

        def block(c):
            tail = jnp.zeros((8, LANE), F32)
            into = tail
            for i in range(p.nz - 1, 0, -1):
                tail = self.ends[i, 0:8, lanes(c)] * tail + self.tails[i, :, lanes(c)]
                into = jnp.where(p.z == i - 1, tail, into)
            scale = self.vec[4:5, lanes(c)]
            rate_sum = jnp.zeros((1, LANE), F32)
            decay_sum, admit_sum = rate_sum, rate_sum
            for r in range(self.rows):
                at = slice(r * self.tok, (r + 1) * self.tok)
                adjoint = self.gelu_pre[at, lanes(c)] + self.q[at, lanes(c)] * into[r : r + 1, :]
                recall, decay, lost = decay_terms(self.decay_pre[at, lanes(c)], scale)
                root = jnp.sqrt(lost)
                since = self.since[r * (self.tok + 16) : r * (self.tok + 16) + self.tok, :]
                reset = (since == 0).astype(F32)
                keep = 1.0 - reset
                conv = self.conv[at, lanes(c)].astype(F32)
                admit = jax.nn.sigmoid(self.admit_pre[at, lanes(c)])
                state = self.state[at, lanes(c)]
                place = lax.broadcasted_iota(jnp.int32, state.shape, 0)
                before = jnp.where(place > 0, pltpu.roll(state, 1, 0), self.carry[r : r + 1, lanes(c)])
                scale_in = reset + keep * root
                grad_log = adjoint * keep * (before * decay - admit * conv * decay * decay / root)
                decay_low = (grad_log * scale * recall * (1.0 - recall)).astype(BF16)
                admit_low = (adjoint * scale_in * conv * admit * (1.0 - admit)).astype(BF16)
                self.hidden[at, lanes(c)] = decay_low
                self.hidden[at, pl.ds(pl.multiple_of(self.lru + c * LANE, LANE), LANE)] = admit_low
                self.admit_pre[at, lanes(c)] = adjoint * scale_in * admit
                rate_sum = rate_sum + jnp.sum(grad_log * recall, axis=0, keepdims=True)
                decay_sum = decay_sum + jnp.sum(decay_low.astype(F32), axis=0, keepdims=True)
                admit_sum = admit_sum + jnp.sum(admit_low.astype(F32), axis=0, keepdims=True)
            self.sums[2:3, lanes(c)] = decay_sum
            self.sums[3:4, lanes(c)] = admit_sum
            self.sums[4:5, lanes(c)] = rate_sum * (DECAY_SCALE * jax.nn.sigmoid(-self.vec[7:8, lanes(c)]))

        loop(self.lru // LANE, block)

    def conv_grads(self):
        rows = self.da.shape[4]
        span = 8 * rows

        def use(j, slot):
            at = lanes(j, span)
            res = back_prod(self.hidden[...], mat(self.w_big[slot]))
            total = (self.admit_pre[:, at] + res).astype(BF16)
            self.grad_conv[:, :, at] = total.reshape(self.rows, self.tok, span)

        stream_tiles(self.p.nz, self.by_z(self.da, self.w_big, self.w_sem), use)

    def rim_copy(self):
        p = self.p
        return pltpu.make_async_remote_copy(
            self.grad_conv.at[:, 0:16, :], self.rim, self.r_send.at[0], self.r_recv.at[0],
            device_id=p.at(jnp.maximum(p.z - 1, 0)), device_id_type=MESH,
        )

    def send_rim(self):
        pl.when(self.p.z > 0)(lambda: self.rim_copy().start())

    def conv_back(self):
        p = self.p
        pl.when(p.z < p.nz - 1)(lambda: self.rim_copy().wait_recv())
        self.ready(["branch"])
        long = self.tok + 16

        def block(c):
            taps = [jnp.zeros((1, LANE), F32)] * 4
            for r in range(self.rows):
                at = slice(r * self.tok, (r + 1) * self.tok)
                since = self.since[r * long : (r + 1) * long, :]
                grad = self.grad_conv[r, :, lanes(c)].astype(F32)
                wide = jnp.concatenate([grad, self.rim[r, :, lanes(c)].astype(F32)], axis=0)
                head = self.branch[self.flat + 16 * r : self.flat + 16 * (r + 1), lanes(c)].astype(F32)
                back = jnp.concatenate([head, self.branch[at, lanes(c)].astype(F32)], axis=0)
                total = jnp.zeros((self.tok, LANE), F32)
                for k in range(4):
                    seen = (since >= k).astype(F32)
                    moved = back if k == 0 else pltpu.roll(back, k, 0)
                    term = jnp.sum(grad * moved[16:] * seen[0 : self.tok], axis=0, keepdims=True)
                    taps[k] = taps[k] + term
                    ahead = wide * seen
                    ahead = ahead if k == 0 else pltpu.roll(ahead, long - k, 0)
                    total = total + self.vec[8 + k : 9 + k, lanes(c)] * ahead[0 : self.tok]
                self.ggi[at, pl.ds(pl.multiple_of(self.lru + c * LANE, LANE), LANE)] = total.astype(BF16)
            for k in range(4):
                self.sums[5 + k : 6 + k, lanes(c)] = taps[k]

        loop(self.lru // LANE, block)

    def norm_one_back(self):
        rows = self.gi.shape[4]

        def use(j, slot):
            self.q[:, lanes(j, 8 * rows)] = back_prod(self.ggi[...], mat(self.w_big[slot, :, :, :, 0:rows, :]))

        stream_tiles(self.p.nz, self.by_z(self.gi, self.w_big, self.w_sem), use)
        self.ready(["xs"])

        def out(rows, val):
            self.grad_out[rows, :] = val.astype(BF16)

        self.norm_back(
            lambda rows: self.cot[rows, :].astype(F32),
            lambda rows: self.q[rows, 0 : self.model],
            0,
            lambda rows: self.middle[rows, :],
            out,
        )

    def x_copy(self, o):
        p = self.p
        feat = self.x_out.shape[2]
        to = lax.rem(p.z + o, p.nz)
        at = pl.ds(pl.multiple_of(to * feat, LANE), feat)
        src = self.grad_out.reshape(self.rows, self.tok, self.model).at[:, :, at]
        dst = self.x_out.at[:, pl.ds(pl.multiple_of(p.z * self.tok, 16), self.tok), :]
        if o == 0:
            return pltpu.make_async_copy(src, dst, self.x_send.at[p.nz - 1])
        return pltpu.make_async_remote_copy(
            src, dst, self.x_send.at[o - 1], self.x_recv.at[o - 1], device_id=p.at(to), device_id_type=MESH
        )

    def send_x(self):
        for o in range(self.p.nz):
            self.x_copy(o).start()

    def spread_sums(self):
        nz = self.p.nz
        for row in range(10):
            hot, mask, width = (self.hot_m, self.mask_m, self.model) if row < 2 else (self.hot_l, self.mask_l, self.lru)
            vals = self.sums[row : row + 1, 0:width] if row < 9 else self.gate_sums[0:1, :]
            wide = mask[...] * vals
            cut = lax.dot_general(
                wide, hot[...].astype(F32), (((1,), (1,)), ((), ())),
                precision=lax.Precision.HIGHEST, preferred_element_type=F32,
            )
            self.s_own[:, :, :, :, row, :] = cut.reshape(nz, 2, 2, 2, LANE)

    def s_copy(self, at):
        p = self.p
        if at == 0:
            src, dst, dev = self.s_own.at[:, :, :, 1 - p.c], self.s_core, p.core
        elif at == 1:
            src, dst, dev = self.s_core.at[:, :, 1 - p.b], self.s_b, p.peer["b"]
        elif at == 2:
            src, dst, dev = self.s_b.at[:, 1 - p.a], self.s_a, p.peer["a"]
        else:
            to = lax.rem(p.z + at - 2, p.nz)
            src, dst, dev = self.s_a.at[to], self.s_z.at[at - 3], p.at(to)
        return pltpu.make_async_remote_copy(
            src, dst, self.s_send.at[at], self.s_recv.at[at], device_id=dev, device_id_type=MESH
        )

    def small_step(self, n):
        p = self.p
        if n == 0:
            self.s_own[...] = jnp.zeros_like(self.s_own)
            self.spread_sums()
            self.s_copy(0).start()
        if n == 1:
            self.s_copy(0).wait_recv()
            self.s_core[...] = self.s_core[...] + self.s_own[:, :, :, p.c]
            self.s_copy(1).start()
        if n == 2:
            self.s_copy(1).wait_recv()
            self.s_b[...] = self.s_b[...] + self.s_core[:, :, p.b]
            self.s_copy(2).start()
        if n == 3:
            self.s_copy(2).wait_recv()
            self.s_a[...] = self.s_a[...] + self.s_b[:, p.a]
            for o in range(1, p.nz):
                self.s_copy(2 + o).start()
        if n == 4:
            total = self.s_a[p.z]
            for o in range(1, p.nz):
                self.s_copy(2 + o).wait_recv()
                total = total + self.s_z[o - 1]
            self.small_out[...] = total

    def finish(self):
        p = self.p
        count = len(self.chunks)
        for k in (count - 2, count - 1):
            for cp in self.out_copies(k):
                cp.wait()
        for o in range(1, p.nz):
            self.tail_copy(o, False).wait_send()
            self.x_copy(o).wait()
            self.s_copy(2 + o).wait_send()
        self.x_copy(0).wait()
        for at in range(3):
            self.s_copy(at).wait_send()
        pl.when(p.z > 0)(lambda: self.rim_copy().wait_send())


def gelu_both(x):
    inner = GELU_C * (x + 0.044715 * x * x * x)
    t = jnp.tanh(inner)
    slope = 0.5 * (1.0 + t) + 0.5 * x * (1.0 - t * t) * GELU_C * (1.0 + 3 * 0.044715 * x * x)
    return 0.5 * x * (1.0 + t), slope


def rms_back(values, gain, grad):
    q = lax.rsqrt(jnp.mean(values * values, axis=-1, keepdims=True) + EPSILON)
    inner = jnp.mean(values * gain * grad, axis=-1, keepdims=True)
    back = q * gain * grad - values * (q * q * q) * inner
    return back, grad * values * q


WEIGHTS = ("gelu", "input", "decay", "admit", "mixer", "gate", "up", "down")
OUT_NAMES = {"gi": ("gelu", "input"), "da": ("decay", "admit"), "mx": ("mixer",), "gu": ("gate", "up"), "dn": ("down",)}
LOADS = (
    "hidden", "cot", "normed_two", "middle", "mixed", "gelu_pre", "state", "decay_pre", "admit_pre", "conv",
    "branch", "normed", "xs",
)


def backward_kernel(seq_count, names, hbm_names, vmem_names, *refs):
    n_in = len(vmem_names) + len(hbm_names)
    given = dict(zip(vmem_names + hbm_names, refs[:n_in]))
    x_out, small_out = refs[n_in : n_in + 2]
    weight_outs = dict(zip(WEIGHTS, refs[n_in + 2 : n_in + 10]))
    table = dict(zip(names, refs[n_in + 10 :]))
    p = Place(seq_count)
    loads = {}
    for i, name in enumerate(LOADS):
        dst = table["cot"] if name == "xs" else table[name]
        loads[name] = (given.pop(name + "_hbm"), dst, i)
    table.update(given)
    table.update(x_out=x_out, small_out=small_out, weight_outs=weight_outs, out_names=OUT_NAMES, loads=loads)
    f = Backward(table, p)
    late = ("xs", "gelu_pre", "state")
    f.load(n for n in LOADS if n not in late)
    f.rim[...] = jnp.zeros_like(f.rim)
    f.tails[...] = jnp.zeros_like(f.tails)
    p.greet()
    f.reduce = Reduce(
        p, {n: table["ring_" + n] for n in Reduce.NAMES}, table["full"], table["send"], table["recv"],
        f.produce, f.deliver,
    )
    count = len(f.chunks)
    f.ready(["hidden", "cot"])

    def reload_cot():
        f.load(late[:1])

    before = {
        2: [f.feed_back, lambda: f.load(late[1:]), lambda: f.ready(["normed_two"])],
        4: [f.norm_two_back, reload_cot],
        5: [f.scan_back, f.send_tails],
        6: [f.gates_back, lambda: f.ready(["mixed"])],
        7: [lambda: f.ready(["normed"])],
        8: [f.conv_grads, f.send_rim],
        9: [f.conv_back],
        11: [f.norm_one_back, f.send_x, lambda: f.small_step(0)],
        12: [lambda: f.small_step(1)],
        13: [lambda: f.small_step(2)],
        14: [lambda: f.small_step(3)],
        15: [lambda: f.small_step(4)],
    }
    for t in range(count + f.reduce.depth - 1):
        for action in before.get(t, ()):
            action()
        f.reduce.tick(t, count)
    f.finish()


def backward_pass(cot, since_ext, vec, full, kept, shard_shapes, seq_count):
    nz = seq_count
    flat, model = cot.shape
    lru, feed = kept["gelu_pre"].shape[1], kept["hidden"].shape[1]
    tok = flat // 2
    vmem_vals = {
        "vec": vec,
        "since": jnp.broadcast_to(since_ext.reshape(-1, 1), (since_ext.size, LANE)),
        "carry": kept["carry"],
        "ends": kept["ends"],
        "gate_sums": kept["sums"],
    }
    vmem_vals.update(zip(("hot_m", "mask_m", "hot_l", "mask_l"), spread_constants(model, lru, nz * 8)))
    hbm_vals = dict(zip(("gi", "da", "mx", "gu", "dn"), full))
    hbm_vals.update(gate_pre=kept["gate_pre"], up=kept["up"])
    source = dict(kept, cot=cot, normed=kept["normed_main"], xs=kept["xs"].reshape(flat, model))
    hbm_vals.update({n + "_hbm": source[n] for n in LOADS})
    dma = pltpu.SemaphoreType.DMA
    v = pltpu.VMEM
    chunks = 12
    scratch = {
        "hidden": v((flat, feed), BF16),
        "cot": v((flat, model), BF16),
        "normed_two": v((flat, model), BF16),
        "normed": v((flat, model), BF16),
        "middle": v((flat, model), F32),
        "mixed": v((flat, lru), BF16),
        "gelu_pre": v((flat, lru), F32),
        "state": v((flat, lru), F32),
        "decay_pre": v((flat, lru), F32),
        "admit_pre": v((flat, lru), F32),
        "conv": v((flat, lru), BF16),
        "branch": v((flat + 32, lru), BF16),
        "ggu": v((flat, 2 * feed), BF16),
        "ggi": v((flat, 2 * lru), BF16),
        "grad_out": v((flat, model), BF16),
        "grad_conv": v((2, tok, lru), BF16),
        "rim": v((2, 16, lru), BF16),
        "q": v((flat, lru), F32),
        "tails": v((nz, 8, lru), F32),
        "sums": v((16, lru), F32),
        "wide_tile": v((flat, feed // nz), F32),
        "w_dn": v((2, 2, 2, 2, full[4].shape[4], model), BF16),
        "w_big": v((2, 2, 2, 2, full[1].shape[4], 2 * lru), BF16),
        "full": v((2, nz, 2, 2, 2, 6, 16, 512), BF16),
        "staged": v((2, 6, 16, 512), F32),
        "s_own": v((nz, 2, 2, 2, 16, LANE), F32),
        "s_core": v((nz, 2, 2, 16, LANE), F32),
        "s_b": v((nz, 2, 16, LANE), F32),
        "s_a": v((nz, 16, LANE), F32),
        "s_z": v((nz, 16, LANE), F32),
        "w_sem": dma((2, 3)),
        "load_sem": dma((len(LOADS),)),
        "out_sem": dma((2, 6)),
        "send": dma((chunks, len(Reduce.NAMES))),
        "recv": dma((chunks, len(Reduce.NAMES))),
        "t_send": dma((nz,)),
        "t_recv": dma((nz,)),
        "r_send": dma((1,)),
        "r_recv": dma((1,)),
        "x_send": dma((nz,)),
        "x_recv": dma((nz,)),
        "s_send": dma((nz + 3,)),
        "s_recv": dma((nz + 3,)),
    }
    scratch.update({"ring_" + n: v(s, BF16) for n, s in Reduce.shapes(nz).items()})
    names = list(scratch)
    hbm = pl.BlockSpec(memory_space=pltpu.HBM)
    vmem = pl.BlockSpec(memory_space=pltpu.VMEM)
    out_shape = [
        jax.ShapeDtypeStruct((2, tok * nz, model // nz), BF16),
        jax.ShapeDtypeStruct((16, LANE), F32),
    ] + [jax.ShapeDtypeStruct(s, F32) for s in shard_shapes]
    outs = pl.pallas_call(
        partial(backward_kernel, nz, names, list(hbm_vals), list(vmem_vals)),
        out_shape=out_shape,
        in_specs=[vmem] * len(vmem_vals) + [hbm] * len(hbm_vals),
        out_specs=[hbm, vmem] + [hbm] * 8,
        scratch_shapes=[scratch[n] for n in names],
        compiler_params=pltpu.CompilerParams(
            collective_id=1, has_side_effects=True, vmem_limit_bytes=61 << 20
        ),
        name="backward_pass",
    )(*vmem_vals.values(), *hbm_vals.values())
    return outs[0], outs[1], outs[2:]


def local_fast(x_heads, cotangent, doc_starts, smalls, shards):
    norm_gain, conv_weight, decay_bias, admit_bias, decay_rate, feed_gain = smalls
    seq_count = lax.axis_size("seq")
    dev_count = seq_count * lax.axis_size("dp")
    row_count, tok_count, model = cotangent.shape
    flat = row_count * tok_count
    lru, taps = shards[0].shape[1], conv_weight.shape[1]
    positions = lax.axis_index("seq") * tok_count + jnp.arange(tok_count + 16, dtype=jnp.int32)
    since_ext = since_start(doc_starts, positions)
    small = small_rows(norm_gain, conv_weight, decay_bias, admit_bias, decay_rate, feed_gain)
    vec, full, kept = forward_pass(x_heads, small, since_ext[:, :tok_count], shards, seq_count, STARTS)
    input_grad, own, grads = backward_pass(
        cotangent.reshape(flat, model), since_ext, vec, full, kept, [s.shape for s in shards], seq_count
    )
    per_model, per_lru = model // dev_count, lru // dev_count
    return (
        kept["block"].reshape(row_count, tok_count, model),
        input_grad,
        own[0, :per_model],
        grads[0],
        grads[1],
        own[5 : 5 + taps, :per_lru].T,
        grads[2],
        own[2, :per_lru],
        grads[3],
        own[3, :per_lru],
        own[4, :per_lru],
        grads[4],
        own[1, :per_model],
        grads[5],
        grads[6],
        grads[7],
        own[9, :per_lru] * (1.0 / float(flat * dev_count)),
    )


def local(
    x_heads,
    cotangent,
    doc_starts,
    norm_gain,
    gelu_weight,
    input_weight,
    conv_weight,
    decay_weight,
    decay_bias,
    admit_weight,
    admit_bias,
    decay_rate,
    mixer_output,
    feed_gain,
    feed_gate,
    feed_up,
    feed_down,
):
    seq_count = lax.axis_size("seq")
    dev_count = seq_count * lax.axis_size("dp")
    seq_at = lax.axis_index("seq")
    row_count, tok_count, model = cotangent.shape
    flat = row_count * tok_count
    lru = gelu_weight.shape[1]
    feed = feed_gate.shape[1]
    taps = conv_weight.shape[1]
    rim = taps - 1

    smalls = (norm_gain, conv_weight, decay_bias, admit_bias, decay_rate, feed_gain)
    shards = (
        gelu_weight, input_weight, decay_weight, admit_weight, mixer_output, feed_gate, feed_up, feed_down,
    )
    if fast_shapes(shards, seq_count, lax.axis_size("dp"), row_count, tok_count):
        return local_fast(x_heads, cotangent, doc_starts, smalls, shards)
    packed = lax.all_gather(pack_small(smalls), ALL, axis=0, tiled=True).astype(F32)
    parts = split_small(packed, [v.size for v in smalls])
    gain_one = parts[0].reshape(-1)
    conv_taps = parts[1].reshape(lru, taps)
    decay_shift, admit_shift, rate_vec, gain_two = [p.reshape(-1) for p in parts[2:]]

    gelu_input = gather_rows(jnp.concatenate([gelu_weight, input_weight], axis=1))
    decay_admit = gather_rows(jnp.concatenate([decay_weight, admit_weight], axis=1))
    mixer_full = gather_rows(mixer_output)
    gate_up = gather_rows(jnp.concatenate([feed_gate, feed_up], axis=1))
    down_full = gather_rows(feed_down)

    stream = lax.all_to_all(x_heads, "seq", split_axis=1, concat_axis=2, tiled=True)
    stream_in = stream.reshape(flat, model).astype(F32)
    normed_one, norm_one_pull = jax.vjp(rms_norm, stream_in, gain_one)
    normed_low = normed_one.astype(BF16)
    both = dot(normed_low, gelu_input)
    gelu_vals, gelu_pull = jax.vjp(smooth_gate, both[:, :lru])
    branch = both[:, lru:].astype(BF16).reshape(row_count, tok_count, lru)
    halo = shift_seq(branch[:, tok_count - rim :, :], 1, seq_count)
    extended = jnp.concatenate([halo, branch], axis=1).astype(F32)
    positions = seq_at * tok_count + jnp.arange(tok_count + rim, dtype=jnp.int32)
    since_ext = since_start(doc_starts, positions)
    since_here = since_ext[:, :tok_count]
    conv_vals = jnp.zeros((row_count, tok_count, lru), F32)
    for k in range(taps):
        window = extended[:, rim - k : rim - k + tok_count, :]
        conv_vals = conv_vals + conv_taps[:, k] * window * (since_here >= k)[..., None].astype(F32)
    conv_low = conv_vals.astype(BF16)
    conv_flat = conv_low.reshape(flat, lru)
    gates = dot(conv_flat, decay_admit)
    decay_pre = (gates[:, :lru] + decay_shift).reshape(row_count, tok_count, lru)
    admit_pre = (gates[:, lru:] + admit_shift).reshape(row_count, tok_count, lru)
    reset_mask = (since_here == 0).astype(F32)[..., None]

    def coefs(dp, ap, cv, rv):
        return coefficients(dp, ap, cv, rv, reset_mask)

    (decay_eff, update, decay_vals), coef_pull = jax.vjp(
        coefs, decay_pre, admit_pre, conv_low.astype(F32), rate_vec
    )
    decay_prod, local_state = lax.associative_scan(compose, (decay_eff, update), axis=1)
    ends = jnp.stack([decay_prod[:, -1], local_state[:, -1]])
    all_ends = lax.all_gather(ends, "seq", axis=0)
    carry = jnp.zeros((row_count, lru), F32)
    carry_in = carry
    for i in range(seq_count - 1):
        carry = all_ends[i, 0] * carry + all_ends[i, 1]
        carry_in = jnp.where(seq_at == i + 1, carry, carry_in)
    state = local_state + decay_prod * carry_in[:, None, :]
    state_flat = state.reshape(flat, lru)
    mixed_low = (state_flat * gelu_vals).astype(BF16)
    middle = stream_in + dot(mixed_low, mixer_full)
    normed_two, norm_two_pull = jax.vjp(rms_norm, middle, gain_two)
    normed_two_low = normed_two.astype(BF16)
    gate_up_pre = dot(normed_two_low, gate_up)
    gate_act, gate_pull = jax.vjp(smooth_gate, gate_up_pre[:, :feed])
    up_vals = gate_up_pre[:, feed:]
    hidden_low = (gate_act * up_vals).astype(BF16)
    block_output = (middle + dot(hidden_low, down_full)).astype(BF16)
    block_output = block_output.reshape(row_count, tok_count, model)

    cot = cotangent.reshape(flat, model)
    down_grad = scatter_rows(outer_sum(hidden_low, cot))
    grad_hidden = back_prod(cot, down_full)
    grad_gate = gate_pull(grad_hidden * up_vals)[0].astype(BF16)
    grad_up = (grad_hidden * gate_act).astype(BF16)
    grad_gu = jnp.concatenate([grad_gate, grad_up], axis=1)
    gate_up_grad = scatter_rows(outer_sum(normed_two_low, grad_gu))
    grad_mid_norm, gain_two_grad = norm_two_pull(back_prod(grad_gu, gate_up))
    grad_middle = cot.astype(F32) + grad_mid_norm
    grad_out = grad_middle.astype(BF16)
    mixer_grad = scatter_rows(outer_sum(mixed_low, grad_out))
    grad_mixed = back_prod(grad_out, mixer_full)
    grad_gelu = gelu_pull(grad_mixed * state_flat)[0].astype(BF16)
    direct = (grad_mixed * gelu_vals).reshape(row_count, tok_count, lru)
    decay_next = jnp.concatenate([decay_eff[:, 1:, :], jnp.ones_like(decay_eff[:, :1, :])], axis=1)
    tail_prod, tail_state = lax.associative_scan(
        compose, (decay_next, direct), axis=1, reverse=True
    )
    back_ends = lax.all_gather(decay_eff[:, 0] * tail_state[:, 0], "seq", axis=0)
    back = jnp.zeros((row_count, lru), F32)
    back_in = back
    for i in range(seq_count - 1, 0, -1):
        back = all_ends[i, 0] * back + back_ends[i]
        back_in = jnp.where(seq_at == i - 1, back, back_in)
    adjoint = tail_state + tail_prod * back_in[:, None, :]
    state_prev = jnp.concatenate([carry_in[:, None, :], state[:, :-1, :]], axis=1)
    decay_pre_grad, admit_pre_grad, conv_direct, rate_grad = coef_pull(
        (adjoint * state_prev, adjoint, jnp.zeros_like(decay_vals))
    )
    grad_decay = decay_pre_grad.reshape(flat, lru).astype(BF16)
    grad_admit = admit_pre_grad.reshape(flat, lru).astype(BF16)
    grad_da = jnp.concatenate([grad_decay, grad_admit], axis=1)
    decay_admit_grad = scatter_rows(outer_sum(conv_flat, grad_da))
    decay_b_grad = jnp.sum(grad_decay, axis=0, dtype=F32)
    admit_b_grad = jnp.sum(grad_admit, axis=0, dtype=F32)
    grad_conv = (conv_direct.reshape(flat, lru) + back_prod(grad_da, decay_admit)).astype(BF16)
    grad_conv = grad_conv.reshape(row_count, tok_count, lru)
    grad_conv_wide = grad_conv.astype(F32)
    tap_grads = []
    for k in range(taps):
        window = extended[:, rim - k : rim - k + tok_count, :]
        mask = (since_here >= k)[..., None].astype(F32)
        tap_grads.append(jnp.sum(grad_conv_wide * window * mask, axis=(0, 1)))
    conv_grad = jnp.stack(tap_grads, axis=1)
    rim_after = shift_seq(grad_conv[:, :rim, :], -1, seq_count)
    grad_ext = jnp.concatenate([grad_conv, rim_after], axis=1).astype(F32)
    branch_grad = jnp.zeros((row_count, tok_count, lru), F32)
    for k in range(taps):
        ahead = (since_ext[:, k : k + tok_count] >= k)[..., None].astype(F32)
        branch_grad = branch_grad + conv_taps[:, k] * grad_ext[:, k : k + tok_count, :] * ahead
    branch_grad_low = branch_grad.reshape(flat, lru).astype(BF16)
    grad_gi = jnp.concatenate([grad_gelu, branch_grad_low], axis=1)
    gelu_input_grad = scatter_rows(outer_sum(normed_low, grad_gi))
    grad_in_norm, gain_one_grad = norm_one_pull(back_prod(grad_gi, gelu_input))
    input_grad_tok = (grad_middle + grad_in_norm).astype(BF16)
    input_grad_tok = input_grad_tok.reshape(row_count, tok_count, model)
    input_grad = lax.all_to_all(input_grad_tok, "seq", split_axis=2, concat_axis=1, tiled=True)
    gate_term = jnp.sum(decay_vals, axis=(0, 1)) / float(flat * dev_count)
    small_grads = (
        gain_one_grad,
        conv_grad,
        decay_b_grad,
        admit_b_grad,
        rate_grad,
        gain_two_grad,
        gate_term,
    )
    packed_grads = jnp.concatenate([g.reshape(dev_count, -1) for g in small_grads], axis=1)
    reduced = lax.psum_scatter(packed_grads, ALL, scatter_dimension=0, tiled=True)
    own = split_small(reduced, [g.size // dev_count for g in small_grads])
    return (
        block_output,
        input_grad,
        own[0].reshape(-1),
        gelu_input_grad[:, :lru],
        gelu_input_grad[:, lru:],
        own[1].reshape(-1, taps),
        decay_admit_grad[:, :lru],
        own[2].reshape(-1),
        decay_admit_grad[:, lru:],
        own[3].reshape(-1),
        own[4].reshape(-1),
        mixer_grad,
        own[5].reshape(-1),
        gate_up_grad[:, :feed],
        gate_up_grad[:, feed:],
        down_grad,
        own[6].reshape(-1),
    )


def solution(mesh):
    rows = P(ALL, None)
    vec = P(ALL)
    placed = (
        P("dp", None, "seq"),
        P("dp", "seq", None),
        P("dp", None),
        vec,
        rows,
        rows,
        rows,
        rows,
        vec,
        rows,
        vec,
        vec,
        rows,
        vec,
        rows,
        rows,
        rows,
    )
    outs = (
        P("dp", "seq", None),
        P("dp", None, "seq"),
        vec,
        rows,
        rows,
        rows,
        rows,
        vec,
        rows,
        vec,
        vec,
        rows,
        vec,
        rows,
        rows,
        rows,
        vec,
    )
    return jax.shard_map(local, mesh=mesh, in_specs=placed, out_specs=outs, check_vma=False)
```

```python
from functools import partial

import jax
import jax.numpy as jnp
from jax import lax
from jax.experimental import pallas as pl
from jax.experimental.pallas import tpu as pltpu
from jax.sharding import PartitionSpec as P

EPSILON = 1e-06
DECAY_SCALE = 8.0
ALL = ("seq", "dp")
F32 = jnp.float32
BF16 = jnp.bfloat16
GELU_C = 0.7978845608028654


class Names:
    def __getattr__(self, name):
        return name


N = Names()
STARTS = (0, 0, 1, 1, 2, 2, 3, 4, 5, 6, 7, 8)


def rms_norm(values, gain_vec):
    return (
        values * lax.rsqrt(jnp.mean(values * values, axis=-1, keepdims=True) + EPSILON) * gain_vec
    )


def smooth_gate(values):
    return jax.nn.gelu(values, approximate=True)


def compose(earlier, latter):
    return (earlier[0] * latter[0], latter[0] * earlier[1] + latter[1])


def since_start(doc_starts, positions):
    begins = jnp.max(
        jnp.where(doc_starts[:, None, :] <= positions[None, :, None], doc_starts[:, None, :], 0),
        axis=-1,
    )
    return positions[None, :] - begins


def coefficients(decay_pre, admit_pre, conv_vals, rate_vec, reset_mask):
    recall = jax.nn.sigmoid(decay_pre)
    admit_vals = jax.nn.sigmoid(admit_pre)
    log_decay = -DECAY_SCALE * recall * jax.nn.softplus(-rate_vec)
    decay_vals = jnp.exp(log_decay)
    keep_mask = 1.0 - reset_mask
    scale_in = reset_mask + keep_mask * jnp.sqrt(-jnp.expm1(2.0 * log_decay))
    return (decay_vals * keep_mask, scale_in * admit_vals * conv_vals, decay_vals)


def dot(left, right):
    return jnp.dot(left, right, preferred_element_type=F32)


def outer_sum(left, right):
    return lax.dot_general(left, right, (((0,), (0,)), ((), ())), preferred_element_type=F32)


def back_prod(grad_rows, weight):
    return lax.dot_general(
        grad_rows, weight, (((1,), (1,)), ((), ())), preferred_element_type=F32
    )


def gather_rows(shard):
    return lax.all_gather(shard, ALL, axis=0, tiled=True)


def scatter_rows(partial):
    return lax.psum_scatter(partial.astype(BF16), ALL, scatter_dimension=0, tiled=True).astype(F32)


def shift_seq(values, step, seq_count):
    pairs = [(i, i + step) for i in range(seq_count) if 0 <= i + step < seq_count]
    return lax.ppermute(values, "seq", pairs)


def pack_small(pieces):
    return jnp.concatenate([p.reshape(1, -1) for p in pieces], axis=1)


def split_small(packed, widths):
    out, at = [], 0
    for width in widths:
        out.append(packed[:, at : at + width])
        at += width
    return out


MESH = pl.DeviceIdType.MESH
PLANE = 2


def fast_shapes(shards, seq_count, dp_count, row_count, tok_count):
    if dp_count != 2 * PLANE * PLANE or seq_count < 2 or row_count != 2 or tok_count != 128:
        return False
    return all(s.shape[0] in (32, 48, 96) and s.shape[1] % 512 == 0 for s in shards)


class Place:
    def __init__(self, seq_count):
        self.nz = seq_count
        self.z = lax.axis_index("seq")
        self.d = lax.axis_index("dp")
        self.c = lax.rem(self.d, 2)
        self.b = lax.rem(self.d // 2, 2)
        self.a = self.d // 4
        self.core = (self.z, self.d + 1 - 2 * self.c)
        self.peer = {
            "b": (self.z, self.d + 2 - 4 * self.b),
            "a": (self.z, self.d + 4 - 8 * self.a),
        }

    def at(self, z):
        return (z, self.d)

    def greet(self):
        barrier = pltpu.get_barrier_semaphore()
        others = [self.core, self.peer["a"], self.peer["b"]]
        others += [self.at(lax.rem(self.z + o, self.nz)) for o in range(1, self.nz)]
        for other in others:
            pl.semaphore_signal(barrier, inc=1, device_id=other, device_id_type=MESH)
        pl.semaphore_wait(barrier, len(others))


def step_cols(width):
    unit = width // 8
    return {"A": (0, 3 * unit), "B": (3 * unit, 6 * unit), "C": (6 * unit, width)}


def chunk_list(shapes):
    chunks = []
    for i, (rows, cols) in enumerate(shapes):
        wide = min(cols, 3072)
        tall = rows if wide < 3072 and rows <= 48 else (48 if wide < 3072 else 16)
        for c0 in range(0, cols, wide):
            for r0 in range(0, rows, tall):
                chunks.append((i, r0, tall, c0, wide))
    return chunks


class Gather:
    def __init__(self, place, outs, chunks, send, recv, starts):
        self.p, self.outs, self.chunks = place, outs, chunks
        self.send, self.recv, self.starts = send, recv, starts
        self.started = []
        nz = place.nz
        self.depth = nz + 4

    def view(self, k, z, a, b, c, route):
        i, r0, nr, c0, nc = self.chunks[k]
        lo, hi = (0, nc) if route is None else step_cols(nc)[route]
        full = slice(None)
        one = lambda v: full if v is None else pl.ds(v, 1)
        return self.outs[i].at[
            one(z), one(a), one(b), one(c), pl.ds(r0, nr), pl.ds(c0 + lo, hi - lo)
        ]

    def copy(self, k, view, s_at, r_at, dev):
        return pltpu.make_async_remote_copy(
            view, view, self.send.at[k, s_at], self.recv.at[k, r_at], device_id=dev, device_id_type=MESH
        )

    def put(self, k, view, s_at, r_at, dev, cond=None):
        cp = self.copy(k, view, s_at, r_at, dev)
        if cond is None:
            cp.start()
        else:
            pl.when(cond)(cp.start)
        self.started.append((cp, cond))

    def take(self, k, view, r_at, cond=None):
        cp = self.copy(k, view, 0, r_at, self.p.core)
        if cond is None:
            cp.wait_recv()
        else:
            pl.when(cond)(cp.wait_recv)

    def sem(self, route, phase, z=0):
        nz = self.p.nz
        slot = {"first": 0, "up": 1, "down": 1 + nz, "mid": 1 + 2 * nz, "last": 1 + 3 * nz}[phase]
        return {"A": 0, "B": 1, "C": 2}[route] * (1 + 4 * nz) + slot + z

    @staticmethod
    def sem_count(nz):
        return 3 * (1 + 4 * nz) + 1

    def order(self, k, route):
        if route == "C":
            return ("a", "b") if k % 2 else ("b", "a")
        return ("b", "a") if route == "A" else ("a", "b")

    def z_unit(self, k, route, z):
        p = self.p
        first = self.order(k, route)[0]
        a = None if route != "C" and first == "a" else p.a
        b = None if route != "C" and first == "b" else p.b
        return self.view(k, z, a, b, p.c, route)

    def z_own(self, k, route):
        p = self.p
        unit = self.z_unit(k, route, p.z)
        self.put(k, unit, self.sem(route, "up", p.z), self.sem(route, "up", p.z), p.at(p.z + 1), p.z < p.nz - 1)
        self.put(k, unit, self.sem(route, "down", p.z), self.sem(route, "down", p.z), p.at(p.z - 1), p.z > 0)
        self.after(k, route, p.z, None)

    def after(self, k, route, z, cond):
        p = self.p
        first, second = self.order(k, route)
        dim = first if route == "C" else second
        name = "mid" if route == "C" else "last"
        self.put(k, self.z_unit(k, route, z), self.sem(route, name, z), self.sem(route, name, z), p.peer[dim], cond)

    def z_hop(self, k, route, h):
        p = self.p
        low, high = p.z - h, p.z + h
        has_low, has_high = low >= 0, high < p.nz
        low_at, high_at = jnp.maximum(low, 0), jnp.minimum(high, p.nz - 1)
        unit = self.z_unit(k, route, low_at)
        self.take(k, unit, self.sem(route, "up", low_at), has_low)
        if h < p.nz - 1:
            self.put(k, unit, self.sem(route, "up", low_at), self.sem(route, "up", low_at), p.at(p.z + 1), has_low & (p.z < p.nz - 1))
        self.after(k, route, low_at, has_low)
        unit = self.z_unit(k, route, high_at)
        self.take(k, unit, self.sem(route, "down", high_at), has_high)
        if h < p.nz - 1:
            self.put(k, unit, self.sem(route, "down", high_at), self.sem(route, "down", high_at), p.at(p.z - 1), has_high & (p.z > 0))
        self.after(k, route, high_at, has_high)

    def c_last(self, k, z, cond):
        p = self.p
        first, second = self.order(k, "C")
        a = None if first == "a" else p.a
        b = None if first == "b" else p.b
        peer_a = 1 - p.a if first == "a" else p.a
        peer_b = 1 - p.b if first == "b" else p.b
        self.take(k, self.view(k, z, peer_a, peer_b, p.c, "C"), self.sem("C", "mid", z), cond)
        self.put(k, self.view(k, z, a, b, p.c, "C"), self.sem("C", "last", z), self.sem("C", "last", z), p.peer[second], cond)

    def c_last_hop(self, k, h):
        p = self.p
        if h == 0:
            self.c_last(k, p.z, None)
            return
        low, high = p.z - h, p.z + h
        self.c_last(k, jnp.maximum(low, 0), low >= 0)
        self.c_last(k, jnp.minimum(high, p.nz - 1), high < p.nz)

    def stage(self, k, s):
        p, nz = self.p, self.p.nz
        if s == 0:
            for route in "AB":
                first = self.order(k, route)[0]
                at = self.sem(route, "first")
                self.put(k, self.view(k, p.z, p.a, p.b, p.c, route), at, at, p.peer[first])
            self.z_own(k, "C")
        if s == 1:
            for route in "AB":
                first = self.order(k, route)[0]
                a = 1 - p.a if first == "a" else p.a
                b = 1 - p.b if first == "b" else p.b
                self.take(k, self.view(k, p.z, a, b, p.c, route), self.sem(route, "first"))
                self.z_own(k, route)
        if 1 <= s < nz:
            self.z_hop(k, "C", s)
        if 2 <= s <= nz:
            self.z_hop(k, "A", s - 1)
            self.z_hop(k, "B", s - 1)
        if 2 <= s < nz + 2:
            self.c_last_hop(k, s - 2)
        if s == nz + 2:
            for z in range(nz):
                for route in "ABC":
                    second = self.order(k, route)[1]
                    a = 1 - p.a if second == "a" else None
                    b = 1 - p.b if second == "b" else None
                    self.take(k, self.view(k, z, a, b, p.c, route), self.sem(route, "last", z))
            at = self.sem_count(nz) - 1
            self.put(k, self.view(k, None, None, None, p.c, None), at, at, p.core)
        if s == nz + 3:
            at = self.sem_count(nz) - 1
            self.take(k, self.view(k, None, None, None, 1 - p.c, None), at)

    def tick(self, t):
        for k in range(len(self.chunks)):
            s = t - self.starts[k]
            if 0 <= s < self.depth:
                self.stage(k, s)

    def ticks(self):
        return max(self.starts) + self.depth

    def finish(self):
        for cp, cond in self.started:
            if cond is None:
                cp.wait_send()
            else:
                pl.when(cond)(cp.wait_send)


LANE = 128


def spread_constants(model, lru, dev_count):
    out = []
    for width in (model, lru):
        per = width // dev_count
        lane = jnp.arange(width, dtype=jnp.int32)[None, :]
        out.append((lane % per == jnp.arange(LANE, dtype=jnp.int32)[:, None]).astype(BF16))
        out.append((lane // per == jnp.arange(dev_count, dtype=jnp.int32)[:, None]).astype(F32))
    return out


def small_rows(norm_gain, conv_weight, decay_bias, admit_bias, decay_rate, feed_gain):
    rate = decay_rate.astype(F32)
    scale = -DECAY_SCALE * jax.nn.softplus(-rate)
    high = lax.reduce_precision(scale, 8, 7)
    mid = lax.reduce_precision(scale - high, 8, 7)
    low = lax.reduce_precision(scale - high - mid, 8, 7)
    taps = [conv_weight[:, k] for k in range(conv_weight.shape[1])]
    rows = [norm_gain, feed_gain, decay_bias, admit_bias, high, mid, low, rate, *taps]
    rows = [jnp.pad(v.astype(F32), (0, LANE - v.shape[0])) for v in rows]
    return jnp.stack(rows + [jnp.zeros((LANE,), F32)] * (16 - len(rows)))


def decay_terms(pre, scale):
    recall = jax.nn.sigmoid(pre)
    log_decay = recall * scale
    decay = jnp.exp(log_decay)
    y = 2.0 * log_decay
    series = 1.0 + y * (1 / 7)
    for n in (6, 5, 4, 3, 2):
        series = 1.0 + y * (1 / n) * series
    lost = jnp.where(y > -0.35, -y * series, 1.0 - decay * decay)
    return recall, decay, lost


def scan_block(prod, state, reverse=False):
    length = prod.shape[0]
    at = lax.broadcasted_iota(jnp.int32, prod.shape, 0)
    step = 1
    while step < length:
        inside = at < length - step if reverse else at >= step
        turn = length - step if reverse else step
        prod_far = jnp.where(inside, pltpu.roll(prod, turn, 0), 1.0)
        state_far = jnp.where(inside, pltpu.roll(state, turn, 0), 0.0)
        state = prod * state_far + state
        prod = prod * prod_far
        step *= 2
    return prod, state


def lanes(c, width=LANE):
    return pl.ds(pl.multiple_of(c * width, width), width)


def loop(count, body):
    def step(i, carry):
        body(i)
        return carry

    lax.fori_loop(0, count, step, 0)


def stream_tiles(count, fetch, use):
    for cp in fetch(0, 0):
        cp.start()

    def step(j, carry):
        slot = lax.rem(j, 2)

        @pl.when(j + 1 < count)
        def _():
            for cp in fetch(j + 1, 1 - slot):
                cp.start()

        for cp in fetch(j, slot):
            cp.wait()
        use(j, slot)
        return carry

    lax.fori_loop(0, count, step, 0)


def mat(value):
    return value.reshape(-1, value.shape[-1])


class Forward:
    def __init__(self, refs, place, weights):
        self.__dict__.update(refs)
        self.p, self.weights = place, weights
        self.tok = self.xs.shape[1]
        self.rows = self.xs.shape[0]
        self.flat = self.rows * self.tok
        self.lru = self.gelu_pre.shape[1]
        self.model = self.xs.shape[2]
        self.feed = self.hidden.shape[1]
        self.stores = []

    def save(self, name):
        cp = pltpu.make_async_copy(getattr(self, name), self.keep[name], self.keep_sem.at[len(self.stores)])
        cp.start()
        self.stores.append(cp)

    def fetch(self, i, buf, sem, starts, width):
        def copies(j, slot):
            out = []
            for n, start in enumerate(starts):
                src = self.weights[i].at[:, :, :, :, :, pl.ds(pl.multiple_of(start + j * width, LANE), width)]
                dst = buf.at[slot, :, :, :, :, :, pl.ds(n * width, width)]
                out.append(pltpu.make_async_copy(src, dst, sem.at[slot, n]))
            return out

        return copies

    def vectors(self):
        cp = pltpu.make_async_copy(self.small_all, self.small_vm, self.misc_sem.at[0])
        cp.start()
        cp.wait()
        nz = self.p.nz

        def spread(row, hot, mask):
            vals = self.small_vm[:, :, row, :].reshape(nz * 8, LANE).astype(BF16)
            wide = jnp.dot(vals, hot[...], preferred_element_type=F32)
            return jnp.sum(wide * mask[...], axis=0, keepdims=True)

        for row in range(2):
            self.vec[row : row + 1, 0 : self.model] = spread(row, self.hot_m, self.mask_m)
        for row in range(2, 12):
            self.vec[row : row + 1, :] = spread(row, self.hot_l, self.mask_l)
        self.vec[4:5, :] = self.vec[4:5, :] + self.vec[5:6, :] + self.vec[6:7, :]

    def norm(self, load, count, gain_row, out):
        gain = self.vec[gain_row : gain_row + 1, 0 : self.model]

        def body(i):
            v = load(i)
            q = lax.rsqrt(jnp.mean(v * v, axis=-1, keepdims=True) + EPSILON)
            out[pl.ds(pl.multiple_of(i * 32, 32), 32), :] = (v * q * gain).astype(BF16)

        loop(count, body)

    def norm_one(self):
        per = self.tok // 32

        def main(i):
            return self.xs[i // per, pl.ds(pl.multiple_of(lax.rem(i, per) * 32, 32), 32), :].astype(F32)

        self.norm(main, self.flat // 32, 0, self.normed.at[0 : self.flat])
        self.norm(
            lambda i: self.halo_x[...].reshape(2 * 16, self.model).astype(F32),
            1,
            0,
            self.normed.at[self.flat : self.flat + 32],
        )
        self.save(N.normed_main)
        self.save(N.xs)

    def gelu_input(self):
        half = self.lru // 512

        def use(j, slot):
            res = jnp.dot(self.normed[0 : self.flat, :], mat(self.w_gi[slot]), preferred_element_type=F32)
            self.gelu_pre[:, lanes(j, 512)] = res

        stream_tiles(half, self.fetch(0, self.w_gi, self.w_sem, (0,), 512), use)

        def use_two(j, slot):
            res = jnp.dot(self.normed[...], mat(self.w_gi[slot]), preferred_element_type=F32).astype(BF16)
            self.branch[:, lanes(j, 512)] = res

        stream_tiles(half, self.fetch(0, self.w_gi, self.w_sem, (self.lru,), 512), use_two)

        def conv(c):
            for r in range(self.rows):
                at = slice(r * self.tok, (r + 1) * self.tok)
                head = self.branch[self.flat + 16 * r : self.flat + 16 * (r + 1), lanes(c)].astype(F32)
                wide = jnp.concatenate([head, self.branch[at, lanes(c)].astype(F32)], axis=0)
                since = self.since[at, :]
                total = jnp.zeros((self.tok, LANE), F32)
                for k in range(4):
                    moved = wide if k == 0 else pltpu.roll(wide, k, 0)
                    tap = self.vec[8 + k : 9 + k, lanes(c)]
                    total = total + tap * moved[16:] * (since >= k).astype(F32)
                self.conv[at, lanes(c)] = total.astype(BF16)

        loop(self.lru // LANE, conv)
        self.save(N.gelu_pre)
        self.save(N.branch)
        self.save(N.conv)

    def gates(self, first, count):
        self.sums[...] = jnp.zeros_like(self.sums) if first == 0 else self.sums[...]

        def use(j, slot):
            self.tile[...] = jnp.dot(self.conv[...], mat(self.w_da[slot]), preferred_element_type=F32)
            base = (first + j) * 4

            def block(i):
                c = base + i
                gate_sum = jnp.zeros((1, LANE), F32)
                for r in range(self.rows):
                    at = slice(r * self.tok, (r + 1) * self.tok)
                    pre = self.tile[at, lanes(i)] + self.vec[2:3, lanes(c)]
                    admit_pre = self.tile[at, lanes(i + 4)] + self.vec[3:4, lanes(c)]
                    self.decay_pre[at, lanes(c)] = pre
                    self.admit_pre[at, lanes(c)] = admit_pre
                    recall, decay, lost = decay_terms(pre, self.vec[4:5, lanes(c)])
                    reset = (self.since[at, :] == 0).astype(F32)
                    keep = 1.0 - reset
                    scale_in = reset + keep * jnp.sqrt(lost)
                    update = scale_in * jax.nn.sigmoid(admit_pre) * self.conv[at, lanes(c)].astype(F32)
                    prod, state = scan_block(decay * keep, update)
                    self.prod[at, lanes(c)] = prod
                    self.state[at, lanes(c)] = state
                    self.ends[self.p.z, r : r + 1, lanes(c)] = prod[self.tok - 1 :, :]
                    self.ends[self.p.z, 8 + r : 9 + r, lanes(c)] = state[self.tok - 1 :, :]
                    gate_sum = gate_sum + jnp.sum(decay, axis=0, keepdims=True)
                self.sums[0:1, lanes(c)] = gate_sum

            loop(4, block)

        starts = (first * 512, self.lru + first * 512)
        stream_tiles(count, self.fetch(1, self.w_da, self.w_sem, starts, 512), use)

    def gates_saved(self):
        self.save(N.decay_pre)
        self.save(N.admit_pre)
        self.save(N.sums)

    def send_ends(self):
        p = self.p
        self.end_moves = []
        for o in range(1, p.nz):
            view = self.ends.at[p.z]
            cp = pltpu.make_async_remote_copy(
                view, view, self.e_send.at[o - 1], self.e_recv.at[o - 1],
                device_id=p.at(lax.rem(p.z + o, p.nz)), device_id_type=MESH,
            )
            cp.start()
            self.end_moves.append(cp)

    def mix(self):
        p = self.p
        for o in range(1, p.nz):
            view = self.ends.at[lax.rem(p.z + p.nz - o, p.nz)]
            pltpu.make_async_remote_copy(
                view, view, self.e_send.at[o - 1], self.e_recv.at[o - 1],
                device_id=p.core, device_id_type=MESH,
            ).wait_recv()

        def block(c):
            carry = jnp.zeros((8, LANE), F32)
            into = carry
            for i in range(p.nz - 1):
                carry = self.ends[i, 0:8, lanes(c)] * carry + self.ends[i, 8:16, lanes(c)]
                into = jnp.where(p.z == i + 1, carry, into)
            self.carry[:, lanes(c)] = into
            for r in range(self.rows):
                at = slice(r * self.tok, (r + 1) * self.tok)
                state = self.state[at, lanes(c)] + self.prod[at, lanes(c)] * into[r : r + 1, :]
                self.state[at, lanes(c)] = state
                gelu = smooth_gate(self.gelu_pre[at, lanes(c)])
                self.mixed[at, lanes(c)] = (state * gelu).astype(BF16)

        loop(self.lru // LANE, block)
        self.save(N.state)
        self.save(N.carry)
        self.save(N.ends)
        self.save(N.mixed)

        def use(j, slot):
            res = jnp.dot(self.mixed[...], mat(self.w_mx[slot]), preferred_element_type=F32)
            x = self.xs[:, :, lanes(j, 512)].astype(F32).reshape(self.flat, 512)
            self.middle[:, lanes(j, 512)] = x + res

        stream_tiles(self.model // 512, self.fetch(2, self.w_mx, self.w_sem, (0,), 512), use)
        self.norm(
            lambda i: self.middle[pl.ds(pl.multiple_of(i * 32, 32), 32), :], self.flat // 32, 1, self.normed_two
        )
        self.save(N.middle)
        self.save(N.normed_two)

    def gate_up(self, first, count):
        def use(j, slot):
            res = jnp.dot(self.normed_two[...], mat(self.w_gu[slot]), preferred_element_type=F32)
            gate, up = res[:, 0:512], res[:, 512:1024]
            at = lanes(first + j, 512)
            self.gate_pre[:, at] = gate
            self.up[:, at] = up
            self.hidden[:, at] = (smooth_gate(gate) * up).astype(BF16)

        starts = (first * 512, self.feed + first * 512)
        stream_tiles(count, self.fetch(3, self.w_gu, self.w_sem, starts, 512), use)

    def gate_saved(self):
        self.save(N.gate_pre)
        self.save(N.up)
        self.save(N.hidden)

    def down(self):
        def use(j, slot):
            res = jnp.dot(self.hidden[...], mat(self.w_dn[slot]), preferred_element_type=F32)
            self.block[:, lanes(j, 256)] = (self.middle[:, lanes(j, 256)] + res).astype(BF16)

        stream_tiles(self.model // 256, self.fetch(4, self.w_dn, self.w_sem, (0,), 256), use)
        self.save(N.block)

    def finish(self):
        for cp in self.stores:
            cp.wait()
        for cp in self.end_moves:
            cp.wait_send()


KEEP = (
    N.xs, N.normed_main, N.gelu_pre, N.branch, N.conv, N.decay_pre, N.admit_pre, N.sums, N.state, N.carry,
    N.ends, N.mixed, N.middle, N.normed_two, N.gate_pre, N.up, N.hidden, N.block,
)


def forward_kernel(seq_count, starts, chunks, names, n_keep, *refs):
    refs = list(refs)
    x_ref, small_ref, since, hot_m, mask_m, hot_l, mask_l = refs[:7]
    srcs = refs[7:15]
    at = 15
    small_all, vec = refs[at : at + 2]
    outs = refs[at + 2 : at + 7]
    keep = dict(zip(KEEP, refs[at + 7 : at + 7 + n_keep]))
    at += 7 + n_keep
    table = dict(zip(names, refs[at : at + len(names)]))
    p = Place(seq_count)
    table.update(
        small_all=small_all, vec=vec, since=since, hot_m=hot_m, mask_m=mask_m, hot_l=hot_l, mask_l=mask_l, keep=keep,
    )
    table[N.normed_main] = table[N.normed].at[0 : since.shape[0]]
    f = Forward(table, p, outs)
    one = pl.ds
    copies = []
    own_sem = table[N.own_sem]
    k = 0
    for out, count in zip(outs, (2, 2, 1, 2, 1)):
        col = 0
        for _ in range(count):
            cols = srcs[k].shape[-1]
            dst = out.at[one(p.z, 1), one(p.a, 1), one(p.b, 1), one(p.c, 1), :, one(col, cols)]
            copies.append(pltpu.make_async_copy(srcs[k], dst, own_sem.at[k]))
            col += cols
            k += 1
    tok, feat = f.tok, x_ref.shape[2]
    here = one(pl.multiple_of(p.z * feat, LANE), feat)
    copies.append(pltpu.make_async_copy(x_ref.at[:, one(p.z * tok, tok), :], f.xs.at[:, :, here], own_sem.at[k]))
    copies.append(pltpu.make_async_copy(small_ref, small_all.at[one(p.z, 1), one(p.d, 1)], own_sem.at[k + 1]))
    for cp in copies:
        cp.start()

    def halo(z):
        return x_ref.at[:, one(pl.multiple_of(jnp.maximum(z * tok - 16, 0), 16), 16), :]

    own_halo = lambda: pltpu.make_async_copy(halo(p.z), f.halo_x.at[:, :, here], own_sem.at[k + 2])

    @pl.when(p.z > 0)
    def _():
        own_halo().start()

    @pl.when(p.z == 0)
    def _():
        f.halo_x[...] = jnp.zeros_like(f.halo_x)

    f.ends[...] = jnp.zeros_like(f.ends)
    f.sums[...] = jnp.zeros_like(f.sums)
    p.greet()
    x_moves = []

    def x_copy(o):
        to = lax.rem(p.z + o, p.nz)
        return pltpu.make_async_remote_copy(
            x_ref.at[:, one(pl.multiple_of(to * tok, 16), tok), :], f.xs.at[:, :, here], table[N.x_send].at[o - 1],
            table[N.x_recv].at[o - 1], device_id=p.at(to), device_id_type=MESH,
        )

    def h_copy(o):
        to = lax.rem(p.z + o, p.nz)
        return to > 0, pltpu.make_async_remote_copy(
            halo(to), f.halo_x.at[:, :, here], table[N.h_send].at[o - 1],
            table[N.h_recv].at[o - 1], device_id=p.at(to), device_id_type=MESH,
        )

    for o in range(1, p.nz):
        x_copy(o).start()
        cond, cp = h_copy(o)
        pl.when(cond)(cp.start)
    for cp in copies:
        cp.wait()
    s_send, s_recv = table[N.s_send], table[N.s_recv]
    s_moves = []

    def small_put(view, at, dev):
        cp = pltpu.make_async_remote_copy(view, view, s_send.at[at], s_recv.at[at], device_id=dev, device_id_type=MESH)
        cp.start()
        s_moves.append(cp)

    def small_view(d, n):
        return small_all.at[one(p.z, 1), one(d, n)]

    small_put(small_view(p.d, 1), 0, p.core)
    g = Gather(p, outs, chunks, table[N.send], table[N.recv], starts)
    last = [max(starts[i] for i in range(len(chunks)) if chunks[i][0] == w) + g.depth - 1 for w in range(5)]
    plan = {
        3: [f.vectors, f.norm_one],
        last[0]: [f.gelu_input],
        max(last[1], last[0] + 1): [lambda: f.gates(0, 2)],
        max(last[1], last[0] + 1) + 1: [lambda: f.gates(2, 1), f.send_ends, f.gates_saved],
        max(last[2], max(last[1], last[0] + 1) + 2): [f.mix],
    }
    plan.setdefault(last[3], []).append(lambda: f.gate_up(0, 2))
    plan.setdefault(last[3] + 1, []).append(lambda: f.gate_up(2, 2))
    plan.setdefault(max(last[3] + 2, last[4]), []).extend([lambda: f.gate_up(4, 2), f.gate_saved, f.down])
    ticks = max(g.ticks(), max(plan) + 1)
    for t in range(ticks):
        g.tick(t)
        if t == 0:
            s_moves[0].wait_recv()
            small_put(small_view(p.d - p.c, 2), 1, p.peer["b"])
        if t == 1:
            s_moves[1].wait_recv()
            small_put(small_view(4 * p.a, 4), 2, p.peer["a"])
        if t == 2:
            s_moves[2].wait_recv()
            for o in range(1, p.nz):
                small_put(small_view(0, 8), 2 + o, p.at(lax.rem(p.z + o, p.nz)))
        if t == 3:
            for cp in s_moves[3:]:
                cp.wait_recv()
            for o in range(1, p.nz):
                x_copy(o).wait_recv()
                pl.when(p.z > 0)(h_copy(o)[1].wait_recv)

            @pl.when(p.z > 0)
            def _():
                own_halo().wait()

        for action in plan.get(t, ()):
            action()
    for cp in s_moves:
        cp.wait_send()
    for o in range(1, p.nz):
        x_copy(o).wait_send()
        cond, cp = h_copy(o)
        pl.when(cond)(cp.wait_send)
    f.finish()
    g.finish()


def forward_pass(x_heads, small, since, shards, seq_count, starts):
    groups = ((0, 1), (2, 3), (4,), (5, 6), (7,))
    rows_cols = [(shards[g[0]].shape[0], sum(shards[i].shape[1] for i in g)) for g in groups]
    chunks = chunk_list(rows_cols)
    row_count, row_len, feat = x_heads.shape
    tok, model = row_len // seq_count, feat * seq_count
    flat = row_count * tok
    lru, feed = rows_cols[0][1] // 2, rows_cols[3][1] // 2
    nz = seq_count
    srcs = [s.reshape(1, 1, 1, 1, *s.shape) for s in shards]
    hbm = pl.BlockSpec(memory_space=pltpu.HBM)
    vmem = pl.BlockSpec(memory_space=pltpu.VMEM)
    keep_shapes = dict(
        xs=((row_count, tok, model), BF16),
        normed_main=((flat, model), BF16),
        gelu_pre=((flat, lru), F32),
        branch=((flat + 32, lru), BF16),
        conv=((flat, lru), BF16),
        decay_pre=((flat, lru), F32),
        admit_pre=((flat, lru), F32),
        sums=((8, lru), F32),
        state=((flat, lru), F32),
        carry=((8, lru), F32),
        ends=((nz, 16, lru), F32),
        mixed=((flat, lru), BF16),
        middle=((flat, model), F32),
        normed_two=((flat, model), BF16),
        gate_pre=((flat, feed), F32),
        up=((flat, feed), F32),
        hidden=((flat, feed), BF16),
        block=((flat, model), BF16),
    )
    scratch = {n: pltpu.VMEM(*s) for n, s in keep_shapes.items() if n != "normed_main"}
    dma = pltpu.SemaphoreType.DMA
    sems = Gather.sem_count(nz)
    scratch.update(
        normed=pltpu.VMEM((flat + 32, model), BF16),
        halo_x=pltpu.VMEM((row_count, 16, model), BF16),
        small_vm=pltpu.VMEM((nz, 8, 16, LANE), F32),
        prod=pltpu.VMEM((flat, lru), F32),
        tile=pltpu.VMEM((flat, 1024), F32),
        w_gi=pltpu.VMEM((2, nz, 2, 2, 2, rows_cols[0][0], 512), BF16),
        w_da=pltpu.VMEM((2, nz, 2, 2, 2, rows_cols[1][0], 1024), BF16),
        w_mx=pltpu.VMEM((2, nz, 2, 2, 2, rows_cols[2][0], 512), BF16),
        w_gu=pltpu.VMEM((2, nz, 2, 2, 2, rows_cols[3][0], 1024), BF16),
        w_dn=pltpu.VMEM((2, nz, 2, 2, 2, rows_cols[4][0], 256), BF16),
        w_sem=dma((2, 2)),
        keep_sem=dma((len(KEEP),)),
        misc_sem=dma((1,)),
        own_sem=dma((len(srcs) + 3,)),
        x_send=dma((nz,)),
        x_recv=dma((nz,)),
        h_send=dma((nz,)),
        h_recv=dma((nz,)),
        s_send=dma((nz + 3,)),
        s_recv=dma((nz + 3,)),
        e_send=dma((nz,)),
        e_recv=dma((nz,)),
        send=dma((len(chunks), sems)),
        recv=dma((len(chunks), sems)),
    )
    names = list(scratch)
    out_shape = [jax.ShapeDtypeStruct((nz, 8, 16, LANE), F32), jax.ShapeDtypeStruct((16, lru), F32)]
    out_shape += [jax.ShapeDtypeStruct((nz, PLANE, PLANE, 2, r, c), BF16) for r, c in rows_cols]
    out_shape += [jax.ShapeDtypeStruct(*keep_shapes[n]) for n in KEEP]
    outs = pl.pallas_call(
        partial(forward_kernel, nz, starts, chunks, names, len(KEEP)),
        out_shape=out_shape,
        in_specs=[hbm] + [vmem] * 14,
        out_specs=[hbm, vmem] + [hbm] * (5 + len(KEEP)),
        scratch_shapes=[scratch[n] for n in names],
        compiler_params=pltpu.CompilerParams(
            collective_id=0, has_side_effects=True, vmem_limit_bytes=61 << 20
        ),
        name="forward_pass",
    )(
        x_heads,
        small.reshape(1, 1, 16, LANE),
        jnp.broadcast_to(since.reshape(flat, 1), (flat, LANE)),
        *spread_constants(model, lru, nz * 8),
        *srcs,
    )
    return outs[1], outs[2:7], dict(zip(KEEP, outs[7:]))


C_RING, RING = 8, 5


class Chunk:
    def __init__(self, name, lhs, rhs, rows, width, first):
        self.name, self.lhs, self.rhs = name, lhs, rhs
        self.rows, self.width, self.first = rows, width, first
        self.across = width // 512


class Reduce:
    NAMES = (N.C, N.YA, N.YB, N.YC, N.PC, N.UA, N.DA, N.UB, N.DB, N.UC, N.DC, N.XA, N.XB)
    PIECES = {"A": pl.ds(0, 2), "B": pl.ds(2, 2), "C": pl.ds(4, 2)}

    @staticmethod
    def shapes(nz):
        tail = (2, 16, 512)
        plane = PLANE
        a, b, c = (nz, 1, plane), (nz, plane, 1), (nz, 1, 1)
        own = (1, 1, 1)
        lead = dict(YA=a, YB=b, YC=b, PC=c, UA=a, DA=a, UB=b, DB=b, UC=c, DC=c, XA=own, XB=own)
        out = {n: (RING, *v, *tail) for n, v in lead.items()}
        out["C"] = (C_RING, nz, plane, plane, 6, 16, 512)
        return out

    def __init__(self, place, bufs, full, send, recv, produce, deliver):
        self.p, self.bufs, self.full = place, bufs, full
        self.send, self.recv = send, recv
        self.produce, self.deliver = produce, deliver
        self.started = {}
        self.depth = place.nz + 4

    def buf(self, k, name):
        return self.bufs[name].at[k % (C_RING if name == "C" else RING)]

    def order(self, k):
        return ("a", "b") if k % 2 else ("b", "a")

    def part(self, k, route, z, a, b):
        full = slice(None)
        one = lambda v: full if v is None else v if isinstance(v, slice) else pl.ds(v, 1)
        return self.buf(k, "C").at[one(z), one(a), one(b), self.PIECES[route]]

    def copy(self, k, name, src, dst, dev):
        at = self.NAMES.index(name)
        return pltpu.make_async_remote_copy(
            src, dst, self.send.at[k, at], self.recv.at[k, at], device_id=dev, device_id_type=MESH
        )

    def put(self, k, name, src, dst, dev):
        make = lambda: self.copy(k, name, src(), dst(), dev)
        make().start()
        self.started.setdefault(k, []).append((make, None))

    def z_put(self, k, route, way, z):
        p = self.p
        name = ("U" if way > 0 else "D") + route
        span = slice(z + 1, p.nz) if way > 0 else slice(0, z)

        def make():
            a = p.a if route != "B" else None
            b = p.b if route != "A" else None
            return self.copy(k, name, self.part(k, route, span, a, b), self.buf(k, name).at[span], p.at(z + way))

        make().start()
        self.started.setdefault(k, []).append((make, z))

    def take(self, k, name, dst):
        self.copy(k, name, dst, dst, self.p.core).wait_recv()

    def add(self, into, other):
        def one(t):
            into[t] = into[t] + other[t]

        loop(into.shape[0], one)

    def wave(self, k, route, s):
        p, nz = self.p, self.p.nz
        low, high = s - 1, nz - s

        def gather(name, span):
            got = self.buf(k, name).at[span]
            self.take(k, name, got)
            a = p.a if route != "B" else None
            b = p.b if route != "A" else None
            self.add(self.part(k, route, span, a, b), got)

        @pl.when(p.z == low)
        def _():
            if low > 0:
                gather("U" + route, slice(low, nz))
            if low < nz - 1:
                self.z_put(k, route, 1, low)

        @pl.when(p.z == high)
        def _():
            if high < nz - 1:
                gather("D" + route, slice(0, high + 1))
            if high > 0:
                self.z_put(k, route, -1, high)

    def yc(self, k):
        buf = self.buf(k, "YC")
        if self.order(k)[1] == "b":
            return buf
        nz, plane, _, n, r, w = buf.shape
        return buf.reshape(nz, 1, plane, n, r, w)

    def stage(self, k, s):
        p, nz = self.p, self.p.nz
        if s == 0:
            self.produce(k)
            slot = self.full.at[k % 2]
            self.put(k, "C", lambda: slot.at[:, :, :, 1 - p.c], lambda: self.buf(k, "C"), p.core)
        if s == 1:
            self.take(k, "C", self.buf(k, "C"))
            into, own = self.buf(k, "C"), self.full.at[k % 2]

            def one(t):
                for a in range(PLANE):
                    for b in range(PLANE):
                        into[t, a, b] = into[t, a, b] + own[t, a, b, p.c]

            loop(nz, one)
            self.put(k, "YA", lambda: self.part(k, "A", None, 1 - p.a, None), lambda: self.buf(k, "YA"), p.peer["a"])
            self.put(k, "YB", lambda: self.part(k, "B", None, None, 1 - p.b), lambda: self.buf(k, "YB"), p.peer["b"])
            q = self.order(k)[1]
            src = lambda: self.part(k, "C", None, 1 - p.a if q == "a" else None, 1 - p.b if q == "b" else None)
            self.put(k, "YC", src, lambda: self.yc(k), p.peer[q])
        if s == 2:
            make, _ = self.started[k].pop(0)
            make().wait_send()
            self.take(k, "YA", self.buf(k, "YA"))
            self.add(self.part(k, "A", None, p.a, None), self.buf(k, "YA"))
            self.take(k, "YB", self.buf(k, "YB"))
            self.add(self.part(k, "B", None, None, p.b), self.buf(k, "YB"))
            first, q = self.order(k)
            self.take(k, "YC", self.yc(k))
            self.add(self.part(k, "C", None, p.a if q == "a" else None, p.b if q == "b" else None), self.yc(k))
            src = lambda: self.part(
                k, "C", None, 1 - p.a if first == "a" else p.a, 1 - p.b if first == "b" else p.b
            )
            self.put(k, "PC", src, lambda: self.buf(k, "PC"), p.peer[first])
        if s == 3:
            self.take(k, "PC", self.buf(k, "PC"))
            self.add(self.part(k, "C", None, p.a, p.b), self.buf(k, "PC"))
        if 2 <= s <= nz + 1:
            self.wave(k, "A", s - 1)
            self.wave(k, "B", s - 1)
        if 3 <= s <= nz + 2:
            self.wave(k, "C", s - 2)
        if s == nz + 1:
            self.put(k, "XA", lambda: self.part(k, "A", p.z, p.a, 1 - p.b), lambda: self.buf(k, "XA"), p.peer["b"])
            self.put(k, "XB", lambda: self.part(k, "B", p.z, 1 - p.a, p.b), lambda: self.buf(k, "XB"), p.peer["a"])
        if s == nz + 2:
            self.take(k, "XA", self.buf(k, "XA"))
            self.take(k, "XB", self.buf(k, "XB"))
            self.deliver(k)
        if s == nz + 3:
            for make, z in self.started.pop(k):
                if z is None:
                    make().wait_send()
                else:

                    @pl.when(p.z == z)
                    def _():
                        make().wait_send()

    def result(self, k, route):
        p = self.p
        block = self.part(k, route, p.z, p.a, p.b)[0, 0, 0].astype(F32)
        if route != "C":
            block = block + self.buf(k, "X" + route)[0, 0, 0].astype(F32)
        return block

    def tick(self, t, count):
        for k in range(count):
            if 0 <= t - k < self.depth:
                self.stage(k, t - k)


class Backward:
    def __init__(self, refs, place):
        self.__dict__.update(refs)
        self.p = place
        self.flat, self.model = self.cot.shape
        self.lru, self.feed = self.q.shape[1], self.hidden.shape[1]
        self.rows = 2
        self.tok = self.flat // self.rows
        self.outs_going = {}
        c = Chunk
        self.chunks = [c(N.dn, N.hidden, N.cot, 96, 512, j * 512) for j in range(2)]
        self.chunks += [c(N.gu, N.normed_two, N.ggu, 32, 1536, j * 1536) for j in range(4)]
        self.chunks += [c(N.mx, N.mixed, N.grad_out, 48, 1024, 0), c(N.gi, N.normed, N.ggi, 32, 1536, 0)]
        self.chunks += [c(N.da, N.conv, N.hidden, 48, 1024, j * 1024) for j in range(3)]
        self.chunks += [c(N.gi, N.normed, N.ggi, 32, 1536, 1536)]

    def load(self, names):
        for name in names:
            self.loader(name).start()

    def loader(self, name):
        src, dst, at = self.loads[name]
        return pltpu.make_async_copy(src, dst, self.load_sem.at[at])

    def ready(self, names):
        for name in names:
            self.loader(name).wait()

    def produce(self, k):
        ch = self.chunks[k]
        lhs, rhs = getattr(self, ch.lhs), getattr(self, ch.rhs)
        span = 8 * ch.rows
        slot = self.full.at[k % 2]

        def one(z):
            left = lhs[:, pl.ds(pl.multiple_of(z * span, LANE), span)]
            for n in range(ch.across):
                right = rhs[:, ch.first + n * 512 : ch.first + (n + 1) * 512]
                val = outer_sum(left, right).astype(BF16).reshape(8, ch.rows // 16, 16, 512)
                for i in range(ch.rows // 16):
                    slot[z, :, :, :, i * ch.across + n] = val[:, i].reshape(2, 2, 2, 16, 512)

        loop(self.p.nz, one)

    def out_copies(self, k):
        ch = self.chunks[k]
        copies = []
        for i in range(ch.rows // 16):
            for n in range(ch.across):
                at = i * ch.across + n
                col = ch.first + n * 512
                names = self.out_names[ch.name]
                width = self.weight_outs[names[0]].shape[1]
                out = self.weight_outs[names[col // width]]
                dst = out.at[pl.ds(i * 16, 16), pl.ds(col % width, 512)]
                copies.append(pltpu.make_async_copy(self.staged.at[k % 2, at], dst, self.out_sem.at[k % 2, at]))
        return copies

    def deliver(self, k):
        if k >= 2:
            for cp in self.out_copies(k - 2):
                cp.wait()
        for route, at in (("A", 0), ("B", 2), ("C", 4)):
            self.staged[k % 2, at : at + 2] = self.reduce.result(k, route)
        for cp in self.out_copies(k):
            cp.start()

    def by_z(self, weight, buf, sem, extra=None, parts=1):
        width = weight.shape[-1] // parts

        def copies(j, slot):
            z = j // parts
            rows = weight.shape[4]
            src = weight.at[z, :, :, :, :, pl.ds(pl.multiple_of(lax.rem(j, parts) * width, LANE), width)]
            dst = buf.at[slot, :, :, :, 0:rows, 0:width]
            out = [pltpu.make_async_copy(src, dst, sem.at[slot, 0])]
            return out + (extra(j, slot) if extra else [])

        return copies

    def feed_back(self):
        span = self.feed // self.p.nz
        half = lambda slot: pl.ds(pl.multiple_of(slot * span, LANE), span)

        def extra(j, slot):
            at = pl.ds(pl.multiple_of(j * span, LANE), span)
            return [
                pltpu.make_async_copy(self.gate_pre.at[:, at], self.gelu_pre.at[:, half(slot)], self.w_sem.at[slot, 1]),
                pltpu.make_async_copy(self.up.at[:, at], self.state.at[:, half(slot)], self.w_sem.at[slot, 2]),
            ]

        def use(j, slot):
            self.wide_tile[...] = back_prod(self.cot[...], mat(self.w_dn[slot]))
            at = pl.ds(pl.multiple_of(j * span, LANE), span)
            at_up = pl.ds(pl.multiple_of(self.feed + j * span, LANE), span)

            def block(i):
                rows = pl.ds(pl.multiple_of(i * 16, 16), 16)
                grad = self.wide_tile[rows, :]
                gate = self.gelu_pre[rows, half(slot)]
                act, slope = gelu_both(gate)
                self.ggu[rows, at] = (slope * self.state[rows, half(slot)] * grad).astype(BF16)
                self.ggu[rows, at_up] = (act * grad).astype(BF16)

            loop(self.flat // 16, block)

        stream_tiles(self.p.nz, self.by_z(self.dn, self.w_dn, self.w_sem, extra), use)

    def norm_back(self, values, grads, gain_row, extra, out):
        gain = self.vec[gain_row : gain_row + 1, 0 : self.model]

        def block(i, total):
            rows = pl.ds(pl.multiple_of(i * 16, 16), 16)
            v, e = values(rows), grads(rows)
            back, terms = rms_back(v, gain, e)
            out(rows, extra(rows) + back)
            return total + jnp.sum(terms, axis=0, keepdims=True)

        total = lax.fori_loop(0, self.flat // 16, block, jnp.zeros((1, self.model), F32))
        self.sums[gain_row : gain_row + 1, 0 : self.model] = total

    def norm_two_back(self):
        half = self.feed

        def use(j, slot):
            left = self.ggu[:, pl.ds(pl.multiple_of(lax.rem(j, 2) * half, LANE), half)]
            rows = self.gu.shape[4]
            res = back_prod(left, mat(self.w_big[slot, :, :, :, 0:rows, 0:half]))
            at = lanes(j // 2, 8 * rows)

            @pl.when(lax.rem(j, 2) == 0)
            def _():
                self.q[:, at] = res

            @pl.when(lax.rem(j, 2) == 1)
            def _():
                self.q[:, at] = self.q[:, at] + res

        stream_tiles(2 * self.p.nz, self.by_z(self.gu, self.w_big, self.w_sem, None, 2), use)
        self.ready([N.middle])

        def out(rows, val):
            self.middle[rows, :] = val
            self.grad_out[rows, :] = val.astype(BF16)

        self.norm_back(
            lambda rows: self.middle[rows, :],
            lambda rows: self.q[rows, 0 : self.model],
            1,
            lambda rows: self.cot[rows, :].astype(F32),
            out,
        )

    def scan_back(self):
        self.ready([N.gelu_pre, N.state, N.decay_pre])
        rows = self.mx.shape[4]
        span = 8 * rows

        def use(j, slot):
            self.wide_tile[:, 0:span] = back_prod(self.grad_out[...], mat(self.w_big[slot, :, :, :, 0:rows, 0 : self.model]))

            def block(i):
                c = j * (span // LANE) + i
                for r in range(self.rows):
                    at = slice(r * self.tok, (r + 1) * self.tok)
                    grad = self.wide_tile[at, lanes(i)]
                    act, slope = gelu_both(self.gelu_pre[at, lanes(c)])
                    self.ggi[at, lanes(c)] = (slope * grad * self.state[at, lanes(c)]).astype(BF16)
                    _, decay, _ = decay_terms(self.decay_pre[at, lanes(c)], self.vec[4:5, lanes(c)])
                    since = self.since[r * (self.tok + 16) : r * (self.tok + 16) + self.tok, :]
                    eff = decay * (since != 0).astype(F32)
                    place = lax.broadcasted_iota(jnp.int32, eff.shape, 0)
                    after = jnp.where(place < self.tok - 1, pltpu.roll(eff, self.tok - 1, 0), 1.0)
                    prod, tail = scan_block(after, act * grad, reverse=True)
                    self.q[at, lanes(c)] = prod
                    self.gelu_pre[at, lanes(c)] = tail
                    self.tails[self.p.z, r : r + 1, lanes(c)] = eff[0:1, :] * tail[0:1, :]

            loop(span // LANE, block)

        stream_tiles(self.p.nz, self.by_z(self.mx, self.w_big, self.w_sem), use)

    def tail_copy(self, o, recv):
        p = self.p
        view = self.tails.at[lax.rem(p.z + p.nz - o, p.nz) if recv else p.z]
        return pltpu.make_async_remote_copy(
            view, view, self.t_send.at[o - 1], self.t_recv.at[o - 1],
            device_id=p.at(lax.rem(p.z + o, p.nz)), device_id_type=MESH,
        )

    def send_tails(self):
        for o in range(1, self.p.nz):
            self.tail_copy(o, False).start()

    def gates_back(self):
        p = self.p
        for o in range(1, p.nz):
            self.tail_copy(o, True).wait_recv()
        self.ready([N.admit_pre, N.conv])

        def block(c):
            tail = jnp.zeros((8, LANE), F32)
            into = tail
            for i in range(p.nz - 1, 0, -1):
                tail = self.ends[i, 0:8, lanes(c)] * tail + self.tails[i, :, lanes(c)]
                into = jnp.where(p.z == i - 1, tail, into)
            scale = self.vec[4:5, lanes(c)]
            rate_sum = jnp.zeros((1, LANE), F32)
            decay_sum, admit_sum = rate_sum, rate_sum
            for r in range(self.rows):
                at = slice(r * self.tok, (r + 1) * self.tok)
                adjoint = self.gelu_pre[at, lanes(c)] + self.q[at, lanes(c)] * into[r : r + 1, :]
                recall, decay, lost = decay_terms(self.decay_pre[at, lanes(c)], scale)
                root = jnp.sqrt(lost)
                since = self.since[r * (self.tok + 16) : r * (self.tok + 16) + self.tok, :]
                reset = (since == 0).astype(F32)
                keep = 1.0 - reset
                conv = self.conv[at, lanes(c)].astype(F32)
                admit = jax.nn.sigmoid(self.admit_pre[at, lanes(c)])
                state = self.state[at, lanes(c)]
                place = lax.broadcasted_iota(jnp.int32, state.shape, 0)
                before = jnp.where(place > 0, pltpu.roll(state, 1, 0), self.carry[r : r + 1, lanes(c)])
                scale_in = reset + keep * root
                grad_log = adjoint * keep * (before * decay - admit * conv * decay * decay / root)
                decay_low = (grad_log * scale * recall * (1.0 - recall)).astype(BF16)
                admit_low = (adjoint * scale_in * conv * admit * (1.0 - admit)).astype(BF16)
                self.hidden[at, lanes(c)] = decay_low
                self.hidden[at, pl.ds(pl.multiple_of(self.lru + c * LANE, LANE), LANE)] = admit_low
                self.admit_pre[at, lanes(c)] = adjoint * scale_in * admit
                rate_sum = rate_sum + jnp.sum(grad_log * recall, axis=0, keepdims=True)
                decay_sum = decay_sum + jnp.sum(decay_low.astype(F32), axis=0, keepdims=True)
                admit_sum = admit_sum + jnp.sum(admit_low.astype(F32), axis=0, keepdims=True)
            self.sums[2:3, lanes(c)] = decay_sum
            self.sums[3:4, lanes(c)] = admit_sum
            self.sums[4:5, lanes(c)] = rate_sum * (DECAY_SCALE * jax.nn.sigmoid(-self.vec[7:8, lanes(c)]))

        loop(self.lru // LANE, block)

    def conv_grads(self):
        rows = self.da.shape[4]
        span = 8 * rows

        def use(j, slot):
            at = lanes(j, span)
            res = back_prod(self.hidden[...], mat(self.w_big[slot]))
            total = (self.admit_pre[:, at] + res).astype(BF16)
            self.grad_conv[:, :, at] = total.reshape(self.rows, self.tok, span)

        stream_tiles(self.p.nz, self.by_z(self.da, self.w_big, self.w_sem), use)

    def rim_copy(self):
        p = self.p
        return pltpu.make_async_remote_copy(
            self.grad_conv.at[:, 0:16, :], self.rim, self.r_send.at[0], self.r_recv.at[0],
            device_id=p.at(jnp.maximum(p.z - 1, 0)), device_id_type=MESH,
        )

    def send_rim(self):
        pl.when(self.p.z > 0)(lambda: self.rim_copy().start())

    def conv_back(self):
        p = self.p
        pl.when(p.z < p.nz - 1)(lambda: self.rim_copy().wait_recv())
        self.ready([N.branch])
        long = self.tok + 16

        def block(c):
            taps = [jnp.zeros((1, LANE), F32)] * 4
            for r in range(self.rows):
                at = slice(r * self.tok, (r + 1) * self.tok)
                since = self.since[r * long : (r + 1) * long, :]
                grad = self.grad_conv[r, :, lanes(c)].astype(F32)
                wide = jnp.concatenate([grad, self.rim[r, :, lanes(c)].astype(F32)], axis=0)
                head = self.branch[self.flat + 16 * r : self.flat + 16 * (r + 1), lanes(c)].astype(F32)
                back = jnp.concatenate([head, self.branch[at, lanes(c)].astype(F32)], axis=0)
                total = jnp.zeros((self.tok, LANE), F32)
                for k in range(4):
                    seen = (since >= k).astype(F32)
                    moved = back if k == 0 else pltpu.roll(back, k, 0)
                    term = jnp.sum(grad * moved[16:] * seen[0 : self.tok], axis=0, keepdims=True)
                    taps[k] = taps[k] + term
                    ahead = wide * seen
                    ahead = ahead if k == 0 else pltpu.roll(ahead, long - k, 0)
                    total = total + self.vec[8 + k : 9 + k, lanes(c)] * ahead[0 : self.tok]
                self.ggi[at, pl.ds(pl.multiple_of(self.lru + c * LANE, LANE), LANE)] = total.astype(BF16)
            for k in range(4):
                self.sums[5 + k : 6 + k, lanes(c)] = taps[k]

        loop(self.lru // LANE, block)

    def norm_one_back(self):
        rows = self.gi.shape[4]

        def use(j, slot):
            self.q[:, lanes(j, 8 * rows)] = back_prod(self.ggi[...], mat(self.w_big[slot, :, :, :, 0:rows, :]))

        stream_tiles(self.p.nz, self.by_z(self.gi, self.w_big, self.w_sem), use)
        self.ready([N.xs])

        def out(rows, val):
            self.grad_out[rows, :] = val.astype(BF16)

        self.norm_back(
            lambda rows: self.cot[rows, :].astype(F32),
            lambda rows: self.q[rows, 0 : self.model],
            0,
            lambda rows: self.middle[rows, :],
            out,
        )

    def x_copy(self, o):
        p = self.p
        feat = self.x_out.shape[2]
        to = lax.rem(p.z + o, p.nz)
        at = pl.ds(pl.multiple_of(to * feat, LANE), feat)
        src = self.grad_out.reshape(self.rows, self.tok, self.model).at[:, :, at]
        dst = self.x_out.at[:, pl.ds(pl.multiple_of(p.z * self.tok, 16), self.tok), :]
        if o == 0:
            return pltpu.make_async_copy(src, dst, self.x_send.at[p.nz - 1])
        return pltpu.make_async_remote_copy(
            src, dst, self.x_send.at[o - 1], self.x_recv.at[o - 1], device_id=p.at(to), device_id_type=MESH
        )

    def send_x(self):
        for o in range(self.p.nz):
            self.x_copy(o).start()

    def spread_sums(self):
        nz = self.p.nz
        for row in range(10):
            hot, mask, width = (self.hot_m, self.mask_m, self.model) if row < 2 else (self.hot_l, self.mask_l, self.lru)
            vals = self.sums[row : row + 1, 0:width] if row < 9 else self.gate_sums[0:1, :]
            wide = mask[...] * vals
            cut = lax.dot_general(
                wide, hot[...].astype(F32), (((1,), (1,)), ((), ())),
                precision=lax.Precision.HIGHEST, preferred_element_type=F32,
            )
            self.s_own[:, :, :, :, row, :] = cut.reshape(nz, 2, 2, 2, LANE)

    def s_copy(self, at):
        p = self.p
        if at == 0:
            src, dst, dev = self.s_own.at[:, :, :, 1 - p.c], self.s_core, p.core
        elif at == 1:
            src, dst, dev = self.s_core.at[:, :, 1 - p.b], self.s_b, p.peer["b"]
        elif at == 2:
            src, dst, dev = self.s_b.at[:, 1 - p.a], self.s_a, p.peer["a"]
        else:
            to = lax.rem(p.z + at - 2, p.nz)
            src, dst, dev = self.s_a.at[to], self.s_z.at[at - 3], p.at(to)
        return pltpu.make_async_remote_copy(
            src, dst, self.s_send.at[at], self.s_recv.at[at], device_id=dev, device_id_type=MESH
        )

    def small_step(self, n):
        p = self.p
        if n == 0:
            self.s_own[...] = jnp.zeros_like(self.s_own)
            self.spread_sums()
            self.s_copy(0).start()
        if n == 1:
            self.s_copy(0).wait_recv()
            self.s_core[...] = self.s_core[...] + self.s_own[:, :, :, p.c]
            self.s_copy(1).start()
        if n == 2:
            self.s_copy(1).wait_recv()
            self.s_b[...] = self.s_b[...] + self.s_core[:, :, p.b]
            self.s_copy(2).start()
        if n == 3:
            self.s_copy(2).wait_recv()
            self.s_a[...] = self.s_a[...] + self.s_b[:, p.a]
            for o in range(1, p.nz):
                self.s_copy(2 + o).start()
        if n == 4:
            total = self.s_a[p.z]
            for o in range(1, p.nz):
                self.s_copy(2 + o).wait_recv()
                total = total + self.s_z[o - 1]
            self.small_out[...] = total

    def finish(self):
        p = self.p
        count = len(self.chunks)
        for k in (count - 2, count - 1):
            for cp in self.out_copies(k):
                cp.wait()
        for o in range(1, p.nz):
            self.tail_copy(o, False).wait_send()
            self.x_copy(o).wait()
            self.s_copy(2 + o).wait_send()
        self.x_copy(0).wait()
        for at in range(3):
            self.s_copy(at).wait_send()
        pl.when(p.z > 0)(lambda: self.rim_copy().wait_send())


def gelu_both(x):
    inner = GELU_C * (x + 0.044715 * x * x * x)
    t = jnp.tanh(inner)
    slope = 0.5 * (1.0 + t) + 0.5 * x * (1.0 - t * t) * GELU_C * (1.0 + 3 * 0.044715 * x * x)
    return 0.5 * x * (1.0 + t), slope


def rms_back(values, gain, grad):
    q = lax.rsqrt(jnp.mean(values * values, axis=-1, keepdims=True) + EPSILON)
    inner = jnp.mean(values * gain * grad, axis=-1, keepdims=True)
    back = q * gain * grad - values * (q * q * q) * inner
    return back, grad * values * q


WEIGHTS = (N.gelu, N.input, N.decay, N.admit, N.mixer, N.gate, N.up, N.down)
OUT_NAMES = dict(gi=WEIGHTS[:2], da=WEIGHTS[2:4], mx=WEIGHTS[4:5], gu=WEIGHTS[5:7], dn=WEIGHTS[7:])
LOADS = (
    N.hidden, N.cot, N.normed_two, N.middle, N.mixed, N.gelu_pre, N.state, N.decay_pre, N.admit_pre, N.conv,
    N.branch, N.normed, N.xs,
)


def backward_kernel(seq_count, names, hbm_names, vmem_names, *refs):
    n_in = len(vmem_names) + len(hbm_names)
    given = dict(zip(vmem_names + hbm_names, refs[:n_in]))
    x_out, small_out = refs[n_in : n_in + 2]
    weight_outs = dict(zip(WEIGHTS, refs[n_in + 2 : n_in + 10]))
    table = dict(zip(names, refs[n_in + 10 :]))
    p = Place(seq_count)
    loads = {}
    for i, name in enumerate(LOADS):
        dst = table[N.cot] if name == "xs" else table[name]
        loads[name] = (given.pop(name + "_hbm"), dst, i)
    table.update(given)
    table.update(x_out=x_out, small_out=small_out, weight_outs=weight_outs, out_names=OUT_NAMES, loads=loads)
    f = Backward(table, p)
    late = (N.xs, N.gelu_pre, N.state)
    f.load(n for n in LOADS if n not in late)
    f.rim[...] = jnp.zeros_like(f.rim)
    f.tails[...] = jnp.zeros_like(f.tails)
    p.greet()
    f.reduce = Reduce(
        p, {n: table["ring_" + n] for n in Reduce.NAMES}, table[N.full], table[N.send], table[N.recv],
        f.produce, f.deliver,
    )
    count = len(f.chunks)
    f.ready([N.hidden, N.cot])

    def reload_cot():
        f.load(late[:1])

    before = {
        2: [f.feed_back, lambda: f.load(late[1:]), lambda: f.ready([N.normed_two])],
        4: [f.norm_two_back, reload_cot],
        5: [f.scan_back, f.send_tails],
        6: [f.gates_back, lambda: f.ready([N.mixed])],
        7: [lambda: f.ready([N.normed])],
        8: [f.conv_grads, f.send_rim],
        9: [f.conv_back],
        11: [f.norm_one_back, f.send_x, lambda: f.small_step(0)],
        12: [lambda: f.small_step(1)],
        13: [lambda: f.small_step(2)],
        14: [lambda: f.small_step(3)],
        15: [lambda: f.small_step(4)],
    }
    for t in range(count + f.reduce.depth - 1):
        for action in before.get(t, ()):
            action()
        f.reduce.tick(t, count)
    f.finish()


def backward_pass(cot, since_ext, vec, full, kept, shard_shapes, seq_count):
    nz = seq_count
    flat, model = cot.shape
    lru, feed = kept[N.gelu_pre].shape[1], kept[N.hidden].shape[1]
    tok = flat // 2
    vmem_vals = dict(
        vec=vec,
        since=jnp.broadcast_to(since_ext.reshape(-1, 1), (since_ext.size, LANE)),
        carry=kept[N.carry],
        ends=kept[N.ends],
        gate_sums=kept[N.sums],
    )
    vmem_vals.update(zip((N.hot_m, N.mask_m, N.hot_l, N.mask_l), spread_constants(model, lru, nz * 8)))
    hbm_vals = dict(zip((N.gi, N.da, N.mx, N.gu, N.dn), full))
    hbm_vals.update(gate_pre=kept[N.gate_pre], up=kept[N.up])
    source = dict(kept, cot=cot, normed=kept[N.normed_main], xs=kept[N.xs].reshape(flat, model))
    hbm_vals.update({n + "_hbm": source[n] for n in LOADS})
    dma = pltpu.SemaphoreType.DMA
    v = pltpu.VMEM
    chunks = 12
    scratch = dict(
        hidden=v((flat, feed), BF16),
        cot=v((flat, model), BF16),
        normed_two=v((flat, model), BF16),
        normed=v((flat, model), BF16),
        middle=v((flat, model), F32),
        mixed=v((flat, lru), BF16),
        gelu_pre=v((flat, lru), F32),
        state=v((flat, lru), F32),
        decay_pre=v((flat, lru), F32),
        admit_pre=v((flat, lru), F32),
        conv=v((flat, lru), BF16),
        branch=v((flat + 32, lru), BF16),
        ggu=v((flat, 2 * feed), BF16),
        ggi=v((flat, 2 * lru), BF16),
        grad_out=v((flat, model), BF16),
        grad_conv=v((2, tok, lru), BF16),
        rim=v((2, 16, lru), BF16),
        q=v((flat, lru), F32),
        tails=v((nz, 8, lru), F32),
        sums=v((16, lru), F32),
        wide_tile=v((flat, feed // nz), F32),
        w_dn=v((2, 2, 2, 2, full[4].shape[4], model), BF16),
        w_big=v((2, 2, 2, 2, full[1].shape[4], 2 * lru), BF16),
        full=v((2, nz, 2, 2, 2, 6, 16, 512), BF16),
        staged=v((2, 6, 16, 512), F32),
        s_own=v((nz, 2, 2, 2, 16, LANE), F32),
        s_core=v((nz, 2, 2, 16, LANE), F32),
        s_b=v((nz, 2, 16, LANE), F32),
        s_a=v((nz, 16, LANE), F32),
        s_z=v((nz, 16, LANE), F32),
        w_sem=dma((2, 3)),
        load_sem=dma((len(LOADS),)),
        out_sem=dma((2, 6)),
        send=dma((chunks, len(Reduce.NAMES))),
        recv=dma((chunks, len(Reduce.NAMES))),
        t_send=dma((nz,)),
        t_recv=dma((nz,)),
        r_send=dma((1,)),
        r_recv=dma((1,)),
        x_send=dma((nz,)),
        x_recv=dma((nz,)),
        s_send=dma((nz + 3,)),
        s_recv=dma((nz + 3,)),
    )
    scratch.update({"ring_" + n: v(s, BF16) for n, s in Reduce.shapes(nz).items()})
    names = list(scratch)
    hbm = pl.BlockSpec(memory_space=pltpu.HBM)
    vmem = pl.BlockSpec(memory_space=pltpu.VMEM)
    out_shape = [
        jax.ShapeDtypeStruct((2, tok * nz, model // nz), BF16),
        jax.ShapeDtypeStruct((16, LANE), F32),
    ] + [jax.ShapeDtypeStruct(s, F32) for s in shard_shapes]
    outs = pl.pallas_call(
        partial(backward_kernel, nz, names, list(hbm_vals), list(vmem_vals)),
        out_shape=out_shape,
        in_specs=[vmem] * len(vmem_vals) + [hbm] * len(hbm_vals),
        out_specs=[hbm, vmem] + [hbm] * 8,
        scratch_shapes=[scratch[n] for n in names],
        compiler_params=pltpu.CompilerParams(
            collective_id=1, has_side_effects=True, vmem_limit_bytes=61 << 20
        ),
        name="backward_pass",
    )(*vmem_vals.values(), *hbm_vals.values())
    return outs[0], outs[1], outs[2:]


def local_fast(x_heads, cotangent, doc_starts, smalls, shards):
    norm_gain, conv_weight, decay_bias, admit_bias, decay_rate, feed_gain = smalls
    seq_count = lax.axis_size("seq")
    dev_count = seq_count * lax.axis_size("dp")
    row_count, tok_count, model = cotangent.shape
    flat = row_count * tok_count
    lru, taps = shards[0].shape[1], conv_weight.shape[1]
    positions = lax.axis_index("seq") * tok_count + jnp.arange(tok_count + 16, dtype=jnp.int32)
    since_ext = since_start(doc_starts, positions)
    small = small_rows(norm_gain, conv_weight, decay_bias, admit_bias, decay_rate, feed_gain)
    vec, full, kept = forward_pass(x_heads, small, since_ext[:, :tok_count], shards, seq_count, STARTS)
    input_grad, own, grads = backward_pass(
        cotangent.reshape(flat, model), since_ext, vec, full, kept, [s.shape for s in shards], seq_count
    )
    per_model, per_lru = model // dev_count, lru // dev_count
    return (
        kept[N.block].reshape(row_count, tok_count, model),
        input_grad,
        own[0, :per_model],
        grads[0],
        grads[1],
        own[5 : 5 + taps, :per_lru].T,
        grads[2],
        own[2, :per_lru],
        grads[3],
        own[3, :per_lru],
        own[4, :per_lru],
        grads[4],
        own[1, :per_model],
        grads[5],
        grads[6],
        grads[7],
        own[9, :per_lru] * (1.0 / float(flat * dev_count)),
    )


def local(
    x_heads,
    cotangent,
    doc_starts,
    norm_gain,
    gelu_weight,
    input_weight,
    conv_weight,
    decay_weight,
    decay_bias,
    admit_weight,
    admit_bias,
    decay_rate,
    mixer_output,
    feed_gain,
    feed_gate,
    feed_up,
    feed_down,
):
    seq_count = lax.axis_size("seq")
    dev_count = seq_count * lax.axis_size("dp")
    seq_at = lax.axis_index("seq")
    row_count, tok_count, model = cotangent.shape
    flat = row_count * tok_count
    lru = gelu_weight.shape[1]
    feed = feed_gate.shape[1]
    taps = conv_weight.shape[1]
    rim = taps - 1

    smalls = (norm_gain, conv_weight, decay_bias, admit_bias, decay_rate, feed_gain)
    shards = (
        gelu_weight, input_weight, decay_weight, admit_weight, mixer_output, feed_gate, feed_up, feed_down,
    )
    if fast_shapes(shards, seq_count, lax.axis_size("dp"), row_count, tok_count):
        return local_fast(x_heads, cotangent, doc_starts, smalls, shards)
    packed = lax.all_gather(pack_small(smalls), ALL, axis=0, tiled=True).astype(F32)
    parts = split_small(packed, [v.size for v in smalls])
    gain_one = parts[0].reshape(-1)
    conv_taps = parts[1].reshape(lru, taps)
    decay_shift, admit_shift, rate_vec, gain_two = [p.reshape(-1) for p in parts[2:]]

    gelu_input = gather_rows(jnp.concatenate([gelu_weight, input_weight], axis=1))
    decay_admit = gather_rows(jnp.concatenate([decay_weight, admit_weight], axis=1))
    mixer_full = gather_rows(mixer_output)
    gate_up = gather_rows(jnp.concatenate([feed_gate, feed_up], axis=1))
    down_full = gather_rows(feed_down)

    stream = lax.all_to_all(x_heads, "seq", split_axis=1, concat_axis=2, tiled=True)
    stream_in = stream.reshape(flat, model).astype(F32)
    normed_one, norm_one_pull = jax.vjp(rms_norm, stream_in, gain_one)
    normed_low = normed_one.astype(BF16)
    both = dot(normed_low, gelu_input)
    gelu_vals, gelu_pull = jax.vjp(smooth_gate, both[:, :lru])
    branch = both[:, lru:].astype(BF16).reshape(row_count, tok_count, lru)
    halo = shift_seq(branch[:, tok_count - rim :, :], 1, seq_count)
    extended = jnp.concatenate([halo, branch], axis=1).astype(F32)
    positions = seq_at * tok_count + jnp.arange(tok_count + rim, dtype=jnp.int32)
    since_ext = since_start(doc_starts, positions)
    since_here = since_ext[:, :tok_count]
    conv_vals = jnp.zeros((row_count, tok_count, lru), F32)
    for k in range(taps):
        window = extended[:, rim - k : rim - k + tok_count, :]
        conv_vals = conv_vals + conv_taps[:, k] * window * (since_here >= k)[..., None].astype(F32)
    conv_low = conv_vals.astype(BF16)
    conv_flat = conv_low.reshape(flat, lru)
    gates = dot(conv_flat, decay_admit)
    decay_pre = (gates[:, :lru] + decay_shift).reshape(row_count, tok_count, lru)
    admit_pre = (gates[:, lru:] + admit_shift).reshape(row_count, tok_count, lru)
    reset_mask = (since_here == 0).astype(F32)[..., None]

    def coefs(dp, ap, cv, rv):
        return coefficients(dp, ap, cv, rv, reset_mask)

    (decay_eff, update, decay_vals), coef_pull = jax.vjp(
        coefs, decay_pre, admit_pre, conv_low.astype(F32), rate_vec
    )
    decay_prod, local_state = lax.associative_scan(compose, (decay_eff, update), axis=1)
    ends = jnp.stack([decay_prod[:, -1], local_state[:, -1]])
    all_ends = lax.all_gather(ends, "seq", axis=0)
    carry = jnp.zeros((row_count, lru), F32)
    carry_in = carry
    for i in range(seq_count - 1):
        carry = all_ends[i, 0] * carry + all_ends[i, 1]
        carry_in = jnp.where(seq_at == i + 1, carry, carry_in)
    state = local_state + decay_prod * carry_in[:, None, :]
    state_flat = state.reshape(flat, lru)
    mixed_low = (state_flat * gelu_vals).astype(BF16)
    middle = stream_in + dot(mixed_low, mixer_full)
    normed_two, norm_two_pull = jax.vjp(rms_norm, middle, gain_two)
    normed_two_low = normed_two.astype(BF16)
    gate_up_pre = dot(normed_two_low, gate_up)
    gate_act, gate_pull = jax.vjp(smooth_gate, gate_up_pre[:, :feed])
    up_vals = gate_up_pre[:, feed:]
    hidden_low = (gate_act * up_vals).astype(BF16)
    block_output = (middle + dot(hidden_low, down_full)).astype(BF16)
    block_output = block_output.reshape(row_count, tok_count, model)

    cot = cotangent.reshape(flat, model)
    down_grad = scatter_rows(outer_sum(hidden_low, cot))
    grad_hidden = back_prod(cot, down_full)
    grad_gate = gate_pull(grad_hidden * up_vals)[0].astype(BF16)
    grad_up = (grad_hidden * gate_act).astype(BF16)
    grad_gu = jnp.concatenate([grad_gate, grad_up], axis=1)
    gate_up_grad = scatter_rows(outer_sum(normed_two_low, grad_gu))
    grad_mid_norm, gain_two_grad = norm_two_pull(back_prod(grad_gu, gate_up))
    grad_middle = cot.astype(F32) + grad_mid_norm
    grad_out = grad_middle.astype(BF16)
    mixer_grad = scatter_rows(outer_sum(mixed_low, grad_out))
    grad_mixed = back_prod(grad_out, mixer_full)
    grad_gelu = gelu_pull(grad_mixed * state_flat)[0].astype(BF16)
    direct = (grad_mixed * gelu_vals).reshape(row_count, tok_count, lru)
    decay_next = jnp.concatenate([decay_eff[:, 1:, :], jnp.ones_like(decay_eff[:, :1, :])], axis=1)
    tail_prod, tail_state = lax.associative_scan(
        compose, (decay_next, direct), axis=1, reverse=True
    )
    back_ends = lax.all_gather(decay_eff[:, 0] * tail_state[:, 0], "seq", axis=0)
    back = jnp.zeros((row_count, lru), F32)
    back_in = back
    for i in range(seq_count - 1, 0, -1):
        back = all_ends[i, 0] * back + back_ends[i]
        back_in = jnp.where(seq_at == i - 1, back, back_in)
    adjoint = tail_state + tail_prod * back_in[:, None, :]
    state_prev = jnp.concatenate([carry_in[:, None, :], state[:, :-1, :]], axis=1)
    decay_pre_grad, admit_pre_grad, conv_direct, rate_grad = coef_pull(
        (adjoint * state_prev, adjoint, jnp.zeros_like(decay_vals))
    )
    grad_decay = decay_pre_grad.reshape(flat, lru).astype(BF16)
    grad_admit = admit_pre_grad.reshape(flat, lru).astype(BF16)
    grad_da = jnp.concatenate([grad_decay, grad_admit], axis=1)
    decay_admit_grad = scatter_rows(outer_sum(conv_flat, grad_da))
    decay_b_grad = jnp.sum(grad_decay, axis=0, dtype=F32)
    admit_b_grad = jnp.sum(grad_admit, axis=0, dtype=F32)
    grad_conv = (conv_direct.reshape(flat, lru) + back_prod(grad_da, decay_admit)).astype(BF16)
    grad_conv = grad_conv.reshape(row_count, tok_count, lru)
    grad_conv_wide = grad_conv.astype(F32)
    tap_grads = []
    for k in range(taps):
        window = extended[:, rim - k : rim - k + tok_count, :]
        mask = (since_here >= k)[..., None].astype(F32)
        tap_grads.append(jnp.sum(grad_conv_wide * window * mask, axis=(0, 1)))
    conv_grad = jnp.stack(tap_grads, axis=1)
    rim_after = shift_seq(grad_conv[:, :rim, :], -1, seq_count)
    grad_ext = jnp.concatenate([grad_conv, rim_after], axis=1).astype(F32)
    branch_grad = jnp.zeros((row_count, tok_count, lru), F32)
    for k in range(taps):
        ahead = (since_ext[:, k : k + tok_count] >= k)[..., None].astype(F32)
        branch_grad = branch_grad + conv_taps[:, k] * grad_ext[:, k : k + tok_count, :] * ahead
    branch_grad_low = branch_grad.reshape(flat, lru).astype(BF16)
    grad_gi = jnp.concatenate([grad_gelu, branch_grad_low], axis=1)
    gelu_input_grad = scatter_rows(outer_sum(normed_low, grad_gi))
    grad_in_norm, gain_one_grad = norm_one_pull(back_prod(grad_gi, gelu_input))
    input_grad_tok = (grad_middle + grad_in_norm).astype(BF16)
    input_grad_tok = input_grad_tok.reshape(row_count, tok_count, model)
    input_grad = lax.all_to_all(input_grad_tok, "seq", split_axis=2, concat_axis=1, tiled=True)
    gate_term = jnp.sum(decay_vals, axis=(0, 1)) / float(flat * dev_count)
    small_grads = (
        gain_one_grad,
        conv_grad,
        decay_b_grad,
        admit_b_grad,
        rate_grad,
        gain_two_grad,
        gate_term,
    )
    packed_grads = jnp.concatenate([g.reshape(dev_count, -1) for g in small_grads], axis=1)
    reduced = lax.psum_scatter(packed_grads, ALL, scatter_dimension=0, tiled=True)
    own = split_small(reduced, [g.size // dev_count for g in small_grads])
    return (
        block_output,
        input_grad,
        own[0].reshape(-1),
        gelu_input_grad[:, :lru],
        gelu_input_grad[:, lru:],
        own[1].reshape(-1, taps),
        decay_admit_grad[:, :lru],
        own[2].reshape(-1),
        decay_admit_grad[:, lru:],
        own[3].reshape(-1),
        own[4].reshape(-1),
        mixer_grad,
        own[5].reshape(-1),
        gate_up_grad[:, :feed],
        gate_up_grad[:, feed:],
        down_grad,
        own[6].reshape(-1),
    )


def solution(mesh):
    rows = P(ALL, None)
    vec = P(ALL)
    placed = (
        P("dp", None, "seq"),
        P("dp", "seq", None),
        P("dp", None),
        vec,
        rows,
        rows,
        rows,
        rows,
        vec,
        rows,
        vec,
        vec,
        rows,
        vec,
        rows,
        rows,
        rows,
    )
    outs = (
        P("dp", "seq", None),
        P("dp", None, "seq"),
        vec,
        rows,
        rows,
        rows,
        rows,
        vec,
        rows,
        vec,
        vec,
        rows,
        vec,
        rows,
        rows,
        rows,
        vec,
    )
    return jax.shard_map(local, mesh=mesh, in_specs=placed, out_specs=outs, check_vma=False)
```

```python
from functools import partial

import jax
import jax.numpy as jnp
import numpy as np
from jax import lax
from jax.experimental import pallas as pl
from jax.experimental.pallas import tpu as pltpu
from jax.sharding import PartitionSpec as P

EPSILON = 1e-06
DECAY_SCALE = 8.0
ALL = ("seq", "dp")
F32 = jnp.float32
BF16 = jnp.bfloat16
GELU_C = 0.7978845608028654


class Names:
    def __getattr__(self, name):
        return name


N = Names()
GATHER_PACE = 1
STARTS = (0, 0, 1, 1, 2, 2, 3, 4, 5, 6, 7, 8)


def rms_norm(values, gain_vec):
    return (
        values * lax.rsqrt(jnp.mean(values * values, axis=-1, keepdims=True) + EPSILON) * gain_vec
    )


def smooth_gate(values):
    return jax.nn.gelu(values, approximate=True)


def compose(earlier, latter):
    return (earlier[0] * latter[0], latter[0] * earlier[1] + latter[1])


def since_start(doc_starts, positions):
    begins = jnp.max(
        jnp.where(doc_starts[:, None, :] <= positions[None, :, None], doc_starts[:, None, :], 0),
        axis=-1,
    )
    return positions[None, :] - begins


def coefficients(decay_pre, admit_pre, conv_vals, rate_vec, reset_mask):
    recall = jax.nn.sigmoid(decay_pre)
    admit_vals = jax.nn.sigmoid(admit_pre)
    log_decay = -DECAY_SCALE * recall * jax.nn.softplus(-rate_vec)
    decay_vals = jnp.exp(log_decay)
    keep_mask = 1.0 - reset_mask
    scale_in = reset_mask + keep_mask * jnp.sqrt(-jnp.expm1(2.0 * log_decay))
    return (decay_vals * keep_mask, scale_in * admit_vals * conv_vals, decay_vals)


def dot(left, right):
    return jnp.dot(left, right, preferred_element_type=F32)


def outer_sum(left, right):
    return lax.dot_general(left, right, (((0,), (0,)), ((), ())), preferred_element_type=F32)


def back_prod(grad_rows, weight):
    return lax.dot_general(
        grad_rows, weight, (((1,), (1,)), ((), ())), preferred_element_type=F32
    )


def gather_rows(shard):
    return lax.all_gather(shard, ALL, axis=0, tiled=True)


def scatter_rows(partial):
    return lax.psum_scatter(partial.astype(BF16), ALL, scatter_dimension=0, tiled=True).astype(F32)


def shift_seq(values, step, seq_count):
    pairs = [(i, i + step) for i in range(seq_count) if 0 <= i + step < seq_count]
    return lax.ppermute(values, "seq", pairs)


def pack_small(pieces):
    return jnp.concatenate([p.reshape(1, -1) for p in pieces], axis=1)


def split_small(packed, widths):
    out, at = [], 0
    for width in widths:
        out.append(packed[:, at : at + width])
        at += width
    return out


MESH = pl.DeviceIdType.MESH
PLANE = 2


def fast_shapes(shards, seq_count, dp_count, row_count, tok_count):
    if dp_count != 2 * PLANE * PLANE or seq_count < 2 or row_count != 2 or tok_count != 128:
        return False
    return all(s.shape[0] in (32, 48, 96) and s.shape[1] % 512 == 0 for s in shards)


class Place:
    def __init__(self, seq_count):
        self.nz = seq_count
        self.z = lax.axis_index("seq")
        self.d = lax.axis_index("dp")
        self.c = lax.rem(self.d, 2)
        self.b = lax.rem(self.d // 2, 2)
        self.a = self.d // 4
        self.core = (self.z, self.d + 1 - 2 * self.c)
        self.peer = {
            "b": (self.z, self.d + 2 - 4 * self.b),
            "a": (self.z, self.d + 4 - 8 * self.a),
        }

    def at(self, z):
        return (z, self.d)

    def greet(self):
        barrier = pltpu.get_barrier_semaphore()
        others = [self.core, self.peer["a"], self.peer["b"]]
        others += [self.at(lax.rem(self.z + o, self.nz)) for o in range(1, self.nz)]
        for other in others:
            pl.semaphore_signal(barrier, inc=1, device_id=other, device_id_type=MESH)
        pl.semaphore_wait(barrier, len(others))


def step_cols(width):
    part = 7 * (width // LANE) // 24 * LANE
    return {"A": (0, part), "B": (part, 2 * part), "C": (2 * part, width)}


def chunk_list(shapes):
    chunks = []
    for i, (rows, cols) in enumerate(shapes):
        wide = min(cols, 3072)
        tall = rows if wide < 3072 and rows <= 48 else (48 if wide < 3072 else 16)
        for c0 in range(0, cols, wide):
            for r0 in range(0, rows, tall):
                chunks.append((i, r0, tall, c0, wide))
    return chunks


class Gather:
    def __init__(self, place, outs, chunks, send, recv, starts):
        self.p, self.outs, self.chunks = place, outs, chunks
        self.send, self.recv, self.starts = send, recv, starts
        self.started = []
        nz = place.nz
        self.depth = nz + 4

    def view(self, k, z, a, b, c, route):
        i, r0, nr, c0, nc = self.chunks[k]
        lo, hi = (0, nc) if route is None else step_cols(nc)[route]
        full = slice(None)
        one = lambda v: full if v is None else pl.ds(v, 1)
        return self.outs[i].at[
            one(z), one(a), one(b), one(c), pl.ds(r0, nr), pl.ds(c0 + lo, hi - lo)
        ]

    def copy(self, k, view, s_at, r_at, dev):
        return pltpu.make_async_remote_copy(
            view, view, self.send.at[k, s_at], self.recv.at[k, r_at], device_id=dev, device_id_type=MESH
        )

    def put(self, k, view, s_at, r_at, dev, cond=None):
        cp = self.copy(k, view, s_at, r_at, dev)
        if cond is None:
            cp.start()
        else:
            pl.when(cond)(cp.start)
        self.started.append((cp, cond))

    def take(self, k, view, r_at, cond=None):
        cp = self.copy(k, view, 0, r_at, self.p.core)
        if cond is None:
            cp.wait_recv()
        else:
            pl.when(cond)(cp.wait_recv)

    def sem(self, route, phase, z=0):
        nz = self.p.nz
        slot = {"first": 0, "up": 1, "down": 1 + nz, "mid": 1 + 2 * nz, "last": 1 + 3 * nz}[phase]
        return {"A": 0, "B": 1, "C": 2}[route] * (1 + 4 * nz) + slot + z

    @staticmethod
    def sem_count(nz):
        return 3 * (1 + 4 * nz) + 1

    def order(self, k, route):
        if route == "C":
            return ("a", "b") if k % 2 else ("b", "a")
        return ("b", "a") if route == "A" else ("a", "b")

    def z_unit(self, k, route, z):
        p = self.p
        first = self.order(k, route)[0]
        a = None if route != "C" and first == "a" else p.a
        b = None if route != "C" and first == "b" else p.b
        return self.view(k, z, a, b, p.c, route)

    def z_own(self, k, route):
        p = self.p
        unit = self.z_unit(k, route, p.z)
        self.put(k, unit, self.sem(route, "up", p.z), self.sem(route, "up", p.z), p.at(p.z + 1), p.z < p.nz - 1)
        self.put(k, unit, self.sem(route, "down", p.z), self.sem(route, "down", p.z), p.at(p.z - 1), p.z > 0)
        self.after(k, route, p.z, None)

    def after(self, k, route, z, cond):
        p = self.p
        first, second = self.order(k, route)
        dim = first if route == "C" else second
        name = "mid" if route == "C" else "last"
        self.put(k, self.z_unit(k, route, z), self.sem(route, name, z), self.sem(route, name, z), p.peer[dim], cond)

    def z_hop(self, k, route, h):
        p = self.p
        low, high = p.z - h, p.z + h
        has_low, has_high = low >= 0, high < p.nz
        low_at, high_at = jnp.maximum(low, 0), jnp.minimum(high, p.nz - 1)
        unit = self.z_unit(k, route, low_at)
        self.take(k, unit, self.sem(route, "up", low_at), has_low)
        if h < p.nz - 1:
            self.put(k, unit, self.sem(route, "up", low_at), self.sem(route, "up", low_at), p.at(p.z + 1), has_low & (p.z < p.nz - 1))
        self.after(k, route, low_at, has_low)
        unit = self.z_unit(k, route, high_at)
        self.take(k, unit, self.sem(route, "down", high_at), has_high)
        if h < p.nz - 1:
            self.put(k, unit, self.sem(route, "down", high_at), self.sem(route, "down", high_at), p.at(p.z - 1), has_high & (p.z > 0))
        self.after(k, route, high_at, has_high)

    def c_last(self, k, z, cond):
        p = self.p
        first, second = self.order(k, "C")
        a = None if first == "a" else p.a
        b = None if first == "b" else p.b
        peer_a = 1 - p.a if first == "a" else p.a
        peer_b = 1 - p.b if first == "b" else p.b
        self.take(k, self.view(k, z, peer_a, peer_b, p.c, "C"), self.sem("C", "mid", z), cond)
        self.put(k, self.view(k, z, a, b, p.c, "C"), self.sem("C", "last", z), self.sem("C", "last", z), p.peer[second], cond)

    def c_last_hop(self, k, h):
        p = self.p
        if h == 0:
            self.c_last(k, p.z, None)
            return
        low, high = p.z - h, p.z + h
        self.c_last(k, jnp.maximum(low, 0), low >= 0)
        self.c_last(k, jnp.minimum(high, p.nz - 1), high < p.nz)

    def stage(self, k, s):
        p, nz = self.p, self.p.nz
        if s == 0:
            for route in "AB":
                first = self.order(k, route)[0]
                at = self.sem(route, "first")
                self.put(k, self.view(k, p.z, p.a, p.b, p.c, route), at, at, p.peer[first])
            self.z_own(k, "C")
        if s == 1:
            for route in "AB":
                first = self.order(k, route)[0]
                a = 1 - p.a if first == "a" else p.a
                b = 1 - p.b if first == "b" else p.b
                self.take(k, self.view(k, p.z, a, b, p.c, route), self.sem(route, "first"))
                self.z_own(k, route)
        if 1 <= s < nz:
            self.z_hop(k, "C", s)
        if 2 <= s <= nz:
            self.z_hop(k, "A", s - 1)
            self.z_hop(k, "B", s - 1)
        if 2 <= s < nz + 2:
            self.c_last_hop(k, s - 2)
        if s == nz + 2:
            for z in range(nz):
                for route in "ABC":
                    second = self.order(k, route)[1]
                    a = 1 - p.a if second == "a" else None
                    b = 1 - p.b if second == "b" else None
                    self.take(k, self.view(k, z, a, b, p.c, route), self.sem(route, "last", z))
            at = self.sem_count(nz) - 1
            self.put(k, self.view(k, None, None, None, p.c, None), at, at, p.core)
        if s == nz + 3:
            at = self.sem_count(nz) - 1
            self.take(k, self.view(k, None, None, None, 1 - p.c, None), at)

    def tick(self, t):
        for k in range(len(self.chunks)):
            s = t - self.starts[k]
            if 0 <= s < GATHER_PACE * self.depth and s % GATHER_PACE == 0:
                self.stage(k, s // GATHER_PACE)

    def ticks(self):
        return max(self.starts) + GATHER_PACE * (self.depth - 1) + 1

    def finish(self):
        for cp, cond in self.started:
            if cond is None:
                cp.wait_send()
            else:
                pl.when(cond)(cp.wait_send)


LANE = 128


def spread_constants(model, lru, dev_count):
    out = []
    for width in (model, lru):
        per = width // dev_count
        lane = np.arange(width)[None, :]
        out.append(jnp.asarray(lane % per == np.arange(LANE)[:, None], BF16))
        out.append(jnp.asarray(lane // per == np.arange(dev_count)[:, None], F32))
    return out


def small_parts(norm_gain, conv_weight, decay_bias, admit_bias, decay_rate, feed_gain):
    scale = -DECAY_SCALE * jax.nn.softplus(-decay_rate.astype(F32))
    parts = [norm_gain, feed_gain, decay_bias, admit_bias, scale, decay_rate]
    return [v.reshape(1, -1) for v in parts] + [conv_weight.T]


def pack_rows(parts, out):
    out[...] = jnp.zeros_like(out)
    gain_one, gain_two, decay_bias, admit_bias, scale, rate, taps = [v[...].astype(F32) for v in parts]
    high = scale.astype(BF16).astype(F32)
    mid = (scale - high).astype(BF16).astype(F32)
    rows = [gain_one, gain_two, decay_bias, admit_bias, high, mid, scale - high - mid, rate]
    for i, row in enumerate(rows):
        out[i : i + 1, 0 : row.shape[1]] = row
    out[8 : 8 + taps.shape[0], 0 : taps.shape[1]] = taps


def decay_terms(pre, scale):
    recall = jax.nn.sigmoid(pre)
    log_decay = recall * scale
    decay = jnp.exp(log_decay)
    y = 2.0 * log_decay
    series = 1.0 + y * (1 / 7)
    for n in (6, 5, 4, 3, 2):
        series = 1.0 + y * (1 / n) * series
    lost = jnp.where(y > -0.35, -y * series, 1.0 - decay * decay)
    return recall, decay, lost


def scan_block(prod, state, reverse=False):
    length = prod.shape[0]
    at = lax.broadcasted_iota(jnp.int32, prod.shape, 0)
    step = 1
    while step < length:
        inside = at < length - step if reverse else at >= step
        turn = length - step if reverse else step
        prod_far = jnp.where(inside, pltpu.roll(prod, turn, 0), 1.0)
        state_far = jnp.where(inside, pltpu.roll(state, turn, 0), 0.0)
        state = prod * state_far + state
        prod = prod * prod_far
        step *= 2
    return prod, state


def lanes(c, width=LANE):
    return pl.ds(pl.multiple_of(c * width, width), width)


def loop(count, body):
    def step(i, carry):
        body(i)
        return carry

    lax.fori_loop(0, count, step, 0)


def stream_tiles(count, fetch, use):
    for cp in fetch(0, 0):
        cp.start()

    def step(j, carry):
        slot = lax.rem(j, 2)

        @pl.when(j + 1 < count)
        def _():
            for cp in fetch(j + 1, 1 - slot):
                cp.start()

        for cp in fetch(j, slot):
            cp.wait()
        use(j, slot)
        return carry

    lax.fori_loop(0, count, step, 0)


def mat(value):
    return value.reshape(-1, value.shape[-1])


class Forward:
    def __init__(self, refs, place, weights):
        self.__dict__.update(refs)
        self.p, self.weights = place, weights
        self.tok = self.xs.shape[1]
        self.rows = self.xs.shape[0]
        self.flat = self.rows * self.tok
        self.lru = self.gelu_pre.shape[1]
        self.model = self.xs.shape[2]
        self.feed = self.hidden.shape[1]
        self.stores = []

    def save(self, name):
        cp = pltpu.make_async_copy(getattr(self, name), self.keep[name], self.keep_sem.at[len(self.stores)])
        cp.start()
        self.stores.append(cp)

    def fetch(self, i, buf, sem, starts, width):
        def copies(j, slot):
            out = []
            for n, start in enumerate(starts):
                src = self.weights[i].at[:, :, :, :, :, pl.ds(pl.multiple_of(start + j * width, LANE), width)]
                dst = buf.at[slot, :, :, :, :, :, pl.ds(n * width, width)]
                out.append(pltpu.make_async_copy(src, dst, sem.at[slot, n]))
            return out

        return copies

    def vectors(self):
        cp = pltpu.make_async_copy(self.small_all, self.small_vm, self.misc_sem.at[0])
        cp.start()
        cp.wait()
        nz = self.p.nz

        def spread(row, hot, mask):
            vals = self.small_vm[:, :, row, :].reshape(nz * 8, LANE).astype(BF16)
            wide = jnp.dot(vals, hot[...], preferred_element_type=F32)
            return jnp.sum(wide * mask[...], axis=0, keepdims=True)

        for row in range(2):
            self.vec[row : row + 1, 0 : self.model] = spread(row, self.hot_m, self.mask_m)
        for row in range(2, 12):
            self.vec[row : row + 1, :] = spread(row, self.hot_l, self.mask_l)
        self.vec[4:5, :] = self.vec[4:5, :] + self.vec[5:6, :] + self.vec[6:7, :]

    def norm(self, load, count, gain_row, out):
        gain = self.vec[gain_row : gain_row + 1, 0 : self.model]

        def body(i):
            v = load(i)
            q = lax.rsqrt(jnp.mean(v * v, axis=-1, keepdims=True) + EPSILON)
            out[pl.ds(pl.multiple_of(i * 32, 32), 32), :] = (v * q * gain).astype(BF16)

        loop(count, body)

    def norm_one(self):
        per = self.tok // 32

        def main(i):
            return self.xs[i // per, pl.ds(pl.multiple_of(lax.rem(i, per) * 32, 32), 32), :].astype(F32)

        self.norm(main, self.flat // 32, 0, self.normed.at[0 : self.flat])
        self.norm(
            lambda i: self.halo_x[...].reshape(2 * 16, self.model).astype(F32),
            1,
            0,
            self.normed.at[self.flat : self.flat + 32],
        )
        self.save(N.normed_main)
        self.save(N.xs)

    def gelu_input(self):
        half = self.lru // 512

        def use(j, slot):
            res = jnp.dot(self.normed[0 : self.flat, :], mat(self.w_gi[slot]), preferred_element_type=F32)
            self.gelu_pre[:, lanes(j, 512)] = res

        stream_tiles(half, self.fetch(0, self.w_gi, self.w_sem, (0,), 512), use)

        def use_two(j, slot):
            res = jnp.dot(self.normed[...], mat(self.w_gi[slot]), preferred_element_type=F32).astype(BF16)
            self.branch[:, lanes(j, 512)] = res

        stream_tiles(half, self.fetch(0, self.w_gi, self.w_sem, (self.lru,), 512), use_two)

        def conv(c):
            for r in range(self.rows):
                at = slice(r * self.tok, (r + 1) * self.tok)
                head = self.branch[self.flat + 16 * r : self.flat + 16 * (r + 1), lanes(c)].astype(F32)
                wide = jnp.concatenate([head, self.branch[at, lanes(c)].astype(F32)], axis=0)
                since = self.since[pl.ds(r * (self.tok + 16), self.tok), :]
                total = jnp.zeros((self.tok, LANE), F32)
                for k in range(4):
                    moved = wide if k == 0 else pltpu.roll(wide, k, 0)
                    tap = self.vec[8 + k : 9 + k, lanes(c)]
                    total = total + tap * moved[16:] * (since >= k).astype(F32)
                self.conv[at, lanes(c)] = total.astype(BF16)

        loop(self.lru // LANE, conv)
        self.save(N.gelu_pre)
        self.save(N.branch)
        self.save(N.conv)

    def gates(self, first, count):
        self.sums[...] = jnp.zeros_like(self.sums) if first == 0 else self.sums[...]

        def use(j, slot):
            self.tile[...] = jnp.dot(self.conv[...], mat(self.w_da[slot]), preferred_element_type=F32)
            base = (first + j) * 4

            def block(i):
                c = base + i
                gate_sum = jnp.zeros((1, LANE), F32)
                for r in range(self.rows):
                    at = slice(r * self.tok, (r + 1) * self.tok)
                    pre = self.tile[at, lanes(i)] + self.vec[2:3, lanes(c)]
                    admit_pre = self.tile[at, lanes(i + 4)] + self.vec[3:4, lanes(c)]
                    self.decay_pre[at, lanes(c)] = pre
                    self.admit_pre[at, lanes(c)] = admit_pre
                    recall, decay, lost = decay_terms(pre, self.vec[4:5, lanes(c)])
                    since = self.since[pl.ds(r * (self.tok + 16), self.tok), :]
                    reset = (since == 0).astype(F32)
                    keep = 1.0 - reset
                    scale_in = reset + keep * jnp.sqrt(lost)
                    update = scale_in * jax.nn.sigmoid(admit_pre) * self.conv[at, lanes(c)].astype(F32)
                    prod, state = scan_block(decay * keep, update)
                    self.prod[at, lanes(c)] = prod
                    self.state[at, lanes(c)] = state
                    self.ends[self.p.z, r : r + 1, lanes(c)] = prod[self.tok - 1 :, :]
                    self.ends[self.p.z, 8 + r : 9 + r, lanes(c)] = state[self.tok - 1 :, :]
                    gate_sum = gate_sum + jnp.sum(decay, axis=0, keepdims=True)
                self.sums[0:1, lanes(c)] = gate_sum

            loop(4, block)

        starts = (first * 512, self.lru + first * 512)
        stream_tiles(count, self.fetch(1, self.w_da, self.w_sem, starts, 512), use)

    def gates_saved(self):
        self.save(N.decay_pre)
        self.save(N.admit_pre)
        self.save(N.sums)

    def send_ends(self):
        p = self.p
        self.end_moves = []
        for o in range(1, p.nz):
            view = self.ends.at[p.z]
            cp = pltpu.make_async_remote_copy(
                view, view, self.e_send.at[o - 1], self.e_recv.at[o - 1],
                device_id=p.at(lax.rem(p.z + o, p.nz)), device_id_type=MESH,
            )
            cp.start()
            self.end_moves.append(cp)

    def mix(self):
        p = self.p
        for o in range(1, p.nz):
            view = self.ends.at[lax.rem(p.z + p.nz - o, p.nz)]
            pltpu.make_async_remote_copy(
                view, view, self.e_send.at[o - 1], self.e_recv.at[o - 1],
                device_id=p.core, device_id_type=MESH,
            ).wait_recv()

        def block(c):
            carry = jnp.zeros((8, LANE), F32)
            into = carry
            for i in range(p.nz - 1):
                carry = self.ends[i, 0:8, lanes(c)] * carry + self.ends[i, 8:16, lanes(c)]
                into = jnp.where(p.z == i + 1, carry, into)
            self.carry[:, lanes(c)] = into
            for r in range(self.rows):
                at = slice(r * self.tok, (r + 1) * self.tok)
                state = self.state[at, lanes(c)] + self.prod[at, lanes(c)] * into[r : r + 1, :]
                self.state[at, lanes(c)] = state
                gelu = smooth_gate(self.gelu_pre[at, lanes(c)])
                self.mixed[at, lanes(c)] = (state * gelu).astype(BF16)

        loop(self.lru // LANE, block)
        self.save(N.state)
        self.save(N.carry)
        self.save(N.ends)
        self.save(N.mixed)

        def use(j, slot):
            res = jnp.dot(self.mixed[...], mat(self.w_mx[slot]), preferred_element_type=F32)
            x = self.xs[:, :, lanes(j, 512)].astype(F32).reshape(self.flat, 512)
            self.middle[:, lanes(j, 512)] = x + res

        stream_tiles(self.model // 512, self.fetch(2, self.w_mx, self.w_sem, (0,), 512), use)
        self.norm(
            lambda i: self.middle[pl.ds(pl.multiple_of(i * 32, 32), 32), :], self.flat // 32, 1, self.normed_two
        )
        self.save(N.middle)
        self.save(N.normed_two)

    def gate_up(self, first, count):
        def use(j, slot):
            res = jnp.dot(self.normed_two[...], mat(self.w_gu[slot]), preferred_element_type=F32)
            gate, up = res[:, 0:512], res[:, 512:1024]
            at = lanes(first + j, 512)
            self.gate_pre[:, at] = gate
            self.up[:, at] = up
            self.hidden[:, at] = (smooth_gate(gate) * up).astype(BF16)

        starts = (first * 512, self.feed + first * 512)
        stream_tiles(count, self.fetch(3, self.w_gu, self.w_sem, starts, 512), use)

    def gate_saved(self):
        self.save(N.gate_pre)
        self.save(N.up)
        self.save(N.hidden)

    def finish(self):
        for cp in self.stores:
            cp.wait()
        for cp in self.end_moves:
            cp.wait_send()


KEEP = (
    N.xs, N.normed_main, N.gelu_pre, N.branch, N.conv, N.decay_pre, N.admit_pre, N.sums, N.state, N.carry,
    N.ends, N.mixed, N.middle, N.normed_two, N.gate_pre, N.up, N.hidden,
)


def forward_kernel(seq_count, starts, chunks, names, n_keep, *refs):
    refs = list(refs)
    x_ref, since, hot_m, mask_m, hot_l, mask_l = refs[:6]
    parts = refs[6:13]
    srcs = refs[13:21]
    at = 21
    small_all, vec = refs[at : at + 2]
    outs = refs[at + 2 : at + 7]
    keep = dict(zip(KEEP, refs[at + 7 : at + 7 + n_keep]))
    at += 7 + n_keep
    table = dict(zip(names, refs[at : at + len(names)]))
    p = Place(seq_count)
    table.update(
        small_all=small_all, vec=vec, since=since, hot_m=hot_m, mask_m=mask_m, hot_l=hot_l, mask_l=mask_l, keep=keep,
    )
    table[N.normed_main] = table[N.normed].at[0 : table[N.conv].shape[0]]
    f = Forward(table, p, outs)
    one = pl.ds
    copies = []
    own_sem = table[N.own_sem]
    k = 0
    for out, count in zip(outs, (2, 2, 1, 2, 1)):
        col = 0
        for _ in range(count):
            cols = srcs[k].shape[-1]
            dst = out.at[one(p.z, 1), one(p.a, 1), one(p.b, 1), one(p.c, 1), :, one(col, cols)]
            copies.append(pltpu.make_async_copy(srcs[k], dst, own_sem.at[k]))
            col += cols
            k += 1
    tok, feat = f.tok, x_ref.shape[2]
    here = one(pl.multiple_of(p.z * feat, LANE), feat)
    copies.append(pltpu.make_async_copy(x_ref.at[:, one(p.z * tok, tok), :], f.xs.at[:, :, here], own_sem.at[k]))
    pack_rows(parts, table[N.small_own])
    own_rows = table[N.small_own].reshape(1, 1, 16, LANE)
    copies.append(pltpu.make_async_copy(own_rows, small_all.at[one(p.z, 1), one(p.d, 1)], own_sem.at[k + 1]))
    for cp in copies:
        cp.start()

    def halo(z):
        return x_ref.at[:, one(pl.multiple_of(jnp.maximum(z * tok - 16, 0), 16), 16), :]

    own_halo = lambda: pltpu.make_async_copy(halo(p.z), f.halo_x.at[:, :, here], own_sem.at[k + 2])

    @pl.when(p.z > 0)
    def _():
        own_halo().start()

    @pl.when(p.z == 0)
    def _():
        f.halo_x[...] = jnp.zeros_like(f.halo_x)

    f.ends[...] = jnp.zeros_like(f.ends)
    f.sums[...] = jnp.zeros_like(f.sums)
    p.greet()
    x_moves = []

    def x_copy(o):
        to = lax.rem(p.z + o, p.nz)
        return pltpu.make_async_remote_copy(
            x_ref.at[:, one(pl.multiple_of(to * tok, 16), tok), :], f.xs.at[:, :, here], table[N.x_send].at[o - 1],
            table[N.x_recv].at[o - 1], device_id=p.at(to), device_id_type=MESH,
        )

    def h_copy(o):
        to = lax.rem(p.z + o, p.nz)
        return to > 0, pltpu.make_async_remote_copy(
            halo(to), f.halo_x.at[:, :, here], table[N.h_send].at[o - 1],
            table[N.h_recv].at[o - 1], device_id=p.at(to), device_id_type=MESH,
        )

    for o in range(1, p.nz):
        x_copy(o).start()
        cond, cp = h_copy(o)
        pl.when(cond)(cp.start)
    for cp in copies:
        cp.wait()
    s_send, s_recv = table[N.s_send], table[N.s_recv]
    s_moves = []

    def small_put(view, at, dev):
        cp = pltpu.make_async_remote_copy(view, view, s_send.at[at], s_recv.at[at], device_id=dev, device_id_type=MESH)
        cp.start()
        s_moves.append(cp)

    def small_view(d, n):
        return small_all.at[one(p.z, 1), one(d, n)]

    small_put(small_view(p.d, 1), 0, p.core)
    g = Gather(p, outs, chunks, table[N.send], table[N.recv], starts)
    last = [max(starts[i] for i in range(len(chunks)) if chunks[i][0] == w) + GATHER_PACE * (g.depth - 1) for w in range(5)]
    plan = {
        3: [f.vectors, f.norm_one],
        last[0]: [f.gelu_input],
        max(last[1], last[0] + 1): [lambda: f.gates(0, 2)],
        max(last[1], last[0] + 1) + 1: [lambda: f.gates(2, 1), f.send_ends, f.gates_saved],
        max(last[2], max(last[1], last[0] + 1) + 2): [f.mix],
    }
    plan.setdefault(last[3], []).append(lambda: f.gate_up(0, 2))
    plan.setdefault(last[3] + 1, []).append(lambda: f.gate_up(2, 2))
    plan.setdefault(max(last[3] + 2, last[4]), []).extend([lambda: f.gate_up(4, 2), f.gate_saved])
    ticks = max(g.ticks(), max(plan) + 1)
    for t in range(ticks):
        g.tick(t)
        if t == 0:
            s_moves[0].wait_recv()
            small_put(small_view(p.d - p.c, 2), 1, p.peer["b"])
        if t == 1:
            s_moves[1].wait_recv()
            small_put(small_view(4 * p.a, 4), 2, p.peer["a"])
        if t == 2:
            s_moves[2].wait_recv()
            for o in range(1, p.nz):
                small_put(small_view(0, 8), 2 + o, p.at(lax.rem(p.z + o, p.nz)))
        if t == 3:
            for cp in s_moves[3:]:
                cp.wait_recv()
            for o in range(1, p.nz):
                x_copy(o).wait_recv()
                pl.when(p.z > 0)(h_copy(o)[1].wait_recv)

            @pl.when(p.z > 0)
            def _():
                own_halo().wait()

        for action in plan.get(t, ()):
            action()
    for cp in s_moves:
        cp.wait_send()
    for o in range(1, p.nz):
        x_copy(o).wait_send()
        cond, cp = h_copy(o)
        pl.when(cond)(cp.wait_send)
    f.finish()
    g.finish()


def forward_pass(x_heads, small, since, shards, seq_count, starts):
    groups = ((0, 1), (2, 3), (4,), (5, 6), (7,))
    rows_cols = [(shards[g[0]].shape[0], sum(shards[i].shape[1] for i in g)) for g in groups]
    chunks = chunk_list(rows_cols)
    row_count, row_len, feat = x_heads.shape
    tok, model = row_len // seq_count, feat * seq_count
    flat = row_count * tok
    lru, feed = rows_cols[0][1] // 2, rows_cols[3][1] // 2
    nz = seq_count
    srcs = [s.reshape(1, 1, 1, 1, *s.shape) for s in shards]
    hbm = pl.BlockSpec(memory_space=pltpu.HBM)
    vmem = pl.BlockSpec(memory_space=pltpu.VMEM)
    keep_shapes = dict(
        xs=((row_count, tok, model), BF16),
        normed_main=((flat, model), BF16),
        gelu_pre=((flat, lru), F32),
        branch=((flat + 32, lru), BF16),
        conv=((flat, lru), BF16),
        decay_pre=((flat, lru), F32),
        admit_pre=((flat, lru), F32),
        sums=((8, lru), F32),
        state=((flat, lru), F32),
        carry=((8, lru), F32),
        ends=((nz, 16, lru), F32),
        mixed=((flat, lru), BF16),
        middle=((flat, model), F32),
        normed_two=((flat, model), BF16),
        gate_pre=((flat, feed), F32),
        up=((flat, feed), F32),
        hidden=((flat, feed), BF16),
    )
    scratch = {n: pltpu.VMEM(*s) for n, s in keep_shapes.items() if n != "normed_main"}
    dma = pltpu.SemaphoreType.DMA
    sems = Gather.sem_count(nz)
    scratch.update(
        normed=pltpu.VMEM((flat + 32, model), BF16),
        halo_x=pltpu.VMEM((row_count, 16, model), BF16),
        small_vm=pltpu.VMEM((nz, 8, 16, LANE), F32),
        small_own=pltpu.VMEM((16, LANE), F32),
        prod=pltpu.VMEM((flat, lru), F32),
        tile=pltpu.VMEM((flat, 1024), F32),
        w_gi=pltpu.VMEM((2, nz, 2, 2, 2, rows_cols[0][0], 512), BF16),
        w_da=pltpu.VMEM((2, nz, 2, 2, 2, rows_cols[1][0], 1024), BF16),
        w_mx=pltpu.VMEM((2, nz, 2, 2, 2, rows_cols[2][0], 512), BF16),
        w_gu=pltpu.VMEM((2, nz, 2, 2, 2, rows_cols[3][0], 1024), BF16),
        w_sem=dma((2, 2)),
        keep_sem=dma((len(KEEP),)),
        misc_sem=dma((1,)),
        own_sem=dma((len(srcs) + 3,)),
        x_send=dma((nz,)),
        x_recv=dma((nz,)),
        h_send=dma((nz,)),
        h_recv=dma((nz,)),
        s_send=dma((nz + 3,)),
        s_recv=dma((nz + 3,)),
        e_send=dma((nz,)),
        e_recv=dma((nz,)),
        send=dma((len(chunks), sems)),
        recv=dma((len(chunks), sems)),
    )
    names = list(scratch)
    out_shape = [jax.ShapeDtypeStruct((nz, 8, 16, LANE), F32), jax.ShapeDtypeStruct((16, lru), F32)]
    out_shape += [jax.ShapeDtypeStruct((nz, PLANE, PLANE, 2, r, c), BF16) for r, c in rows_cols]
    out_shape += [jax.ShapeDtypeStruct(*keep_shapes[n]) for n in KEEP]
    outs = pl.pallas_call(
        partial(forward_kernel, nz, starts, chunks, names, len(KEEP)),
        out_shape=out_shape,
        in_specs=[hbm] + [vmem] * 20,
        out_specs=[hbm, vmem] + [hbm] * (5 + len(KEEP)),
        scratch_shapes=[scratch[n] for n in names],
        compiler_params=pltpu.CompilerParams(
            collective_id=0, has_side_effects=True, vmem_limit_bytes=61 << 20
        ),
        name="forward_pass",
    )(
        x_heads,
        since,
        *spread_constants(model, lru, nz * 8),
        *small,
        *srcs,
    )
    return outs[1], outs[2:7], dict(zip(KEEP, outs[7:]))


PACE = 2
C_RING, RING, SLOTS, PIECE = 8 * PACE, 5 * PACE, 2 * PACE, 256


class Chunk:
    def __init__(self, name, lhs, rhs, rows, width, first):
        self.name, self.lhs, self.rhs = name, lhs, rhs
        self.rows, self.width, self.first = rows, width, first
        self.across = width // PIECE


class Reduce:
    NAMES = (N.C, N.YA, N.YB, N.YC, N.PC, N.UA, N.DA, N.UB, N.DB, N.UC, N.DC, N.XA, N.XB)
    PIECES = {"A": pl.ds(0, 2), "B": pl.ds(2, 2), "C": pl.ds(4, 2)}

    @staticmethod
    def shapes(nz):
        tail = (2, 16, PIECE)
        plane = PLANE
        a, b, c = (nz, 1, plane), (nz, plane, 1), (nz, 1, 1)
        own = (1, 1, 1)
        lead = dict(YA=a, YB=b, YC=b, PC=c, UA=a, DA=a, UB=b, DB=b, UC=c, DC=c, XA=own, XB=own)
        out = {n: (RING, *v, *tail) for n, v in lead.items()}
        out["C"] = (C_RING, nz, plane, plane, 6, 16, PIECE)
        return out

    def __init__(self, place, bufs, full, send, recv, produce, deliver):
        self.p, self.bufs, self.full = place, bufs, full
        self.send, self.recv = send, recv
        self.produce, self.deliver = produce, deliver
        self.started = {}
        self.depth = place.nz + 4

    def buf(self, k, name):
        return self.bufs[name].at[k % (C_RING if name == "C" else RING)]

    def order(self, k):
        return ("a", "b") if k % 2 else ("b", "a")

    def part(self, k, route, z, a, b):
        full = slice(None)
        one = lambda v: full if v is None else v if isinstance(v, slice) else pl.ds(v, 1)
        return self.buf(k, "C").at[one(z), one(a), one(b), self.PIECES[route]]

    def copy(self, k, name, src, dst, dev):
        at = self.NAMES.index(name)
        return pltpu.make_async_remote_copy(
            src, dst, self.send.at[k, at], self.recv.at[k, at], device_id=dev, device_id_type=MESH
        )

    def put(self, k, name, src, dst, dev):
        make = lambda: self.copy(k, name, src(), dst(), dev)
        make().start()
        self.started.setdefault(k, []).append((make, None))

    def z_put(self, k, route, way, z):
        p = self.p
        name = ("U" if way > 0 else "D") + route
        span = slice(z + 1, p.nz) if way > 0 else slice(0, z)

        def make():
            a = p.a if route != "B" else None
            b = p.b if route != "A" else None
            return self.copy(k, name, self.part(k, route, span, a, b), self.buf(k, name).at[span], p.at(z + way))

        make().start()
        self.started.setdefault(k, []).append((make, z))

    def take(self, k, name, dst):
        self.copy(k, name, dst, dst, self.p.core).wait_recv()

    def add(self, into, other):
        def one(t):
            into[t] = into[t] + other[t]

        loop(into.shape[0], one)

    def wave(self, k, route, s):
        p, nz = self.p, self.p.nz
        low, high = s - 1, nz - s

        def gather(name, span):
            got = self.buf(k, name).at[span]
            self.take(k, name, got)
            a = p.a if route != "B" else None
            b = p.b if route != "A" else None
            self.add(self.part(k, route, span, a, b), got)

        @pl.when(p.z == low)
        def _():
            if low > 0:
                gather("U" + route, slice(low, nz))
            if low < nz - 1:
                self.z_put(k, route, 1, low)

        @pl.when(p.z == high)
        def _():
            if high < nz - 1:
                gather("D" + route, slice(0, high + 1))
            if high > 0:
                self.z_put(k, route, -1, high)

    def yc(self, k):
        buf = self.buf(k, "YC")
        if self.order(k)[1] == "b":
            return buf
        nz, plane, _, n, r, w = buf.shape
        return buf.reshape(nz, 1, plane, n, r, w)

    def stage(self, k, s):
        p, nz = self.p, self.p.nz
        if s == 0:
            self.produce(k)
            slot = self.full.at[k % SLOTS]
            self.put(k, "C", lambda: slot.at[:, :, :, 1 - p.c], lambda: self.buf(k, "C"), p.core)
        if s == 1:
            self.take(k, "C", self.buf(k, "C"))
            into, own = self.buf(k, "C"), self.full.at[k % SLOTS]

            def one(t):
                for a in range(PLANE):
                    for b in range(PLANE):
                        into[t, a, b] = into[t, a, b] + own[t, a, b, p.c]

            loop(nz, one)
            self.put(k, "YA", lambda: self.part(k, "A", None, 1 - p.a, None), lambda: self.buf(k, "YA"), p.peer["a"])
            self.put(k, "YB", lambda: self.part(k, "B", None, None, 1 - p.b), lambda: self.buf(k, "YB"), p.peer["b"])
            q = self.order(k)[1]
            src = lambda: self.part(k, "C", None, 1 - p.a if q == "a" else None, 1 - p.b if q == "b" else None)
            self.put(k, "YC", src, lambda: self.yc(k), p.peer[q])
        if s == 2:
            make, _ = self.started[k].pop(0)
            make().wait_send()
            self.take(k, "YA", self.buf(k, "YA"))
            self.add(self.part(k, "A", None, p.a, None), self.buf(k, "YA"))
            self.take(k, "YB", self.buf(k, "YB"))
            self.add(self.part(k, "B", None, None, p.b), self.buf(k, "YB"))
            first, q = self.order(k)
            self.take(k, "YC", self.yc(k))
            self.add(self.part(k, "C", None, p.a if q == "a" else None, p.b if q == "b" else None), self.yc(k))
            src = lambda: self.part(
                k, "C", None, 1 - p.a if first == "a" else p.a, 1 - p.b if first == "b" else p.b
            )
            self.put(k, "PC", src, lambda: self.buf(k, "PC"), p.peer[first])
        if s == 3:
            self.take(k, "PC", self.buf(k, "PC"))
            self.add(self.part(k, "C", None, p.a, p.b), self.buf(k, "PC"))
        if 2 <= s <= nz + 1:
            self.wave(k, "A", s - 1)
            self.wave(k, "B", s - 1)
        if 3 <= s <= nz + 2:
            self.wave(k, "C", s - 2)
        if s == nz + 1:
            self.put(k, "XA", lambda: self.part(k, "A", p.z, p.a, 1 - p.b), lambda: self.buf(k, "XA"), p.peer["b"])
            self.put(k, "XB", lambda: self.part(k, "B", p.z, 1 - p.a, p.b), lambda: self.buf(k, "XB"), p.peer["a"])
        if s == nz + 2:
            self.take(k, "XA", self.buf(k, "XA"))
            self.take(k, "XB", self.buf(k, "XB"))
            self.deliver(k)
        if s == nz + 3:
            for make, z in self.started.pop(k):
                if z is None:
                    make().wait_send()
                else:

                    @pl.when(p.z == z)
                    def _():
                        make().wait_send()

    def result(self, k, route):
        p = self.p
        block = self.part(k, route, p.z, p.a, p.b)[0, 0, 0].astype(F32)
        if route != "C":
            block = block + self.buf(k, "X" + route)[0, 0, 0].astype(F32)
        return block

    def tick(self, t, count):
        for k in range(count):
            if 0 <= t - k < PACE * self.depth and (t - k) % PACE == 0:
                self.stage(k, (t - k) // PACE)

    def ticks(self, count):
        return count + PACE * (self.depth - 1)


class Backward:
    def __init__(self, refs, place):
        self.__dict__.update(refs)
        self.p = place
        self.flat, self.model = self.cot.shape
        self.lru, self.feed = self.q.shape[1], self.hidden.shape[1]
        self.rows = 2
        self.tok = self.flat // self.rows
        self.outs_going = {}
        c = Chunk
        wide, tall, full = 3 * PIECE, 2 * PIECE, PIECE
        self.chunks = [c(N.dn, N.hidden, N.cot, 96, full, j) for j in range(0, self.model, full)]
        self.chunks += [c(N.gu, N.normed_two, N.ggu, 32, wide, j) for j in range(0, 2 * self.feed, wide)]
        self.chunks += [c(N.mx, N.mixed, N.grad_out, 48, tall, j) for j in range(0, self.model, tall)]
        self.chunks += [c(N.gi, N.normed, N.ggi, 32, wide, j) for j in range(0, self.lru, wide)]
        self.chunks += [c(N.da, N.conv, N.hidden, 48, tall, j) for j in range(0, 2 * self.lru, tall)]
        self.chunks += [c(N.gi, N.normed, N.ggi, 32, wide, j) for j in range(self.lru, 2 * self.lru, wide)]

    def first_of(self, name, at=0):
        return min(k for k, ch in enumerate(self.chunks) if ch.name == name and ch.first >= at)

    def load(self, names):
        for name in names:
            self.loader(name).start()

    def loader(self, name):
        src, dst, at = self.loads[name]
        return pltpu.make_async_copy(src, dst, self.load_sem.at[at])

    def ready(self, names):
        for name in names:
            self.loader(name).wait()

    def produce(self, k):
        ch = self.chunks[k]
        lhs, rhs = getattr(self, ch.lhs), getattr(self, ch.rhs)
        span = 8 * ch.rows
        slot = self.full.at[k % SLOTS]

        def one(z):
            left = lhs[:, pl.ds(pl.multiple_of(z * span, LANE), span)]
            for n in range(ch.across):
                right = rhs[:, ch.first + n * PIECE : ch.first + (n + 1) * PIECE]
                val = outer_sum(left, right).astype(BF16).reshape(8, ch.rows // 16, 16, PIECE)
                for i in range(ch.rows // 16):
                    slot[z, :, :, :, i * ch.across + n] = val[:, i].reshape(2, 2, 2, 16, PIECE)

        loop(self.p.nz, one)

    def out_copies(self, k):
        ch = self.chunks[k]
        copies = []
        for i in range(ch.rows // 16):
            for n in range(ch.across):
                at = i * ch.across + n
                col = ch.first + n * PIECE
                names = self.out_names[ch.name]
                width = self.weight_outs[names[0]].shape[1]
                out = self.weight_outs[names[col // width]]
                dst = out.at[pl.ds(i * 16, 16), pl.ds(col % width, PIECE)]
                copies.append(pltpu.make_async_copy(self.staged.at[k % 2, at], dst, self.out_sem.at[k % 2, at]))
        return copies

    def deliver(self, k):
        if k >= 2:
            for cp in self.out_copies(k - 2):
                cp.wait()
        for route, at in (("A", 0), ("B", 2), ("C", 4)):
            self.staged[k % 2, at : at + 2] = self.reduce.result(k, route)
        for cp in self.out_copies(k):
            cp.start()

    def by_z(self, weight, buf, sem, extra=None, parts=1):
        width = weight.shape[-1] // parts

        def copies(j, slot):
            z = j // parts
            rows = weight.shape[4]
            src = weight.at[z, :, :, :, :, pl.ds(pl.multiple_of(lax.rem(j, parts) * width, LANE), width)]
            dst = buf.at[slot, :, :, :, 0:rows, 0:width]
            out = [pltpu.make_async_copy(src, dst, sem.at[slot, 0])]
            return out + (extra(j, slot) if extra else [])

        return copies

    def feed_back(self):
        span = self.feed // self.p.nz
        half = lambda slot: pl.ds(pl.multiple_of(slot * span, LANE), span)

        def extra(j, slot):
            at = pl.ds(pl.multiple_of(j * span, LANE), span)
            return [
                pltpu.make_async_copy(self.gate_pre.at[:, at], self.gelu_pre.at[:, half(slot)], self.w_sem.at[slot, 1]),
                pltpu.make_async_copy(self.up.at[:, at], self.state.at[:, half(slot)], self.w_sem.at[slot, 2]),
            ]

        def use(j, slot):
            self.wide_tile[...] = back_prod(self.cot[...], mat(self.w_dn[slot]))
            out = self.q.at[:, 0 : self.model]
            start = jnp.where(j == 0, self.middle[...], out[...])
            left = self.hidden[:, pl.ds(pl.multiple_of(j * span, LANE), span)]
            out[...] = start + jnp.dot(left, mat(self.w_dn[slot]), preferred_element_type=F32)
            at = pl.ds(pl.multiple_of(j * span, LANE), span)
            at_up = pl.ds(pl.multiple_of(self.feed + j * span, LANE), span)

            def block(i):
                rows = pl.ds(pl.multiple_of(i * 16, 16), 16)
                grad = self.wide_tile[rows, :]
                gate = self.gelu_pre[rows, half(slot)]
                act, slope = gelu_both(gate)
                self.ggu[rows, at] = (slope * self.state[rows, half(slot)] * grad).astype(BF16)
                self.ggu[rows, at_up] = (act * grad).astype(BF16)

            loop(self.flat // 16, block)

        self.ready([N.middle])
        stream_tiles(self.p.nz, self.by_z(self.dn, self.w_dn, self.w_sem, extra), use)
        self.grad_out[...] = self.q[:, 0 : self.model].astype(BF16)
        self.block_copy().start()

    def block_copy(self):
        return pltpu.make_async_copy(self.grad_out, self.block_out, self.block_sem.at[0])

    def norm_back(self, values, grads, gain_row, extra, out):
        gain = self.vec[gain_row : gain_row + 1, 0 : self.model]

        def block(i, total):
            rows = pl.ds(pl.multiple_of(i * 16, 16), 16)
            v, e = values(rows), grads(rows)
            back, terms = rms_back(v, gain, e)
            out(rows, extra(rows) + back)
            return total + jnp.sum(terms, axis=0, keepdims=True)

        total = lax.fori_loop(0, self.flat // 16, block, jnp.zeros((1, self.model), F32))
        self.sums[gain_row : gain_row + 1, 0 : self.model] = total

    def norm_two_back(self):
        half = self.feed

        def use(j, slot):
            left = self.ggu[:, pl.ds(pl.multiple_of(lax.rem(j, 2) * half, LANE), half)]
            rows = self.gu.shape[4]
            res = back_prod(left, mat(self.w_big[slot, :, :, :, 0:rows, 0:half]))
            at = lanes(j // 2, 8 * rows)

            @pl.when(lax.rem(j, 2) == 0)
            def _():
                self.q[:, at] = res

            @pl.when(lax.rem(j, 2) == 1)
            def _():
                self.q[:, at] = self.q[:, at] + res

        stream_tiles(2 * self.p.nz, self.by_z(self.gu, self.w_big, self.w_sem, None, 2), use)
        self.block_copy().wait()

        def out(rows, val):
            self.middle[rows, :] = val
            self.grad_out[rows, :] = val.astype(BF16)

        self.norm_back(
            lambda rows: self.middle[rows, :],
            lambda rows: self.q[rows, 0 : self.model],
            1,
            lambda rows: self.cot[rows, :].astype(F32),
            out,
        )

    def scan_back(self):
        self.ready([N.gelu_pre, N.state, N.decay_pre])
        rows = self.mx.shape[4]
        span = 8 * rows

        def use(j, slot):
            self.wide_tile[:, 0:span] = back_prod(self.grad_out[...], mat(self.w_big[slot, :, :, :, 0:rows, 0 : self.model]))

            def block(i):
                c = j * (span // LANE) + i
                for r in range(self.rows):
                    at = slice(r * self.tok, (r + 1) * self.tok)
                    grad = self.wide_tile[at, lanes(i)]
                    act, slope = gelu_both(self.gelu_pre[at, lanes(c)])
                    self.ggi[at, lanes(c)] = (slope * grad * self.state[at, lanes(c)]).astype(BF16)
                    _, decay, _ = decay_terms(self.decay_pre[at, lanes(c)], self.vec[4:5, lanes(c)])
                    since = self.since[r * (self.tok + 16) : r * (self.tok + 16) + self.tok, :]
                    eff = decay * (since != 0).astype(F32)
                    place = lax.broadcasted_iota(jnp.int32, eff.shape, 0)
                    after = jnp.where(place < self.tok - 1, pltpu.roll(eff, self.tok - 1, 0), 1.0)
                    prod, tail = scan_block(after, act * grad, reverse=True)
                    self.q[at, lanes(c)] = prod
                    self.gelu_pre[at, lanes(c)] = tail
                    self.tails[self.p.z, r : r + 1, lanes(c)] = eff[0:1, :] * tail[0:1, :]

            loop(span // LANE, block)

        stream_tiles(self.p.nz, self.by_z(self.mx, self.w_big, self.w_sem), use)

    def tail_copy(self, o, recv):
        p = self.p
        view = self.tails.at[lax.rem(p.z + p.nz - o, p.nz) if recv else p.z]
        return pltpu.make_async_remote_copy(
            view, view, self.t_send.at[o - 1], self.t_recv.at[o - 1],
            device_id=p.at(lax.rem(p.z + o, p.nz)), device_id_type=MESH,
        )

    def send_tails(self):
        for o in range(1, self.p.nz):
            self.tail_copy(o, False).start()

    def gates_back(self):
        p = self.p
        for o in range(1, p.nz):
            self.tail_copy(o, True).wait_recv()
        self.ready([N.admit_pre, N.conv])

        def block(c):
            tail = jnp.zeros((8, LANE), F32)
            into = tail
            for i in range(p.nz - 1, 0, -1):
                tail = self.ends[i, 0:8, lanes(c)] * tail + self.tails[i, :, lanes(c)]
                into = jnp.where(p.z == i - 1, tail, into)
            scale = self.vec[4:5, lanes(c)]
            rate_sum = jnp.zeros((1, LANE), F32)
            decay_sum, admit_sum = rate_sum, rate_sum
            for r in range(self.rows):
                at = slice(r * self.tok, (r + 1) * self.tok)
                adjoint = self.gelu_pre[at, lanes(c)] + self.q[at, lanes(c)] * into[r : r + 1, :]
                recall, decay, lost = decay_terms(self.decay_pre[at, lanes(c)], scale)
                root = jnp.sqrt(lost)
                since = self.since[r * (self.tok + 16) : r * (self.tok + 16) + self.tok, :]
                reset = (since == 0).astype(F32)
                keep = 1.0 - reset
                conv = self.conv[at, lanes(c)].astype(F32)
                admit = jax.nn.sigmoid(self.admit_pre[at, lanes(c)])
                state = self.state[at, lanes(c)]
                place = lax.broadcasted_iota(jnp.int32, state.shape, 0)
                before = jnp.where(place > 0, pltpu.roll(state, 1, 0), self.carry[r : r + 1, lanes(c)])
                scale_in = reset + keep * root
                grad_log = adjoint * keep * (before * decay - admit * conv * decay * decay / root)
                decay_low = (grad_log * scale * recall * (1.0 - recall)).astype(BF16)
                admit_low = (adjoint * scale_in * conv * admit * (1.0 - admit)).astype(BF16)
                self.hidden[at, lanes(c)] = decay_low
                self.hidden[at, pl.ds(pl.multiple_of(self.lru + c * LANE, LANE), LANE)] = admit_low
                self.admit_pre[at, lanes(c)] = adjoint * scale_in * admit
                rate_sum = rate_sum + jnp.sum(grad_log * recall, axis=0, keepdims=True)
                decay_sum = decay_sum + jnp.sum(decay_low.astype(F32), axis=0, keepdims=True)
                admit_sum = admit_sum + jnp.sum(admit_low.astype(F32), axis=0, keepdims=True)
            self.sums[2:3, lanes(c)] = decay_sum
            self.sums[3:4, lanes(c)] = admit_sum
            self.sums[4:5, lanes(c)] = rate_sum * (DECAY_SCALE * jax.nn.sigmoid(-self.vec[7:8, lanes(c)]))

        loop(self.lru // LANE, block)

    def conv_grads(self):
        rows = self.da.shape[4]
        span = 8 * rows

        def use(j, slot):
            at = lanes(j, span)
            res = back_prod(self.hidden[...], mat(self.w_big[slot]))
            total = (self.admit_pre[:, at] + res).astype(BF16)
            self.grad_conv[:, :, at] = total.reshape(self.rows, self.tok, span)

        stream_tiles(self.p.nz, self.by_z(self.da, self.w_big, self.w_sem), use)

    def rim_copy(self):
        p = self.p
        return pltpu.make_async_remote_copy(
            self.grad_conv.at[:, 0:16, :], self.rim, self.r_send.at[0], self.r_recv.at[0],
            device_id=p.at(jnp.maximum(p.z - 1, 0)), device_id_type=MESH,
        )

    def send_rim(self):
        pl.when(self.p.z > 0)(lambda: self.rim_copy().start())

    def conv_back(self):
        p = self.p
        pl.when(p.z < p.nz - 1)(lambda: self.rim_copy().wait_recv())
        self.ready([N.branch])
        long = self.tok + 16

        def block(c):
            taps = [jnp.zeros((1, LANE), F32)] * 4
            for r in range(self.rows):
                at = slice(r * self.tok, (r + 1) * self.tok)
                since = self.since[r * long : (r + 1) * long, :]
                grad = self.grad_conv[r, :, lanes(c)].astype(F32)
                wide = jnp.concatenate([grad, self.rim[r, :, lanes(c)].astype(F32)], axis=0)
                head = self.branch[self.flat + 16 * r : self.flat + 16 * (r + 1), lanes(c)].astype(F32)
                back = jnp.concatenate([head, self.branch[at, lanes(c)].astype(F32)], axis=0)
                total = jnp.zeros((self.tok, LANE), F32)
                for k in range(4):
                    seen = (since >= k).astype(F32)
                    moved = back if k == 0 else pltpu.roll(back, k, 0)
                    term = jnp.sum(grad * moved[16:] * seen[0 : self.tok], axis=0, keepdims=True)
                    taps[k] = taps[k] + term
                    ahead = wide * seen
                    ahead = ahead if k == 0 else pltpu.roll(ahead, long - k, 0)
                    total = total + self.vec[8 + k : 9 + k, lanes(c)] * ahead[0 : self.tok]
                self.ggi[at, pl.ds(pl.multiple_of(self.lru + c * LANE, LANE), LANE)] = total.astype(BF16)
            for k in range(4):
                self.sums[5 + k : 6 + k, lanes(c)] = taps[k]

        loop(self.lru // LANE, block)

    def norm_one_back(self):
        rows = self.gi.shape[4]

        def use(j, slot):
            self.q[:, lanes(j, 8 * rows)] = back_prod(self.ggi[...], mat(self.w_big[slot, :, :, :, 0:rows, :]))

        stream_tiles(self.p.nz, self.by_z(self.gi, self.w_big, self.w_sem), use)
        self.ready([N.xs])

        def out(rows, val):
            self.grad_out[rows, :] = val.astype(BF16)

        self.norm_back(
            lambda rows: self.cot[rows, :].astype(F32),
            lambda rows: self.q[rows, 0 : self.model],
            0,
            lambda rows: self.middle[rows, :],
            out,
        )

    def x_copy(self, o):
        p = self.p
        feat = self.x_out.shape[2]
        to = lax.rem(p.z + o, p.nz)
        at = pl.ds(pl.multiple_of(to * feat, LANE), feat)
        src = self.grad_out.reshape(self.rows, self.tok, self.model).at[:, :, at]
        dst = self.x_out.at[:, pl.ds(pl.multiple_of(p.z * self.tok, 16), self.tok), :]
        if o == 0:
            return pltpu.make_async_copy(src, dst, self.x_send.at[p.nz - 1])
        return pltpu.make_async_remote_copy(
            src, dst, self.x_send.at[o - 1], self.x_recv.at[o - 1], device_id=p.at(to), device_id_type=MESH
        )

    def send_x(self):
        for o in range(self.p.nz):
            self.x_copy(o).start()

    def spread_sums(self):
        nz = self.p.nz
        for row in range(10):
            hot, mask, width = (self.hot_m, self.mask_m, self.model) if row < 2 else (self.hot_l, self.mask_l, self.lru)
            vals = self.sums[row : row + 1, 0:width] if row < 9 else self.gate_sums[0:1, :]
            wide = mask[...] * vals
            cut = lax.dot_general(
                wide, hot[...].astype(F32), (((1,), (1,)), ((), ())),
                precision=lax.Precision.HIGHEST, preferred_element_type=F32,
            )
            self.s_own[:, :, :, :, row, :] = cut.reshape(nz, 2, 2, 2, LANE)

    def s_copy(self, at):
        p = self.p
        if at == 0:
            src, dst, dev = self.s_own.at[:, :, :, 1 - p.c], self.s_core, p.core
        elif at == 1:
            src, dst, dev = self.s_core.at[:, :, 1 - p.b], self.s_b, p.peer["b"]
        elif at == 2:
            src, dst, dev = self.s_b.at[:, 1 - p.a], self.s_a, p.peer["a"]
        else:
            to = lax.rem(p.z + at - 2, p.nz)
            src, dst, dev = self.s_a.at[to], self.s_z.at[at - 3], p.at(to)
        return pltpu.make_async_remote_copy(
            src, dst, self.s_send.at[at], self.s_recv.at[at], device_id=dev, device_id_type=MESH
        )

    def small_step(self, n):
        p = self.p
        if n == 0:
            self.s_own[...] = jnp.zeros_like(self.s_own)
            self.spread_sums()
            self.s_copy(0).start()
        if n == 1:
            self.s_copy(0).wait_recv()
            self.s_core[...] = self.s_core[...] + self.s_own[:, :, :, p.c]
            self.s_copy(1).start()
        if n == 2:
            self.s_copy(1).wait_recv()
            self.s_b[...] = self.s_b[...] + self.s_core[:, :, p.b]
            self.s_copy(2).start()
        if n == 3:
            self.s_copy(2).wait_recv()
            self.s_a[...] = self.s_a[...] + self.s_b[:, p.a]
            for o in range(1, p.nz):
                self.s_copy(2 + o).start()
        if n == 4:
            total = self.s_a[p.z]
            for o in range(1, p.nz):
                self.s_copy(2 + o).wait_recv()
                total = total + self.s_z[o - 1]
            self.small_out[...] = total

    def finish(self):
        p = self.p
        count = len(self.chunks)
        for k in (count - 2, count - 1):
            for cp in self.out_copies(k):
                cp.wait()
        for o in range(1, p.nz):
            self.tail_copy(o, False).wait_send()
            self.x_copy(o).wait()
            self.s_copy(2 + o).wait_send()
        self.x_copy(0).wait()
        for at in range(3):
            self.s_copy(at).wait_send()
        pl.when(p.z > 0)(lambda: self.rim_copy().wait_send())


def gelu_both(x):
    inner = GELU_C * (x + 0.044715 * x * x * x)
    t = jnp.tanh(inner)
    slope = 0.5 * (1.0 + t) + 0.5 * x * (1.0 - t * t) * GELU_C * (1.0 + 3 * 0.044715 * x * x)
    return 0.5 * x * (1.0 + t), slope


def rms_back(values, gain, grad):
    q = lax.rsqrt(jnp.mean(values * values, axis=-1, keepdims=True) + EPSILON)
    inner = jnp.mean(values * gain * grad, axis=-1, keepdims=True)
    back = q * gain * grad - values * (q * q * q) * inner
    return back, grad * values * q


WEIGHTS = (N.gelu, N.input, N.decay, N.admit, N.mixer, N.gate, N.up, N.down)
OUT_NAMES = dict(gi=WEIGHTS[:2], da=WEIGHTS[2:4], mx=WEIGHTS[4:5], gu=WEIGHTS[5:7], dn=WEIGHTS[7:])
LOADS = (
    N.hidden, N.cot, N.normed_two, N.middle, N.mixed, N.gelu_pre, N.state, N.decay_pre, N.admit_pre, N.conv,
    N.branch, N.normed, N.xs,
)


def backward_kernel(seq_count, names, hbm_names, vmem_names, *refs):
    n_in = len(vmem_names) + len(hbm_names)
    given = dict(zip(vmem_names + hbm_names, refs[:n_in]))
    x_out, small_out, block_out = refs[n_in : n_in + 3]
    weight_outs = dict(zip(WEIGHTS, refs[n_in + 3 : n_in + 11]))
    table = dict(zip(names, refs[n_in + 11 :]))
    p = Place(seq_count)
    shared = dict(xs=N.cot, normed=N.normed_two)
    loads = {}
    for i, name in enumerate(LOADS):
        dst = table[shared.get(name, name)]
        loads[name] = (given.pop(name + "_hbm"), dst, i)
    table.update(given)
    table[N.normed] = table[N.normed_two]
    table[N.grad_conv] = table[N.mixed].reshape(2, table[N.mixed].shape[0] // 2, table[N.mixed].shape[1])
    table.update(x_out=x_out, small_out=small_out, block_out=block_out, weight_outs=weight_outs, out_names=OUT_NAMES, loads=loads)
    f = Backward(table, p)
    late = (N.xs, N.normed, N.gelu_pre, N.state)
    f.load(n for n in LOADS if n not in late)
    f.rim[...] = jnp.zeros_like(f.rim)
    f.tails[...] = jnp.zeros_like(f.tails)
    p.greet()
    f.reduce = Reduce(
        p, {n: table["ring_" + n] for n in Reduce.NAMES}, table[N.full], table[N.send], table[N.recv],
        f.produce, f.deliver,
    )
    count = len(f.chunks)
    f.ready([N.hidden, N.cot])

    def reload_cot():
        f.load(late[:1])

    first = f.first_of
    gu_count = first(N.mx) - first(N.gu)
    last = first(N.gi, f.lru)
    before = {
        first(N.gu): [f.feed_back, lambda: f.load(late[2:]), lambda: f.ready([N.normed_two])],
        first(N.gu) + gu_count // 2: [f.norm_two_back, reload_cot],
        first(N.mx) - 1: [f.scan_back, f.send_tails],
        first(N.mx): [lambda: f.load(late[1:2]), f.gates_back, lambda: f.ready([N.mixed])],
        first(N.gi): [lambda: f.ready([N.normed])],
        first(N.da): [f.conv_grads, f.send_rim],
        first(N.da) + 2: [f.conv_back],
        last: [f.norm_one_back, f.send_x, lambda: f.small_step(0)],
    }
    for n in range(1, 5):
        before[last + n] = [partial(f.small_step, n)]
    for t in range(f.reduce.ticks(count)):
        for action in before.get(t, ()):
            action()
        f.reduce.tick(t, count)
    f.finish()


def backward_pass(cot, since, vec, full, kept, shard_shapes, seq_count):
    nz = seq_count
    flat, model = cot.shape
    lru, feed = kept[N.gelu_pre].shape[1], kept[N.hidden].shape[1]
    tok = flat // 2
    vmem_vals = dict(
        vec=vec,
        since=since,
        carry=kept[N.carry],
        ends=kept[N.ends],
        gate_sums=kept[N.sums],
    )
    vmem_vals.update(zip((N.hot_m, N.mask_m, N.hot_l, N.mask_l), spread_constants(model, lru, nz * 8)))
    hbm_vals = dict(zip((N.gi, N.da, N.mx, N.gu, N.dn), full))
    hbm_vals.update(gate_pre=kept[N.gate_pre], up=kept[N.up])
    source = dict(kept, cot=cot, normed=kept[N.normed_main], xs=kept[N.xs].reshape(flat, model))
    hbm_vals.update({n + "_hbm": source[n] for n in LOADS})
    dma = pltpu.SemaphoreType.DMA
    v = pltpu.VMEM
    chunks = 12 * 512 // PIECE
    scratch = dict(
        hidden=v((flat, feed), BF16),
        cot=v((flat, model), BF16),
        normed_two=v((flat, model), BF16),
        middle=v((flat, model), F32),
        mixed=v((flat, lru), BF16),
        gelu_pre=v((flat, lru), F32),
        state=v((flat, lru), F32),
        decay_pre=v((flat, lru), F32),
        admit_pre=v((flat, lru), F32),
        conv=v((flat, lru), BF16),
        branch=v((flat + 32, lru), BF16),
        ggu=v((flat, 2 * feed), BF16),
        ggi=v((flat, 2 * lru), BF16),
        grad_out=v((flat, model), BF16),
        rim=v((2, 16, lru), BF16),
        q=v((flat, lru), F32),
        tails=v((nz, 8, lru), F32),
        sums=v((16, lru), F32),
        wide_tile=v((flat, feed // nz), F32),
        w_dn=v((2, 2, 2, 2, full[4].shape[4], model), BF16),
        w_big=v((2, 2, 2, 2, full[1].shape[4], 2 * lru), BF16),
        full=v((SLOTS, nz, 2, 2, 2, 6, 16, PIECE), BF16),
        staged=v((2, 6, 16, PIECE), F32),
        s_own=v((nz, 2, 2, 2, 16, LANE), F32),
        s_core=v((nz, 2, 2, 16, LANE), F32),
        s_b=v((nz, 2, 16, LANE), F32),
        s_a=v((nz, 16, LANE), F32),
        s_z=v((nz, 16, LANE), F32),
        w_sem=dma((2, 3)),
        block_sem=dma((1,)),
        load_sem=dma((len(LOADS),)),
        out_sem=dma((2, 6)),
        send=dma((chunks, len(Reduce.NAMES))),
        recv=dma((chunks, len(Reduce.NAMES))),
        t_send=dma((nz,)),
        t_recv=dma((nz,)),
        r_send=dma((1,)),
        r_recv=dma((1,)),
        x_send=dma((nz,)),
        x_recv=dma((nz,)),
        s_send=dma((nz + 3,)),
        s_recv=dma((nz + 3,)),
    )
    scratch.update({"ring_" + n: v(s, BF16) for n, s in Reduce.shapes(nz).items()})
    names = list(scratch)
    hbm = pl.BlockSpec(memory_space=pltpu.HBM)
    vmem = pl.BlockSpec(memory_space=pltpu.VMEM)
    out_shape = [
        jax.ShapeDtypeStruct((2, tok * nz, model // nz), BF16),
        jax.ShapeDtypeStruct((16, LANE), F32),
        jax.ShapeDtypeStruct((flat, model), BF16),
    ] + [jax.ShapeDtypeStruct(s, F32) for s in shard_shapes]
    outs = pl.pallas_call(
        partial(backward_kernel, nz, names, list(hbm_vals), list(vmem_vals)),
        out_shape=out_shape,
        in_specs=[vmem] * len(vmem_vals) + [hbm] * len(hbm_vals),
        out_specs=[hbm, vmem] + [hbm] * 9,
        scratch_shapes=[scratch[n] for n in names],
        compiler_params=pltpu.CompilerParams(
            collective_id=1, has_side_effects=True, vmem_limit_bytes=61 << 20
        ),
        name="backward_pass",
    )(*vmem_vals.values(), *hbm_vals.values())
    return outs[0], outs[1], outs[2], outs[3:]


def hand_over_kernel(count, rows, *refs):
    srcs, own = refs[:count], refs[count]
    outs, small = refs[count + 1 : 2 * count + 1], refs[2 * count + 1 : 2 * count + 1 + len(rows)]
    bufs, sems = refs[2 * count + 1 + len(rows) : -1], refs[-1]
    loads = [pltpu.make_async_copy(s, b, sems.at[0, i]) for i, (s, b) in enumerate(zip(srcs, bufs))]
    stores = [pltpu.make_async_copy(b, o, sems.at[1, i]) for i, (b, o) in enumerate(zip(bufs, outs))]
    for cp in loads:
        cp.start()
    for out, (row, width) in zip(small, rows):
        out[...] = own[row : row + 1, 0:width]
    for load, store in zip(loads, stores):
        load.wait()
        store.start()
    for cp in stores:
        cp.wait()


def hand_over(arrays, own, rows):
    hbm = pl.BlockSpec(memory_space=pltpu.HBM)
    vmem = pl.BlockSpec(memory_space=pltpu.VMEM)
    outs = pl.pallas_call(
        partial(hand_over_kernel, len(arrays), rows),
        out_shape=[jax.ShapeDtypeStruct(a.shape, a.dtype) for a in arrays]
        + [jax.ShapeDtypeStruct((1, w), F32) for _, w in rows],
        in_specs=[hbm] * len(arrays) + [vmem],
        out_specs=[hbm] * len(arrays) + [vmem] * len(rows),
        scratch_shapes=[pltpu.VMEM(a.shape, a.dtype) for a in arrays] + [pltpu.SemaphoreType.DMA((2, len(arrays)))],
        compiler_params=pltpu.CompilerParams(vmem_limit_bytes=60 << 20),
        name="hand_over",
    )(*arrays, own)
    return outs[: len(arrays)], outs[len(arrays) :]


def local_fast(x_heads, cotangent, doc_starts, smalls, shards):
    norm_gain, conv_weight, decay_bias, admit_bias, decay_rate, feed_gain = smalls
    seq_count = lax.axis_size("seq")
    dev_count = seq_count * lax.axis_size("dp")
    row_count, tok_count, model = cotangent.shape
    flat = row_count * tok_count
    lru, taps = shards[0].shape[1], conv_weight.shape[1]
    positions = lax.axis_index("seq") * tok_count + jnp.arange(tok_count + 16, dtype=jnp.int32)
    since_ext = since_start(doc_starts, positions)
    since = jnp.broadcast_to(since_ext.reshape(-1, 1), (since_ext.size, LANE))
    small = small_parts(norm_gain, conv_weight, decay_bias, admit_bias, decay_rate, feed_gain)
    vec, full, kept = forward_pass(x_heads, small, since, shards, seq_count, STARTS)
    input_grad, own, block, grads = backward_pass(
        cotangent.reshape(flat, model), since, vec, full, kept, [s.shape for s in shards], seq_count
    )
    per_model, per_lru = model // dev_count, lru // dev_count
    rows = ((0, per_model), (2, per_lru), (3, per_lru), (4, per_lru), (1, per_model), (9, per_lru))
    block = block.reshape(row_count, tok_count, model)
    big, small = hand_over([block, input_grad, *grads], own, rows)
    small = [v.reshape(-1) for v in small]
    return (
        big[0],
        big[1],
        small[0],
        big[2],
        big[3],
        own[5 : 5 + taps, :per_lru].T,
        big[4],
        small[1],
        big[5],
        small[2],
        small[3],
        big[6],
        small[4],
        big[7],
        big[8],
        big[9],
        small[5] * (1.0 / float(flat * dev_count)),
    )


def local(
    x_heads,
    cotangent,
    doc_starts,
    norm_gain,
    gelu_weight,
    input_weight,
    conv_weight,
    decay_weight,
    decay_bias,
    admit_weight,
    admit_bias,
    decay_rate,
    mixer_output,
    feed_gain,
    feed_gate,
    feed_up,
    feed_down,
):
    seq_count = lax.axis_size("seq")
    dev_count = seq_count * lax.axis_size("dp")
    seq_at = lax.axis_index("seq")
    row_count, tok_count, model = cotangent.shape
    flat = row_count * tok_count
    lru = gelu_weight.shape[1]
    feed = feed_gate.shape[1]
    taps = conv_weight.shape[1]
    rim = taps - 1

    smalls = (norm_gain, conv_weight, decay_bias, admit_bias, decay_rate, feed_gain)
    shards = (
        gelu_weight, input_weight, decay_weight, admit_weight, mixer_output, feed_gate, feed_up, feed_down,
    )
    if fast_shapes(shards, seq_count, lax.axis_size("dp"), row_count, tok_count):
        return local_fast(x_heads, cotangent, doc_starts, smalls, shards)
    packed = lax.all_gather(pack_small(smalls), ALL, axis=0, tiled=True).astype(F32)
    parts = split_small(packed, [v.size for v in smalls])
    gain_one = parts[0].reshape(-1)
    conv_taps = parts[1].reshape(lru, taps)
    decay_shift, admit_shift, rate_vec, gain_two = [p.reshape(-1) for p in parts[2:]]

    gelu_input = gather_rows(jnp.concatenate([gelu_weight, input_weight], axis=1))
    decay_admit = gather_rows(jnp.concatenate([decay_weight, admit_weight], axis=1))
    mixer_full = gather_rows(mixer_output)
    gate_up = gather_rows(jnp.concatenate([feed_gate, feed_up], axis=1))
    down_full = gather_rows(feed_down)

    stream = lax.all_to_all(x_heads, "seq", split_axis=1, concat_axis=2, tiled=True)
    stream_in = stream.reshape(flat, model).astype(F32)
    normed_one, norm_one_pull = jax.vjp(rms_norm, stream_in, gain_one)
    normed_low = normed_one.astype(BF16)
    both = dot(normed_low, gelu_input)
    gelu_vals, gelu_pull = jax.vjp(smooth_gate, both[:, :lru])
    branch = both[:, lru:].astype(BF16).reshape(row_count, tok_count, lru)
    halo = shift_seq(branch[:, tok_count - rim :, :], 1, seq_count)
    extended = jnp.concatenate([halo, branch], axis=1).astype(F32)
    positions = seq_at * tok_count + jnp.arange(tok_count + rim, dtype=jnp.int32)
    since_ext = since_start(doc_starts, positions)
    since_here = since_ext[:, :tok_count]
    conv_vals = jnp.zeros((row_count, tok_count, lru), F32)
    for k in range(taps):
        window = extended[:, rim - k : rim - k + tok_count, :]
        conv_vals = conv_vals + conv_taps[:, k] * window * (since_here >= k)[..., None].astype(F32)
    conv_low = conv_vals.astype(BF16)
    conv_flat = conv_low.reshape(flat, lru)
    gates = dot(conv_flat, decay_admit)
    decay_pre = (gates[:, :lru] + decay_shift).reshape(row_count, tok_count, lru)
    admit_pre = (gates[:, lru:] + admit_shift).reshape(row_count, tok_count, lru)
    reset_mask = (since_here == 0).astype(F32)[..., None]

    def coefs(dp, ap, cv, rv):
        return coefficients(dp, ap, cv, rv, reset_mask)

    (decay_eff, update, decay_vals), coef_pull = jax.vjp(
        coefs, decay_pre, admit_pre, conv_low.astype(F32), rate_vec
    )
    decay_prod, local_state = lax.associative_scan(compose, (decay_eff, update), axis=1)
    ends = jnp.stack([decay_prod[:, -1], local_state[:, -1]])
    all_ends = lax.all_gather(ends, "seq", axis=0)
    carry = jnp.zeros((row_count, lru), F32)
    carry_in = carry
    for i in range(seq_count - 1):
        carry = all_ends[i, 0] * carry + all_ends[i, 1]
        carry_in = jnp.where(seq_at == i + 1, carry, carry_in)
    state = local_state + decay_prod * carry_in[:, None, :]
    state_flat = state.reshape(flat, lru)
    mixed_low = (state_flat * gelu_vals).astype(BF16)
    middle = stream_in + dot(mixed_low, mixer_full)
    normed_two, norm_two_pull = jax.vjp(rms_norm, middle, gain_two)
    normed_two_low = normed_two.astype(BF16)
    gate_up_pre = dot(normed_two_low, gate_up)
    gate_act, gate_pull = jax.vjp(smooth_gate, gate_up_pre[:, :feed])
    up_vals = gate_up_pre[:, feed:]
    hidden_low = (gate_act * up_vals).astype(BF16)
    block_output = (middle + dot(hidden_low, down_full)).astype(BF16)
    block_output = block_output.reshape(row_count, tok_count, model)

    cot = cotangent.reshape(flat, model)
    down_grad = scatter_rows(outer_sum(hidden_low, cot))
    grad_hidden = back_prod(cot, down_full)
    grad_gate = gate_pull(grad_hidden * up_vals)[0].astype(BF16)
    grad_up = (grad_hidden * gate_act).astype(BF16)
    grad_gu = jnp.concatenate([grad_gate, grad_up], axis=1)
    gate_up_grad = scatter_rows(outer_sum(normed_two_low, grad_gu))
    grad_mid_norm, gain_two_grad = norm_two_pull(back_prod(grad_gu, gate_up))
    grad_middle = cot.astype(F32) + grad_mid_norm
    grad_out = grad_middle.astype(BF16)
    mixer_grad = scatter_rows(outer_sum(mixed_low, grad_out))
    grad_mixed = back_prod(grad_out, mixer_full)
    grad_gelu = gelu_pull(grad_mixed * state_flat)[0].astype(BF16)
    direct = (grad_mixed * gelu_vals).reshape(row_count, tok_count, lru)
    decay_next = jnp.concatenate([decay_eff[:, 1:, :], jnp.ones_like(decay_eff[:, :1, :])], axis=1)
    tail_prod, tail_state = lax.associative_scan(
        compose, (decay_next, direct), axis=1, reverse=True
    )
    back_ends = lax.all_gather(decay_eff[:, 0] * tail_state[:, 0], "seq", axis=0)
    back = jnp.zeros((row_count, lru), F32)
    back_in = back
    for i in range(seq_count - 1, 0, -1):
        back = all_ends[i, 0] * back + back_ends[i]
        back_in = jnp.where(seq_at == i - 1, back, back_in)
    adjoint = tail_state + tail_prod * back_in[:, None, :]
    state_prev = jnp.concatenate([carry_in[:, None, :], state[:, :-1, :]], axis=1)
    decay_pre_grad, admit_pre_grad, conv_direct, rate_grad = coef_pull(
        (adjoint * state_prev, adjoint, jnp.zeros_like(decay_vals))
    )
    grad_decay = decay_pre_grad.reshape(flat, lru).astype(BF16)
    grad_admit = admit_pre_grad.reshape(flat, lru).astype(BF16)
    grad_da = jnp.concatenate([grad_decay, grad_admit], axis=1)
    decay_admit_grad = scatter_rows(outer_sum(conv_flat, grad_da))
    decay_b_grad = jnp.sum(grad_decay, axis=0, dtype=F32)
    admit_b_grad = jnp.sum(grad_admit, axis=0, dtype=F32)
    grad_conv = (conv_direct.reshape(flat, lru) + back_prod(grad_da, decay_admit)).astype(BF16)
    grad_conv = grad_conv.reshape(row_count, tok_count, lru)
    grad_conv_wide = grad_conv.astype(F32)
    tap_grads = []
    for k in range(taps):
        window = extended[:, rim - k : rim - k + tok_count, :]
        mask = (since_here >= k)[..., None].astype(F32)
        tap_grads.append(jnp.sum(grad_conv_wide * window * mask, axis=(0, 1)))
    conv_grad = jnp.stack(tap_grads, axis=1)
    rim_after = shift_seq(grad_conv[:, :rim, :], -1, seq_count)
    grad_ext = jnp.concatenate([grad_conv, rim_after], axis=1).astype(F32)
    branch_grad = jnp.zeros((row_count, tok_count, lru), F32)
    for k in range(taps):
        ahead = (since_ext[:, k : k + tok_count] >= k)[..., None].astype(F32)
        branch_grad = branch_grad + conv_taps[:, k] * grad_ext[:, k : k + tok_count, :] * ahead
    branch_grad_low = branch_grad.reshape(flat, lru).astype(BF16)
    grad_gi = jnp.concatenate([grad_gelu, branch_grad_low], axis=1)
    gelu_input_grad = scatter_rows(outer_sum(normed_low, grad_gi))
    grad_in_norm, gain_one_grad = norm_one_pull(back_prod(grad_gi, gelu_input))
    input_grad_tok = (grad_middle + grad_in_norm).astype(BF16)
    input_grad_tok = input_grad_tok.reshape(row_count, tok_count, model)
    input_grad = lax.all_to_all(input_grad_tok, "seq", split_axis=2, concat_axis=1, tiled=True)
    gate_term = jnp.sum(decay_vals, axis=(0, 1)) / float(flat * dev_count)
    small_grads = (
        gain_one_grad,
        conv_grad,
        decay_b_grad,
        admit_b_grad,
        rate_grad,
        gain_two_grad,
        gate_term,
    )
    packed_grads = jnp.concatenate([g.reshape(dev_count, -1) for g in small_grads], axis=1)
    reduced = lax.psum_scatter(packed_grads, ALL, scatter_dimension=0, tiled=True)
    own = split_small(reduced, [g.size // dev_count for g in small_grads])
    return (
        block_output,
        input_grad,
        own[0].reshape(-1),
        gelu_input_grad[:, :lru],
        gelu_input_grad[:, lru:],
        own[1].reshape(-1, taps),
        decay_admit_grad[:, :lru],
        own[2].reshape(-1),
        decay_admit_grad[:, lru:],
        own[3].reshape(-1),
        own[4].reshape(-1),
        mixer_grad,
        own[5].reshape(-1),
        gate_up_grad[:, :feed],
        gate_up_grad[:, feed:],
        down_grad,
        own[6].reshape(-1),
    )


def solution(mesh):
    rows = P(ALL, None)
    vec = P(ALL)
    placed = (
        P("dp", None, "seq"),
        P("dp", "seq", None),
        P("dp", None),
        vec,
        rows,
        rows,
        rows,
        rows,
        vec,
        rows,
        vec,
        vec,
        rows,
        vec,
        rows,
        rows,
        rows,
    )
    outs = (
        P("dp", "seq", None),
        P("dp", None, "seq"),
        vec,
        rows,
        rows,
        rows,
        rows,
        vec,
        rows,
        vec,
        vec,
        rows,
        vec,
        rows,
        rows,
        rows,
        vec,
    )
    return jax.shard_map(local, mesh=mesh, in_specs=placed, out_specs=outs, check_vma=False)
```

```python
from functools import partial

import jax
import jax.numpy as jnp
import numpy as np
from jax import lax
from jax.experimental import pallas as pl
from jax.experimental.pallas import tpu as pltpu
from jax.sharding import PartitionSpec as P

EPSILON = 1e-06
DECAY_SCALE = 8.0
ALL = ("seq", "dp")
F32 = jnp.float32
BF16 = jnp.bfloat16
GELU_C = 0.7978845608028654


class Names:
    def __getattr__(self, name):
        return name


N = Names()
GATHER_PACE = 1
STARTS = (0, 0, 1, 1, 2, 3, 4, 5, 6, 7, 8, 9)


def rms_norm(values, gain_vec):
    return (
        values * lax.rsqrt(jnp.mean(values * values, axis=-1, keepdims=True) + EPSILON) * gain_vec
    )


def smooth_gate(values):
    return jax.nn.gelu(values, approximate=True)


def compose(earlier, latter):
    return (earlier[0] * latter[0], latter[0] * earlier[1] + latter[1])


def since_start(doc_starts, positions):
    begins = jnp.max(
        jnp.where(doc_starts[:, None, :] <= positions[None, :, None], doc_starts[:, None, :], 0),
        axis=-1,
    )
    return positions[None, :] - begins


def coefficients(decay_pre, admit_pre, conv_vals, rate_vec, reset_mask):
    recall = jax.nn.sigmoid(decay_pre)
    admit_vals = jax.nn.sigmoid(admit_pre)
    log_decay = -DECAY_SCALE * recall * jax.nn.softplus(-rate_vec)
    decay_vals = jnp.exp(log_decay)
    keep_mask = 1.0 - reset_mask
    scale_in = reset_mask + keep_mask * jnp.sqrt(-jnp.expm1(2.0 * log_decay))
    return (decay_vals * keep_mask, scale_in * admit_vals * conv_vals, decay_vals)


def dot(left, right):
    return jnp.dot(left, right, preferred_element_type=F32)


def outer_sum(left, right):
    return lax.dot_general(left, right, (((0,), (0,)), ((), ())), preferred_element_type=F32)


def back_prod(grad_rows, weight):
    return lax.dot_general(
        grad_rows, weight, (((1,), (1,)), ((), ())), preferred_element_type=F32
    )


def gather_rows(shard):
    return lax.all_gather(shard, ALL, axis=0, tiled=True)


def scatter_rows(partial):
    return lax.psum_scatter(partial.astype(BF16), ALL, scatter_dimension=0, tiled=True).astype(F32)


def shift_seq(values, step, seq_count):
    pairs = [(i, i + step) for i in range(seq_count) if 0 <= i + step < seq_count]
    return lax.ppermute(values, "seq", pairs)


def pack_small(pieces):
    return jnp.concatenate([p.reshape(1, -1) for p in pieces], axis=1)


def split_small(packed, widths):
    out, at = [], 0
    for width in widths:
        out.append(packed[:, at : at + width])
        at += width
    return out


MESH = pl.DeviceIdType.MESH
PLANE = 2


def fast_shapes(shards, seq_count, dp_count, row_count, tok_count):
    if dp_count != 2 * PLANE * PLANE or seq_count < 2 or row_count != 2 or tok_count != 128:
        return False
    return all(s.shape[0] in (32, 48, 96) and s.shape[1] % 512 == 0 for s in shards)


class Place:
    def __init__(self, seq_count):
        self.nz = seq_count
        self.z = lax.axis_index("seq")
        self.d = lax.axis_index("dp")
        self.c = lax.rem(self.d, 2)
        self.b = lax.rem(self.d // 2, 2)
        self.a = self.d // 4
        self.core = (self.z, self.d + 1 - 2 * self.c)
        self.peer = {
            "b": (self.z, self.d + 2 - 4 * self.b),
            "a": (self.z, self.d + 4 - 8 * self.a),
        }

    def at(self, z):
        return (z, self.d)

    def greet(self):
        barrier = pltpu.get_barrier_semaphore()
        others = [self.core, self.peer["a"], self.peer["b"]]
        others += [self.at(lax.rem(self.z + o, self.nz)) for o in range(1, self.nz)]
        for other in others:
            pl.semaphore_signal(barrier, inc=1, device_id=other, device_id_type=MESH)
        pl.semaphore_wait(barrier, len(others))


def step_cols(width):
    part = 7 * (width // LANE) // 24 * LANE
    return {"A": (0, part), "B": (part, 2 * part), "C": (2 * part, width)}


def chunk_list(shapes):
    chunks = []
    for i, (rows, cols) in enumerate(shapes):
        wide = min(cols, 3072)
        tall = rows if wide < 3072 and rows <= 48 else (48 if wide < 3072 else 16)
        for c0 in range(0, cols, wide):
            for r0 in range(0, rows, tall):
                chunks.append((i, r0, tall, c0, wide))
    return chunks


class Gather:
    def __init__(self, place, outs, chunks, send, recv, starts):
        self.p, self.outs, self.chunks = place, outs, chunks
        self.send, self.recv, self.starts = send, recv, starts
        self.started = []
        nz = place.nz
        self.depth = nz + 4

    def view(self, k, z, a, b, c, route):
        i, r0, nr, c0, nc = self.chunks[k]
        lo, hi = (0, nc) if route is None else step_cols(nc)[route]
        full = slice(None)
        one = lambda v: full if v is None else pl.ds(v, 1)
        return self.outs[i].at[
            one(z), one(a), one(b), one(c), pl.ds(r0, nr), pl.ds(c0 + lo, hi - lo)
        ]

    def copy(self, k, view, s_at, r_at, dev):
        return pltpu.make_async_remote_copy(
            view, view, self.send.at[k, s_at], self.recv.at[k, r_at], device_id=dev, device_id_type=MESH
        )

    def put(self, k, view, s_at, r_at, dev, cond=None):
        cp = self.copy(k, view, s_at, r_at, dev)
        if cond is None:
            cp.start()
        else:
            pl.when(cond)(cp.start)
        self.started.append((cp, cond))

    def take(self, k, view, r_at, cond=None):
        cp = self.copy(k, view, 0, r_at, self.p.core)
        if cond is None:
            cp.wait_recv()
        else:
            pl.when(cond)(cp.wait_recv)

    def sem(self, route, phase, z=0):
        nz = self.p.nz
        slot = {"first": 0, "up": 1, "down": 1 + nz, "mid": 1 + 2 * nz, "last": 1 + 3 * nz}[phase]
        return {"A": 0, "B": 1, "C": 2}[route] * (1 + 4 * nz) + slot + z

    @staticmethod
    def sem_count(nz):
        return 3 * (1 + 4 * nz) + 1

    def order(self, k, route):
        if route == "C":
            return ("a", "b") if k % 2 else ("b", "a")
        return ("b", "a") if route == "A" else ("a", "b")

    def z_unit(self, k, route, z):
        p = self.p
        first = self.order(k, route)[0]
        a = None if route != "C" and first == "a" else p.a
        b = None if route != "C" and first == "b" else p.b
        return self.view(k, z, a, b, p.c, route)

    def z_own(self, k, route):
        p = self.p
        unit = self.z_unit(k, route, p.z)
        self.put(k, unit, self.sem(route, "up", p.z), self.sem(route, "up", p.z), p.at(p.z + 1), p.z < p.nz - 1)
        self.put(k, unit, self.sem(route, "down", p.z), self.sem(route, "down", p.z), p.at(p.z - 1), p.z > 0)
        self.after(k, route, p.z, None)

    def after(self, k, route, z, cond):
        p = self.p
        first, second = self.order(k, route)
        dim = first if route == "C" else second
        name = "mid" if route == "C" else "last"
        self.put(k, self.z_unit(k, route, z), self.sem(route, name, z), self.sem(route, name, z), p.peer[dim], cond)

    def z_hop(self, k, route, h):
        p = self.p
        low, high = p.z - h, p.z + h
        has_low, has_high = low >= 0, high < p.nz
        low_at, high_at = jnp.maximum(low, 0), jnp.minimum(high, p.nz - 1)
        unit = self.z_unit(k, route, low_at)
        self.take(k, unit, self.sem(route, "up", low_at), has_low)
        if h < p.nz - 1:
            self.put(k, unit, self.sem(route, "up", low_at), self.sem(route, "up", low_at), p.at(p.z + 1), has_low & (p.z < p.nz - 1))
        self.after(k, route, low_at, has_low)
        unit = self.z_unit(k, route, high_at)
        self.take(k, unit, self.sem(route, "down", high_at), has_high)
        if h < p.nz - 1:
            self.put(k, unit, self.sem(route, "down", high_at), self.sem(route, "down", high_at), p.at(p.z - 1), has_high & (p.z > 0))
        self.after(k, route, high_at, has_high)

    def c_last(self, k, z, cond):
        p = self.p
        first, second = self.order(k, "C")
        a = None if first == "a" else p.a
        b = None if first == "b" else p.b
        peer_a = 1 - p.a if first == "a" else p.a
        peer_b = 1 - p.b if first == "b" else p.b
        self.take(k, self.view(k, z, peer_a, peer_b, p.c, "C"), self.sem("C", "mid", z), cond)
        self.put(k, self.view(k, z, a, b, p.c, "C"), self.sem("C", "last", z), self.sem("C", "last", z), p.peer[second], cond)

    def c_last_hop(self, k, h):
        p = self.p
        if h == 0:
            self.c_last(k, p.z, None)
            return
        low, high = p.z - h, p.z + h
        self.c_last(k, jnp.maximum(low, 0), low >= 0)
        self.c_last(k, jnp.minimum(high, p.nz - 1), high < p.nz)

    def stage(self, k, s):
        p, nz = self.p, self.p.nz
        if s == 0:
            for route in "AB":
                first = self.order(k, route)[0]
                at = self.sem(route, "first")
                self.put(k, self.view(k, p.z, p.a, p.b, p.c, route), at, at, p.peer[first])
            self.z_own(k, "C")
        if s == 1:
            for route in "AB":
                first = self.order(k, route)[0]
                a = 1 - p.a if first == "a" else p.a
                b = 1 - p.b if first == "b" else p.b
                self.take(k, self.view(k, p.z, a, b, p.c, route), self.sem(route, "first"))
                self.z_own(k, route)
        if 1 <= s < nz:
            self.z_hop(k, "C", s)
        if 2 <= s <= nz:
            self.z_hop(k, "A", s - 1)
            self.z_hop(k, "B", s - 1)
        if 2 <= s < nz + 2:
            self.c_last_hop(k, s - 2)
        if s == nz + 2:
            for z in range(nz):
                for route in "ABC":
                    second = self.order(k, route)[1]
                    a = 1 - p.a if second == "a" else None
                    b = 1 - p.b if second == "b" else None
                    self.take(k, self.view(k, z, a, b, p.c, route), self.sem(route, "last", z))
            at = self.sem_count(nz) - 1
            self.put(k, self.view(k, None, None, None, p.c, None), at, at, p.core)
        if s == nz + 3:
            at = self.sem_count(nz) - 1
            self.take(k, self.view(k, None, None, None, 1 - p.c, None), at)

    def tick(self, t):
        for k in range(len(self.chunks)):
            s = t - self.starts[k]
            if 0 <= s < GATHER_PACE * self.depth and s % GATHER_PACE == 0:
                self.stage(k, s // GATHER_PACE)

    def ticks(self):
        return max(self.starts) + GATHER_PACE * (self.depth - 1) + 1

    def finish(self):
        for cp, cond in self.started:
            if cond is None:
                cp.wait_send()
            else:
                pl.when(cond)(cp.wait_send)


LANE = 128


def spread_constants(model, lru, dev_count):
    out = []
    for width in (model, lru):
        per = width // dev_count
        lane = np.arange(width)[None, :]
        out.append(jnp.asarray(lane % per == np.arange(LANE)[:, None], BF16))
        out.append(jnp.asarray(lane // per == np.arange(dev_count)[:, None], F32))
    return out


def small_parts(norm_gain, conv_weight, decay_bias, admit_bias, decay_rate, feed_gain):
    scale = -DECAY_SCALE * jax.nn.softplus(-decay_rate.astype(F32))
    parts = [norm_gain, feed_gain, decay_bias, admit_bias, scale, decay_rate]
    return [v.reshape(1, -1) for v in parts] + [conv_weight.T]


def pack_rows(parts, out):
    out[...] = jnp.zeros_like(out)
    gain_one, gain_two, decay_bias, admit_bias, scale, rate, taps = [v[...].astype(F32) for v in parts]
    high = scale.astype(BF16).astype(F32)
    mid = (scale - high).astype(BF16).astype(F32)
    rows = [gain_one, gain_two, decay_bias, admit_bias, high, mid, scale - high - mid, rate]
    for i, row in enumerate(rows):
        out[i : i + 1, 0 : row.shape[1]] = row
    out[8 : 8 + taps.shape[0], 0 : taps.shape[1]] = taps


def decay_terms(pre, scale):
    recall = jax.nn.sigmoid(pre)
    log_decay = recall * scale
    decay = jnp.exp(log_decay)
    y = 2.0 * log_decay
    series = 1.0 + y * (1 / 7)
    for n in (6, 5, 4, 3, 2):
        series = 1.0 + y * (1 / n) * series
    lost = jnp.where(y > -0.35, -y * series, 1.0 - decay * decay)
    return recall, decay, lost


def scan_block(prod, state, reverse=False):
    length = prod.shape[0]
    at = lax.broadcasted_iota(jnp.int32, prod.shape, 0)
    step = 1
    while step < length:
        inside = at < length - step if reverse else at >= step
        turn = length - step if reverse else step
        prod_far = jnp.where(inside, pltpu.roll(prod, turn, 0), 1.0)
        state_far = jnp.where(inside, pltpu.roll(state, turn, 0), 0.0)
        state = prod * state_far + state
        prod = prod * prod_far
        step *= 2
    return prod, state


def lanes(c, width=LANE):
    return pl.ds(pl.multiple_of(c * width, width), width)


def loop(count, body):
    def step(i, carry):
        body(i)
        return carry

    lax.fori_loop(0, count, step, 0)


def stream_tiles(count, fetch, use):
    for cp in fetch(0, 0):
        cp.start()

    def step(j, carry):
        slot = lax.rem(j, 2)

        @pl.when(j + 1 < count)
        def _():
            for cp in fetch(j + 1, 1 - slot):
                cp.start()

        for cp in fetch(j, slot):
            cp.wait()
        use(j, slot)
        return carry

    lax.fori_loop(0, count, step, 0)


def mat(value):
    return value.reshape(-1, value.shape[-1])


class Forward:
    def __init__(self, refs, place, weights):
        self.__dict__.update(refs)
        self.p, self.weights = place, weights
        self.tok = self.xs.shape[1]
        self.rows = self.xs.shape[0]
        self.flat = self.rows * self.tok
        self.lru = self.gelu_pre.shape[1]
        self.model = self.xs.shape[2]
        self.feed = self.hidden.shape[1]
        self.stores = []

    def save(self, name):
        cp = pltpu.make_async_copy(getattr(self, name), self.keep[name], self.keep_sem.at[len(self.stores)])
        cp.start()
        self.stores.append(cp)

    def fetch(self, i, buf, sem, starts, width):
        def copies(j, slot):
            out = []
            for n, start in enumerate(starts):
                src = self.weights[i].at[:, :, :, :, :, pl.ds(pl.multiple_of(start + j * width, LANE), width)]
                dst = buf.at[slot, :, :, :, :, :, pl.ds(n * width, width)]
                out.append(pltpu.make_async_copy(src, dst, sem.at[slot, n]))
            return out

        return copies

    def vectors(self):
        cp = pltpu.make_async_copy(self.small_all, self.small_vm, self.misc_sem.at[0])
        cp.start()
        cp.wait()
        nz = self.p.nz

        def spread(row, hot, mask):
            vals = self.small_vm[:, :, row, :].reshape(nz * 8, LANE).astype(BF16)
            wide = jnp.dot(vals, hot[...], preferred_element_type=F32)
            return jnp.sum(wide * mask[...], axis=0, keepdims=True)

        for row in range(2):
            self.vec[row : row + 1, 0 : self.model] = spread(row, self.hot_m, self.mask_m)
        for row in range(2, 12):
            self.vec[row : row + 1, :] = spread(row, self.hot_l, self.mask_l)
        self.vec[4:5, :] = self.vec[4:5, :] + self.vec[5:6, :] + self.vec[6:7, :]

    def norm(self, load, count, gain_row, out):
        gain = self.vec[gain_row : gain_row + 1, 0 : self.model]

        def body(i):
            v = load(i)
            q = lax.rsqrt(jnp.mean(v * v, axis=-1, keepdims=True) + EPSILON)
            out[pl.ds(pl.multiple_of(i * 32, 32), 32), :] = (v * q * gain).astype(BF16)

        loop(count, body)

    def norm_one(self):
        per = self.tok // 32

        def main(i):
            return self.xs[i // per, pl.ds(pl.multiple_of(lax.rem(i, per) * 32, 32), 32), :].astype(F32)

        self.norm(main, self.flat // 32, 0, self.normed.at[0 : self.flat])
        self.norm(
            lambda i: self.halo_x[...].reshape(2 * 16, self.model).astype(F32),
            1,
            0,
            self.normed.at[self.flat : self.flat + 32],
        )
        self.save(N.normed_main)
        self.save(N.xs)

    def gelu_side(self):
        def use(j, slot):
            res = jnp.dot(self.normed[0 : self.flat, :], mat(self.w_gi[slot]), preferred_element_type=F32)
            self.gelu_pre[:, lanes(j, 512)] = res

        stream_tiles(self.lru // 512, self.fetch(0, self.w_gi, self.w_sem, (0,), 512), use)
        self.save(N.gelu_pre)

    def branch_side(self):
        half = self.lru // 512

        def use_two(j, slot):
            res = jnp.dot(self.normed[...], mat(self.w_gi[slot]), preferred_element_type=F32).astype(BF16)
            self.branch[:, lanes(j, 512)] = res

        stream_tiles(half, self.fetch(0, self.w_gi, self.w_sem, (self.lru,), 512), use_two)

        def conv(c):
            for r in range(self.rows):
                at = slice(r * self.tok, (r + 1) * self.tok)
                head = self.branch[self.flat + 16 * r : self.flat + 16 * (r + 1), lanes(c)].astype(F32)
                wide = jnp.concatenate([head, self.branch[at, lanes(c)].astype(F32)], axis=0)
                since = self.since[pl.ds(r * (self.tok + 16), self.tok), :]
                total = jnp.zeros((self.tok, LANE), F32)
                for k in range(4):
                    moved = wide if k == 0 else pltpu.roll(wide, k, 0)
                    tap = self.vec[8 + k : 9 + k, lanes(c)]
                    total = total + tap * moved[16:] * (since >= k).astype(F32)
                self.conv[at, lanes(c)] = total.astype(BF16)

        loop(self.lru // LANE, conv)
        self.save(N.branch)
        self.save(N.conv)

    def gates(self, first, count):
        self.sums[...] = jnp.zeros_like(self.sums) if first == 0 else self.sums[...]

        def use(j, slot):
            self.tile[...] = jnp.dot(self.conv[...], mat(self.w_da[slot]), preferred_element_type=F32)
            base = (first + j) * 4

            def block(i):
                c = base + i
                gate_sum = jnp.zeros((1, LANE), F32)
                for r in range(self.rows):
                    at = slice(r * self.tok, (r + 1) * self.tok)
                    pre = self.tile[at, lanes(i)] + self.vec[2:3, lanes(c)]
                    admit_pre = self.tile[at, lanes(i + 4)] + self.vec[3:4, lanes(c)]
                    self.decay_pre[at, lanes(c)] = pre
                    self.admit_pre[at, lanes(c)] = admit_pre
                    recall, decay, lost = decay_terms(pre, self.vec[4:5, lanes(c)])
                    since = self.since[pl.ds(r * (self.tok + 16), self.tok), :]
                    reset = (since == 0).astype(F32)
                    keep = 1.0 - reset
                    scale_in = reset + keep * jnp.sqrt(lost)
                    update = scale_in * jax.nn.sigmoid(admit_pre) * self.conv[at, lanes(c)].astype(F32)
                    prod, state = scan_block(decay * keep, update)
                    self.prod[at, lanes(c)] = prod
                    self.state[at, lanes(c)] = state
                    self.ends[self.p.z, r : r + 1, lanes(c)] = prod[self.tok - 1 :, :]
                    self.ends[self.p.z, 8 + r : 9 + r, lanes(c)] = state[self.tok - 1 :, :]
                    gate_sum = gate_sum + jnp.sum(decay, axis=0, keepdims=True)
                self.sums[0:1, lanes(c)] = gate_sum

            loop(4, block)

        starts = (first * 512, self.lru + first * 512)
        stream_tiles(count, self.fetch(1, self.w_da, self.w_sem, starts, 512), use)

    def gates_saved(self):
        self.save(N.decay_pre)
        self.save(N.admit_pre)
        self.save(N.sums)

    def send_ends(self):
        p = self.p
        self.end_moves = []
        for o in range(1, p.nz):
            view = self.ends.at[p.z]
            cp = pltpu.make_async_remote_copy(
                view, view, self.e_send.at[o - 1], self.e_recv.at[o - 1],
                device_id=p.at(lax.rem(p.z + o, p.nz)), device_id_type=MESH,
            )
            cp.start()
            self.end_moves.append(cp)

    def mix(self):
        p = self.p
        for o in range(1, p.nz):
            view = self.ends.at[lax.rem(p.z + p.nz - o, p.nz)]
            pltpu.make_async_remote_copy(
                view, view, self.e_send.at[o - 1], self.e_recv.at[o - 1],
                device_id=p.core, device_id_type=MESH,
            ).wait_recv()

        def block(c):
            carry = jnp.zeros((8, LANE), F32)
            into = carry
            for i in range(p.nz - 1):
                carry = self.ends[i, 0:8, lanes(c)] * carry + self.ends[i, 8:16, lanes(c)]
                into = jnp.where(p.z == i + 1, carry, into)
            self.carry[:, lanes(c)] = into
            for r in range(self.rows):
                at = slice(r * self.tok, (r + 1) * self.tok)
                state = self.state[at, lanes(c)] + self.prod[at, lanes(c)] * into[r : r + 1, :]
                self.state[at, lanes(c)] = state
                gelu = smooth_gate(self.gelu_pre[at, lanes(c)])
                self.mixed[at, lanes(c)] = (state * gelu).astype(BF16)

        loop(self.lru // LANE, block)
        self.save(N.state)
        self.save(N.carry)
        self.save(N.ends)
        self.save(N.mixed)

        def use(j, slot):
            res = jnp.dot(self.mixed[...], mat(self.w_mx[slot]), preferred_element_type=F32)
            x = self.xs[:, :, lanes(j, 512)].astype(F32).reshape(self.flat, 512)
            self.middle[:, lanes(j, 512)] = x + res

        stream_tiles(self.model // 512, self.fetch(2, self.w_mx, self.w_sem, (0,), 512), use)
        self.norm(
            lambda i: self.middle[pl.ds(pl.multiple_of(i * 32, 32), 32), :], self.flat // 32, 1, self.normed_two
        )
        self.save(N.middle)
        self.save(N.normed_two)

    def gate_up(self, first, count):
        def use(j, slot):
            res = jnp.dot(self.normed_two[...], mat(self.w_gu[slot]), preferred_element_type=F32)
            gate, up = res[:, 0:512], res[:, 512:1024]
            at = lanes(first + j, 512)
            self.gate_pre[:, at] = gate
            self.up[:, at] = up
            self.hidden[:, at] = (smooth_gate(gate) * up).astype(BF16)

        starts = (first * 512, self.feed + first * 512)
        stream_tiles(count, self.fetch(3, self.w_gu, self.w_sem, starts, 512), use)

    def gate_saved(self):
        self.save(N.gate_pre)
        self.save(N.up)
        self.save(N.hidden)

    def finish(self):
        for cp in self.stores:
            cp.wait()
        for cp in self.end_moves:
            cp.wait_send()


KEEP = (
    N.xs, N.normed_main, N.gelu_pre, N.branch, N.conv, N.decay_pre, N.admit_pre, N.sums, N.state, N.carry,
    N.ends, N.mixed, N.middle, N.normed_two, N.gate_pre, N.up, N.hidden,
)


def forward_kernel(seq_count, starts, chunks, names, n_keep, *refs):
    refs = list(refs)
    x_ref, since, hot_m, mask_m, hot_l, mask_l = refs[:6]
    parts = refs[6:13]
    srcs = refs[13:21]
    at = 21
    small_all, vec = refs[at : at + 2]
    outs = refs[at + 2 : at + 7]
    keep = dict(zip(KEEP, refs[at + 7 : at + 7 + n_keep]))
    at += 7 + n_keep
    table = dict(zip(names, refs[at : at + len(names)]))
    p = Place(seq_count)
    table.update(
        small_all=small_all, vec=vec, since=since, hot_m=hot_m, mask_m=mask_m, hot_l=hot_l, mask_l=mask_l, keep=keep,
    )
    table[N.normed_main] = table[N.normed].at[0 : table[N.conv].shape[0]]
    f = Forward(table, p, outs)
    one = pl.ds
    copies = []
    own_sem = table[N.own_sem]
    k = 0
    for out, count in zip(outs, (2, 2, 1, 2, 1)):
        col = 0
        for _ in range(count):
            cols = srcs[k].shape[-1]
            dst = out.at[one(p.z, 1), one(p.a, 1), one(p.b, 1), one(p.c, 1), :, one(col, cols)]
            copies.append(pltpu.make_async_copy(srcs[k], dst, own_sem.at[k]))
            col += cols
            k += 1
    tok, feat = f.tok, x_ref.shape[2]
    here = one(pl.multiple_of(p.z * feat, LANE), feat)
    copies.append(pltpu.make_async_copy(x_ref.at[:, one(p.z * tok, tok), :], f.xs.at[:, :, here], own_sem.at[k]))
    pack_rows(parts, table[N.small_own])
    own_rows = table[N.small_own].reshape(1, 1, 16, LANE)
    copies.append(pltpu.make_async_copy(own_rows, small_all.at[one(p.z, 1), one(p.d, 1)], own_sem.at[k + 1]))
    for cp in copies:
        cp.start()

    def halo(z):
        return x_ref.at[:, one(pl.multiple_of(jnp.maximum(z * tok - 16, 0), 16), 16), :]

    own_halo = lambda: pltpu.make_async_copy(halo(p.z), f.halo_x.at[:, :, here], own_sem.at[k + 2])

    @pl.when(p.z > 0)
    def _():
        own_halo().start()

    @pl.when(p.z == 0)
    def _():
        f.halo_x[...] = jnp.zeros_like(f.halo_x)

    f.ends[...] = jnp.zeros_like(f.ends)
    f.sums[...] = jnp.zeros_like(f.sums)
    p.greet()
    x_moves = []

    def x_copy(o):
        to = lax.rem(p.z + o, p.nz)
        return pltpu.make_async_remote_copy(
            x_ref.at[:, one(pl.multiple_of(to * tok, 16), tok), :], f.xs.at[:, :, here], table[N.x_send].at[o - 1],
            table[N.x_recv].at[o - 1], device_id=p.at(to), device_id_type=MESH,
        )

    def h_copy(o):
        to = lax.rem(p.z + o, p.nz)
        return to > 0, pltpu.make_async_remote_copy(
            halo(to), f.halo_x.at[:, :, here], table[N.h_send].at[o - 1],
            table[N.h_recv].at[o - 1], device_id=p.at(to), device_id_type=MESH,
        )

    for o in range(1, p.nz):
        x_copy(o).start()
        cond, cp = h_copy(o)
        pl.when(cond)(cp.start)
    for cp in copies:
        cp.wait()
    s_send, s_recv = table[N.s_send], table[N.s_recv]
    s_moves = []

    def small_put(view, at, dev):
        cp = pltpu.make_async_remote_copy(view, view, s_send.at[at], s_recv.at[at], device_id=dev, device_id_type=MESH)
        cp.start()
        s_moves.append(cp)

    def small_view(d, n):
        return small_all.at[one(p.z, 1), one(d, n)]

    small_put(small_view(p.d, 1), 0, p.core)
    g = Gather(p, outs, chunks, table[N.send], table[N.recv], starts)
    last = [max(starts[i] for i in range(len(chunks)) if chunks[i][0] == w) + GATHER_PACE * (g.depth - 1) for w in range(5)]
    at = last[0]
    da_at = max(last[1], at + 2)
    plan = {
        3: [f.vectors, f.norm_one],
        at: [f.branch_side],
        at + 1: [f.gelu_side],
        da_at: [lambda: f.gates(0, 1)],
        da_at + 1: [lambda: f.gates(1, 1)],
        da_at + 2: [lambda: f.gates(2, 1), f.send_ends, f.gates_saved],
        max(last[2], da_at + 3): [f.mix],
    }
    for n in range(3):
        plan.setdefault(max(last[3], da_at + 4) + n, []).append(partial(f.gate_up, 2 * n, 2))
    plan[max(plan)].append(f.gate_saved)
    ticks = max(g.ticks(), max(plan) + 1)
    for t in range(ticks):
        g.tick(t)
        if t == 0:
            s_moves[0].wait_recv()
            small_put(small_view(p.d - p.c, 2), 1, p.peer["b"])
        if t == 1:
            s_moves[1].wait_recv()
            small_put(small_view(4 * p.a, 4), 2, p.peer["a"])
        if t == 2:
            s_moves[2].wait_recv()
            for o in range(1, p.nz):
                small_put(small_view(0, 8), 2 + o, p.at(lax.rem(p.z + o, p.nz)))
        if t == 3:
            for cp in s_moves[3:]:
                cp.wait_recv()
            for o in range(1, p.nz):
                x_copy(o).wait_recv()
                pl.when(p.z > 0)(h_copy(o)[1].wait_recv)

            @pl.when(p.z > 0)
            def _():
                own_halo().wait()

        for action in plan.get(t, ()):
            action()
    for cp in s_moves:
        cp.wait_send()
    for o in range(1, p.nz):
        x_copy(o).wait_send()
        cond, cp = h_copy(o)
        pl.when(cond)(cp.wait_send)
    f.finish()
    g.finish()


def forward_pass(x_heads, small, since, shards, seq_count, starts):
    groups = ((0, 1), (2, 3), (4,), (5, 6), (7,))
    rows_cols = [(shards[g[0]].shape[0], sum(shards[i].shape[1] for i in g)) for g in groups]
    chunks = chunk_list(rows_cols)
    row_count, row_len, feat = x_heads.shape
    tok, model = row_len // seq_count, feat * seq_count
    flat = row_count * tok
    lru, feed = rows_cols[0][1] // 2, rows_cols[3][1] // 2
    nz = seq_count
    srcs = [s.reshape(1, 1, 1, 1, *s.shape) for s in shards]
    hbm = pl.BlockSpec(memory_space=pltpu.HBM)
    vmem = pl.BlockSpec(memory_space=pltpu.VMEM)
    keep_shapes = dict(
        xs=((row_count, tok, model), BF16),
        normed_main=((flat, model), BF16),
        gelu_pre=((flat, lru), F32),
        branch=((flat + 32, lru), BF16),
        conv=((flat, lru), BF16),
        decay_pre=((flat, lru), F32),
        admit_pre=((flat, lru), F32),
        sums=((8, lru), F32),
        state=((flat, lru), F32),
        carry=((8, lru), F32),
        ends=((nz, 16, lru), F32),
        mixed=((flat, lru), BF16),
        middle=((flat, model), F32),
        normed_two=((flat, model), BF16),
        gate_pre=((flat, feed), F32),
        up=((flat, feed), F32),
        hidden=((flat, feed), BF16),
    )
    scratch = {n: pltpu.VMEM(*s) for n, s in keep_shapes.items() if n != "normed_main"}
    dma = pltpu.SemaphoreType.DMA
    sems = Gather.sem_count(nz)
    scratch.update(
        normed=pltpu.VMEM((flat + 32, model), BF16),
        halo_x=pltpu.VMEM((row_count, 16, model), BF16),
        small_vm=pltpu.VMEM((nz, 8, 16, LANE), F32),
        small_own=pltpu.VMEM((16, LANE), F32),
        prod=pltpu.VMEM((flat, lru), F32),
        tile=pltpu.VMEM((flat, 1024), F32),
        w_gi=pltpu.VMEM((2, nz, 2, 2, 2, rows_cols[0][0], 512), BF16),
        w_da=pltpu.VMEM((2, nz, 2, 2, 2, rows_cols[1][0], 1024), BF16),
        w_mx=pltpu.VMEM((2, nz, 2, 2, 2, rows_cols[2][0], 512), BF16),
        w_gu=pltpu.VMEM((2, nz, 2, 2, 2, rows_cols[3][0], 1024), BF16),
        w_sem=dma((2, 2)),
        keep_sem=dma((len(KEEP),)),
        misc_sem=dma((1,)),
        own_sem=dma((len(srcs) + 3,)),
        x_send=dma((nz,)),
        x_recv=dma((nz,)),
        h_send=dma((nz,)),
        h_recv=dma((nz,)),
        s_send=dma((nz + 3,)),
        s_recv=dma((nz + 3,)),
        e_send=dma((nz,)),
        e_recv=dma((nz,)),
        send=dma((len(chunks), sems)),
        recv=dma((len(chunks), sems)),
    )
    names = list(scratch)
    out_shape = [jax.ShapeDtypeStruct((nz, 8, 16, LANE), F32), jax.ShapeDtypeStruct((16, lru), F32)]
    out_shape += [jax.ShapeDtypeStruct((nz, PLANE, PLANE, 2, r, c), BF16) for r, c in rows_cols]
    out_shape += [jax.ShapeDtypeStruct(*keep_shapes[n]) for n in KEEP]
    outs = pl.pallas_call(
        partial(forward_kernel, nz, starts, chunks, names, len(KEEP)),
        out_shape=out_shape,
        in_specs=[hbm] + [vmem] * 20,
        out_specs=[hbm, vmem] + [hbm] * (5 + len(KEEP)),
        scratch_shapes=[scratch[n] for n in names],
        compiler_params=pltpu.CompilerParams(
            collective_id=0, has_side_effects=True, vmem_limit_bytes=61 << 20
        ),
        name="forward_pass",
    )(
        x_heads,
        since,
        *spread_constants(model, lru, nz * 8),
        *small,
        *srcs,
    )
    return outs[1], outs[2:7], dict(zip(KEEP, outs[7:]))


PACE = 2
C_RING, RING, SLOTS, PIECE = 8 * PACE, 5 * PACE, 2 * PACE, 256


class Chunk:
    def __init__(self, name, lhs, rhs, rows, width, first):
        self.name, self.lhs, self.rhs = name, lhs, rhs
        self.rows, self.width, self.first = rows, width, first
        self.across = width // PIECE


class Reduce:
    NAMES = (N.C, N.YA, N.YB, N.YC, N.PC, N.UA, N.DA, N.UB, N.DB, N.UC, N.DC, N.XA, N.XB)
    PIECES = {"A": pl.ds(0, 2), "B": pl.ds(2, 2), "C": pl.ds(4, 2)}

    @staticmethod
    def shapes(nz):
        tail = (2, 16, PIECE)
        plane = PLANE
        a, b, c = (nz, 1, plane), (nz, plane, 1), (nz, 1, 1)
        own = (1, 1, 1)
        lead = dict(YA=a, YB=b, YC=b, PC=c, UA=a, DA=a, UB=b, DB=b, UC=c, DC=c, XA=own, XB=own)
        out = {n: (RING, *v, *tail) for n, v in lead.items()}
        out["C"] = (C_RING, nz, plane, plane, 6, 16, PIECE)
        return out

    def __init__(self, place, bufs, full, send, recv, produce, deliver):
        self.p, self.bufs, self.full = place, bufs, full
        self.send, self.recv = send, recv
        self.produce, self.deliver = produce, deliver
        self.started = {}
        self.depth = place.nz + 4

    def buf(self, k, name):
        return self.bufs[name].at[k % (C_RING if name == "C" else RING)]

    def order(self, k):
        return ("a", "b") if k % 2 else ("b", "a")

    def part(self, k, route, z, a, b):
        full = slice(None)
        one = lambda v: full if v is None else v if isinstance(v, slice) else pl.ds(v, 1)
        return self.buf(k, "C").at[one(z), one(a), one(b), self.PIECES[route]]

    def copy(self, k, name, src, dst, dev):
        at = self.NAMES.index(name)
        return pltpu.make_async_remote_copy(
            src, dst, self.send.at[k, at], self.recv.at[k, at], device_id=dev, device_id_type=MESH
        )

    def put(self, k, name, src, dst, dev):
        make = lambda: self.copy(k, name, src(), dst(), dev)
        make().start()
        self.started.setdefault(k, []).append((make, None))

    def z_put(self, k, route, way, z):
        p = self.p
        name = ("U" if way > 0 else "D") + route
        span = slice(z + 1, p.nz) if way > 0 else slice(0, z)

        def make():
            a = p.a if route != "B" else None
            b = p.b if route != "A" else None
            return self.copy(k, name, self.part(k, route, span, a, b), self.buf(k, name).at[span], p.at(z + way))

        make().start()
        self.started.setdefault(k, []).append((make, z))

    def take(self, k, name, dst):
        self.copy(k, name, dst, dst, self.p.core).wait_recv()

    def add(self, into, other):
        def one(t):
            into[t] = into[t] + other[t]

        loop(into.shape[0], one)

    def wave(self, k, route, s):
        p, nz = self.p, self.p.nz
        low, high = s - 1, nz - s

        def gather(name, span):
            got = self.buf(k, name).at[span]
            self.take(k, name, got)
            a = p.a if route != "B" else None
            b = p.b if route != "A" else None
            self.add(self.part(k, route, span, a, b), got)

        @pl.when(p.z == low)
        def _():
            if low > 0:
                gather("U" + route, slice(low, nz))
            if low < nz - 1:
                self.z_put(k, route, 1, low)

        @pl.when(p.z == high)
        def _():
            if high < nz - 1:
                gather("D" + route, slice(0, high + 1))
            if high > 0:
                self.z_put(k, route, -1, high)

    def yc(self, k):
        buf = self.buf(k, "YC")
        if self.order(k)[1] == "b":
            return buf
        nz, plane, _, n, r, w = buf.shape
        return buf.reshape(nz, 1, plane, n, r, w)

    def stage(self, k, s):
        p, nz = self.p, self.p.nz
        if s == 0:
            self.produce(k)
            slot = self.full.at[k % SLOTS]
            self.put(k, "C", lambda: slot.at[:, :, :, 1 - p.c], lambda: self.buf(k, "C"), p.core)
        if s == 1:
            self.take(k, "C", self.buf(k, "C"))
            into, own = self.buf(k, "C"), self.full.at[k % SLOTS]

            def one(t):
                for a in range(PLANE):
                    for b in range(PLANE):
                        into[t, a, b] = into[t, a, b] + own[t, a, b, p.c]

            loop(nz, one)
            self.put(k, "YA", lambda: self.part(k, "A", None, 1 - p.a, None), lambda: self.buf(k, "YA"), p.peer["a"])
            self.put(k, "YB", lambda: self.part(k, "B", None, None, 1 - p.b), lambda: self.buf(k, "YB"), p.peer["b"])
            q = self.order(k)[1]
            src = lambda: self.part(k, "C", None, 1 - p.a if q == "a" else None, 1 - p.b if q == "b" else None)
            self.put(k, "YC", src, lambda: self.yc(k), p.peer[q])
        if s == 2:
            make, _ = self.started[k].pop(0)
            make().wait_send()
            self.take(k, "YA", self.buf(k, "YA"))
            self.add(self.part(k, "A", None, p.a, None), self.buf(k, "YA"))
            self.take(k, "YB", self.buf(k, "YB"))
            self.add(self.part(k, "B", None, None, p.b), self.buf(k, "YB"))
            first, q = self.order(k)
            self.take(k, "YC", self.yc(k))
            self.add(self.part(k, "C", None, p.a if q == "a" else None, p.b if q == "b" else None), self.yc(k))
            src = lambda: self.part(
                k, "C", None, 1 - p.a if first == "a" else p.a, 1 - p.b if first == "b" else p.b
            )
            self.put(k, "PC", src, lambda: self.buf(k, "PC"), p.peer[first])
        if s == 3:
            self.take(k, "PC", self.buf(k, "PC"))
            self.add(self.part(k, "C", None, p.a, p.b), self.buf(k, "PC"))
        if 2 <= s <= nz + 1:
            self.wave(k, "A", s - 1)
            self.wave(k, "B", s - 1)
        if 3 <= s <= nz + 2:
            self.wave(k, "C", s - 2)
        if s == nz + 1:
            self.put(k, "XA", lambda: self.part(k, "A", p.z, p.a, 1 - p.b), lambda: self.buf(k, "XA"), p.peer["b"])
            self.put(k, "XB", lambda: self.part(k, "B", p.z, 1 - p.a, p.b), lambda: self.buf(k, "XB"), p.peer["a"])
        if s == nz + 2:
            self.take(k, "XA", self.buf(k, "XA"))
            self.take(k, "XB", self.buf(k, "XB"))
            self.deliver(k)
        if s == nz + 3:
            for make, z in self.started.pop(k):
                if z is None:
                    make().wait_send()
                else:

                    @pl.when(p.z == z)
                    def _():
                        make().wait_send()

    def result(self, k, route):
        p = self.p
        block = self.part(k, route, p.z, p.a, p.b)[0, 0, 0].astype(F32)
        if route != "C":
            block = block + self.buf(k, "X" + route)[0, 0, 0].astype(F32)
        return block

    def tick(self, t, count):
        for k in range(count):
            if 0 <= t - k < PACE * self.depth and (t - k) % PACE == 0:
                self.stage(k, (t - k) // PACE)

    def ticks(self, count):
        return count + PACE * (self.depth - 1)


class Backward:
    def __init__(self, refs, place):
        self.__dict__.update(refs)
        self.p = place
        self.flat, self.model = self.cot.shape
        self.lru, self.feed = self.q.shape[1], self.hidden.shape[1]
        self.rows = 2
        self.tok = self.flat // self.rows
        self.outs_going = {}
        c = Chunk
        wide, tall, full = 3 * PIECE, 2 * PIECE, PIECE
        self.chunks = [c(N.dn, N.hidden, N.cot, 96, full, j) for j in range(0, self.model, full)]
        self.chunks += [c(N.gu, N.normed_two, N.ggu, 32, wide, j) for j in range(0, 2 * self.feed, wide)]
        self.chunks += [c(N.mx, N.mixed, N.grad_out, 48, tall, j) for j in range(0, self.model, tall)]
        self.chunks += [c(N.gi, N.normed, N.ggi, 32, wide, j) for j in range(0, self.lru, wide)]
        self.chunks += [c(N.da, N.conv, N.hidden, 48, tall, j) for j in range(0, 2 * self.lru, tall)]
        self.chunks += [c(N.gi, N.normed, N.ggi, 32, wide, j) for j in range(self.lru, 2 * self.lru, wide)]

    def first_of(self, name, at=0):
        return min(k for k, ch in enumerate(self.chunks) if ch.name == name and ch.first >= at)

    def load(self, names):
        for name in names:
            self.loader(name).start()

    def loader(self, name):
        src, dst, at = self.loads[name]
        return pltpu.make_async_copy(src, dst, self.load_sem.at[at])

    def ready(self, names):
        for name in names:
            self.loader(name).wait()

    def produce(self, k):
        ch = self.chunks[k]
        lhs, rhs = getattr(self, ch.lhs), getattr(self, ch.rhs)
        span = 8 * ch.rows
        slot = self.full.at[k % SLOTS]

        def one(z):
            left = lhs[:, pl.ds(pl.multiple_of(z * span, LANE), span)]
            for n in range(ch.across):
                right = rhs[:, ch.first + n * PIECE : ch.first + (n + 1) * PIECE]
                val = outer_sum(left, right).astype(BF16).reshape(8, ch.rows // 16, 16, PIECE)
                for i in range(ch.rows // 16):
                    slot[z, :, :, :, i * ch.across + n] = val[:, i].reshape(2, 2, 2, 16, PIECE)

        loop(self.p.nz, one)

    def out_copies(self, k):
        ch = self.chunks[k]
        copies = []
        for i in range(ch.rows // 16):
            for n in range(ch.across):
                at = i * ch.across + n
                col = ch.first + n * PIECE
                names = self.out_names[ch.name]
                width = self.weight_outs[names[0]].shape[1]
                out = self.weight_outs[names[col // width]]
                dst = out.at[pl.ds(i * 16, 16), pl.ds(col % width, PIECE)]
                copies.append(pltpu.make_async_copy(self.staged.at[k % 2, at], dst, self.out_sem.at[k % 2, at]))
        return copies

    def deliver(self, k):
        if k >= 2:
            for cp in self.out_copies(k - 2):
                cp.wait()
        for route, at in (("A", 0), ("B", 2), ("C", 4)):
            self.staged[k % 2, at : at + 2] = self.reduce.result(k, route)
        for cp in self.out_copies(k):
            cp.start()

    def by_z(self, weight, buf, sem, extra=None, parts=1):
        width = weight.shape[-1] // parts

        def copies(j, slot):
            z = j // parts
            rows = weight.shape[4]
            src = weight.at[z, :, :, :, :, pl.ds(pl.multiple_of(lax.rem(j, parts) * width, LANE), width)]
            dst = buf.at[slot, :, :, :, 0:rows, 0:width]
            out = [pltpu.make_async_copy(src, dst, sem.at[slot, 0])]
            return out + (extra(j, slot) if extra else [])

        return copies

    def feed_back(self):
        span = self.feed // self.p.nz
        half = lambda slot: pl.ds(pl.multiple_of(slot * span, LANE), span)

        def extra(j, slot):
            at = pl.ds(pl.multiple_of(j * span, LANE), span)
            return [
                pltpu.make_async_copy(self.gate_pre.at[:, at], self.gelu_pre.at[:, half(slot)], self.w_sem.at[slot, 1]),
                pltpu.make_async_copy(self.up.at[:, at], self.state.at[:, half(slot)], self.w_sem.at[slot, 2]),
            ]

        def use(j, slot):
            self.wide_tile[...] = back_prod(self.cot[...], mat(self.w_dn[slot]))
            out = self.q.at[:, 0 : self.model]
            start = jnp.where(j == 0, self.middle[...], out[...])
            left = self.hidden[:, pl.ds(pl.multiple_of(j * span, LANE), span)]
            out[...] = start + jnp.dot(left, mat(self.w_dn[slot]), preferred_element_type=F32)
            at = pl.ds(pl.multiple_of(j * span, LANE), span)
            at_up = pl.ds(pl.multiple_of(self.feed + j * span, LANE), span)

            def block(i):
                rows = pl.ds(pl.multiple_of(i * 16, 16), 16)
                grad = self.wide_tile[rows, :]
                gate = self.gelu_pre[rows, half(slot)]
                act, slope = gelu_both(gate)
                self.ggu[rows, at] = (slope * self.state[rows, half(slot)] * grad).astype(BF16)
                self.ggu[rows, at_up] = (act * grad).astype(BF16)

            loop(self.flat // 16, block)

        self.ready([N.middle])
        stream_tiles(self.p.nz, self.by_z(self.dn, self.w_dn, self.w_sem, extra), use)
        self.grad_out[...] = self.q[:, 0 : self.model].astype(BF16)
        self.block_copy().start()

    def block_copy(self):
        return pltpu.make_async_copy(self.grad_out, self.block_out, self.block_sem.at[0])

    def norm_back(self, values, grads, gain_row, extra, out):
        gain = self.vec[gain_row : gain_row + 1, 0 : self.model]

        def block(i, total):
            rows = pl.ds(pl.multiple_of(i * 16, 16), 16)
            v, e = values(rows), grads(rows)
            back, terms = rms_back(v, gain, e)
            out(rows, extra(rows) + back)
            return total + jnp.sum(terms, axis=0, keepdims=True)

        total = lax.fori_loop(0, self.flat // 16, block, jnp.zeros((1, self.model), F32))
        self.sums[gain_row : gain_row + 1, 0 : self.model] = total

    def norm_two_back(self):
        half = self.feed

        def use(j, slot):
            left = self.ggu[:, pl.ds(pl.multiple_of(lax.rem(j, 2) * half, LANE), half)]
            rows = self.gu.shape[4]
            res = back_prod(left, mat(self.w_big[slot, :, :, :, 0:rows, 0:half]))
            at = lanes(j // 2, 8 * rows)

            @pl.when(lax.rem(j, 2) == 0)
            def _():
                self.q[:, at] = res

            @pl.when(lax.rem(j, 2) == 1)
            def _():
                self.q[:, at] = self.q[:, at] + res

        stream_tiles(2 * self.p.nz, self.by_z(self.gu, self.w_big, self.w_sem, None, 2), use)
        self.block_copy().wait()

        def out(rows, val):
            self.middle[rows, :] = val
            self.grad_out[rows, :] = val.astype(BF16)

        self.norm_back(
            lambda rows: self.middle[rows, :],
            lambda rows: self.q[rows, 0 : self.model],
            1,
            lambda rows: self.cot[rows, :].astype(F32),
            out,
        )

    def scan_back(self):
        self.ready([N.gelu_pre, N.state, N.decay_pre])
        rows = self.mx.shape[4]
        span = 8 * rows

        def use(j, slot):
            self.wide_tile[:, 0:span] = back_prod(self.grad_out[...], mat(self.w_big[slot, :, :, :, 0:rows, 0 : self.model]))

            def block(i):
                c = j * (span // LANE) + i
                for r in range(self.rows):
                    at = slice(r * self.tok, (r + 1) * self.tok)
                    grad = self.wide_tile[at, lanes(i)]
                    act, slope = gelu_both(self.gelu_pre[at, lanes(c)])
                    self.ggi[at, lanes(c)] = (slope * grad * self.state[at, lanes(c)]).astype(BF16)
                    _, decay, _ = decay_terms(self.decay_pre[at, lanes(c)], self.vec[4:5, lanes(c)])
                    since = self.since[r * (self.tok + 16) : r * (self.tok + 16) + self.tok, :]
                    eff = decay * (since != 0).astype(F32)
                    place = lax.broadcasted_iota(jnp.int32, eff.shape, 0)
                    after = jnp.where(place < self.tok - 1, pltpu.roll(eff, self.tok - 1, 0), 1.0)
                    prod, tail = scan_block(after, act * grad, reverse=True)
                    self.q[at, lanes(c)] = prod
                    self.gelu_pre[at, lanes(c)] = tail
                    self.tails[self.p.z, r : r + 1, lanes(c)] = eff[0:1, :] * tail[0:1, :]

            loop(span // LANE, block)

        stream_tiles(self.p.nz, self.by_z(self.mx, self.w_big, self.w_sem), use)

    def tail_copy(self, o, recv):
        p = self.p
        view = self.tails.at[lax.rem(p.z + p.nz - o, p.nz) if recv else p.z]
        return pltpu.make_async_remote_copy(
            view, view, self.t_send.at[o - 1], self.t_recv.at[o - 1],
            device_id=p.at(lax.rem(p.z + o, p.nz)), device_id_type=MESH,
        )

    def send_tails(self):
        for o in range(1, self.p.nz):
            self.tail_copy(o, False).start()

    def tails_here(self):
        for o in range(1, self.p.nz):
            self.tail_copy(o, True).wait_recv()
        self.ready([N.admit_pre, N.conv])

    def gates_back(self, third):
        p = self.p
        count = self.lru // LANE // 3

        def block(i):
            c = third * count + i
            tail = jnp.zeros((8, LANE), F32)
            into = tail
            for i in range(p.nz - 1, 0, -1):
                tail = self.ends[i, 0:8, lanes(c)] * tail + self.tails[i, :, lanes(c)]
                into = jnp.where(p.z == i - 1, tail, into)
            scale = self.vec[4:5, lanes(c)]
            rate_sum = jnp.zeros((1, LANE), F32)
            decay_sum, admit_sum = rate_sum, rate_sum
            for r in range(self.rows):
                at = slice(r * self.tok, (r + 1) * self.tok)
                adjoint = self.gelu_pre[at, lanes(c)] + self.q[at, lanes(c)] * into[r : r + 1, :]
                recall, decay, lost = decay_terms(self.decay_pre[at, lanes(c)], scale)
                root = jnp.sqrt(lost)
                since = self.since[r * (self.tok + 16) : r * (self.tok + 16) + self.tok, :]
                reset = (since == 0).astype(F32)
                keep = 1.0 - reset
                conv = self.conv[at, lanes(c)].astype(F32)
                admit = jax.nn.sigmoid(self.admit_pre[at, lanes(c)])
                state = self.state[at, lanes(c)]
                place = lax.broadcasted_iota(jnp.int32, state.shape, 0)
                before = jnp.where(place > 0, pltpu.roll(state, 1, 0), self.carry[r : r + 1, lanes(c)])
                scale_in = reset + keep * root
                grad_log = adjoint * keep * (before * decay - admit * conv * decay * decay / root)
                decay_low = (grad_log * scale * recall * (1.0 - recall)).astype(BF16)
                admit_low = (adjoint * scale_in * conv * admit * (1.0 - admit)).astype(BF16)
                self.hidden[at, lanes(c)] = decay_low
                self.hidden[at, pl.ds(pl.multiple_of(self.lru + c * LANE, LANE), LANE)] = admit_low
                self.admit_pre[at, lanes(c)] = adjoint * scale_in * admit
                rate_sum = rate_sum + jnp.sum(grad_log * recall, axis=0, keepdims=True)
                decay_sum = decay_sum + jnp.sum(decay_low.astype(F32), axis=0, keepdims=True)
                admit_sum = admit_sum + jnp.sum(admit_low.astype(F32), axis=0, keepdims=True)
            self.sums[2:3, lanes(c)] = decay_sum
            self.sums[3:4, lanes(c)] = admit_sum
            self.sums[4:5, lanes(c)] = rate_sum * (DECAY_SCALE * jax.nn.sigmoid(-self.vec[7:8, lanes(c)]))

        loop(count, block)

    def conv_grads(self):
        rows = self.da.shape[4]
        span = 8 * rows

        def use(j, slot):
            at = lanes(j, span)
            res = back_prod(self.hidden[...], mat(self.w_big[slot]))
            total = (self.admit_pre[:, at] + res).astype(BF16)
            self.grad_conv[:, :, at] = total.reshape(self.rows, self.tok, span)

        stream_tiles(self.p.nz, self.by_z(self.da, self.w_big, self.w_sem), use)

    def rim_copy(self):
        p = self.p
        return pltpu.make_async_remote_copy(
            self.grad_conv.at[:, 0:16, :], self.rim, self.r_send.at[0], self.r_recv.at[0],
            device_id=p.at(jnp.maximum(p.z - 1, 0)), device_id_type=MESH,
        )

    def send_rim(self):
        pl.when(self.p.z > 0)(lambda: self.rim_copy().start())

    def conv_back(self):
        p = self.p
        pl.when(p.z < p.nz - 1)(lambda: self.rim_copy().wait_recv())
        self.ready([N.branch])
        long = self.tok + 16

        def block(c):
            taps = [jnp.zeros((1, LANE), F32)] * 4
            for r in range(self.rows):
                at = slice(r * self.tok, (r + 1) * self.tok)
                since = self.since[r * long : (r + 1) * long, :]
                grad = self.grad_conv[r, :, lanes(c)].astype(F32)
                wide = jnp.concatenate([grad, self.rim[r, :, lanes(c)].astype(F32)], axis=0)
                head = self.branch[self.flat + 16 * r : self.flat + 16 * (r + 1), lanes(c)].astype(F32)
                back = jnp.concatenate([head, self.branch[at, lanes(c)].astype(F32)], axis=0)
                total = jnp.zeros((self.tok, LANE), F32)
                for k in range(4):
                    seen = (since >= k).astype(F32)
                    moved = back if k == 0 else pltpu.roll(back, k, 0)
                    term = jnp.sum(grad * moved[16:] * seen[0 : self.tok], axis=0, keepdims=True)
                    taps[k] = taps[k] + term
                    ahead = wide * seen
                    ahead = ahead if k == 0 else pltpu.roll(ahead, long - k, 0)
                    total = total + self.vec[8 + k : 9 + k, lanes(c)] * ahead[0 : self.tok]
                self.ggi[at, pl.ds(pl.multiple_of(self.lru + c * LANE, LANE), LANE)] = total.astype(BF16)
            for k in range(4):
                self.sums[5 + k : 6 + k, lanes(c)] = taps[k]

        loop(self.lru // LANE, block)

    def norm_one_back(self):
        rows = self.gi.shape[4]

        def use(j, slot):
            self.q[:, lanes(j, 8 * rows)] = back_prod(self.ggi[...], mat(self.w_big[slot, :, :, :, 0:rows, :]))

        stream_tiles(self.p.nz, self.by_z(self.gi, self.w_big, self.w_sem), use)
        self.ready([N.xs])

        def out(rows, val):
            self.grad_out[rows, :] = val.astype(BF16)

        self.norm_back(
            lambda rows: self.cot[rows, :].astype(F32),
            lambda rows: self.q[rows, 0 : self.model],
            0,
            lambda rows: self.middle[rows, :],
            out,
        )

    def x_copy(self, o):
        p = self.p
        feat = self.x_out.shape[2]
        to = lax.rem(p.z + o, p.nz)
        at = pl.ds(pl.multiple_of(to * feat, LANE), feat)
        src = self.grad_out.reshape(self.rows, self.tok, self.model).at[:, :, at]
        dst = self.x_out.at[:, pl.ds(pl.multiple_of(p.z * self.tok, 16), self.tok), :]
        if o == 0:
            return pltpu.make_async_copy(src, dst, self.x_send.at[p.nz - 1])
        return pltpu.make_async_remote_copy(
            src, dst, self.x_send.at[o - 1], self.x_recv.at[o - 1], device_id=p.at(to), device_id_type=MESH
        )

    def send_x(self):
        for o in range(self.p.nz):
            self.x_copy(o).start()

    def spread_sums(self):
        nz = self.p.nz
        for row in range(10):
            hot, mask, width = (self.hot_m, self.mask_m, self.model) if row < 2 else (self.hot_l, self.mask_l, self.lru)
            vals = self.sums[row : row + 1, 0:width] if row < 9 else self.gate_sums[0:1, :]
            wide = mask[...] * vals
            cut = lax.dot_general(
                wide, hot[...].astype(F32), (((1,), (1,)), ((), ())),
                precision=lax.Precision.HIGHEST, preferred_element_type=F32,
            )
            self.s_own[:, :, :, :, row, :] = cut.reshape(nz, 2, 2, 2, LANE)

    def s_copy(self, at):
        p = self.p
        if at == 0:
            src, dst, dev = self.s_own.at[:, :, :, 1 - p.c], self.s_core, p.core
        elif at == 1:
            src, dst, dev = self.s_core.at[:, :, 1 - p.b], self.s_b, p.peer["b"]
        elif at == 2:
            src, dst, dev = self.s_b.at[:, 1 - p.a], self.s_a, p.peer["a"]
        else:
            to = lax.rem(p.z + at - 2, p.nz)
            src, dst, dev = self.s_a.at[to], self.s_z.at[at - 3], p.at(to)
        return pltpu.make_async_remote_copy(
            src, dst, self.s_send.at[at], self.s_recv.at[at], device_id=dev, device_id_type=MESH
        )

    def small_step(self, n):
        p = self.p
        if n == 0:
            self.s_own[...] = jnp.zeros_like(self.s_own)
            self.spread_sums()
            self.s_copy(0).start()
        if n == 1:
            self.s_copy(0).wait_recv()
            self.s_core[...] = self.s_core[...] + self.s_own[:, :, :, p.c]
            self.s_copy(1).start()
        if n == 2:
            self.s_copy(1).wait_recv()
            self.s_b[...] = self.s_b[...] + self.s_core[:, :, p.b]
            self.s_copy(2).start()
        if n == 3:
            self.s_copy(2).wait_recv()
            self.s_a[...] = self.s_a[...] + self.s_b[:, p.a]
            for o in range(1, p.nz):
                self.s_copy(2 + o).start()
        if n == 4:
            total = self.s_a[p.z]
            for o in range(1, p.nz):
                self.s_copy(2 + o).wait_recv()
                total = total + self.s_z[o - 1]
            self.small_out[...] = total

    def finish(self):
        p = self.p
        count = len(self.chunks)
        for k in (count - 2, count - 1):
            for cp in self.out_copies(k):
                cp.wait()
        for o in range(1, p.nz):
            self.tail_copy(o, False).wait_send()
            self.x_copy(o).wait()
            self.s_copy(2 + o).wait_send()
        self.x_copy(0).wait()
        for at in range(3):
            self.s_copy(at).wait_send()
        pl.when(p.z > 0)(lambda: self.rim_copy().wait_send())


def gelu_both(x):
    inner = GELU_C * (x + 0.044715 * x * x * x)
    t = jnp.tanh(inner)
    slope = 0.5 * (1.0 + t) + 0.5 * x * (1.0 - t * t) * GELU_C * (1.0 + 3 * 0.044715 * x * x)
    return 0.5 * x * (1.0 + t), slope


def rms_back(values, gain, grad):
    q = lax.rsqrt(jnp.mean(values * values, axis=-1, keepdims=True) + EPSILON)
    inner = jnp.mean(values * gain * grad, axis=-1, keepdims=True)
    back = q * gain * grad - values * (q * q * q) * inner
    return back, grad * values * q


WEIGHTS = (N.gelu, N.input, N.decay, N.admit, N.mixer, N.gate, N.up, N.down)
OUT_NAMES = dict(gi=WEIGHTS[:2], da=WEIGHTS[2:4], mx=WEIGHTS[4:5], gu=WEIGHTS[5:7], dn=WEIGHTS[7:])
LOADS = (
    N.hidden, N.cot, N.normed_two, N.middle, N.mixed, N.gelu_pre, N.state, N.decay_pre, N.admit_pre, N.conv,
    N.branch, N.normed, N.xs,
)


def backward_kernel(seq_count, names, hbm_names, vmem_names, *refs):
    n_in = len(vmem_names) + len(hbm_names)
    given = dict(zip(vmem_names + hbm_names, refs[:n_in]))
    x_out, small_out, block_out = refs[n_in : n_in + 3]
    weight_outs = dict(zip(WEIGHTS, refs[n_in + 3 : n_in + 11]))
    table = dict(zip(names, refs[n_in + 11 :]))
    p = Place(seq_count)
    shared = dict(xs=N.cot, normed=N.normed_two)
    loads = {}
    for i, name in enumerate(LOADS):
        dst = table[shared.get(name, name)]
        loads[name] = (given.pop(name + "_hbm"), dst, i)
    table.update(given)
    table[N.normed] = table[N.normed_two]
    table[N.grad_conv] = table[N.mixed].reshape(2, table[N.mixed].shape[0] // 2, table[N.mixed].shape[1])
    table.update(x_out=x_out, small_out=small_out, block_out=block_out, weight_outs=weight_outs, out_names=OUT_NAMES, loads=loads)
    f = Backward(table, p)
    late = (N.xs, N.normed, N.gelu_pre, N.state)
    f.load(n for n in LOADS if n not in late)
    f.rim[...] = jnp.zeros_like(f.rim)
    f.tails[...] = jnp.zeros_like(f.tails)
    p.greet()
    f.reduce = Reduce(
        p, {n: table["ring_" + n] for n in Reduce.NAMES}, table[N.full], table[N.send], table[N.recv],
        f.produce, f.deliver,
    )
    count = len(f.chunks)
    f.ready([N.hidden, N.cot])

    def reload_cot():
        f.load(late[:1])

    first = f.first_of
    gu_count = first(N.mx) - first(N.gu)
    last = first(N.gi, f.lru)
    before = {
        first(N.gu): [f.feed_back, lambda: f.load(late[2:]), lambda: f.ready([N.normed_two])],
        first(N.gu) + gu_count // 2 - 1: [f.norm_two_back, reload_cot],
        first(N.mx) - 3: [f.scan_back, f.send_tails],
        first(N.mx) - 1: [f.tails_here, lambda: f.gates_back(0)],
        first(N.mx): [lambda: f.load(late[1:2]), lambda: f.gates_back(1), lambda: f.ready([N.mixed])],
        first(N.mx) + 1: [lambda: f.gates_back(2)],
        first(N.gi): [lambda: f.ready([N.normed])],
        first(N.da): [f.conv_grads, f.send_rim],
        first(N.da) + 2: [f.conv_back],
        last: [f.norm_one_back, f.send_x, lambda: f.small_step(0)],
    }
    for n in range(1, 5):
        before[last + n] = [partial(f.small_step, n)]
    for t in range(f.reduce.ticks(count)):
        for action in before.get(t, ()):
            action()
        f.reduce.tick(t, count)
    f.finish()


def backward_pass(cot, since, vec, full, kept, shard_shapes, seq_count):
    nz = seq_count
    flat, model = cot.shape
    lru, feed = kept[N.gelu_pre].shape[1], kept[N.hidden].shape[1]
    tok = flat // 2
    vmem_vals = dict(
        vec=vec,
        since=since,
        carry=kept[N.carry],
        ends=kept[N.ends],
        gate_sums=kept[N.sums],
    )
    vmem_vals.update(zip((N.hot_m, N.mask_m, N.hot_l, N.mask_l), spread_constants(model, lru, nz * 8)))
    hbm_vals = dict(zip((N.gi, N.da, N.mx, N.gu, N.dn), full))
    hbm_vals.update(gate_pre=kept[N.gate_pre], up=kept[N.up])
    source = dict(kept, cot=cot, normed=kept[N.normed_main], xs=kept[N.xs].reshape(flat, model))
    hbm_vals.update({n + "_hbm": source[n] for n in LOADS})
    dma = pltpu.SemaphoreType.DMA
    v = pltpu.VMEM
    chunks = 12 * 512 // PIECE
    scratch = dict(
        hidden=v((flat, feed), BF16),
        cot=v((flat, model), BF16),
        normed_two=v((flat, model), BF16),
        middle=v((flat, model), F32),
        mixed=v((flat, lru), BF16),
        gelu_pre=v((flat, lru), F32),
        state=v((flat, lru), F32),
        decay_pre=v((flat, lru), F32),
        admit_pre=v((flat, lru), F32),
        conv=v((flat, lru), BF16),
        branch=v((flat + 32, lru), BF16),
        ggu=v((flat, 2 * feed), BF16),
        ggi=v((flat, 2 * lru), BF16),
        grad_out=v((flat, model), BF16),
        rim=v((2, 16, lru), BF16),
        q=v((flat, lru), F32),
        tails=v((nz, 8, lru), F32),
        sums=v((16, lru), F32),
        wide_tile=v((flat, feed // nz), F32),
        w_dn=v((2, 2, 2, 2, full[4].shape[4], model), BF16),
        w_big=v((2, 2, 2, 2, full[1].shape[4], 2 * lru), BF16),
        full=v((SLOTS, nz, 2, 2, 2, 6, 16, PIECE), BF16),
        staged=v((2, 6, 16, PIECE), F32),
        s_own=v((nz, 2, 2, 2, 16, LANE), F32),
        s_core=v((nz, 2, 2, 16, LANE), F32),
        s_b=v((nz, 2, 16, LANE), F32),
        s_a=v((nz, 16, LANE), F32),
        s_z=v((nz, 16, LANE), F32),
        w_sem=dma((2, 3)),
        block_sem=dma((1,)),
        load_sem=dma((len(LOADS),)),
        out_sem=dma((2, 6)),
        send=dma((chunks, len(Reduce.NAMES))),
        recv=dma((chunks, len(Reduce.NAMES))),
        t_send=dma((nz,)),
        t_recv=dma((nz,)),
        r_send=dma((1,)),
        r_recv=dma((1,)),
        x_send=dma((nz,)),
        x_recv=dma((nz,)),
        s_send=dma((nz + 3,)),
        s_recv=dma((nz + 3,)),
    )
    scratch.update({"ring_" + n: v(s, BF16) for n, s in Reduce.shapes(nz).items()})
    names = list(scratch)
    hbm = pl.BlockSpec(memory_space=pltpu.HBM)
    vmem = pl.BlockSpec(memory_space=pltpu.VMEM)
    out_shape = [
        jax.ShapeDtypeStruct((2, tok * nz, model // nz), BF16),
        jax.ShapeDtypeStruct((16, LANE), F32),
        jax.ShapeDtypeStruct((flat, model), BF16),
    ] + [jax.ShapeDtypeStruct(s, F32) for s in shard_shapes]
    outs = pl.pallas_call(
        partial(backward_kernel, nz, names, list(hbm_vals), list(vmem_vals)),
        out_shape=out_shape,
        in_specs=[vmem] * len(vmem_vals) + [hbm] * len(hbm_vals),
        out_specs=[hbm, vmem] + [hbm] * 9,
        scratch_shapes=[scratch[n] for n in names],
        compiler_params=pltpu.CompilerParams(
            collective_id=1, has_side_effects=True, vmem_limit_bytes=61 << 20
        ),
        name="backward_pass",
    )(*vmem_vals.values(), *hbm_vals.values())
    return outs[0], outs[1], outs[2], outs[3:]


def hand_over_kernel(count, rows, *refs):
    srcs, own = refs[:count], refs[count]
    outs, small = refs[count + 1 : 2 * count + 1], refs[2 * count + 1 : 2 * count + 1 + len(rows)]
    bufs, sems = refs[2 * count + 1 + len(rows) : -1], refs[-1]
    loads = [pltpu.make_async_copy(s, b, sems.at[0, i]) for i, (s, b) in enumerate(zip(srcs, bufs))]
    stores = [pltpu.make_async_copy(b, o, sems.at[1, i]) for i, (b, o) in enumerate(zip(bufs, outs))]
    for cp in loads:
        cp.start()
    for out, (row, width) in zip(small, rows):
        out[...] = own[row : row + 1, 0:width]
    for load, store in zip(loads, stores):
        load.wait()
        store.start()
    for cp in stores:
        cp.wait()


def hand_over(arrays, own, rows):
    hbm = pl.BlockSpec(memory_space=pltpu.HBM)
    vmem = pl.BlockSpec(memory_space=pltpu.VMEM)
    outs = pl.pallas_call(
        partial(hand_over_kernel, len(arrays), rows),
        out_shape=[jax.ShapeDtypeStruct(a.shape, a.dtype) for a in arrays]
        + [jax.ShapeDtypeStruct((1, w), F32) for _, w in rows],
        in_specs=[hbm] * len(arrays) + [vmem],
        out_specs=[hbm] * len(arrays) + [vmem] * len(rows),
        scratch_shapes=[pltpu.VMEM(a.shape, a.dtype) for a in arrays] + [pltpu.SemaphoreType.DMA((2, len(arrays)))],
        compiler_params=pltpu.CompilerParams(vmem_limit_bytes=60 << 20),
        name="hand_over",
    )(*arrays, own)
    return outs[: len(arrays)], outs[len(arrays) :]


def local_fast(x_heads, cotangent, doc_starts, smalls, shards):
    norm_gain, conv_weight, decay_bias, admit_bias, decay_rate, feed_gain = smalls
    seq_count = lax.axis_size("seq")
    dev_count = seq_count * lax.axis_size("dp")
    row_count, tok_count, model = cotangent.shape
    flat = row_count * tok_count
    lru, taps = shards[0].shape[1], conv_weight.shape[1]
    positions = lax.axis_index("seq") * tok_count + jnp.arange(tok_count + 16, dtype=jnp.int32)
    since_ext = since_start(doc_starts, positions)
    since = jnp.broadcast_to(since_ext.reshape(-1, 1), (since_ext.size, LANE))
    small = small_parts(norm_gain, conv_weight, decay_bias, admit_bias, decay_rate, feed_gain)
    vec, full, kept = forward_pass(x_heads, small, since, shards, seq_count, STARTS)
    input_grad, own, block, grads = backward_pass(
        cotangent.reshape(flat, model), since, vec, full, kept, [s.shape for s in shards], seq_count
    )
    per_model, per_lru = model // dev_count, lru // dev_count
    rows = ((0, per_model), (2, per_lru), (3, per_lru), (4, per_lru), (1, per_model), (9, per_lru))
    block = block.reshape(row_count, tok_count, model)
    big, small = hand_over([block, input_grad, *grads], own, rows)
    small = [v.reshape(-1) for v in small]
    return (
        big[0],
        big[1],
        small[0],
        big[2],
        big[3],
        own[5 : 5 + taps, :per_lru].T,
        big[4],
        small[1],
        big[5],
        small[2],
        small[3],
        big[6],
        small[4],
        big[7],
        big[8],
        big[9],
        small[5] * (1.0 / float(flat * dev_count)),
    )


def local(
    x_heads,
    cotangent,
    doc_starts,
    norm_gain,
    gelu_weight,
    input_weight,
    conv_weight,
    decay_weight,
    decay_bias,
    admit_weight,
    admit_bias,
    decay_rate,
    mixer_output,
    feed_gain,
    feed_gate,
    feed_up,
    feed_down,
):
    seq_count = lax.axis_size("seq")
    dev_count = seq_count * lax.axis_size("dp")
    seq_at = lax.axis_index("seq")
    row_count, tok_count, model = cotangent.shape
    flat = row_count * tok_count
    lru = gelu_weight.shape[1]
    feed = feed_gate.shape[1]
    taps = conv_weight.shape[1]
    rim = taps - 1

    smalls = (norm_gain, conv_weight, decay_bias, admit_bias, decay_rate, feed_gain)
    shards = (
        gelu_weight, input_weight, decay_weight, admit_weight, mixer_output, feed_gate, feed_up, feed_down,
    )
    if fast_shapes(shards, seq_count, lax.axis_size("dp"), row_count, tok_count):
        return local_fast(x_heads, cotangent, doc_starts, smalls, shards)
    packed = lax.all_gather(pack_small(smalls), ALL, axis=0, tiled=True).astype(F32)
    parts = split_small(packed, [v.size for v in smalls])
    gain_one = parts[0].reshape(-1)
    conv_taps = parts[1].reshape(lru, taps)
    decay_shift, admit_shift, rate_vec, gain_two = [p.reshape(-1) for p in parts[2:]]

    gelu_input = gather_rows(jnp.concatenate([gelu_weight, input_weight], axis=1))
    decay_admit = gather_rows(jnp.concatenate([decay_weight, admit_weight], axis=1))
    mixer_full = gather_rows(mixer_output)
    gate_up = gather_rows(jnp.concatenate([feed_gate, feed_up], axis=1))
    down_full = gather_rows(feed_down)

    stream = lax.all_to_all(x_heads, "seq", split_axis=1, concat_axis=2, tiled=True)
    stream_in = stream.reshape(flat, model).astype(F32)
    normed_one, norm_one_pull = jax.vjp(rms_norm, stream_in, gain_one)
    normed_low = normed_one.astype(BF16)
    both = dot(normed_low, gelu_input)
    gelu_vals, gelu_pull = jax.vjp(smooth_gate, both[:, :lru])
    branch = both[:, lru:].astype(BF16).reshape(row_count, tok_count, lru)
    halo = shift_seq(branch[:, tok_count - rim :, :], 1, seq_count)
    extended = jnp.concatenate([halo, branch], axis=1).astype(F32)
    positions = seq_at * tok_count + jnp.arange(tok_count + rim, dtype=jnp.int32)
    since_ext = since_start(doc_starts, positions)
    since_here = since_ext[:, :tok_count]
    conv_vals = jnp.zeros((row_count, tok_count, lru), F32)
    for k in range(taps):
        window = extended[:, rim - k : rim - k + tok_count, :]
        conv_vals = conv_vals + conv_taps[:, k] * window * (since_here >= k)[..., None].astype(F32)
    conv_low = conv_vals.astype(BF16)
    conv_flat = conv_low.reshape(flat, lru)
    gates = dot(conv_flat, decay_admit)
    decay_pre = (gates[:, :lru] + decay_shift).reshape(row_count, tok_count, lru)
    admit_pre = (gates[:, lru:] + admit_shift).reshape(row_count, tok_count, lru)
    reset_mask = (since_here == 0).astype(F32)[..., None]

    def coefs(dp, ap, cv, rv):
        return coefficients(dp, ap, cv, rv, reset_mask)

    (decay_eff, update, decay_vals), coef_pull = jax.vjp(
        coefs, decay_pre, admit_pre, conv_low.astype(F32), rate_vec
    )
    decay_prod, local_state = lax.associative_scan(compose, (decay_eff, update), axis=1)
    ends = jnp.stack([decay_prod[:, -1], local_state[:, -1]])
    all_ends = lax.all_gather(ends, "seq", axis=0)
    carry = jnp.zeros((row_count, lru), F32)
    carry_in = carry
    for i in range(seq_count - 1):
        carry = all_ends[i, 0] * carry + all_ends[i, 1]
        carry_in = jnp.where(seq_at == i + 1, carry, carry_in)
    state = local_state + decay_prod * carry_in[:, None, :]
    state_flat = state.reshape(flat, lru)
    mixed_low = (state_flat * gelu_vals).astype(BF16)
    middle = stream_in + dot(mixed_low, mixer_full)
    normed_two, norm_two_pull = jax.vjp(rms_norm, middle, gain_two)
    normed_two_low = normed_two.astype(BF16)
    gate_up_pre = dot(normed_two_low, gate_up)
    gate_act, gate_pull = jax.vjp(smooth_gate, gate_up_pre[:, :feed])
    up_vals = gate_up_pre[:, feed:]
    hidden_low = (gate_act * up_vals).astype(BF16)
    block_output = (middle + dot(hidden_low, down_full)).astype(BF16)
    block_output = block_output.reshape(row_count, tok_count, model)

    cot = cotangent.reshape(flat, model)
    down_grad = scatter_rows(outer_sum(hidden_low, cot))
    grad_hidden = back_prod(cot, down_full)
    grad_gate = gate_pull(grad_hidden * up_vals)[0].astype(BF16)
    grad_up = (grad_hidden * gate_act).astype(BF16)
    grad_gu = jnp.concatenate([grad_gate, grad_up], axis=1)
    gate_up_grad = scatter_rows(outer_sum(normed_two_low, grad_gu))
    grad_mid_norm, gain_two_grad = norm_two_pull(back_prod(grad_gu, gate_up))
    grad_middle = cot.astype(F32) + grad_mid_norm
    grad_out = grad_middle.astype(BF16)
    mixer_grad = scatter_rows(outer_sum(mixed_low, grad_out))
    grad_mixed = back_prod(grad_out, mixer_full)
    grad_gelu = gelu_pull(grad_mixed * state_flat)[0].astype(BF16)
    direct = (grad_mixed * gelu_vals).reshape(row_count, tok_count, lru)
    decay_next = jnp.concatenate([decay_eff[:, 1:, :], jnp.ones_like(decay_eff[:, :1, :])], axis=1)
    tail_prod, tail_state = lax.associative_scan(
        compose, (decay_next, direct), axis=1, reverse=True
    )
    back_ends = lax.all_gather(decay_eff[:, 0] * tail_state[:, 0], "seq", axis=0)
    back = jnp.zeros((row_count, lru), F32)
    back_in = back
    for i in range(seq_count - 1, 0, -1):
        back = all_ends[i, 0] * back + back_ends[i]
        back_in = jnp.where(seq_at == i - 1, back, back_in)
    adjoint = tail_state + tail_prod * back_in[:, None, :]
    state_prev = jnp.concatenate([carry_in[:, None, :], state[:, :-1, :]], axis=1)
    decay_pre_grad, admit_pre_grad, conv_direct, rate_grad = coef_pull(
        (adjoint * state_prev, adjoint, jnp.zeros_like(decay_vals))
    )
    grad_decay = decay_pre_grad.reshape(flat, lru).astype(BF16)
    grad_admit = admit_pre_grad.reshape(flat, lru).astype(BF16)
    grad_da = jnp.concatenate([grad_decay, grad_admit], axis=1)
    decay_admit_grad = scatter_rows(outer_sum(conv_flat, grad_da))
    decay_b_grad = jnp.sum(grad_decay, axis=0, dtype=F32)
    admit_b_grad = jnp.sum(grad_admit, axis=0, dtype=F32)
    grad_conv = (conv_direct.reshape(flat, lru) + back_prod(grad_da, decay_admit)).astype(BF16)
    grad_conv = grad_conv.reshape(row_count, tok_count, lru)
    grad_conv_wide = grad_conv.astype(F32)
    tap_grads = []
    for k in range(taps):
        window = extended[:, rim - k : rim - k + tok_count, :]
        mask = (since_here >= k)[..., None].astype(F32)
        tap_grads.append(jnp.sum(grad_conv_wide * window * mask, axis=(0, 1)))
    conv_grad = jnp.stack(tap_grads, axis=1)
    rim_after = shift_seq(grad_conv[:, :rim, :], -1, seq_count)
    grad_ext = jnp.concatenate([grad_conv, rim_after], axis=1).astype(F32)
    branch_grad = jnp.zeros((row_count, tok_count, lru), F32)
    for k in range(taps):
        ahead = (since_ext[:, k : k + tok_count] >= k)[..., None].astype(F32)
        branch_grad = branch_grad + conv_taps[:, k] * grad_ext[:, k : k + tok_count, :] * ahead
    branch_grad_low = branch_grad.reshape(flat, lru).astype(BF16)
    grad_gi = jnp.concatenate([grad_gelu, branch_grad_low], axis=1)
    gelu_input_grad = scatter_rows(outer_sum(normed_low, grad_gi))
    grad_in_norm, gain_one_grad = norm_one_pull(back_prod(grad_gi, gelu_input))
    input_grad_tok = (grad_middle + grad_in_norm).astype(BF16)
    input_grad_tok = input_grad_tok.reshape(row_count, tok_count, model)
    input_grad = lax.all_to_all(input_grad_tok, "seq", split_axis=2, concat_axis=1, tiled=True)
    gate_term = jnp.sum(decay_vals, axis=(0, 1)) / float(flat * dev_count)
    small_grads = (
        gain_one_grad,
        conv_grad,
        decay_b_grad,
        admit_b_grad,
        rate_grad,
        gain_two_grad,
        gate_term,
    )
    packed_grads = jnp.concatenate([g.reshape(dev_count, -1) for g in small_grads], axis=1)
    reduced = lax.psum_scatter(packed_grads, ALL, scatter_dimension=0, tiled=True)
    own = split_small(reduced, [g.size // dev_count for g in small_grads])
    return (
        block_output,
        input_grad,
        own[0].reshape(-1),
        gelu_input_grad[:, :lru],
        gelu_input_grad[:, lru:],
        own[1].reshape(-1, taps),
        decay_admit_grad[:, :lru],
        own[2].reshape(-1),
        decay_admit_grad[:, lru:],
        own[3].reshape(-1),
        own[4].reshape(-1),
        mixer_grad,
        own[5].reshape(-1),
        gate_up_grad[:, :feed],
        gate_up_grad[:, feed:],
        down_grad,
        own[6].reshape(-1),
    )


def solution(mesh):
    rows = P(ALL, None)
    vec = P(ALL)
    placed = (
        P("dp", None, "seq"),
        P("dp", "seq", None),
        P("dp", None),
        vec,
        rows,
        rows,
        rows,
        rows,
        vec,
        rows,
        vec,
        vec,
        rows,
        vec,
        rows,
        rows,
        rows,
    )
    outs = (
        P("dp", "seq", None),
        P("dp", None, "seq"),
        vec,
        rows,
        rows,
        rows,
        rows,
        vec,
        rows,
        vec,
        vec,
        rows,
        vec,
        rows,
        rows,
        rows,
        vec,
    )
    return jax.shard_map(local, mesh=mesh, in_specs=placed, out_specs=outs, check_vma=False)
```

```python
from functools import partial

import jax
import jax.numpy as jnp
import numpy as np
from jax import lax
from jax.experimental import pallas as pl
from jax.experimental.pallas import tpu as pltpu
from jax.sharding import PartitionSpec as P

EPSILON = 1e-06
DECAY_SCALE = 8.0
ALL = ("seq", "dp")
F32 = jnp.float32
BF16 = jnp.bfloat16
GELU_C = 0.7978845608028654


class Names:
    def __getattr__(self, name):
        return name


N = Names()
GATHER_PACE = 1
STARTS = (0, 0, 1, 1, 2, 3, 4, 5, 6, 7, 8, 9)


def rms_norm(values, gain_vec):
    return (
        values * lax.rsqrt(jnp.mean(values * values, axis=-1, keepdims=True) + EPSILON) * gain_vec
    )


def smooth_gate(values):
    return jax.nn.gelu(values, approximate=True)


def compose(earlier, latter):
    return (earlier[0] * latter[0], latter[0] * earlier[1] + latter[1])


def since_start(doc_starts, positions):
    begins = jnp.max(
        jnp.where(doc_starts[:, None, :] <= positions[None, :, None], doc_starts[:, None, :], 0),
        axis=-1,
    )
    return positions[None, :] - begins


def coefficients(decay_pre, admit_pre, conv_vals, rate_vec, reset_mask):
    recall = jax.nn.sigmoid(decay_pre)
    admit_vals = jax.nn.sigmoid(admit_pre)
    log_decay = -DECAY_SCALE * recall * jax.nn.softplus(-rate_vec)
    decay_vals = jnp.exp(log_decay)
    keep_mask = 1.0 - reset_mask
    scale_in = reset_mask + keep_mask * jnp.sqrt(-jnp.expm1(2.0 * log_decay))
    return (decay_vals * keep_mask, scale_in * admit_vals * conv_vals, decay_vals)


def dot(left, right):
    return jnp.dot(left, right, preferred_element_type=F32)


def outer_sum(left, right):
    return lax.dot_general(left, right, (((0,), (0,)), ((), ())), preferred_element_type=F32)


def back_prod(grad_rows, weight):
    return lax.dot_general(
        grad_rows, weight, (((1,), (1,)), ((), ())), preferred_element_type=F32
    )


def gather_rows(shard):
    return lax.all_gather(shard, ALL, axis=0, tiled=True)


def scatter_rows(partial):
    return lax.psum_scatter(partial.astype(BF16), ALL, scatter_dimension=0, tiled=True).astype(F32)


def shift_seq(values, step, seq_count):
    pairs = [(i, i + step) for i in range(seq_count) if 0 <= i + step < seq_count]
    return lax.ppermute(values, "seq", pairs)


def pack_small(pieces):
    return jnp.concatenate([p.reshape(1, -1) for p in pieces], axis=1)


def split_small(packed, widths):
    out, at = [], 0
    for width in widths:
        out.append(packed[:, at : at + width])
        at += width
    return out


MESH = pl.DeviceIdType.MESH
PLANE = 2


def fast_shapes(shards, seq_count, dp_count, row_count, tok_count):
    if dp_count != 2 * PLANE * PLANE or seq_count < 2 or row_count != 2 or tok_count != 128:
        return False
    return all(s.shape[0] in (32, 48, 96) and s.shape[1] % 512 == 0 for s in shards)


class Place:
    def __init__(self, seq_count):
        self.nz = seq_count
        self.z = lax.axis_index("seq")
        self.d = lax.axis_index("dp")
        self.c = lax.rem(self.d, 2)
        self.b = lax.rem(self.d // 2, 2)
        self.a = self.d // 4
        self.core = (self.z, self.d + 1 - 2 * self.c)
        self.peer = {
            "b": (self.z, self.d + 2 - 4 * self.b),
            "a": (self.z, self.d + 4 - 8 * self.a),
        }

    def at(self, z):
        return (z, self.d)

    def greet(self):
        barrier = pltpu.get_barrier_semaphore()
        others = [self.core, self.peer["a"], self.peer["b"]]
        others += [self.at(lax.rem(self.z + o, self.nz)) for o in range(1, self.nz)]
        for other in others:
            pl.semaphore_signal(barrier, inc=1, device_id=other, device_id_type=MESH)
        pl.semaphore_wait(barrier, len(others))


def step_cols(width):
    part = 7 * (width // LANE) // 24 * LANE
    return {"A": (0, part), "B": (part, 2 * part), "C": (2 * part, width)}


def chunk_list(shapes):
    chunks = []
    for i, (rows, cols) in enumerate(shapes):
        wide = min(cols, 3072)
        tall = rows if wide < 3072 and rows <= 48 else (48 if wide < 3072 else 16)
        for c0 in range(0, cols, wide):
            for r0 in range(0, rows, tall):
                chunks.append((i, r0, tall, c0, wide))
    return chunks


class Gather:
    def __init__(self, place, outs, chunks, send, recv, starts):
        self.p, self.outs, self.chunks = place, outs, chunks
        self.send, self.recv, self.starts = send, recv, starts
        self.started = []
        nz = place.nz
        self.depth = nz + 4

    def view(self, k, z, a, b, c, route):
        i, r0, nr, c0, nc = self.chunks[k]
        lo, hi = (0, nc) if route is None else step_cols(nc)[route]
        full = slice(None)
        one = lambda v: full if v is None else pl.ds(v, 1)
        return self.outs[i].at[
            one(z), one(a), one(b), one(c), pl.ds(r0, nr), pl.ds(c0 + lo, hi - lo)
        ]

    def copy(self, k, view, s_at, r_at, dev):
        return pltpu.make_async_remote_copy(
            view, view, self.send.at[k, s_at], self.recv.at[k, r_at], device_id=dev, device_id_type=MESH
        )

    def put(self, k, view, s_at, r_at, dev, cond=None):
        cp = self.copy(k, view, s_at, r_at, dev)
        if cond is None:
            cp.start()
        else:
            pl.when(cond)(cp.start)
        self.started.append((cp, cond))

    def take(self, k, view, r_at, cond=None):
        cp = self.copy(k, view, 0, r_at, self.p.core)
        if cond is None:
            cp.wait_recv()
        else:
            pl.when(cond)(cp.wait_recv)

    def sem(self, route, phase, z=0):
        nz = self.p.nz
        slot = {"first": 0, "up": 1, "down": 1 + nz, "mid": 1 + 2 * nz, "last": 1 + 3 * nz}[phase]
        return {"A": 0, "B": 1, "C": 2}[route] * (1 + 4 * nz) + slot + z

    @staticmethod
    def sem_count(nz):
        return 3 * (1 + 4 * nz) + 1

    def order(self, k, route):
        if route == "C":
            return ("a", "b") if k % 2 else ("b", "a")
        return ("b", "a") if route == "A" else ("a", "b")

    def z_unit(self, k, route, z):
        p = self.p
        first = self.order(k, route)[0]
        a = None if route != "C" and first == "a" else p.a
        b = None if route != "C" and first == "b" else p.b
        return self.view(k, z, a, b, p.c, route)

    def z_own(self, k, route):
        p = self.p
        unit = self.z_unit(k, route, p.z)
        self.put(k, unit, self.sem(route, "up", p.z), self.sem(route, "up", p.z), p.at(p.z + 1), p.z < p.nz - 1)
        self.put(k, unit, self.sem(route, "down", p.z), self.sem(route, "down", p.z), p.at(p.z - 1), p.z > 0)
        self.after(k, route, p.z, None)

    def after(self, k, route, z, cond):
        p = self.p
        first, second = self.order(k, route)
        dim = first if route == "C" else second
        name = "mid" if route == "C" else "last"
        self.put(k, self.z_unit(k, route, z), self.sem(route, name, z), self.sem(route, name, z), p.peer[dim], cond)

    def z_hop(self, k, route, h):
        p = self.p
        low, high = p.z - h, p.z + h
        has_low, has_high = low >= 0, high < p.nz
        low_at, high_at = jnp.maximum(low, 0), jnp.minimum(high, p.nz - 1)
        unit = self.z_unit(k, route, low_at)
        self.take(k, unit, self.sem(route, "up", low_at), has_low)
        if h < p.nz - 1:
            self.put(k, unit, self.sem(route, "up", low_at), self.sem(route, "up", low_at), p.at(p.z + 1), has_low & (p.z < p.nz - 1))
        self.after(k, route, low_at, has_low)
        unit = self.z_unit(k, route, high_at)
        self.take(k, unit, self.sem(route, "down", high_at), has_high)
        if h < p.nz - 1:
            self.put(k, unit, self.sem(route, "down", high_at), self.sem(route, "down", high_at), p.at(p.z - 1), has_high & (p.z > 0))
        self.after(k, route, high_at, has_high)

    def c_last(self, k, z, cond):
        p = self.p
        first, second = self.order(k, "C")
        a = None if first == "a" else p.a
        b = None if first == "b" else p.b
        peer_a = 1 - p.a if first == "a" else p.a
        peer_b = 1 - p.b if first == "b" else p.b
        self.take(k, self.view(k, z, peer_a, peer_b, p.c, "C"), self.sem("C", "mid", z), cond)
        self.put(k, self.view(k, z, a, b, p.c, "C"), self.sem("C", "last", z), self.sem("C", "last", z), p.peer[second], cond)

    def c_last_hop(self, k, h):
        p = self.p
        if h == 0:
            self.c_last(k, p.z, None)
            return
        low, high = p.z - h, p.z + h
        self.c_last(k, jnp.maximum(low, 0), low >= 0)
        self.c_last(k, jnp.minimum(high, p.nz - 1), high < p.nz)

    def stage(self, k, s):
        p, nz = self.p, self.p.nz
        if s == 0:
            for route in "AB":
                first = self.order(k, route)[0]
                at = self.sem(route, "first")
                self.put(k, self.view(k, p.z, p.a, p.b, p.c, route), at, at, p.peer[first])
            self.z_own(k, "C")
        if s == 1:
            for route in "AB":
                first = self.order(k, route)[0]
                a = 1 - p.a if first == "a" else p.a
                b = 1 - p.b if first == "b" else p.b
                self.take(k, self.view(k, p.z, a, b, p.c, route), self.sem(route, "first"))
                self.z_own(k, route)
        if 1 <= s < nz:
            self.z_hop(k, "C", s)
        if 2 <= s <= nz:
            self.z_hop(k, "A", s - 1)
            self.z_hop(k, "B", s - 1)
        if 2 <= s < nz + 2:
            self.c_last_hop(k, s - 2)
        if s == nz + 2:
            for z in range(nz):
                for route in "ABC":
                    second = self.order(k, route)[1]
                    a = 1 - p.a if second == "a" else None
                    b = 1 - p.b if second == "b" else None
                    self.take(k, self.view(k, z, a, b, p.c, route), self.sem(route, "last", z))
            at = self.sem_count(nz) - 1
            self.put(k, self.view(k, None, None, None, p.c, None), at, at, p.core)
        if s == nz + 3:
            at = self.sem_count(nz) - 1
            self.take(k, self.view(k, None, None, None, 1 - p.c, None), at)

    def tick(self, t):
        for k in range(len(self.chunks)):
            s = t - self.starts[k]
            if 0 <= s < GATHER_PACE * self.depth and s % GATHER_PACE == 0:
                self.stage(k, s // GATHER_PACE)

    def ticks(self):
        return max(self.starts) + GATHER_PACE * (self.depth - 1) + 1

    def finish(self):
        for cp, cond in self.started:
            if cond is None:
                cp.wait_send()
            else:
                pl.when(cond)(cp.wait_send)


LANE = 128


def spread_constants(model, lru, dev_count):
    out = []
    for width in (model, lru):
        per = width // dev_count
        lane = np.arange(width)[None, :]
        out.append(jnp.asarray(lane % per == np.arange(LANE)[:, None], BF16))
        out.append(jnp.asarray(lane // per == np.arange(dev_count)[:, None], F32))
    return out


def small_parts(norm_gain, conv_weight, decay_bias, admit_bias, decay_rate, feed_gain):
    scale = -DECAY_SCALE * jax.nn.softplus(-decay_rate.astype(F32))
    parts = [norm_gain, feed_gain, decay_bias, admit_bias, scale, decay_rate]
    return [v.reshape(1, -1) for v in parts] + [conv_weight.T]


def pack_rows(parts, out):
    out[...] = jnp.zeros_like(out)
    gain_one, gain_two, decay_bias, admit_bias, scale, rate, taps = [v[...].astype(F32) for v in parts]
    high = scale.astype(BF16).astype(F32)
    mid = (scale - high).astype(BF16).astype(F32)
    rows = [gain_one, gain_two, decay_bias, admit_bias, high, mid, scale - high - mid, rate]
    for i, row in enumerate(rows):
        out[i : i + 1, 0 : row.shape[1]] = row
    out[8 : 8 + taps.shape[0], 0 : taps.shape[1]] = taps


def decay_terms(pre, scale):
    recall = jax.nn.sigmoid(pre)
    log_decay = recall * scale
    decay = jnp.exp(log_decay)
    y = 2.0 * log_decay
    series = 1.0 + y * (1 / 7)
    for n in (6, 5, 4, 3, 2):
        series = 1.0 + y * (1 / n) * series
    lost = jnp.where(y > -0.35, -y * series, 1.0 - decay * decay)
    return recall, decay, lost


def scan_block(prod, state, reverse=False):
    length = prod.shape[0]
    at = lax.broadcasted_iota(jnp.int32, prod.shape, 0)
    step = 1
    while step < length:
        inside = at < length - step if reverse else at >= step
        turn = length - step if reverse else step
        prod_far = jnp.where(inside, pltpu.roll(prod, turn, 0), 1.0)
        state_far = jnp.where(inside, pltpu.roll(state, turn, 0), 0.0)
        state = prod * state_far + state
        prod = prod * prod_far
        step *= 2
    return prod, state


def lanes(c, width=LANE):
    return pl.ds(pl.multiple_of(c * width, width), width)


def loop(count, body):
    def step(i, carry):
        body(i)
        return carry

    lax.fori_loop(0, count, step, 0)


def stream_tiles(count, fetch, use):
    for cp in fetch(0, 0):
        cp.start()

    def step(j, carry):
        slot = lax.rem(j, 2)

        @pl.when(j + 1 < count)
        def _():
            for cp in fetch(j + 1, 1 - slot):
                cp.start()

        for cp in fetch(j, slot):
            cp.wait()
        use(j, slot)
        return carry

    lax.fori_loop(0, count, step, 0)


def mat(value):
    return value.reshape(-1, value.shape[-1])


class Forward:
    def __init__(self, refs, place, weights):
        self.__dict__.update(refs)
        self.p, self.weights = place, weights
        self.tok = self.xs.shape[1]
        self.rows = self.xs.shape[0]
        self.flat = self.rows * self.tok
        self.lru = self.gelu_pre.shape[1]
        self.model = self.xs.shape[2]
        self.feed = self.hidden.shape[1]
        self.stores = []

    def save(self, name):
        cp = pltpu.make_async_copy(getattr(self, name), self.keep[name], self.keep_sem.at[len(self.stores)])
        cp.start()
        self.stores.append(cp)

    def fetch(self, i, buf, sem, starts, width):
        def copies(j, slot):
            out = []
            for n, start in enumerate(starts):
                src = self.weights[i].at[:, :, :, :, :, pl.ds(pl.multiple_of(start + j * width, LANE), width)]
                dst = buf.at[slot, :, :, :, :, :, pl.ds(n * width, width)]
                out.append(pltpu.make_async_copy(src, dst, sem.at[slot, n]))
            return out

        return copies

    def vectors(self):
        cp = pltpu.make_async_copy(self.small_all, self.small_vm, self.misc_sem.at[0])
        cp.start()
        cp.wait()
        nz = self.p.nz

        def spread(row, hot, mask):
            vals = self.small_vm[:, :, row, :].reshape(nz * 8, LANE).astype(BF16)
            wide = jnp.dot(vals, hot[...], preferred_element_type=F32)
            return jnp.sum(wide * mask[...], axis=0, keepdims=True)

        for row in range(2):
            self.vec[row : row + 1, 0 : self.model] = spread(row, self.hot_m, self.mask_m)
        for row in range(2, 12):
            self.vec[row : row + 1, :] = spread(row, self.hot_l, self.mask_l)
        self.vec[4:5, :] = self.vec[4:5, :] + self.vec[5:6, :] + self.vec[6:7, :]

    def norm(self, load, count, gain_row, out):
        gain = self.vec[gain_row : gain_row + 1, 0 : self.model]

        def body(i):
            v = load(i)
            q = lax.rsqrt(jnp.mean(v * v, axis=-1, keepdims=True) + EPSILON)
            out[pl.ds(pl.multiple_of(i * 32, 32), 32), :] = (v * q * gain).astype(BF16)

        loop(count, body)

    def norm_one(self):
        per = self.tok // 32

        def main(i):
            return self.xs[i // per, pl.ds(pl.multiple_of(lax.rem(i, per) * 32, 32), 32), :].astype(F32)

        self.norm(main, self.flat // 32, 0, self.normed.at[0 : self.flat])
        self.norm(
            lambda i: self.halo_x[...].reshape(2 * 16, self.model).astype(F32),
            1,
            0,
            self.normed.at[self.flat : self.flat + 32],
        )
        self.save(N.normed_main)
        self.save(N.xs)

    def gelu_side(self):
        def use(j, slot):
            res = jnp.dot(self.normed[0 : self.flat, :], mat(self.w_gi[slot]), preferred_element_type=F32)
            self.gelu_pre[:, lanes(j, 512)] = res

        stream_tiles(self.lru // 512, self.fetch(0, self.w_gi, self.w_sem, (0,), 512), use)
        self.save(N.gelu_pre)

    def branch_side(self):
        half = self.lru // 512

        def use_two(j, slot):
            res = jnp.dot(self.normed[...], mat(self.w_gi[slot]), preferred_element_type=F32).astype(BF16)
            self.branch[:, lanes(j, 512)] = res

        stream_tiles(half, self.fetch(0, self.w_gi, self.w_sem, (self.lru,), 512), use_two)

        def conv(c):
            for r in range(self.rows):
                at = slice(r * self.tok, (r + 1) * self.tok)
                head = self.branch[self.flat + 16 * r : self.flat + 16 * (r + 1), lanes(c)].astype(F32)
                wide = jnp.concatenate([head, self.branch[at, lanes(c)].astype(F32)], axis=0)
                since = self.since[pl.ds(r * (self.tok + 16), self.tok), :]
                total = jnp.zeros((self.tok, LANE), F32)
                for k in range(4):
                    moved = wide if k == 0 else pltpu.roll(wide, k, 0)
                    tap = self.vec[8 + k : 9 + k, lanes(c)]
                    total = total + tap * moved[16:] * (since >= k).astype(F32)
                self.conv[at, lanes(c)] = total.astype(BF16)

        loop(self.lru // LANE, conv)
        self.save(N.branch)
        self.save(N.conv)

    def gates(self, first, count):
        self.sums[...] = jnp.zeros_like(self.sums) if first == 0 else self.sums[...]

        def use(j, slot):
            self.tile[...] = jnp.dot(self.conv[...], mat(self.w_da[slot]), preferred_element_type=F32)
            base = (first + j) * 4

            def block(i):
                c = base + i
                gate_sum = jnp.zeros((1, LANE), F32)
                for r in range(self.rows):
                    at = slice(r * self.tok, (r + 1) * self.tok)
                    pre = self.tile[at, lanes(i)] + self.vec[2:3, lanes(c)]
                    admit_pre = self.tile[at, lanes(i + 4)] + self.vec[3:4, lanes(c)]
                    self.decay_pre[at, lanes(c)] = pre
                    self.admit_pre[at, lanes(c)] = admit_pre
                    recall, decay, lost = decay_terms(pre, self.vec[4:5, lanes(c)])
                    since = self.since[pl.ds(r * (self.tok + 16), self.tok), :]
                    reset = (since == 0).astype(F32)
                    keep = 1.0 - reset
                    scale_in = reset + keep * jnp.sqrt(lost)
                    update = scale_in * jax.nn.sigmoid(admit_pre) * self.conv[at, lanes(c)].astype(F32)
                    prod, state = scan_block(decay * keep, update)
                    self.prod[at, lanes(c)] = prod
                    self.state[at, lanes(c)] = state
                    self.ends[self.p.z, r : r + 1, lanes(c)] = prod[self.tok - 1 :, :]
                    self.ends[self.p.z, 8 + r : 9 + r, lanes(c)] = state[self.tok - 1 :, :]
                    gate_sum = gate_sum + jnp.sum(decay, axis=0, keepdims=True)
                self.sums[0:1, lanes(c)] = gate_sum

            loop(4, block)

        starts = (first * 512, self.lru + first * 512)
        stream_tiles(count, self.fetch(1, self.w_da, self.w_sem, starts, 512), use)

    def gates_saved(self):
        self.save(N.decay_pre)
        self.save(N.admit_pre)
        self.save(N.sums)

    def send_ends(self):
        p = self.p
        self.end_moves = []
        for o in range(1, p.nz):
            view = self.ends.at[p.z]
            cp = pltpu.make_async_remote_copy(
                view, view, self.e_send.at[o - 1], self.e_recv.at[o - 1],
                device_id=p.at(lax.rem(p.z + o, p.nz)), device_id_type=MESH,
            )
            cp.start()
            self.end_moves.append(cp)

    def mix(self):
        p = self.p
        for o in range(1, p.nz):
            view = self.ends.at[lax.rem(p.z + p.nz - o, p.nz)]
            pltpu.make_async_remote_copy(
                view, view, self.e_send.at[o - 1], self.e_recv.at[o - 1],
                device_id=p.core, device_id_type=MESH,
            ).wait_recv()

        def block(c):
            carry = jnp.zeros((8, LANE), F32)
            into = carry
            for i in range(p.nz - 1):
                carry = self.ends[i, 0:8, lanes(c)] * carry + self.ends[i, 8:16, lanes(c)]
                into = jnp.where(p.z == i + 1, carry, into)
            self.carry[:, lanes(c)] = into
            for r in range(self.rows):
                at = slice(r * self.tok, (r + 1) * self.tok)
                state = self.state[at, lanes(c)] + self.prod[at, lanes(c)] * into[r : r + 1, :]
                self.state[at, lanes(c)] = state
                gelu = smooth_gate(self.gelu_pre[at, lanes(c)])
                self.mixed[at, lanes(c)] = (state * gelu).astype(BF16)

        loop(self.lru // LANE, block)
        self.save(N.state)
        self.save(N.carry)
        self.save(N.ends)
        self.save(N.mixed)

        def use(j, slot):
            res = jnp.dot(self.mixed[...], mat(self.w_mx[slot]), preferred_element_type=F32)
            x = self.xs[:, :, lanes(j, 512)].astype(F32).reshape(self.flat, 512)
            self.middle[:, lanes(j, 512)] = x + res

        stream_tiles(self.model // 512, self.fetch(2, self.w_mx, self.w_sem, (0,), 512), use)
        self.norm(
            lambda i: self.middle[pl.ds(pl.multiple_of(i * 32, 32), 32), :], self.flat // 32, 1, self.normed_two
        )
        self.save(N.middle)
        self.save(N.normed_two)

    def gate_up(self, first, count):
        def use(j, slot):
            res = jnp.dot(self.normed_two[...], mat(self.w_gu[slot]), preferred_element_type=F32)
            gate, up = res[:, 0:512], res[:, 512:1024]
            at = lanes(first + j, 512)
            self.gate_pre[:, at] = gate
            self.up[:, at] = up
            self.hidden[:, at] = (smooth_gate(gate) * up).astype(BF16)

        starts = (first * 512, self.feed + first * 512)
        stream_tiles(count, self.fetch(3, self.w_gu, self.w_sem, starts, 512), use)

    def gate_saved(self):
        self.save(N.gate_pre)
        self.save(N.up)
        self.save(N.hidden)

    def finish(self):
        for cp in self.stores:
            cp.wait()
        for cp in self.end_moves:
            cp.wait_send()


KEEP = (
    N.xs, N.normed_main, N.gelu_pre, N.branch, N.conv, N.decay_pre, N.admit_pre, N.sums, N.state, N.carry,
    N.ends, N.mixed, N.middle, N.normed_two, N.gate_pre, N.up, N.hidden,
)


def forward_kernel(seq_count, starts, chunks, names, n_keep, *refs):
    refs = list(refs)
    x_ref, since, hot_m, mask_m, hot_l, mask_l = refs[:6]
    parts = refs[6:13]
    srcs = refs[13:21]
    at = 21
    small_all, vec = refs[at : at + 2]
    outs = refs[at + 2 : at + 7]
    keep = dict(zip(KEEP, refs[at + 7 : at + 7 + n_keep]))
    at += 7 + n_keep
    table = dict(zip(names, refs[at : at + len(names)]))
    p = Place(seq_count)
    table.update(
        small_all=small_all, vec=vec, since=since, hot_m=hot_m, mask_m=mask_m, hot_l=hot_l, mask_l=mask_l, keep=keep,
    )
    table[N.normed_main] = table[N.normed].at[0 : table[N.conv].shape[0]]
    f = Forward(table, p, outs)
    one = pl.ds
    copies = []
    own_sem = table[N.own_sem]
    k = 0
    for out, count in zip(outs, (2, 2, 1, 2, 1)):
        col = 0
        for _ in range(count):
            cols = srcs[k].shape[-1]
            dst = out.at[one(p.z, 1), one(p.a, 1), one(p.b, 1), one(p.c, 1), :, one(col, cols)]
            copies.append(pltpu.make_async_copy(srcs[k], dst, own_sem.at[k]))
            col += cols
            k += 1
    tok, feat = f.tok, x_ref.shape[2]
    here = one(pl.multiple_of(p.z * feat, LANE), feat)
    copies.append(pltpu.make_async_copy(x_ref.at[:, one(p.z * tok, tok), :], f.xs.at[:, :, here], own_sem.at[k]))
    pack_rows(parts, table[N.small_own])
    own_rows = table[N.small_own].reshape(1, 1, 16, LANE)
    copies.append(pltpu.make_async_copy(own_rows, small_all.at[one(p.z, 1), one(p.d, 1)], own_sem.at[k + 1]))
    for cp in copies:
        cp.start()

    def halo(z):
        return x_ref.at[:, one(pl.multiple_of(jnp.maximum(z * tok - 16, 0), 16), 16), :]

    own_halo = lambda: pltpu.make_async_copy(halo(p.z), f.halo_x.at[:, :, here], own_sem.at[k + 2])

    @pl.when(p.z > 0)
    def _():
        own_halo().start()

    @pl.when(p.z == 0)
    def _():
        f.halo_x[...] = jnp.zeros_like(f.halo_x)

    f.ends[...] = jnp.zeros_like(f.ends)
    f.sums[...] = jnp.zeros_like(f.sums)
    p.greet()
    x_moves = []

    def x_copy(o):
        to = lax.rem(p.z + o, p.nz)
        return pltpu.make_async_remote_copy(
            x_ref.at[:, one(pl.multiple_of(to * tok, 16), tok), :], f.xs.at[:, :, here], table[N.x_send].at[o - 1],
            table[N.x_recv].at[o - 1], device_id=p.at(to), device_id_type=MESH,
        )

    def h_copy(o):
        to = lax.rem(p.z + o, p.nz)
        return to > 0, pltpu.make_async_remote_copy(
            halo(to), f.halo_x.at[:, :, here], table[N.h_send].at[o - 1],
            table[N.h_recv].at[o - 1], device_id=p.at(to), device_id_type=MESH,
        )

    for o in range(1, p.nz):
        x_copy(o).start()
        cond, cp = h_copy(o)
        pl.when(cond)(cp.start)
    for cp in copies:
        cp.wait()
    s_send, s_recv = table[N.s_send], table[N.s_recv]
    s_moves = []

    def small_put(view, at, dev):
        cp = pltpu.make_async_remote_copy(view, view, s_send.at[at], s_recv.at[at], device_id=dev, device_id_type=MESH)
        cp.start()
        s_moves.append(cp)

    def small_view(d, n):
        return small_all.at[one(p.z, 1), one(d, n)]

    small_put(small_view(p.d, 1), 0, p.core)
    g = Gather(p, outs, chunks, table[N.send], table[N.recv], starts)
    last = [max(starts[i] for i in range(len(chunks)) if chunks[i][0] == w) + GATHER_PACE * (g.depth - 1) for w in range(5)]
    at = last[0]
    da_at = max(last[1], at + 2)
    plan = {
        3: [f.vectors, f.norm_one],
        at: [f.branch_side],
        at + 1: [f.gelu_side],
        da_at: [lambda: f.gates(0, 1)],
        da_at + 1: [lambda: f.gates(1, 1)],
        da_at + 2: [lambda: f.gates(2, 1), f.send_ends, f.gates_saved],
        max(last[2], da_at + 3): [f.mix],
    }
    for n in range(3):
        plan.setdefault(max(last[3], da_at + 4) + n, []).append(partial(f.gate_up, 2 * n, 2))
    plan[max(plan)].append(f.gate_saved)
    ticks = max(g.ticks(), max(plan) + 1)
    for t in range(ticks):
        g.tick(t)
        if t == 0:
            s_moves[0].wait_recv()
            small_put(small_view(p.d - p.c, 2), 1, p.peer["b"])
        if t == 1:
            s_moves[1].wait_recv()
            small_put(small_view(4 * p.a, 4), 2, p.peer["a"])
        if t == 2:
            s_moves[2].wait_recv()
            for o in range(1, p.nz):
                small_put(small_view(0, 8), 2 + o, p.at(lax.rem(p.z + o, p.nz)))
        if t == 3:
            for cp in s_moves[3:]:
                cp.wait_recv()
            for o in range(1, p.nz):
                x_copy(o).wait_recv()
                pl.when(p.z > 0)(h_copy(o)[1].wait_recv)

            @pl.when(p.z > 0)
            def _():
                own_halo().wait()

        for action in plan.get(t, ()):
            action()
    for cp in s_moves:
        cp.wait_send()
    for o in range(1, p.nz):
        x_copy(o).wait_send()
        cond, cp = h_copy(o)
        pl.when(cond)(cp.wait_send)
    f.finish()
    g.finish()


def forward_pass(x_heads, small, since, shards, seq_count, starts):
    groups = ((0, 1), (2, 3), (4,), (5, 6), (7,))
    rows_cols = [(shards[g[0]].shape[0], sum(shards[i].shape[1] for i in g)) for g in groups]
    chunks = chunk_list(rows_cols)
    row_count, row_len, feat = x_heads.shape
    tok, model = row_len // seq_count, feat * seq_count
    flat = row_count * tok
    lru, feed = rows_cols[0][1] // 2, rows_cols[3][1] // 2
    nz = seq_count
    srcs = [s.reshape(1, 1, 1, 1, *s.shape) for s in shards]
    hbm = pl.BlockSpec(memory_space=pltpu.HBM)
    vmem = pl.BlockSpec(memory_space=pltpu.VMEM)
    keep_shapes = dict(
        xs=((row_count, tok, model), BF16),
        normed_main=((flat, model), BF16),
        gelu_pre=((flat, lru), F32),
        branch=((flat + 32, lru), BF16),
        conv=((flat, lru), BF16),
        decay_pre=((flat, lru), F32),
        admit_pre=((flat, lru), F32),
        sums=((8, lru), F32),
        state=((flat, lru), F32),
        carry=((8, lru), F32),
        ends=((nz, 16, lru), F32),
        mixed=((flat, lru), BF16),
        middle=((flat, model), F32),
        normed_two=((flat, model), BF16),
        gate_pre=((flat, feed), F32),
        up=((flat, feed), F32),
        hidden=((flat, feed), BF16),
    )
    scratch = {n: pltpu.VMEM(*s) for n, s in keep_shapes.items() if n != "normed_main"}
    dma = pltpu.SemaphoreType.DMA
    sems = Gather.sem_count(nz)
    scratch.update(
        normed=pltpu.VMEM((flat + 32, model), BF16),
        halo_x=pltpu.VMEM((row_count, 16, model), BF16),
        small_vm=pltpu.VMEM((nz, 8, 16, LANE), F32),
        small_own=pltpu.VMEM((16, LANE), F32),
        prod=pltpu.VMEM((flat, lru), F32),
        tile=pltpu.VMEM((flat, 1024), F32),
        w_gi=pltpu.VMEM((2, nz, 2, 2, 2, rows_cols[0][0], 512), BF16),
        w_da=pltpu.VMEM((2, nz, 2, 2, 2, rows_cols[1][0], 1024), BF16),
        w_mx=pltpu.VMEM((2, nz, 2, 2, 2, rows_cols[2][0], 512), BF16),
        w_gu=pltpu.VMEM((2, nz, 2, 2, 2, rows_cols[3][0], 1024), BF16),
        w_sem=dma((2, 2)),
        keep_sem=dma((len(KEEP),)),
        misc_sem=dma((1,)),
        own_sem=dma((len(srcs) + 3,)),
        x_send=dma((nz,)),
        x_recv=dma((nz,)),
        h_send=dma((nz,)),
        h_recv=dma((nz,)),
        s_send=dma((nz + 3,)),
        s_recv=dma((nz + 3,)),
        e_send=dma((nz,)),
        e_recv=dma((nz,)),
        send=dma((len(chunks), sems)),
        recv=dma((len(chunks), sems)),
    )
    names = list(scratch)
    out_shape = [jax.ShapeDtypeStruct((nz, 8, 16, LANE), F32), jax.ShapeDtypeStruct((16, lru), F32)]
    out_shape += [jax.ShapeDtypeStruct((nz, PLANE, PLANE, 2, r, c), BF16) for r, c in rows_cols]
    out_shape += [jax.ShapeDtypeStruct(*keep_shapes[n]) for n in KEEP]
    outs = pl.pallas_call(
        partial(forward_kernel, nz, starts, chunks, names, len(KEEP)),
        out_shape=out_shape,
        in_specs=[hbm] + [vmem] * 20,
        out_specs=[hbm, vmem] + [hbm] * (5 + len(KEEP)),
        scratch_shapes=[scratch[n] for n in names],
        compiler_params=pltpu.CompilerParams(
            collective_id=0, has_side_effects=True, vmem_limit_bytes=61 << 20
        ),
        name="forward_pass",
    )(
        x_heads,
        since,
        *spread_constants(model, lru, nz * 8),
        *small,
        *srcs,
    )
    return outs[1], outs[2:7], dict(zip(KEEP, outs[7:]))


PACE = 2
C_RING, RING, SLOTS, PIECE = 8 * PACE, 5 * PACE, 2 * PACE, 128


class Chunk:
    def __init__(self, name, lhs, rhs, rows, width, first):
        self.name, self.lhs, self.rhs = name, lhs, rhs
        self.rows, self.width, self.first = rows, width, first
        self.across = width // PIECE


class Reduce:
    NAMES = (N.C, N.YA, N.YB, N.YC, N.PC, N.UA, N.DA, N.UB, N.DB, N.UC, N.DC, N.XA, N.XB)
    PIECES = {"A": pl.ds(0, 3), "B": pl.ds(3, 3), "C": pl.ds(6, 6)}

    @staticmethod
    def shapes(nz):
        plane = PLANE
        a, b, c = (nz, 1, plane), (nz, plane, 1), (nz, 1, 1)
        own = (1, 1, 1)
        lead = dict(YA=a, YB=b, YC=b, PC=c, UA=a, DA=a, UB=b, DB=b, UC=c, DC=c, XA=own, XB=own)
        out = {n: (RING, *v, 6 if n[1] == N.C else 3, 16, PIECE) for n, v in lead.items()}
        out["C"] = (C_RING, nz, plane, plane, 12, 16, PIECE)
        return out

    def __init__(self, place, bufs, full, send, recv, produce, deliver):
        self.p, self.bufs, self.full = place, bufs, full
        self.send, self.recv = send, recv
        self.produce, self.deliver = produce, deliver
        self.started = {}
        self.depth = place.nz + 4

    def buf(self, k, name):
        return self.bufs[name].at[k % (C_RING if name == "C" else RING)]

    def order(self, k):
        return ("a", "b") if k % 2 else ("b", "a")

    def part(self, k, route, z, a, b):
        full = slice(None)
        one = lambda v: full if v is None else v if isinstance(v, slice) else pl.ds(v, 1)
        return self.buf(k, "C").at[one(z), one(a), one(b), self.PIECES[route]]

    def copy(self, k, name, src, dst, dev):
        at = self.NAMES.index(name)
        return pltpu.make_async_remote_copy(
            src, dst, self.send.at[k, at], self.recv.at[k, at], device_id=dev, device_id_type=MESH
        )

    def put(self, k, name, src, dst, dev):
        make = lambda: self.copy(k, name, src(), dst(), dev)
        make().start()
        self.started.setdefault(k, []).append((make, None))

    def z_put(self, k, route, way, z):
        p = self.p
        name = ("U" if way > 0 else "D") + route
        span = slice(z + 1, p.nz) if way > 0 else slice(0, z)

        def make():
            a = p.a if route != "B" else None
            b = p.b if route != "A" else None
            return self.copy(k, name, self.part(k, route, span, a, b), self.buf(k, name).at[span], p.at(z + way))

        make().start()
        self.started.setdefault(k, []).append((make, z))

    def take(self, k, name, dst):
        self.copy(k, name, dst, dst, self.p.core).wait_recv()

    def add(self, into, other):
        def one(t):
            into[t] = into[t] + other[t]

        loop(into.shape[0], one)

    def wave(self, k, route, s):
        p, nz = self.p, self.p.nz
        low, high = s - 1, nz - s

        def gather(name, span):
            got = self.buf(k, name).at[span]
            self.take(k, name, got)
            a = p.a if route != "B" else None
            b = p.b if route != "A" else None
            self.add(self.part(k, route, span, a, b), got)

        @pl.when(p.z == low)
        def _():
            if low > 0:
                gather("U" + route, slice(low, nz))
            if low < nz - 1:
                self.z_put(k, route, 1, low)

        @pl.when(p.z == high)
        def _():
            if high < nz - 1:
                gather("D" + route, slice(0, high + 1))
            if high > 0:
                self.z_put(k, route, -1, high)

    def yc(self, k):
        buf = self.buf(k, "YC")
        if self.order(k)[1] == "b":
            return buf
        nz, plane, _, n, r, w = buf.shape
        return buf.reshape(nz, 1, plane, n, r, w)

    def stage(self, k, s):
        p, nz = self.p, self.p.nz
        if s == 0:
            self.produce(k)
            slot = self.full.at[k % SLOTS]
            self.put(k, "C", lambda: slot.at[:, :, :, 1 - p.c], lambda: self.buf(k, "C"), p.core)
        if s == 1:
            self.take(k, "C", self.buf(k, "C"))
            into, own = self.buf(k, "C"), self.full.at[k % SLOTS]

            def one(t):
                for a in range(PLANE):
                    for b in range(PLANE):
                        into[t, a, b] = into[t, a, b] + own[t, a, b, p.c]

            loop(nz, one)
            self.put(k, "YA", lambda: self.part(k, "A", None, 1 - p.a, None), lambda: self.buf(k, "YA"), p.peer["a"])
            self.put(k, "YB", lambda: self.part(k, "B", None, None, 1 - p.b), lambda: self.buf(k, "YB"), p.peer["b"])
            q = self.order(k)[1]
            src = lambda: self.part(k, "C", None, 1 - p.a if q == "a" else None, 1 - p.b if q == "b" else None)
            self.put(k, "YC", src, lambda: self.yc(k), p.peer[q])
        if s == 2:
            make, _ = self.started[k].pop(0)
            make().wait_send()
            self.take(k, "YA", self.buf(k, "YA"))
            self.add(self.part(k, "A", None, p.a, None), self.buf(k, "YA"))
            self.take(k, "YB", self.buf(k, "YB"))
            self.add(self.part(k, "B", None, None, p.b), self.buf(k, "YB"))
            first, q = self.order(k)
            self.take(k, "YC", self.yc(k))
            self.add(self.part(k, "C", None, p.a if q == "a" else None, p.b if q == "b" else None), self.yc(k))
            src = lambda: self.part(
                k, "C", None, 1 - p.a if first == "a" else p.a, 1 - p.b if first == "b" else p.b
            )
            self.put(k, "PC", src, lambda: self.buf(k, "PC"), p.peer[first])
        if s == 3:
            self.take(k, "PC", self.buf(k, "PC"))
            self.add(self.part(k, "C", None, p.a, p.b), self.buf(k, "PC"))
        if 2 <= s <= nz + 1:
            self.wave(k, "A", s - 1)
            self.wave(k, "B", s - 1)
        if 3 <= s <= nz + 2:
            self.wave(k, "C", s - 2)
        if s == nz + 1:
            self.put(k, "XA", lambda: self.part(k, "A", p.z, p.a, 1 - p.b), lambda: self.buf(k, "XA"), p.peer["b"])
            self.put(k, "XB", lambda: self.part(k, "B", p.z, 1 - p.a, p.b), lambda: self.buf(k, "XB"), p.peer["a"])
        if s == nz + 2:
            self.take(k, "XA", self.buf(k, "XA"))
            self.take(k, "XB", self.buf(k, "XB"))
            self.deliver(k)
        if s == nz + 3:
            for make, z in self.started.pop(k):
                if z is None:
                    make().wait_send()
                else:

                    @pl.when(p.z == z)
                    def _():
                        make().wait_send()

    def result(self, k, route):
        p = self.p
        block = self.part(k, route, p.z, p.a, p.b)[0, 0, 0].astype(F32)
        if route != "C":
            block = block + self.buf(k, "X" + route)[0, 0, 0].astype(F32)
        return block

    def tick(self, t, count):
        for k in range(count):
            if 0 <= t - k < PACE * self.depth and (t - k) % PACE == 0:
                self.stage(k, (t - k) // PACE)

    def ticks(self, count):
        return count + PACE * (self.depth - 1)


class Backward:
    def __init__(self, refs, place):
        self.__dict__.update(refs)
        self.p = place
        self.flat, self.model = self.cot.shape
        self.lru, self.feed = self.q.shape[1], self.hidden.shape[1]
        self.rows = 2
        self.tok = self.flat // self.rows
        self.outs_going = {}
        c = Chunk
        wide, tall, full = 6 * PIECE, 4 * PIECE, 2 * PIECE
        self.chunks = [c(N.dn, N.hidden, N.cot, 96, full, j) for j in range(0, self.model, full)]
        self.chunks += [c(N.gu, N.normed_two, N.ggu, 32, wide, j) for j in range(0, 2 * self.feed, wide)]
        self.chunks += [c(N.mx, N.mixed, N.grad_out, 48, tall, j) for j in range(0, self.model, tall)]
        self.chunks += [c(N.gi, N.normed, N.ggi, 32, wide, j) for j in range(0, self.lru, wide)]
        self.chunks += [c(N.da, N.conv, N.hidden, 48, tall, j) for j in range(0, 2 * self.lru, tall)]
        self.chunks += [c(N.gi, N.normed, N.ggi, 32, wide, j) for j in range(self.lru, 2 * self.lru, wide)]

    def first_of(self, name, at=0):
        return min(k for k, ch in enumerate(self.chunks) if ch.name == name and ch.first >= at)

    def load(self, names):
        for name in names:
            self.loader(name).start()

    def loader(self, name):
        src, dst, at = self.loads[name]
        return pltpu.make_async_copy(src, dst, self.load_sem.at[at])

    def ready(self, names):
        for name in names:
            self.loader(name).wait()

    def produce(self, k):
        ch = self.chunks[k]
        lhs, rhs = getattr(self, ch.lhs), getattr(self, ch.rhs)
        span = 8 * ch.rows
        slot = self.full.at[k % SLOTS]

        def one(z):
            left = lhs[:, pl.ds(pl.multiple_of(z * span, LANE), span)]
            for n in range(0, ch.across, 2):
                right = rhs[:, ch.first + n * PIECE : ch.first + (n + 2) * PIECE]
                val = outer_sum(left, right).astype(BF16).reshape(8, ch.rows // 16, 16, 2 * PIECE)
                for i in range(ch.rows // 16):
                    for m in range(2):
                        piece = val[:, i, :, m * PIECE : (m + 1) * PIECE]
                        slot[z, :, :, :, i * ch.across + n + m] = piece.reshape(2, 2, 2, 16, PIECE)

        loop(self.p.nz, one)

    def out_copies(self, k):
        ch = self.chunks[k]
        copies = []
        for i in range(ch.rows // 16):
            for n in range(ch.across):
                at = i * ch.across + n
                col = ch.first + n * PIECE
                names = self.out_names[ch.name]
                width = self.weight_outs[names[0]].shape[1]
                out = self.weight_outs[names[col // width]]
                dst = out.at[pl.ds(i * 16, 16), pl.ds(col % width, PIECE)]
                copies.append(pltpu.make_async_copy(self.staged.at[k % 2, at], dst, self.out_sem.at[k % 2, at]))
        return copies

    def deliver(self, k):
        if k >= 2:
            for cp in self.out_copies(k - 2):
                cp.wait()
        for route, at, n in (("A", 0, 3), ("B", 3, 3), ("C", 6, 6)):
            self.staged[k % 2, at : at + n] = self.reduce.result(k, route)
        for cp in self.out_copies(k):
            cp.start()

    def by_z(self, weight, buf, sem, extra=None, parts=1):
        width = weight.shape[-1] // parts

        def copies(j, slot):
            z = j // parts
            rows = weight.shape[4]
            src = weight.at[z, :, :, :, :, pl.ds(pl.multiple_of(lax.rem(j, parts) * width, LANE), width)]
            dst = buf.at[slot, :, :, :, 0:rows, 0:width]
            out = [pltpu.make_async_copy(src, dst, sem.at[slot, 0])]
            return out + (extra(j, slot) if extra else [])

        return copies

    def feed_back(self):
        span = self.feed // self.p.nz
        half = lambda slot: pl.ds(pl.multiple_of(slot * span, LANE), span)

        def extra(j, slot):
            at = pl.ds(pl.multiple_of(j * span, LANE), span)
            return [
                pltpu.make_async_copy(self.gate_pre.at[:, at], self.gelu_pre.at[:, half(slot)], self.w_sem.at[slot, 1]),
                pltpu.make_async_copy(self.up.at[:, at], self.state.at[:, half(slot)], self.w_sem.at[slot, 2]),
            ]

        def use(j, slot):
            self.wide_tile[...] = back_prod(self.cot[...], mat(self.w_dn[slot]))
            out = self.q.at[:, 0 : self.model]
            start = jnp.where(j == 0, self.middle[...], out[...])
            left = self.hidden[:, pl.ds(pl.multiple_of(j * span, LANE), span)]
            out[...] = start + jnp.dot(left, mat(self.w_dn[slot]), preferred_element_type=F32)
            at = pl.ds(pl.multiple_of(j * span, LANE), span)
            at_up = pl.ds(pl.multiple_of(self.feed + j * span, LANE), span)

            def block(i):
                rows = pl.ds(pl.multiple_of(i * 16, 16), 16)
                grad = self.wide_tile[rows, :]
                gate = self.gelu_pre[rows, half(slot)]
                act, slope = gelu_both(gate)
                self.ggu[rows, at] = (slope * self.state[rows, half(slot)] * grad).astype(BF16)
                self.ggu[rows, at_up] = (act * grad).astype(BF16)

            loop(self.flat // 16, block)

        self.ready([N.middle])
        stream_tiles(self.p.nz, self.by_z(self.dn, self.w_dn, self.w_sem, extra), use)
        self.grad_out[...] = self.q[:, 0 : self.model].astype(BF16)
        self.block_copy().start()

    def block_copy(self):
        return pltpu.make_async_copy(self.grad_out, self.block_out, self.block_sem.at[0])

    def norm_back(self, values, grads, gain_row, extra, out):
        gain = self.vec[gain_row : gain_row + 1, 0 : self.model]

        def block(i, total):
            rows = pl.ds(pl.multiple_of(i * 16, 16), 16)
            v, e = values(rows), grads(rows)
            back, terms = rms_back(v, gain, e)
            out(rows, extra(rows) + back)
            return total + jnp.sum(terms, axis=0, keepdims=True)

        total = lax.fori_loop(0, self.flat // 16, block, jnp.zeros((1, self.model), F32))
        self.sums[gain_row : gain_row + 1, 0 : self.model] = total

    def norm_two_back(self):
        half = self.feed

        def use(j, slot):
            left = self.ggu[:, pl.ds(pl.multiple_of(lax.rem(j, 2) * half, LANE), half)]
            rows = self.gu.shape[4]
            res = back_prod(left, mat(self.w_big[slot, :, :, :, 0:rows, 0:half]))
            at = lanes(j // 2, 8 * rows)

            @pl.when(lax.rem(j, 2) == 0)
            def _():
                self.q[:, at] = res

            @pl.when(lax.rem(j, 2) == 1)
            def _():
                self.q[:, at] = self.q[:, at] + res

        stream_tiles(2 * self.p.nz, self.by_z(self.gu, self.w_big, self.w_sem, None, 2), use)
        self.block_copy().wait()

        def out(rows, val):
            self.middle[rows, :] = val
            self.grad_out[rows, :] = val.astype(BF16)

        self.norm_back(
            lambda rows: self.middle[rows, :],
            lambda rows: self.q[rows, 0 : self.model],
            1,
            lambda rows: self.cot[rows, :].astype(F32),
            out,
        )

    def scan_back(self):
        self.ready([N.gelu_pre, N.state, N.decay_pre])
        rows = self.mx.shape[4]
        span = 8 * rows

        def use(j, slot):
            self.wide_tile[:, 0:span] = back_prod(self.grad_out[...], mat(self.w_big[slot, :, :, :, 0:rows, 0 : self.model]))

            def block(i):
                c = j * (span // LANE) + i
                for r in range(self.rows):
                    at = slice(r * self.tok, (r + 1) * self.tok)
                    grad = self.wide_tile[at, lanes(i)]
                    act, slope = gelu_both(self.gelu_pre[at, lanes(c)])
                    self.ggi[at, lanes(c)] = (slope * grad * self.state[at, lanes(c)]).astype(BF16)
                    _, decay, _ = decay_terms(self.decay_pre[at, lanes(c)], self.vec[4:5, lanes(c)])
                    since = self.since[r * (self.tok + 16) : r * (self.tok + 16) + self.tok, :]
                    eff = decay * (since != 0).astype(F32)
                    place = lax.broadcasted_iota(jnp.int32, eff.shape, 0)
                    after = jnp.where(place < self.tok - 1, pltpu.roll(eff, self.tok - 1, 0), 1.0)
                    prod, tail = scan_block(after, act * grad, reverse=True)
                    self.q[at, lanes(c)] = prod
                    self.gelu_pre[at, lanes(c)] = tail
                    self.tails[self.p.z, r : r + 1, lanes(c)] = eff[0:1, :] * tail[0:1, :]

            loop(span // LANE, block)

        stream_tiles(self.p.nz, self.by_z(self.mx, self.w_big, self.w_sem), use)

    def tail_copy(self, o, recv):
        p = self.p
        view = self.tails.at[lax.rem(p.z + p.nz - o, p.nz) if recv else p.z]
        return pltpu.make_async_remote_copy(
            view, view, self.t_send.at[o - 1], self.t_recv.at[o - 1],
            device_id=p.at(lax.rem(p.z + o, p.nz)), device_id_type=MESH,
        )

    def send_tails(self):
        for o in range(1, self.p.nz):
            self.tail_copy(o, False).start()

    def tails_here(self):
        for o in range(1, self.p.nz):
            self.tail_copy(o, True).wait_recv()
        self.ready([N.admit_pre, N.conv])

    def gates_back(self, third):
        p = self.p
        count = self.lru // LANE // 3

        def block(i):
            c = third * count + i
            tail = jnp.zeros((8, LANE), F32)
            into = tail
            for i in range(p.nz - 1, 0, -1):
                tail = self.ends[i, 0:8, lanes(c)] * tail + self.tails[i, :, lanes(c)]
                into = jnp.where(p.z == i - 1, tail, into)
            scale = self.vec[4:5, lanes(c)]
            rate_sum = jnp.zeros((1, LANE), F32)
            decay_sum, admit_sum = rate_sum, rate_sum
            for r in range(self.rows):
                at = slice(r * self.tok, (r + 1) * self.tok)
                adjoint = self.gelu_pre[at, lanes(c)] + self.q[at, lanes(c)] * into[r : r + 1, :]
                recall, decay, lost = decay_terms(self.decay_pre[at, lanes(c)], scale)
                root = jnp.sqrt(lost)
                since = self.since[r * (self.tok + 16) : r * (self.tok + 16) + self.tok, :]
                reset = (since == 0).astype(F32)
                keep = 1.0 - reset
                conv = self.conv[at, lanes(c)].astype(F32)
                admit = jax.nn.sigmoid(self.admit_pre[at, lanes(c)])
                state = self.state[at, lanes(c)]
                place = lax.broadcasted_iota(jnp.int32, state.shape, 0)
                before = jnp.where(place > 0, pltpu.roll(state, 1, 0), self.carry[r : r + 1, lanes(c)])
                scale_in = reset + keep * root
                grad_log = adjoint * keep * (before * decay - admit * conv * decay * decay / root)
                decay_low = (grad_log * scale * recall * (1.0 - recall)).astype(BF16)
                admit_low = (adjoint * scale_in * conv * admit * (1.0 - admit)).astype(BF16)
                self.hidden[at, lanes(c)] = decay_low
                self.hidden[at, pl.ds(pl.multiple_of(self.lru + c * LANE, LANE), LANE)] = admit_low
                self.admit_pre[at, lanes(c)] = adjoint * scale_in * admit
                rate_sum = rate_sum + jnp.sum(grad_log * recall, axis=0, keepdims=True)
                decay_sum = decay_sum + jnp.sum(decay_low.astype(F32), axis=0, keepdims=True)
                admit_sum = admit_sum + jnp.sum(admit_low.astype(F32), axis=0, keepdims=True)
            self.sums[2:3, lanes(c)] = decay_sum
            self.sums[3:4, lanes(c)] = admit_sum
            self.sums[4:5, lanes(c)] = rate_sum * (DECAY_SCALE * jax.nn.sigmoid(-self.vec[7:8, lanes(c)]))

        loop(count, block)

    def conv_grads(self):
        rows = self.da.shape[4]
        span = 8 * rows

        def use(j, slot):
            at = lanes(j, span)
            res = back_prod(self.hidden[...], mat(self.w_big[slot]))
            total = (self.admit_pre[:, at] + res).astype(BF16)
            self.grad_conv[:, :, at] = total.reshape(self.rows, self.tok, span)

        stream_tiles(self.p.nz, self.by_z(self.da, self.w_big, self.w_sem), use)

    def rim_copy(self):
        p = self.p
        return pltpu.make_async_remote_copy(
            self.grad_conv.at[:, 0:16, :], self.rim, self.r_send.at[0], self.r_recv.at[0],
            device_id=p.at(jnp.maximum(p.z - 1, 0)), device_id_type=MESH,
        )

    def send_rim(self):
        pl.when(self.p.z > 0)(lambda: self.rim_copy().start())

    def conv_back(self):
        p = self.p
        pl.when(p.z < p.nz - 1)(lambda: self.rim_copy().wait_recv())
        self.ready([N.branch])
        long = self.tok + 16

        def block(c):
            taps = [jnp.zeros((1, LANE), F32)] * 4
            for r in range(self.rows):
                at = slice(r * self.tok, (r + 1) * self.tok)
                since = self.since[r * long : (r + 1) * long, :]
                grad = self.grad_conv[r, :, lanes(c)].astype(F32)
                wide = jnp.concatenate([grad, self.rim[r, :, lanes(c)].astype(F32)], axis=0)
                head = self.branch[self.flat + 16 * r : self.flat + 16 * (r + 1), lanes(c)].astype(F32)
                back = jnp.concatenate([head, self.branch[at, lanes(c)].astype(F32)], axis=0)
                total = jnp.zeros((self.tok, LANE), F32)
                for k in range(4):
                    seen = (since >= k).astype(F32)
                    moved = back if k == 0 else pltpu.roll(back, k, 0)
                    term = jnp.sum(grad * moved[16:] * seen[0 : self.tok], axis=0, keepdims=True)
                    taps[k] = taps[k] + term
                    ahead = wide * seen
                    ahead = ahead if k == 0 else pltpu.roll(ahead, long - k, 0)
                    total = total + self.vec[8 + k : 9 + k, lanes(c)] * ahead[0 : self.tok]
                self.ggi[at, pl.ds(pl.multiple_of(self.lru + c * LANE, LANE), LANE)] = total.astype(BF16)
            for k in range(4):
                self.sums[5 + k : 6 + k, lanes(c)] = taps[k]

        loop(self.lru // LANE, block)

    def norm_one_back(self):
        rows = self.gi.shape[4]

        def use(j, slot):
            self.q[:, lanes(j, 8 * rows)] = back_prod(self.ggi[...], mat(self.w_big[slot, :, :, :, 0:rows, :]))

        stream_tiles(self.p.nz, self.by_z(self.gi, self.w_big, self.w_sem), use)
        self.ready([N.xs])

        def out(rows, val):
            self.grad_out[rows, :] = val.astype(BF16)

        self.norm_back(
            lambda rows: self.cot[rows, :].astype(F32),
            lambda rows: self.q[rows, 0 : self.model],
            0,
            lambda rows: self.middle[rows, :],
            out,
        )

    def x_copy(self, o):
        p = self.p
        feat = self.x_out.shape[2]
        to = lax.rem(p.z + o, p.nz)
        at = pl.ds(pl.multiple_of(to * feat, LANE), feat)
        src = self.grad_out.reshape(self.rows, self.tok, self.model).at[:, :, at]
        dst = self.x_out.at[:, pl.ds(pl.multiple_of(p.z * self.tok, 16), self.tok), :]
        if o == 0:
            return pltpu.make_async_copy(src, dst, self.x_send.at[p.nz - 1])
        return pltpu.make_async_remote_copy(
            src, dst, self.x_send.at[o - 1], self.x_recv.at[o - 1], device_id=p.at(to), device_id_type=MESH
        )

    def send_x(self):
        for o in range(self.p.nz):
            self.x_copy(o).start()

    def spread_sums(self):
        nz = self.p.nz
        for row in range(10):
            hot, mask, width = (self.hot_m, self.mask_m, self.model) if row < 2 else (self.hot_l, self.mask_l, self.lru)
            vals = self.sums[row : row + 1, 0:width] if row < 9 else self.gate_sums[0:1, :]
            wide = mask[...] * vals
            cut = lax.dot_general(
                wide, hot[...].astype(F32), (((1,), (1,)), ((), ())),
                precision=lax.Precision.HIGHEST, preferred_element_type=F32,
            )
            self.s_own[:, :, :, :, row, :] = cut.reshape(nz, 2, 2, 2, LANE)

    def s_copy(self, at):
        p = self.p
        if at == 0:
            src, dst, dev = self.s_own.at[:, :, :, 1 - p.c], self.s_core, p.core
        elif at == 1:
            src, dst, dev = self.s_core.at[:, :, 1 - p.b], self.s_b, p.peer["b"]
        elif at == 2:
            src, dst, dev = self.s_b.at[:, 1 - p.a], self.s_a, p.peer["a"]
        else:
            to = lax.rem(p.z + at - 2, p.nz)
            src, dst, dev = self.s_a.at[to], self.s_z.at[at - 3], p.at(to)
        return pltpu.make_async_remote_copy(
            src, dst, self.s_send.at[at], self.s_recv.at[at], device_id=dev, device_id_type=MESH
        )

    def small_step(self, n):
        p = self.p
        if n == 0:
            self.s_own[...] = jnp.zeros_like(self.s_own)
            self.spread_sums()
            self.s_copy(0).start()
        if n == 1:
            self.s_copy(0).wait_recv()
            self.s_core[...] = self.s_core[...] + self.s_own[:, :, :, p.c]
            self.s_copy(1).start()
        if n == 2:
            self.s_copy(1).wait_recv()
            self.s_b[...] = self.s_b[...] + self.s_core[:, :, p.b]
            self.s_copy(2).start()
        if n == 3:
            self.s_copy(2).wait_recv()
            self.s_a[...] = self.s_a[...] + self.s_b[:, p.a]
            for o in range(1, p.nz):
                self.s_copy(2 + o).start()
        if n == 4:
            total = self.s_a[p.z]
            for o in range(1, p.nz):
                self.s_copy(2 + o).wait_recv()
                total = total + self.s_z[o - 1]
            self.small_out[...] = total

    def finish(self):
        p = self.p
        count = len(self.chunks)
        for k in (count - 2, count - 1):
            for cp in self.out_copies(k):
                cp.wait()
        for o in range(1, p.nz):
            self.tail_copy(o, False).wait_send()
            self.x_copy(o).wait()
            self.s_copy(2 + o).wait_send()
        self.x_copy(0).wait()
        for at in range(3):
            self.s_copy(at).wait_send()
        pl.when(p.z > 0)(lambda: self.rim_copy().wait_send())


def gelu_both(x):
    inner = GELU_C * (x + 0.044715 * x * x * x)
    t = jnp.tanh(inner)
    slope = 0.5 * (1.0 + t) + 0.5 * x * (1.0 - t * t) * GELU_C * (1.0 + 3 * 0.044715 * x * x)
    return 0.5 * x * (1.0 + t), slope


def rms_back(values, gain, grad):
    q = lax.rsqrt(jnp.mean(values * values, axis=-1, keepdims=True) + EPSILON)
    inner = jnp.mean(values * gain * grad, axis=-1, keepdims=True)
    back = q * gain * grad - values * (q * q * q) * inner
    return back, grad * values * q


WEIGHTS = (N.gelu, N.input, N.decay, N.admit, N.mixer, N.gate, N.up, N.down)
OUT_NAMES = dict(gi=WEIGHTS[:2], da=WEIGHTS[2:4], mx=WEIGHTS[4:5], gu=WEIGHTS[5:7], dn=WEIGHTS[7:])
LOADS = (
    N.hidden, N.cot, N.normed_two, N.middle, N.mixed, N.gelu_pre, N.state, N.decay_pre, N.admit_pre, N.conv,
    N.branch, N.normed, N.xs,
)


def backward_kernel(seq_count, names, hbm_names, vmem_names, *refs):
    n_in = len(vmem_names) + len(hbm_names)
    given = dict(zip(vmem_names + hbm_names, refs[:n_in]))
    x_out, small_out, block_out = refs[n_in : n_in + 3]
    weight_outs = dict(zip(WEIGHTS, refs[n_in + 3 : n_in + 11]))
    table = dict(zip(names, refs[n_in + 11 :]))
    p = Place(seq_count)
    shared = dict(xs=N.cot, normed=N.normed_two)
    loads = {}
    for i, name in enumerate(LOADS):
        dst = table[shared.get(name, name)]
        loads[name] = (given.pop(name + "_hbm"), dst, i)
    table.update(given)
    table[N.normed] = table[N.normed_two]
    table[N.grad_conv] = table[N.mixed].reshape(2, table[N.mixed].shape[0] // 2, table[N.mixed].shape[1])
    table.update(x_out=x_out, small_out=small_out, block_out=block_out, weight_outs=weight_outs, out_names=OUT_NAMES, loads=loads)
    f = Backward(table, p)
    late = (N.xs, N.normed, N.gelu_pre, N.state)
    f.load(n for n in LOADS if n not in late)
    f.rim[...] = jnp.zeros_like(f.rim)
    f.tails[...] = jnp.zeros_like(f.tails)
    p.greet()
    f.reduce = Reduce(
        p, {n: table["ring_" + n] for n in Reduce.NAMES}, table[N.full], table[N.send], table[N.recv],
        f.produce, f.deliver,
    )
    count = len(f.chunks)
    f.ready([N.hidden, N.cot])

    def reload_cot():
        f.load(late[:1])

    first = f.first_of
    gu_count = first(N.mx) - first(N.gu)
    last = first(N.gi, f.lru)
    before = {
        first(N.gu): [f.feed_back, lambda: f.load(late[2:]), lambda: f.ready([N.normed_two])],
        first(N.gu) + gu_count // 2 - 1: [f.norm_two_back, reload_cot],
        first(N.mx) - 3: [f.scan_back, f.send_tails],
        first(N.mx) - 1: [f.tails_here, lambda: f.gates_back(0)],
        first(N.mx): [lambda: f.load(late[1:2]), lambda: f.gates_back(1), lambda: f.ready([N.mixed])],
        first(N.mx) + 1: [lambda: f.gates_back(2)],
        first(N.gi): [lambda: f.ready([N.normed])],
        first(N.da): [f.conv_grads, f.send_rim],
        first(N.da) + 2: [f.conv_back],
        last: [f.norm_one_back, f.send_x, lambda: f.small_step(0)],
    }
    for n in range(1, 5):
        before[last + n] = [partial(f.small_step, n)]
    for t in range(f.reduce.ticks(count)):
        for action in before.get(t, ()):
            action()
        f.reduce.tick(t, count)
    f.finish()


def backward_pass(cot, since, vec, full, kept, shard_shapes, seq_count):
    nz = seq_count
    flat, model = cot.shape
    lru, feed = kept[N.gelu_pre].shape[1], kept[N.hidden].shape[1]
    tok = flat // 2
    vmem_vals = dict(
        vec=vec,
        since=since,
        carry=kept[N.carry],
        ends=kept[N.ends],
        gate_sums=kept[N.sums],
    )
    vmem_vals.update(zip((N.hot_m, N.mask_m, N.hot_l, N.mask_l), spread_constants(model, lru, nz * 8)))
    hbm_vals = dict(zip((N.gi, N.da, N.mx, N.gu, N.dn), full))
    hbm_vals.update(gate_pre=kept[N.gate_pre], up=kept[N.up])
    source = dict(kept, cot=cot, normed=kept[N.normed_main], xs=kept[N.xs].reshape(flat, model))
    hbm_vals.update({n + "_hbm": source[n] for n in LOADS})
    dma = pltpu.SemaphoreType.DMA
    v = pltpu.VMEM
    chunks = 24
    scratch = dict(
        hidden=v((flat, feed), BF16),
        cot=v((flat, model), BF16),
        normed_two=v((flat, model), BF16),
        middle=v((flat, model), F32),
        mixed=v((flat, lru), BF16),
        gelu_pre=v((flat, lru), F32),
        state=v((flat, lru), F32),
        decay_pre=v((flat, lru), F32),
        admit_pre=v((flat, lru), F32),
        conv=v((flat, lru), BF16),
        branch=v((flat + 32, lru), BF16),
        ggu=v((flat, 2 * feed), BF16),
        ggi=v((flat, 2 * lru), BF16),
        grad_out=v((flat, model), BF16),
        rim=v((2, 16, lru), BF16),
        q=v((flat, lru), F32),
        tails=v((nz, 8, lru), F32),
        sums=v((16, lru), F32),
        wide_tile=v((flat, feed // nz), F32),
        w_dn=v((2, 2, 2, 2, full[4].shape[4], model), BF16),
        w_big=v((2, 2, 2, 2, full[1].shape[4], 2 * lru), BF16),
        full=v((SLOTS, nz, 2, 2, 2, 12, 16, PIECE), BF16),
        staged=v((2, 12, 16, PIECE), F32),
        s_own=v((nz, 2, 2, 2, 16, LANE), F32),
        s_core=v((nz, 2, 2, 16, LANE), F32),
        s_b=v((nz, 2, 16, LANE), F32),
        s_a=v((nz, 16, LANE), F32),
        s_z=v((nz, 16, LANE), F32),
        w_sem=dma((2, 3)),
        block_sem=dma((1,)),
        load_sem=dma((len(LOADS),)),
        out_sem=dma((2, 12)),
        send=dma((chunks, len(Reduce.NAMES))),
        recv=dma((chunks, len(Reduce.NAMES))),
        t_send=dma((nz,)),
        t_recv=dma((nz,)),
        r_send=dma((1,)),
        r_recv=dma((1,)),
        x_send=dma((nz,)),
        x_recv=dma((nz,)),
        s_send=dma((nz + 3,)),
        s_recv=dma((nz + 3,)),
    )
    scratch.update({"ring_" + n: v(s, BF16) for n, s in Reduce.shapes(nz).items()})
    names = list(scratch)
    hbm = pl.BlockSpec(memory_space=pltpu.HBM)
    vmem = pl.BlockSpec(memory_space=pltpu.VMEM)
    out_shape = [
        jax.ShapeDtypeStruct((2, tok * nz, model // nz), BF16),
        jax.ShapeDtypeStruct((16, LANE), F32),
        jax.ShapeDtypeStruct((flat, model), BF16),
    ] + [jax.ShapeDtypeStruct(s, F32) for s in shard_shapes]
    outs = pl.pallas_call(
        partial(backward_kernel, nz, names, list(hbm_vals), list(vmem_vals)),
        out_shape=out_shape,
        in_specs=[vmem] * len(vmem_vals) + [hbm] * len(hbm_vals),
        out_specs=[hbm, vmem] + [hbm] * 9,
        scratch_shapes=[scratch[n] for n in names],
        compiler_params=pltpu.CompilerParams(
            collective_id=1, has_side_effects=True, vmem_limit_bytes=61 << 20
        ),
        name="backward_pass",
    )(*vmem_vals.values(), *hbm_vals.values())
    return outs[0], outs[1], outs[2], outs[3:]


def hand_over_kernel(count, rows, *refs):
    srcs, own = refs[:count], refs[count]
    outs, small = refs[count + 1 : 2 * count + 1], refs[2 * count + 1 : 2 * count + 1 + len(rows)]
    bufs, sems = refs[2 * count + 1 + len(rows) : -1], refs[-1]
    loads = [pltpu.make_async_copy(s, b, sems.at[0, i]) for i, (s, b) in enumerate(zip(srcs, bufs))]
    stores = [pltpu.make_async_copy(b, o, sems.at[1, i]) for i, (b, o) in enumerate(zip(bufs, outs))]
    for cp in loads:
        cp.start()
    for out, (row, width, factor) in zip(small, rows):
        out[...] = own[row : row + 1, 0:width] * factor
    for load, store in zip(loads, stores):
        load.wait()
        store.start()
    for cp in stores:
        cp.wait()


def hand_over(arrays, own, rows):
    hbm = pl.BlockSpec(memory_space=pltpu.HBM)
    vmem = pl.BlockSpec(memory_space=pltpu.VMEM)
    outs = pl.pallas_call(
        partial(hand_over_kernel, len(arrays), rows),
        out_shape=[jax.ShapeDtypeStruct(a.shape, a.dtype) for a in arrays]
        + [jax.ShapeDtypeStruct((1, w), F32) for _, w, _ in rows],
        in_specs=[hbm] * len(arrays) + [vmem],
        out_specs=[hbm] * len(arrays) + [vmem] * len(rows),
        scratch_shapes=[pltpu.VMEM(a.shape, a.dtype) for a in arrays] + [pltpu.SemaphoreType.DMA((2, len(arrays)))],
        compiler_params=pltpu.CompilerParams(vmem_limit_bytes=60 << 20),
        name="hand_over",
    )(*arrays, own)
    return outs[: len(arrays)], outs[len(arrays) :]


def local_fast(x_heads, cotangent, doc_starts, smalls, shards):
    norm_gain, conv_weight, decay_bias, admit_bias, decay_rate, feed_gain = smalls
    seq_count = lax.axis_size("seq")
    dev_count = seq_count * lax.axis_size("dp")
    row_count, tok_count, model = cotangent.shape
    flat = row_count * tok_count
    lru, taps = shards[0].shape[1], conv_weight.shape[1]
    positions = lax.axis_index("seq") * tok_count + jnp.arange(tok_count + 16, dtype=jnp.int32)
    since_ext = since_start(doc_starts, positions)
    since = jnp.broadcast_to(since_ext.reshape(-1, 1), (since_ext.size, LANE))
    small = small_parts(norm_gain, conv_weight, decay_bias, admit_bias, decay_rate, feed_gain)
    vec, full, kept = forward_pass(x_heads, small, since, shards, seq_count, STARTS)
    input_grad, own, block, grads = backward_pass(
        cotangent.reshape(flat, model), since, vec, full, kept, [s.shape for s in shards], seq_count
    )
    per_model, per_lru = model // dev_count, lru // dev_count
    widths = (per_model, per_model, per_lru, per_lru, per_lru)
    rows = [(row, widths[row], 1.0) for row in (0, 2, 3, 4, 1)] + [(9, per_lru, 1.0 / float(flat * dev_count))]
    block = block.reshape(row_count, tok_count, model)
    big, small = hand_over([block, input_grad, *grads], own, rows)
    small = [v.reshape(-1) for v in small]
    return (
        big[0],
        big[1],
        small[0],
        big[2],
        big[3],
        own[5 : 5 + taps, :per_lru].T,
        big[4],
        small[1],
        big[5],
        small[2],
        small[3],
        big[6],
        small[4],
        big[7],
        big[8],
        big[9],
        small[5],
    )


def local(
    x_heads,
    cotangent,
    doc_starts,
    norm_gain,
    gelu_weight,
    input_weight,
    conv_weight,
    decay_weight,
    decay_bias,
    admit_weight,
    admit_bias,
    decay_rate,
    mixer_output,
    feed_gain,
    feed_gate,
    feed_up,
    feed_down,
):
    seq_count = lax.axis_size("seq")
    dev_count = seq_count * lax.axis_size("dp")
    seq_at = lax.axis_index("seq")
    row_count, tok_count, model = cotangent.shape
    flat = row_count * tok_count
    lru = gelu_weight.shape[1]
    feed = feed_gate.shape[1]
    taps = conv_weight.shape[1]
    rim = taps - 1

    smalls = (norm_gain, conv_weight, decay_bias, admit_bias, decay_rate, feed_gain)
    shards = (
        gelu_weight, input_weight, decay_weight, admit_weight, mixer_output, feed_gate, feed_up, feed_down,
    )
    if fast_shapes(shards, seq_count, lax.axis_size("dp"), row_count, tok_count):
        return local_fast(x_heads, cotangent, doc_starts, smalls, shards)
    packed = lax.all_gather(pack_small(smalls), ALL, axis=0, tiled=True).astype(F32)
    parts = split_small(packed, [v.size for v in smalls])
    gain_one = parts[0].reshape(-1)
    conv_taps = parts[1].reshape(lru, taps)
    decay_shift, admit_shift, rate_vec, gain_two = [p.reshape(-1) for p in parts[2:]]

    gelu_input = gather_rows(jnp.concatenate([gelu_weight, input_weight], axis=1))
    decay_admit = gather_rows(jnp.concatenate([decay_weight, admit_weight], axis=1))
    mixer_full = gather_rows(mixer_output)
    gate_up = gather_rows(jnp.concatenate([feed_gate, feed_up], axis=1))
    down_full = gather_rows(feed_down)

    stream = lax.all_to_all(x_heads, "seq", split_axis=1, concat_axis=2, tiled=True)
    stream_in = stream.reshape(flat, model).astype(F32)
    normed_one, norm_one_pull = jax.vjp(rms_norm, stream_in, gain_one)
    normed_low = normed_one.astype(BF16)
    both = dot(normed_low, gelu_input)
    gelu_vals, gelu_pull = jax.vjp(smooth_gate, both[:, :lru])
    branch = both[:, lru:].astype(BF16).reshape(row_count, tok_count, lru)
    halo = shift_seq(branch[:, tok_count - rim :, :], 1, seq_count)
    extended = jnp.concatenate([halo, branch], axis=1).astype(F32)
    positions = seq_at * tok_count + jnp.arange(tok_count + rim, dtype=jnp.int32)
    since_ext = since_start(doc_starts, positions)
    since_here = since_ext[:, :tok_count]
    conv_vals = jnp.zeros((row_count, tok_count, lru), F32)
    for k in range(taps):
        window = extended[:, rim - k : rim - k + tok_count, :]
        conv_vals = conv_vals + conv_taps[:, k] * window * (since_here >= k)[..., None].astype(F32)
    conv_low = conv_vals.astype(BF16)
    conv_flat = conv_low.reshape(flat, lru)
    gates = dot(conv_flat, decay_admit)
    decay_pre = (gates[:, :lru] + decay_shift).reshape(row_count, tok_count, lru)
    admit_pre = (gates[:, lru:] + admit_shift).reshape(row_count, tok_count, lru)
    reset_mask = (since_here == 0).astype(F32)[..., None]

    def coefs(dp, ap, cv, rv):
        return coefficients(dp, ap, cv, rv, reset_mask)

    (decay_eff, update, decay_vals), coef_pull = jax.vjp(
        coefs, decay_pre, admit_pre, conv_low.astype(F32), rate_vec
    )
    decay_prod, local_state = lax.associative_scan(compose, (decay_eff, update), axis=1)
    ends = jnp.stack([decay_prod[:, -1], local_state[:, -1]])
    all_ends = lax.all_gather(ends, "seq", axis=0)
    carry = jnp.zeros((row_count, lru), F32)
    carry_in = carry
    for i in range(seq_count - 1):
        carry = all_ends[i, 0] * carry + all_ends[i, 1]
        carry_in = jnp.where(seq_at == i + 1, carry, carry_in)
    state = local_state + decay_prod * carry_in[:, None, :]
    state_flat = state.reshape(flat, lru)
    mixed_low = (state_flat * gelu_vals).astype(BF16)
    middle = stream_in + dot(mixed_low, mixer_full)
    normed_two, norm_two_pull = jax.vjp(rms_norm, middle, gain_two)
    normed_two_low = normed_two.astype(BF16)
    gate_up_pre = dot(normed_two_low, gate_up)
    gate_act, gate_pull = jax.vjp(smooth_gate, gate_up_pre[:, :feed])
    up_vals = gate_up_pre[:, feed:]
    hidden_low = (gate_act * up_vals).astype(BF16)
    block_output = (middle + dot(hidden_low, down_full)).astype(BF16)
    block_output = block_output.reshape(row_count, tok_count, model)

    cot = cotangent.reshape(flat, model)
    down_grad = scatter_rows(outer_sum(hidden_low, cot))
    grad_hidden = back_prod(cot, down_full)
    grad_gate = gate_pull(grad_hidden * up_vals)[0].astype(BF16)
    grad_up = (grad_hidden * gate_act).astype(BF16)
    grad_gu = jnp.concatenate([grad_gate, grad_up], axis=1)
    gate_up_grad = scatter_rows(outer_sum(normed_two_low, grad_gu))
    grad_mid_norm, gain_two_grad = norm_two_pull(back_prod(grad_gu, gate_up))
    grad_middle = cot.astype(F32) + grad_mid_norm
    grad_out = grad_middle.astype(BF16)
    mixer_grad = scatter_rows(outer_sum(mixed_low, grad_out))
    grad_mixed = back_prod(grad_out, mixer_full)
    grad_gelu = gelu_pull(grad_mixed * state_flat)[0].astype(BF16)
    direct = (grad_mixed * gelu_vals).reshape(row_count, tok_count, lru)
    decay_next = jnp.concatenate([decay_eff[:, 1:, :], jnp.ones_like(decay_eff[:, :1, :])], axis=1)
    tail_prod, tail_state = lax.associative_scan(
        compose, (decay_next, direct), axis=1, reverse=True
    )
    back_ends = lax.all_gather(decay_eff[:, 0] * tail_state[:, 0], "seq", axis=0)
    back = jnp.zeros((row_count, lru), F32)
    back_in = back
    for i in range(seq_count - 1, 0, -1):
        back = all_ends[i, 0] * back + back_ends[i]
        back_in = jnp.where(seq_at == i - 1, back, back_in)
    adjoint = tail_state + tail_prod * back_in[:, None, :]
    state_prev = jnp.concatenate([carry_in[:, None, :], state[:, :-1, :]], axis=1)
    decay_pre_grad, admit_pre_grad, conv_direct, rate_grad = coef_pull(
        (adjoint * state_prev, adjoint, jnp.zeros_like(decay_vals))
    )
    grad_decay = decay_pre_grad.reshape(flat, lru).astype(BF16)
    grad_admit = admit_pre_grad.reshape(flat, lru).astype(BF16)
    grad_da = jnp.concatenate([grad_decay, grad_admit], axis=1)
    decay_admit_grad = scatter_rows(outer_sum(conv_flat, grad_da))
    decay_b_grad = jnp.sum(grad_decay, axis=0, dtype=F32)
    admit_b_grad = jnp.sum(grad_admit, axis=0, dtype=F32)
    grad_conv = (conv_direct.reshape(flat, lru) + back_prod(grad_da, decay_admit)).astype(BF16)
    grad_conv = grad_conv.reshape(row_count, tok_count, lru)
    grad_conv_wide = grad_conv.astype(F32)
    tap_grads = []
    for k in range(taps):
        window = extended[:, rim - k : rim - k + tok_count, :]
        mask = (since_here >= k)[..., None].astype(F32)
        tap_grads.append(jnp.sum(grad_conv_wide * window * mask, axis=(0, 1)))
    conv_grad = jnp.stack(tap_grads, axis=1)
    rim_after = shift_seq(grad_conv[:, :rim, :], -1, seq_count)
    grad_ext = jnp.concatenate([grad_conv, rim_after], axis=1).astype(F32)
    branch_grad = jnp.zeros((row_count, tok_count, lru), F32)
    for k in range(taps):
        ahead = (since_ext[:, k : k + tok_count] >= k)[..., None].astype(F32)
        branch_grad = branch_grad + conv_taps[:, k] * grad_ext[:, k : k + tok_count, :] * ahead
    branch_grad_low = branch_grad.reshape(flat, lru).astype(BF16)
    grad_gi = jnp.concatenate([grad_gelu, branch_grad_low], axis=1)
    gelu_input_grad = scatter_rows(outer_sum(normed_low, grad_gi))
    grad_in_norm, gain_one_grad = norm_one_pull(back_prod(grad_gi, gelu_input))
    input_grad_tok = (grad_middle + grad_in_norm).astype(BF16)
    input_grad_tok = input_grad_tok.reshape(row_count, tok_count, model)
    input_grad = lax.all_to_all(input_grad_tok, "seq", split_axis=2, concat_axis=1, tiled=True)
    gate_term = jnp.sum(decay_vals, axis=(0, 1)) / float(flat * dev_count)
    small_grads = (
        gain_one_grad,
        conv_grad,
        decay_b_grad,
        admit_b_grad,
        rate_grad,
        gain_two_grad,
        gate_term,
    )
    packed_grads = jnp.concatenate([g.reshape(dev_count, -1) for g in small_grads], axis=1)
    reduced = lax.psum_scatter(packed_grads, ALL, scatter_dimension=0, tiled=True)
    own = split_small(reduced, [g.size // dev_count for g in small_grads])
    return (
        block_output,
        input_grad,
        own[0].reshape(-1),
        gelu_input_grad[:, :lru],
        gelu_input_grad[:, lru:],
        own[1].reshape(-1, taps),
        decay_admit_grad[:, :lru],
        own[2].reshape(-1),
        decay_admit_grad[:, lru:],
        own[3].reshape(-1),
        own[4].reshape(-1),
        mixer_grad,
        own[5].reshape(-1),
        gate_up_grad[:, :feed],
        gate_up_grad[:, feed:],
        down_grad,
        own[6].reshape(-1),
    )


def solution(mesh):
    rows = P(ALL, None)
    vec = P(ALL)
    placed = (
        P("dp", None, "seq"),
        P("dp", "seq", None),
        P("dp", None),
        vec,
        rows,
        rows,
        rows,
        rows,
        vec,
        rows,
        vec,
        vec,
        rows,
        vec,
        rows,
        rows,
        rows,
    )
    outs = (
        P("dp", "seq", None),
        P("dp", None, "seq"),
        vec,
        rows,
        rows,
        rows,
        rows,
        vec,
        rows,
        vec,
        vec,
        rows,
        vec,
        rows,
        rows,
        rows,
        vec,
    )
    return jax.shard_map(local, mesh=mesh, in_specs=placed, out_specs=outs, check_vma=False)
```
